32 devices in a mesh: dp: 2 (over x), rows: 4 (over y, core), cols: 4 (over z).
Axes of the slice: x: 2, y: 2, z: 4, core: 2. Of those that a mesh axis runs over, the one named last changes fastest.
Arguments:
- hidden_in: float32 [1280, 4, 1024], P('cols', 'dp', 'rows'), may hold values from -6 to 6
- lengths: int32 [4], P('dp'), may hold values from 1024 to 1280, as said below
- conv_norm: float32 [1024], P('rows'), may hold values from 0.5 to 1.5
- conv_in: float32 [1024, 3, 1024], P('rows', None, 'cols'), may hold values from -0.1875 to 0.1875
- conv_kernel: float32 [3, 1024], P(None, 'cols'), may hold values from -3.5 to 3.5
- conv_out: float32 [1024, 1024], P('cols', 'rows'), may hold values from -0.1875 to 0.1875
- conv_ffn_norm: float32 [1024], P('rows'), may hold values from 0.5 to 1.5
- conv_ffn_in: float32 [1024, 2, 4608], P('rows', None, 'cols'), may hold values from -0.1875 to 0.1875
- conv_ffn_out: float32 [4608, 1024], P('cols', 'rows'), may hold values from -0.09375 to 0.09375
- attn_norm: float32 [1024], P('rows'), may hold values from 0.5 to 1.5
- attn_q: float32 [1024, 1024], P('rows', 'cols'), may hold values from -0.1875 to 0.1875
- attn_kv: float32 [1024, 2, 512], P('rows', None, 'cols'), may hold values from -0.1875 to 0.1875
- q_gain: float32 [64], replicated, may hold values from 1 to 2
- k_gain: float32 [64], replicated, may hold values from 1 to 2
- attn_out: float32 [1024, 1024], P('cols', 'rows'), may hold values from -1.5 to 1.5
- attn_ffn_norm: float32 [1024], P('rows'), may hold values from 0.5 to 1.5
- attn_ffn_in: float32 [1024, 2, 4608], P('rows', None, 'cols'), may hold values from -0.1875 to 0.1875
- attn_ffn_out: float32 [4608, 1024], P('cols', 'rows'), may hold values from -0.09375 to 0.09375
- grad_out: float32 [1280, 4, 1024], P('cols', 'dp', 'rows'), may hold values from -6 to 6
Outputs:
- output: float32 [1280, 4, 1024], P('cols', 'dp', 'rows')
- grad_in: float32 [1280, 4, 1024], P('cols', 'dp', 'rows')
- grad_conv_norm: float32 [1024], P('rows')
- grad_conv_in: float32 [1024, 3, 1024], P('rows', None, 'cols')
- grad_conv_kernel: float32 [3, 1024], P(None, 'cols')
- grad_conv_out: float32 [1024, 1024], P('cols', 'rows')
- grad_conv_ffn_norm: float32 [1024], P('rows')
- grad_conv_ffn_in: float32 [1024, 2, 4608], P('rows', None, 'cols')
- grad_conv_ffn_out: float32 [4608, 1024], P('cols', 'rows')
- grad_attn_norm: float32 [1024], P('rows')
- grad_attn_q: float32 [1024, 1024], P('rows', 'cols')
- grad_attn_kv: float32 [1024, 2, 512], P('rows', None, 'cols')
- grad_q_gain: float32 [64], replicated
- grad_k_gain: float32 [64], replicated
- grad_attn_out: float32 [1024, 1024], P('cols', 'rows')
- grad_attn_ffn_norm: float32 [1024], P('rows')
- grad_attn_ffn_in: float32 [1024, 2, 4608], P('rows', None, 'cols')
- grad_attn_ffn_out: float32 [4608, 1024], P('cols', 'rows')
The draws below stay inside these ranges and needn't reach their ends.
Inputs may be any that keep to these rules, and one draw needn't show every extreme that they name: `lengths`: one sequence has exactly 1280 valid tokens and another exactly 1024.
All inputs are finite; a program needn't handle non-finite values.
Results may differ from the reference program's by a relative error of at most 0.028.
Values may be sent and summed in bfloat16 or wider, within the bound.
A program may use at most 192 MiB of HBM per device.

```python
import jax
import jax.numpy as jnp
from jax import lax

D = 1024
FF = 4608
H = 16
KV = 8
HD = 64
CONV = 3
LMAX = 1280
LMIN = 1024
SEQS = 4


def draw_lengths(key, part):
    key_values, key_long, key_short = jax.random.split(key, 3)
    values = jax.random.randint(key_values, (SEQS,), LMIN, LMAX + 1, dtype=jnp.int32)
    longest = jax.random.randint(key_long, (), 0, SEQS, dtype=jnp.int32)
    offset = jax.random.randint(key_short, (), 1, SEQS, dtype=jnp.int32)
    shortest = (longest + offset) % SEQS
    position_ids = jnp.arange(SEQS, dtype=jnp.int32)
    values = jnp.where(position_ids == longest, LMAX, values)
    values = jnp.where(position_ids == shortest, LMIN, values)
    return values


def steps_of(stream_key, extent, cuts, low, largest):
    gain = 1.0
    for dim, parts in cuts:
        draws = jax.random.uniform(jax.random.fold_in(jax.random.fold_in(stream_key, 6), dim), (parts,), jnp.float32, low / len(cuts), largest / len(cuts))
        gain = gain * jnp.repeat(jnp.exp(draws), extent[dim] // parts).reshape((-1,) + (1,) * (len(extent) - 1 - dim))
    return gain


def bell_draw(rng, dims, deviation, limit, pieces=(), kind=jnp.bfloat16):
    loudness = steps_of(rng, dims, pieces, -0.22, 0.18) if pieces else 1.0
    entries = jax.random.normal(rng, dims, jnp.float32) * deviation * loudness
    return jnp.minimum(jnp.maximum(entries, -limit), limit).astype(kind)


def setup_inputs(seed: int = 0) -> dict:
    streams_of = jax.random.split(jax.random.key(seed), 20)
    return {
        "hidden_in": bell_draw(streams_of[0], (LMAX, SEQS, D), 1.0, 6.0, ((0, 4), (1, 2), (2, 4)), jnp.float32),
        "lengths": draw_lengths(jax.random.fold_in(streams_of[19], 71), 0),
        "conv_norm": jnp.clip(1.0 + 0.1 * jax.random.normal(streams_of[2], (D,), jnp.float32), 0.5, 1.5),
        "conv_in": bell_draw(streams_of[3], (D, 3, D), D ** -0.5, 0.1875, ((0, 4), (2, 4)), jnp.float32),
        "conv_kernel": bell_draw(streams_of[4], (CONV, D), CONV ** -0.5, 3.5, ((1, 4),), jnp.float32),
        "conv_out": bell_draw(streams_of[5], (D, D), D ** -0.5, 0.1875, ((0, 4), (1, 4)), jnp.float32),
        "conv_ffn_norm": jnp.clip(1.0 + 0.1 * jax.random.normal(streams_of[6], (D,), jnp.float32), 0.5, 1.5),
        "conv_ffn_in": bell_draw(streams_of[7], (D, 2, FF), D ** -0.5, 0.1875, ((0, 4), (2, 4)), jnp.float32),
        "conv_ffn_out": bell_draw(streams_of[8], (FF, D), FF ** -0.5, 0.09375, ((0, 4), (1, 4)), jnp.float32),
        "attn_norm": jnp.clip(1.0 + 0.1 * jax.random.normal(streams_of[9], (D,), jnp.float32), 0.5, 1.5),
        "attn_q": bell_draw(streams_of[10], (D, H * HD), D ** -0.5, 0.1875, ((0, 4), (1, 4)), jnp.float32),
        "attn_kv": bell_draw(streams_of[11], (D, 2, KV * HD), D ** -0.5, 0.1875, ((0, 4), (2, 4)), jnp.float32),
        "q_gain": jnp.clip(jax.random.uniform(streams_of[12], (HD,), jnp.float32, 1.0, 2.0), 1.0, 2.0),
        "k_gain": jnp.clip(jax.random.uniform(streams_of[13], (HD,), jnp.float32, 1.0, 2.0), 1.0, 2.0),
        "attn_out": bell_draw(streams_of[14], (H * HD, D), (D // 64) ** -0.5, 1.5, ((0, 4), (1, 4)), jnp.float32),
        "attn_ffn_norm": jnp.clip(1.0 + 0.1 * jax.random.normal(streams_of[15], (D,), jnp.float32), 0.5, 1.5),
        "attn_ffn_in": bell_draw(streams_of[16], (D, 2, FF), D ** -0.5, 0.1875, ((0, 4), (2, 4)), jnp.float32),
        "attn_ffn_out": bell_draw(streams_of[17], (FF, D), FF ** -0.5, 0.09375, ((0, 4), (1, 4)), jnp.float32),
        "grad_out": bell_draw(streams_of[18], (LMAX, SEQS, D), 1.0, 6.0, ((0, 4), (1, 2), (2, 4)), jnp.float32),
    }


epsilon = 1e-05
rope_base = 1000000.0
highest = lax.Precision.HIGHEST

@jax.custom_vjp
def low(v):
    return lax.optimization_barrier(v.astype(jnp.bfloat16)).astype(jnp.float32)

@jax.custom_vjp
def low_back(v):
    return v

def low_keep(v):
    return (low(v), None)

def low_pass(kept, grad):
    return (grad,)

def back_keep(v):
    return (v, None)

def back_low(kept, grad):
    return (low(grad),)
low.defvjp(low_keep, low_pass)
low_back.defvjp(back_keep, back_low)

def rms_norm(values, gain_vec):
    return values * lax.rsqrt(lax.optimization_barrier(jnp.mean(values * values, axis=-1, keepdims=True)) + epsilon) * gain_vec

def project(values, weight):
    return jnp.einsum('tsd,dn->tsn', values, weight, precision=highest)

def rope_tables():
    positions = jnp.arange(LMAX, dtype=jnp.float32)
    frequency = jnp.power(rope_base, -(jnp.arange(HD // 2, dtype=jnp.float32) * 2.0) / HD)
    angles = positions[:, None] * frequency[None, :]
    return (jnp.cos(angles), jnp.sin(angles))

def rotate(values, cosine, sine):
    half_size = values.shape[-1] // 2
    front = values[..., :half_size]
    back_half = values[..., half_size:]
    cos_wide = cosine[:, None, None, :]
    sin_wide = sine[:, None, None, :]
    return jnp.concatenate([front * cos_wide - back_half * sin_wide, back_half * cos_wide + front * sin_wide], axis=-1)

def attend_one(operands):
    query_seq, key_seq, value_seq, length_seq = operands
    kv_heads = key_seq.shape[1]
    group_size = query_seq.shape[1] // kv_heads
    grouped = query_seq.reshape(LMAX, kv_heads, group_size, HD)
    scores = low_back(jnp.einsum('ikgd,jkd->kgij', grouped, key_seq, precision=highest) * HD ** (-0.5))
    key_pos = jnp.arange(LMAX, dtype=jnp.int32)
    allowed = (key_pos[None, :] <= key_pos[:, None]) & (key_pos[None, :] < length_seq)
    masked = jnp.where(allowed, scores, -1e+30)
    row_top = lax.optimization_barrier(jnp.max(masked, axis=-1, keepdims=True))
    weights = jnp.where(allowed, jnp.exp(masked - row_top), 0.0)
    probabilities = weights / lax.optimization_barrier(jnp.sum(weights, axis=-1, keepdims=True))
    mixed = jnp.einsum('kgij,jkd->ikgd', low(probabilities), value_seq, precision=highest)
    return mixed.reshape(LMAX, query_seq.shape[1], HD)

def feed_forward(values, norm_gain, weight_in, weight_out):
    normed = low(rms_norm(values, norm_gain))
    gate_up = low_back(project(normed, low(weight_in).reshape(D, 2 * FF)))
    gate_up = gate_up.reshape(values.shape[0], values.shape[1], 2, FF)
    hidden = low(jax.nn.silu(gate_up[:, :, 0]) * gate_up[:, :, 1])
    return low_back(project(hidden, low(weight_out)))

def forward(arrays, lengths):
    hidden_in, conv_norm, conv_in, conv_kernel, conv_out, conv_ffn_norm, conv_ffn_in, conv_ffn_out, attn_norm, attn_q, attn_kv, q_gain, k_gain, attn_out, attn_ffn_norm, attn_ffn_in, attn_ffn_out = arrays
    keep = (jnp.arange(LMAX, dtype=jnp.int32)[:, None] < lengths[None, :]).astype(jnp.float32)[:, :, None]
    begin = hidden_in * keep
    normed = low(rms_norm(begin, conv_norm))
    mixed_in = low_back(project(normed, low(conv_in).reshape(D, 3 * D))).reshape(LMAX, SEQS, 3, D)
    gate_b = mixed_in[:, :, 0]
    gate_c = mixed_in[:, :, 1]
    inner_part = mixed_in[:, :, 2]
    product = gate_b * inner_part
    padded = jnp.pad(product, ((CONV - 1, 0), (0, 0), (0, 0)))
    convolved = sum((conv_kernel[tap_index] * padded[tap_index:tap_index + LMAX] for tap_index in range(CONV)))
    conv_mix = low(gate_c * convolved)
    after_conv = begin + low_back(project(conv_mix, low(conv_out)))
    after_ffn = after_conv + feed_forward(after_conv, conv_ffn_norm, conv_ffn_in, conv_ffn_out)
    normed_attn = low(rms_norm(after_ffn, attn_norm))
    both_weights = jnp.concatenate([low(attn_q), low(attn_kv).reshape(D, 2 * KV * HD)], axis=1)
    projected = low_back(project(normed_attn, both_weights))
    query_raw = projected[:, :, :H * HD].reshape(LMAX, SEQS, H, HD)
    key_raw = projected[:, :, H * HD:(H + KV) * HD].reshape(LMAX, SEQS, KV, HD)
    value_raw = projected[:, :, (H + KV) * HD:].reshape(LMAX, SEQS, KV, HD)
    cosine, sine = rope_tables()
    query_rot = low(rotate(rms_norm(query_raw, q_gain), cosine, sine))
    key_rot = low(rotate(rms_norm(key_raw, k_gain), cosine, sine))
    value_low = low(value_raw)
    attended = lax.map(jax.checkpoint(attend_one), (jnp.moveaxis(query_rot, 1, 0), jnp.moveaxis(key_rot, 1, 0), jnp.moveaxis(value_low, 1, 0), lengths))
    attended = low(low_back(jnp.moveaxis(attended, 0, 1))).reshape(LMAX, SEQS, H * HD)
    after_attn = after_ffn + low_back(project(attended, low(attn_out)))
    final = after_attn + feed_forward(after_attn, attn_ffn_norm, attn_ffn_in, attn_ffn_out)
    return final * keep

def reference(hidden_in, lengths, conv_norm, conv_in, conv_kernel, conv_out, conv_ffn_norm, conv_ffn_in, conv_ffn_out, attn_norm, attn_q, attn_kv, q_gain, k_gain, attn_out, attn_ffn_norm, attn_ffn_in, attn_ffn_out, grad_out):

    def wrapped(*arrays):
        return forward(arrays, lengths)
    output, pull = jax.vjp(wrapped, hidden_in, conv_norm, conv_in, conv_kernel, conv_out, conv_ffn_norm, conv_ffn_in, conv_ffn_out, attn_norm, attn_q, attn_kv, q_gain, k_gain, attn_out, attn_ffn_norm, attn_ffn_in, attn_ffn_out)
    grads = pull(grad_out)
    return (output, grads[0], grads[1], grads[2], grads[3], grads[4], grads[5], grads[6], grads[7], grads[8], grads[9], grads[10], grads[11], grads[12], grads[13], grads[14], grads[15], grads[16])
```

```python
import functools

import jax
import jax.numpy as jnp
from jax import lax
from jax.experimental import pallas as pl
from jax.experimental.pallas import tpu as pltpu
from jax.sharding import PartitionSpec as P

D = 1024
HD = 64
CONV = 3
epsilon = 1e-05
rope_base = 1000000.0
bf16 = jnp.bfloat16
f32 = jnp.float32
MESH = pl.DeviceIdType.MESH
ANY = pl.BlockSpec(memory_space=pl.ANY)
VMEM = pl.BlockSpec(memory_space=pltpu.VMEM)


def dot(a, b, ca, cb):
    return lax.dot_general(a, b, (((ca,), (cb,)), ((), ())), preferred_element_type=f32)


def place(m):
    d, r = lax.axis_index("dp"), lax.axis_index("rows")
    pair, half = lax.rem(d, 2), r // 2
    return lax.rem(pair + lax.rem(m, 2), 2), lax.rem(half + m // 2, 2)


def peer(m):
    d, r = lax.axis_index("dp"), lax.axis_index("rows")
    pm, hm = place(m)
    return {"dp": d - lax.rem(d, 2) + pm, "rows": hm * 2 + lax.rem(r, 2)}


def sibling():
    r = lax.axis_index("rows")
    return {"rows": r + 1 - 2 * lax.rem(r, 2)}


def remote(src, dst, send, recv, to):
    return pltpu.make_async_remote_copy(
        src_ref=src, dst_ref=dst, send_sem=send, recv_sem=recv, device_id=to, device_id_type=MESH
    )


def share(sh, mine):
    k = lax.rem(lax.axis_index("rows"), 2)
    k = k if mine else 1 - k
    return pl.ds(pl.multiple_of(k * sh, 16), sh)


def greet():
    barrier = pltpu.get_barrier_semaphore()
    for to in [sibling()] + [peer(m) for m in (1, 2, 3)]:
        pl.semaphore_signal(barrier, inc=1, device_id=to, device_id_type=MESH)
    pl.semaphore_wait(barrier, 4)


def gather_copy(buf, sh, sems, m, to):
    pm, hm = place(0)
    own = buf.at[pm, :, hm, share(sh, True)]
    return remote(own, own, sems.at[0, m], sems.at[1, m], to)


def start_gather(buf, sh, sems):
    gather_copy(buf, sh, sems, 0, sibling()).start()
    for m in (1, 2, 3):
        gather_copy(buf, sh, sems, m, peer(m)).start()


def forward_copy(buf, sh, sems, m, mine):
    pm, hm = place(m)
    part = buf.at[pm, :, hm, share(sh, mine)]
    return remote(part, part, sems.at[2, m], sems.at[3, m], sibling())


def arrive(buf, sh, sems, m):
    @pl.when(m == 0)
    def _():
        pm, hm = place(0)
        got = buf.at[pm, :, hm, share(sh, False)]
        remote(got, got, sems.at[0, 0], sems.at[1, 0], sibling()).wait_recv()

    @pl.when(m > 0)
    def _():
        pm, hm = place(m)
        got = buf.at[pm, :, hm, share(sh, True)]
        remote(got, got, sems.at[0, m], sems.at[1, m], peer(m)).wait_recv()
        forward_copy(buf, sh, sems, m, True).start()
        forward_copy(buf, sh, sems, m, False).wait_recv()


def end_gather(buf, sh, sems):
    gather_copy(buf, sh, sems, 0, sibling()).wait_send()
    for m in (1, 2, 3):
        gather_copy(buf, sh, sems, m, peer(m)).wait_send()
        forward_copy(buf, sh, sems, m, True).wait_send()


def scatter(part, xr, ys, yr, sh, sems, m):
    across = remote(
        part.at[m, :, share(sh, False)], xr.at[m], sems.at[4, m], sems.at[5, m], sibling()
    )
    across.start()
    across.wait_recv()
    both = part[m, :, share(sh, True)] + xr[m]

    @pl.when(m == 0)
    def _():
        xr[0] = both

    @pl.when(m > 0)
    def _():
        ys[m] = both.astype(bf16)
        remote(ys.at[m], yr.at[m], sems.at[6, m], sems.at[7, m], peer(m)).start()


def end_scatter(part, xr, ys, yr, sh, sems):
    total = xr[0]
    for m in (1, 2, 3):
        copy = remote(ys.at[m], yr.at[m], sems.at[6, m], sems.at[7, m], peer(m))
        copy.wait_recv()
        total = total + yr[m].astype(f32)
        copy.wait_send()
    for m in range(4):
        remote(
            part.at[m, :, share(sh, False)], xr.at[m], sems.at[4, m], sems.at[5, m], sibling()
        ).wait_send()
    return total


def rms(x):
    return lax.rsqrt(jnp.mean(x * x, axis=-1, keepdims=True) + epsilon)


def put_own(buf, sh, value):
    pm, hm = place(0)
    buf[pm, :, hm, share(sh, True)] = value.astype(bf16)


def norm_own(x_ref, gain_ref):
    x = x_ref[...]
    return x * rms(x) * gain_ref[...]


def norm_back(n, x_ref, gain_ref, grad_ref, out_ref, gain_out):
    x = x_ref[...]
    q = rms(x)
    scaled = n * gain_ref[...]
    dots = jnp.mean(scaled * x, axis=-1, keepdims=True)
    out_ref[...] = grad_ref[...] + scaled * q - x * (q * q * q) * dots
    gain_out[...] = jnp.sum(n * x * q, axis=(0, 1))[None]


def flat(x):
    return x.reshape(x.shape[0] * x.shape[1], x.shape[2])


def tiles(width):
    return [(a, min(256, width - a)) for a in range(0, width, 256)]


def padded(width):
    return -(-width // 128) * 128


def load_copies(w_ref, wbuf, wide, sem):
    return [
        pltpu.make_async_copy(
            w_ref.at[c, pl.ds(g * wide, wide)], wbuf.at[g, pl.ds(c * wide, wide)], sem.at[c * 3 + g]
        )
        for c in range(w_ref.shape[0])
        for g in range(3)
    ]


def zero_pad(wbuf, used):
    if wbuf.shape[1] > used:
        wbuf[:, used:] = jnp.zeros((3, wbuf.shape[1] - used, wbuf.shape[2]), bf16)


def ffn_forward_kernel(sh, wide, x_ref, gain_ref, w_ref, out_ref, n_ref, gu_ref,
                       buf, wbuf, gu, hid, part, xr, ys, yr, sems, wsem, osem):
    loads = load_copies(w_ref, wbuf, wide, wsem)
    for copy in loads:
        copy.start()
    zero_pad(wbuf, w_ref.shape[0] * wide)
    put_own(buf, sh, norm_own(x_ref, gain_ref))
    greet()
    start_gather(buf, sh, sems)
    for copy in loads:
        copy.wait()
    width = wbuf.shape[1]

    def step(m, carry):
        arrive(buf, sh, sems, m)
        pm, hm = place(m)
        x = flat(buf[pm, :, hm])
        for a, n in tiles(width):
            g = dot(x, wbuf[0, a : a + n], 1, 1)
            u = dot(x, wbuf[1, a : a + n], 1, 1)
            gu[m, 0, :, a : a + n] = g
            gu[m, 1, :, a : a + n] = u
            hid[:, a : a + n] = (g * jax.nn.sigmoid(g) * u).astype(bf16)
        pltpu.make_async_copy(gu.at[m], gu_ref.at[m], osem.at[m]).start()
        for a, n in tiles(D):
            y = dot(hid[...], wbuf[2, :, a : a + n], 1, 0)
            part[m, :, :, a : a + n] = y.reshape(part.shape[1], part.shape[2], n)
        scatter(part, xr, ys, yr, sh, sems, m)
        return carry

    lax.fori_loop(0, 4, step, 0)
    save = pltpu.make_async_copy(buf, n_ref, osem.at[4])
    save.start()
    out_ref[...] = x_ref[...] + end_scatter(part, xr, ys, yr, sh, sems)
    end_gather(buf, sh, sems)
    for m in range(4):
        pltpu.make_async_copy(gu.at[m], gu_ref.at[m], osem.at[m]).wait()
    save.wait()


def ffn_backward_kernel(sh, wide, grad_ref, x_ref, gain_ref, w_ref, n_ref, gu_ref,
                        out_ref, gain_out, dw_ref,
                        buf, nbuf, wbuf, gu, hid, dw, part, xr, ys, yr, sems, wsem, osem):
    cols = w_ref.shape[0]
    gloads = [pltpu.make_async_copy(gu_ref.at[m], gu.at[m], osem.at[m]) for m in range(4)]
    nload = pltpu.make_async_copy(n_ref, nbuf, osem.at[4])
    loads = load_copies(w_ref, wbuf, wide, wsem)
    for copy in loads + gloads + [nload]:
        copy.start()
    zero_pad(wbuf, cols * wide)
    put_own(buf, sh, grad_ref[...])
    greet()
    start_gather(buf, sh, sems)
    for copy in loads + gloads:
        copy.wait()
    width = wbuf.shape[1]

    def step(m, carry):
        arrive(buf, sh, sems, m)
        pm, hm = place(m)
        gg = flat(buf[pm, :, hm])
        for a, n in tiles(width):
            gh = dot(gg, wbuf[2, a : a + n], 1, 1)
            g = gu[m, 0, :, a : a + n]
            u = gu[m, 1, :, a : a + n]
            s = jax.nn.sigmoid(g)
            silu = g * s
            shape = (part.shape[1], part.shape[2], n)
            hid[0, pm, :, hm, :, a : a + n] = (gh * u * (s * (1.0 + g * (1.0 - s)))).astype(bf16).reshape(shape)
            hid[1, pm, :, hm, :, a : a + n] = (gh * silu).astype(bf16).reshape(shape)
            hid[2, pm, :, hm, :, a : a + n] = (silu * u).astype(bf16).reshape(shape)
        for a, n in tiles(D):
            y = dot(flat(hid[0, pm, :, hm]), wbuf[0, :, a : a + n], 1, 0)
            y = y + dot(flat(hid[1, pm, :, hm]), wbuf[1, :, a : a + n], 1, 0)
            part[m, :, :, a : a + n] = y.reshape(part.shape[1], part.shape[2], n)
        scatter(part, xr, ys, yr, sh, sems, m)
        return carry

    lax.fori_loop(0, 4, step, 0)
    nload.wait()
    tokens = 8 * buf.shape[3]

    def grads(other, g):
        def one(i, carry):
            at = pl.ds(pl.multiple_of(i * 128, 128), 128)
            left = hid[g, :, :, :, :, at].reshape(tokens, 128)
            dw[g, at] = dot(left, other[...].reshape(tokens, D), 0, 0).astype(bf16)
            return carry

        lax.fori_loop(0, width // 128, one, 0)

    grads(nbuf, 0)
    grads(nbuf, 1)
    grads(buf, 2)
    stores = [
        pltpu.make_async_copy(
            dw.at[g, pl.ds(c * wide, wide)], dw_ref.at[c, pl.ds(g * wide, wide)], wsem.at[c * 3 + g]
        )
        for c in range(cols)
        for g in range(3)
    ]
    for copy in stores:
        copy.start()
    n = end_scatter(part, xr, ys, yr, sh, sems)
    norm_back(n, x_ref, gain_ref, grad_ref, out_ref, gain_out)
    end_gather(buf, sh, sems)
    for copy in stores:
        copy.wait()


def project_kernel(sh, normed, *refs):
    if normed:
        x_ref, gain_ref, w_ref, y_ref, n_ref, buf, sems, osem = refs
        put_own(buf, sh, norm_own(x_ref, gain_ref))
    else:
        x_ref, w_ref, y_ref, n_ref, buf, sems, osem = refs
        put_own(buf, sh, x_ref[...])
    greet()
    start_gather(buf, sh, sems)

    def step(m, carry):
        arrive(buf, sh, sems, m)
        pm, hm = place(m)
        y = dot(flat(buf[pm, :, hm]), w_ref[...], 1, 1)
        y_ref[pm, :, hm] = y.reshape(y_ref.shape[1], y_ref.shape[3], y_ref.shape[4])
        return carry

    lax.fori_loop(0, 4, step, 0)
    save = pltpu.make_async_copy(buf, n_ref, osem.at[0])
    save.start()
    end_gather(buf, sh, sems)
    save.wait()


def merge_kernel(sh, back, *refs):
    if back:
        y_ref, w_ref, x_ref, gain_ref, grad_ref, out_ref, gain_out, part, xr, ys, yr, sems = refs
    else:
        y_ref, w_ref, x_ref, out_ref, part, xr, ys, yr, sems = refs
    greet()

    def step(i, carry):
        m = lax.rem(i + 1, 4)
        pm, hm = place(m)
        y = flat(y_ref[pm, :, hm])
        for a, n in tiles(D):
            z = dot(y, w_ref[:, a : a + n], 1, 0)
            part[m, :, :, a : a + n] = z.reshape(part.shape[1], part.shape[2], n)
        scatter(part, xr, ys, yr, sh, sems, m)
        return carry

    lax.fori_loop(0, 4, step, 0)
    total = end_scatter(part, xr, ys, yr, sh, sems)
    if back:
        norm_back(total, x_ref, gain_ref, grad_ref, out_ref, gain_out)
    else:
        out_ref[...] = x_ref[...] + total


def shape(dims, kind):
    return jax.ShapeDtypeStruct(dims, kind)


def scatter_scratch(seqs, sh):
    return [
        pltpu.VMEM((4, seqs, 2 * sh, D), f32),
        pltpu.VMEM((4, seqs, sh, D), f32),
        pltpu.VMEM((4, seqs, sh, D), bf16),
        pltpu.VMEM((4, seqs, sh, D), bf16),
    ]


def call(kernel, name, cid, outs, out_specs, in_specs, scratch, args, flops=10**9, limit=60):
    return pl.pallas_call(
        kernel,
        name=name,
        out_shape=outs,
        in_specs=in_specs,
        out_specs=out_specs,
        scratch_shapes=scratch,
        cost_estimate=pl.CostEstimate(flops=flops, bytes_accessed=10**7, transcendentals=0),
        compiler_params=pltpu.CompilerParams(
            collective_id=cid, has_side_effects=True, vmem_limit_bytes=limit << 20
        ),
    )(*args)


DMA = pltpu.SemaphoreType.DMA


def ffn_forward(cid, x, gain, w, wide):
    seqs, sh, _ = x.shape
    cols = w.shape[0]
    width = padded(cols * wide)
    full = (2, seqs, 2, 2 * sh, D)
    rows = seqs * 2 * sh
    return call(
        functools.partial(ffn_forward_kernel, sh, wide), "ffn_forward", cid,
        (shape(x.shape, f32), shape(full, bf16), shape((4, 2, rows, width), f32)),
        (VMEM, ANY, ANY), (VMEM, VMEM, ANY),
        [
            pltpu.VMEM(full, bf16), pltpu.VMEM((3, width, D), bf16),
            pltpu.VMEM((4, 2, rows, width), f32), pltpu.VMEM((rows, width), bf16),
        ] + scatter_scratch(seqs, sh) + [DMA((8, 4)), DMA((3 * cols,)), DMA((5,))],
        (x, gain, w),
    )


def ffn_backward(cid, grad, x, gain, w, n, gu, wide):
    seqs, sh, _ = x.shape
    cols = w.shape[0]
    width = padded(cols * wide)
    full = (2, seqs, 2, 2 * sh, D)
    rows = seqs * 2 * sh
    return call(
        functools.partial(ffn_backward_kernel, sh, wide), "ffn_backward", cid,
        (shape(x.shape, f32), shape((1, D), f32), shape(w.shape, bf16)),
        (VMEM, VMEM, ANY), (VMEM, VMEM, VMEM, ANY, ANY, ANY),
        [
            pltpu.VMEM(full, bf16), pltpu.VMEM(full, bf16), pltpu.VMEM((3, width, D), bf16),
            pltpu.VMEM((4, 2, rows, width), f32), pltpu.VMEM((3,) + full[:4] + (width,), bf16),
            pltpu.VMEM((3, width, D), bf16),
        ] + scatter_scratch(seqs, sh) + [DMA((8, 4)), DMA((3 * cols,)), DMA((5,))],
        (grad, x, gain, w, n, gu),
    )


def project(cid, x, gain, w):
    seqs, sh, _ = x.shape
    full = (2, seqs, 2, 2 * sh, D)
    args = (x, w) if gain is None else (x, gain, w)
    y, n = call(
        functools.partial(project_kernel, sh, gain is not None), "project", cid,
        (shape(full[:4] + (w.shape[0],), f32), shape(full, bf16)),
        (VMEM, ANY), (VMEM,) * len(args),
        [pltpu.VMEM(full, bf16), DMA((4, 4)), DMA((1,))],
        args, limit=30,
    )
    return y.reshape(2 * seqs, 4 * sh, -1), n


def merge(cid, y, w, x, gain=None, grad=None):
    seqs, sh, _ = x.shape
    y = y.reshape(2, seqs, 2, 2 * sh, -1)
    args = (y, w, x) if gain is None else (y, w, x, gain, grad)
    outs = (shape(x.shape, f32),) + (() if gain is None else (shape((1, D), f32),))
    got = call(
        functools.partial(merge_kernel, sh, gain is not None), "merge", cid,
        outs, (VMEM,) * len(outs), (VMEM,) * len(args),
        scatter_scratch(seqs, sh) + [DMA((8, 4))],
        args, limit=30,
    )
    return got[0] if gain is None else got


def to_rows(pieces):
    got = lax.all_to_all(pieces, "rows", 0, 0, tiled=True)
    return got.transpose(1, 0, 2).reshape(pieces.shape[1], -1)


def from_rows(grad):
    rows = lax.axis_size("rows")
    pieces = grad.reshape(grad.shape[0], rows, -1).transpose(1, 0, 2)
    return lax.all_to_all(pieces, "rows", 0, 0, tiled=True)


def both_pairs(x):
    count = lax.axis_size("dp")
    if count == 2:
        return lax.all_gather(x, "dp", axis=0)
    pair = lax.rem(lax.axis_index("dp"), 2)
    slots = jnp.arange(2).reshape((2,) + (1,) * x.ndim) == pair
    return lax.psum(jnp.where(slots, x[None], jnp.zeros_like(x)[None]), "dp")


def own_tokens(x):
    got = lax.all_to_all(x, "rows", 0, 2, tiled=True)
    return got.transpose(1, 0, 2)


def native_tokens(x):
    return lax.all_to_all(x.transpose(1, 0, 2), "rows", 2, 0, tiled=True)


def rotate(values, cos, sin):
    a, b = jnp.split(values, 2, axis=-1)
    return jnp.concatenate([a * cos - b * sin, b * cos + a * sin], axis=-1)


def rotate_back(values, cos, sin):
    a, b = jnp.split(values, 2, axis=-1)
    return jnp.concatenate([a * cos + b * sin, b * cos - a * sin], axis=-1)


def head_norm(v, gain):
    inv = lax.rsqrt(jnp.mean(v * v, axis=-1, keepdims=True) + epsilon)
    return v * inv * gain, inv


def head_norm_back(v, inv, gain, g):
    scaled = g * gain
    dots = jnp.mean(scaled * v, axis=-1, keepdims=True)
    grad = scaled * inv - v * (inv * inv * inv) * dots
    return grad, jnp.sum((g * v * inv).reshape(-1, v.shape[-1]), axis=0)


def per_device(
    hidden_in, lengths, conv_norm, conv_in, conv_kernel, conv_out, conv_ffn_norm, conv_ffn_in,
    conv_ffn_out, attn_norm, attn_q, attn_kv, q_gain, k_gain, attn_out, attn_ffn_norm,
    attn_ffn_in, attn_ffn_out, grad_out,
):
    rows, cols = lax.axis_size("rows"), lax.axis_size("cols")
    tp = 2 * rows
    r, c, d = lax.axis_index("rows"), lax.axis_index("cols"), lax.axis_index("dp")
    pair = lax.rem(d, 2)
    me = pair * rows + r
    slots, seqs, feat = hidden_in.shape
    sh = slots // rows
    all_seqs = 2 * seqs
    tokens = all_seqs * slots

    def halves(x, axis):
        return lax.dynamic_slice_in_dim(x, pair * rows, rows, axis)

    def cut_in(w):
        parts, width = w.shape[1], w.shape[2] // tp
        x = w.astype(bf16).transpose(1, 2, 0).reshape(parts, tp, width, feat)
        return halves(x, 1).transpose(1, 0, 2, 3).reshape(rows, parts * width, feat)

    def cut_out(w):
        return halves(w.astype(bf16).reshape(tp, -1, feat), 0)

    def spread(pieces):
        return lax.all_gather(to_rows(pieces), "cols", axis=0)

    wide = conv_ffn_in.shape[2] // tp
    chan = conv_in.shape[2] // tp
    conv_all = spread(jnp.concatenate([cut_in(conv_in), cut_out(conv_out)], axis=1))
    w_conv = conv_all[:, : 3 * chan].reshape(cols, 3, chan, D).transpose(1, 0, 2, 3)
    w_conv = w_conv.reshape(3 * cols * chan, D)
    w_cout = conv_all[:, 3 * chan :].reshape(cols * chan, D)

    def ffn_weights(w_in, w_out):
        return spread(jnp.concatenate([cut_in(w_in), cut_out(w_out)], axis=1))

    w_ffn1 = ffn_weights(conv_ffn_in, conv_ffn_out)
    per_col = tp // cols
    q_w = attn_q.shape[1] // per_col
    kv_w = attn_kv.shape[2] // per_col
    parts = jnp.concatenate(
        [
            attn_q.astype(bf16).T.reshape(per_col, q_w, feat),
            attn_kv[:, 0].astype(bf16).T.reshape(per_col, kv_w, feat),
            attn_kv[:, 1].astype(bf16).T.reshape(per_col, kv_w, feat),
            attn_out.astype(bf16).reshape(per_col, q_w, feat),
        ],
        axis=1,
    )
    targets = pair * rows + jnp.arange(rows)
    mine = (targets // per_col == c)[:, None, None]
    pieces = jnp.where(mine, jnp.take(parts, targets % per_col, axis=0), jnp.zeros((), bf16))
    attn_all = lax.psum(to_rows(pieces), "cols")
    w_qkv = attn_all[: q_w + 2 * kv_w]
    w_aout = attn_all[q_w + 2 * kv_w :]
    w_ffn2 = ffn_weights(attn_ffn_in, attn_ffn_out)

    gains_own = jnp.stack([conv_norm, conv_ffn_norm, attn_norm, attn_ffn_norm])
    gains = lax.all_gather(gains_own, "rows", axis=1, tiled=True)[:, None]
    kern = lax.dynamic_slice_in_dim(conv_kernel, me * chan, chan, 1)
    kern = lax.all_gather(kern, "cols", axis=1, tiled=True)
    len_all = lax.all_gather(lengths, "dp", axis=0, tiled=True)
    len_here = lax.dynamic_slice_in_dim(len_all, (d // 2) * all_seqs, all_seqs)

    slot_ids = c * slots + jnp.arange(slots, dtype=jnp.int32)
    keep = (slot_ids[:, None] < lengths[None, :]).astype(f32)[:, :, None]
    begin = own_tokens(hidden_in * keep)
    grad_final = own_tokens(grad_out * keep)
    mixed, n_conv = project(1, begin, gains[0], w_conv)
    channels = cols * chan
    gate_b, gate_c, inner = (mixed[:, :, i * channels : (i + 1) * channels] for i in range(3))
    product = gate_b * inner
    before = lax.ppermute(
        product[:, slots - (CONV - 1) :], "cols", [(i, i + 1) for i in range(cols - 1)]
    )
    extended = jnp.concatenate([before, product], axis=1)
    convolved = sum(kern[k] * extended[:, k : k + slots] for k in range(CONV))
    conv_mix = (gate_c * convolved).astype(bf16)
    after_conv = merge(2, conv_mix, w_cout, begin)

    after_ffn, n_1, gu_1 = ffn_forward(3, after_conv, gains[1], w_ffn1, wide)

    projected, n_attn = project(4, after_ffn, gains[2], w_qkv)
    heads = q_w // HD
    kvh = kv_w // HD
    query_raw = projected[:, :, :q_w].reshape(all_seqs, slots, heads, HD)
    key_raw = projected[:, :, q_w : q_w + kv_w].reshape(all_seqs, slots, kvh, HD)
    value_raw = projected[:, :, q_w + kv_w :].reshape(all_seqs, slots, kvh, HD)
    frequency = jnp.power(rope_base, -(jnp.arange(HD // 2, dtype=f32) * 2.0) / HD)
    angles = slot_ids.astype(f32)[:, None] * frequency[None, :]
    cos, sin = jnp.cos(angles)[:, None, :], jnp.sin(angles)[:, None, :]
    q_normed, q_inv = head_norm(query_raw, q_gain)
    k_normed, k_inv = head_norm(key_raw, k_gain)
    query = rotate(q_normed, cos, sin).astype(bf16)
    key = rotate(k_normed, cos, sin).astype(bf16)
    value = value_raw.astype(bf16)
    key_all = lax.all_gather(key, "cols", axis=1, tiled=True)
    value_all = lax.all_gather(value, "cols", axis=1, tiled=True)
    scale = HD ** (-0.5)
    grouped = query.reshape(all_seqs, slots, kvh, heads // kvh, HD)
    ein = lambda spec, a, b: jnp.einsum(spec, a, b, preferred_element_type=f32)
    key_pos = jnp.arange(slots * cols, dtype=jnp.int32)
    allowed = (key_pos[None, :] <= slot_ids[:, None])[None, None, None] & (
        key_pos[None, :] < len_here[:, None]
    )[:, None, None, None, :]
    scores = ein("sikgd,sjkd->skgij", grouped, key_all) * scale
    masked = jnp.where(allowed, scores, -1e30)
    top = jnp.max(masked, axis=-1, keepdims=True)
    weights = jnp.where(allowed, jnp.exp(masked - top), 0.0)
    total = jnp.sum(weights, axis=-1, keepdims=True)
    prob = weights / total
    log_total = top + jnp.log(total)
    attended = ein("skgij,sjkd->sikgd", prob.astype(bf16), value_all).astype(bf16)
    attended = attended.reshape(all_seqs, slots, q_w)
    after_attn = merge(5, attended, w_aout, after_ffn)

    final, n_2, gu_2 = ffn_forward(6, after_attn, gains[3], w_ffn2, wide)
    output = native_tokens(final) * keep

    def collect(packed):
        part = lax.psum_scatter(packed, "cols", scatter_dimension=0)
        pieces = both_pairs(from_rows(part))
        return pieces.reshape((tp,) + pieces.shape[2:]).astype(f32)

    def native_in(x, count):
        x = x.reshape(tp, count, -1, feat)
        return x.transpose(3, 1, 0, 2).reshape(feat, count, -1)

    def native_out(x):
        return x.reshape(-1, feat)

    grad_attn_res, gain_p3, packed2 = ffn_backward(
        7, grad_final, after_attn, gains[3], w_ffn2, n_2, gu_2, wide
    )
    got2 = collect(packed2)
    g_attn_ffn_in, g_attn_ffn_out = native_in(got2[:, : 2 * wide], 2), native_out(got2[:, 2 * wide :])

    grad_attended, gg = project(8, grad_attn_res, None, w_aout)
    gg = gg.reshape(tokens, D)
    grad_attended = grad_attended.astype(bf16)
    grad_aout = dot(attended.reshape(tokens, q_w), gg, 0, 0)
    grad_grouped = grad_attended.reshape(all_seqs, slots, kvh, heads // kvh, HD)
    prob = jnp.where(allowed, jnp.exp(scores - log_total), 0.0)
    grad_prob = ein("sikgd,sjkd->skgij", grad_grouped, value_all)
    delta = jnp.sum(prob * grad_prob, axis=-1, keepdims=True)
    grad_scores = (prob * (grad_prob - delta)).astype(bf16)
    grad_query = ein("skgij,sjkd->sikgd", grad_scores, key_all) * scale
    grad_keys = ein("skgij,sikgd->sjkd", grad_scores, grouped) * scale
    grad_values = ein("skgij,sikgd->sjkd", prob.astype(bf16), grad_grouped)
    grad_kv = jnp.stack([grad_keys, grad_values]).astype(bf16)
    grad_kv = lax.psum_scatter(grad_kv, "cols", scatter_dimension=2, tiled=True).astype(f32)
    grad_query_raw, q_gain_part = head_norm_back(
        query_raw, q_inv, q_gain, rotate_back(grad_query.reshape(query_raw.shape), cos, sin)
    )
    grad_key_raw, k_gain_part = head_norm_back(
        key_raw, k_inv, k_gain, rotate_back(grad_kv[0], cos, sin)
    )
    grad_proj = jnp.concatenate(
        [x.reshape(all_seqs, slots, -1) for x in (grad_query_raw, grad_key_raw, grad_kv[1])], axis=2
    ).astype(bf16)
    grad_qkv = dot(grad_proj.reshape(tokens, -1), n_attn.reshape(tokens, D), 0, 0)
    grad_after_ffn, gain_p2 = merge(9, grad_proj, w_qkv, after_ffn, gains[2], grad_attn_res)
    packed_a = lax.psum(jnp.concatenate([grad_qkv, grad_aout], axis=0).astype(bf16), "cols")
    held = packed_a.reshape(-1, rows, feat).transpose(1, 0, 2)[:, None]
    slot_here = (jnp.arange(per_col) == me % per_col)[None, :, None, None] & (me // per_col == c)
    held = jnp.where(slot_here, held, jnp.zeros((), bf16))
    got_a = lax.psum(lax.psum_scatter(held, "rows", scatter_dimension=0), "dp").astype(f32)
    g_q = got_a[:, :q_w].reshape(-1, feat).T
    g_kv = jnp.stack(
        [
            got_a[:, q_w : q_w + kv_w].reshape(-1, feat).T,
            got_a[:, q_w + kv_w : q_w + 2 * kv_w].reshape(-1, feat).T,
        ],
        axis=1,
    )
    g_aout = got_a[:, q_w + 2 * kv_w :].reshape(-1, feat)

    grad_after_conv, gain_p1, packed1 = ffn_backward(
        10, grad_after_ffn, after_conv, gains[1], w_ffn1, n_1, gu_1, wide
    )
    got1 = collect(packed1)
    g_conv_ffn_in, g_conv_ffn_out = native_in(got1[:, : 2 * wide], 2), native_out(got1[:, 2 * wide :])

    grad_mix, gg = project(11, grad_after_conv, None, w_cout)
    gg = gg.reshape(tokens, D)
    grad_cout = dot(conv_mix.reshape(tokens, channels), gg, 0, 0)
    grad_c = grad_mix * convolved
    grad_conv = grad_mix * gate_c
    after = lax.ppermute(grad_conv[:, : CONV - 1], "cols", [(i + 1, i) for i in range(cols - 1)])
    grad_ext = jnp.concatenate([grad_conv, after], axis=1)
    grad_product = sum(kern[k] * grad_ext[:, CONV - 1 - k : CONV - 1 - k + slots] for k in range(CONV))
    kern_part = jnp.stack(
        [jnp.sum(grad_conv * extended[:, k : k + slots], axis=(0, 1)) for k in range(CONV)]
    )
    grad_mixed = jnp.concatenate([grad_product * inner, grad_c, grad_product * gate_b], axis=2).astype(bf16)
    grad_cin = dot(grad_mixed.reshape(tokens, -1), n_conv.reshape(tokens, D), 0, 0)
    grad_cin = grad_cin.reshape(3, cols, chan, D).transpose(1, 0, 2, 3)
    grad_begin, gain_p0 = merge(12, grad_mixed, w_conv, begin, gains[0], grad_after_conv)
    grad_in = native_tokens(grad_begin) * keep
    packed0 = jnp.concatenate(
        [grad_cin.reshape(cols, 3 * chan, D), grad_cout.reshape(cols, chan, D)], axis=1
    ).astype(bf16)
    got0 = collect(packed0)
    g_conv_in, g_conv_out = native_in(got0[:, : 3 * chan], 3), native_out(got0[:, 3 * chan :])

    zero = jnp.zeros((), jnp.int32)
    kern_full = lax.dynamic_update_slice(
        jnp.zeros((CONV, cols, tp, chan), f32),
        kern_part.reshape(CONV, cols, 1, chan),
        (zero, zero, me, zero),
    )
    s_gain, s_kern, s_head = lax.psum(
        (
            jnp.concatenate([gain_p0, gain_p1, gain_p2, gain_p3]),
            kern_full.reshape(CONV, D),
            jnp.stack([q_gain_part, k_gain_part]),
        ),
        ("dp", "rows", "cols"),
    )
    g_gain = lax.dynamic_slice(s_gain, (zero, r * feat), (4, feat))
    g_kern = lax.dynamic_slice(s_kern, (zero, c * conv_kernel.shape[1]), conv_kernel.shape)
    return (
        output, grad_in, g_gain[0], g_conv_in, g_kern, g_conv_out, g_gain[1],
        g_conv_ffn_in, g_conv_ffn_out, g_gain[2], g_q, g_kv, s_head[0], s_head[1], g_aout,
        g_gain[3], g_attn_ffn_in, g_attn_ffn_out,
    )


def solution(mesh):
    tokens, vec, mat = P("cols", "dp", "rows"), P("rows"), P("rows", "cols")
    mat3, out, taps = P("rows", None, "cols"), P("cols", "rows"), P(None, "cols")
    weights = (vec, mat3, taps, out, vec, mat3, out, vec, mat, mat3, P(), P(), out, vec, mat3, out)
    return jax.shard_map(
        per_device,
        mesh=mesh,
        in_specs=(tokens, P("dp")) + weights + (tokens,),
        out_specs=(tokens, tokens) + weights,
        check_vma=False,
    )
```

```python
import functools

import jax
import jax.numpy as jnp
from jax import lax
from jax.experimental import pallas as pl
from jax.experimental.pallas import tpu as pltpu
from jax.sharding import PartitionSpec as P

D = 1024
HD = 64
CONV = 3
epsilon = 1e-05
rope_base = 1000000.0
bf16 = jnp.bfloat16
f32 = jnp.float32
MESH = pl.DeviceIdType.MESH
ANY = pl.BlockSpec(memory_space=pl.ANY)
VMEM = pl.BlockSpec(memory_space=pltpu.VMEM)


def dot(a, b, ca, cb):
    return lax.dot_general(a, b, (((ca,), (cb,)), ((), ())), preferred_element_type=f32)


def place(m):
    d, r = lax.axis_index("dp"), lax.axis_index("rows")
    pair, half = lax.rem(d, 2), r // 2
    return lax.rem(pair + lax.rem(m, 2), 2), lax.rem(half + m // 2, 2)


def peer(m):
    d, r = lax.axis_index("dp"), lax.axis_index("rows")
    pm, hm = place(m)
    return {"dp": d - lax.rem(d, 2) + pm, "rows": hm * 2 + lax.rem(r, 2)}


def sibling():
    r = lax.axis_index("rows")
    return {"rows": r + 1 - 2 * lax.rem(r, 2)}


def remote(src, dst, send, recv, to):
    return pltpu.make_async_remote_copy(
        src_ref=src, dst_ref=dst, send_sem=send, recv_sem=recv, device_id=to, device_id_type=MESH
    )


def share(sh, mine):
    k = lax.rem(lax.axis_index("rows"), 2)
    k = k if mine else 1 - k
    return pl.ds(pl.multiple_of(k * sh, 16), sh)


def greet():
    barrier = pltpu.get_barrier_semaphore()
    for to in [sibling()] + [peer(m) for m in (1, 2, 3)]:
        pl.semaphore_signal(barrier, inc=1, device_id=to, device_id_type=MESH)
    pl.semaphore_wait(barrier, 4)


def gather_copy(buf, sh, sems, m, to):
    pm, hm = place(0)
    own = buf.at[pm, :, hm, share(sh, True)]
    return remote(own, own, sems.at[0, m], sems.at[1, m], to)


def relay_copy(buf, sh, sems, m):
    pm, hm = place(m)
    part = buf.at[pm, m - 1, hm, share(sh, True)]
    return remote(part, part, sems.at[8, m], sems.at[9, m], peer(3 - m))


def start_gather(buf, sh, sems):
    gather_copy(buf, sh, sems, 0, sibling()).start()
    for m in (1, 2):
        gather_copy(buf, sh, sems, m, peer(m)).start()


def forward_copy(buf, sh, sems, m, mine):
    pm, hm = place(m)
    part = buf.at[pm, :, hm, share(sh, mine)]
    return remote(part, part, sems.at[2, m], sems.at[3, m], sibling())


def arrive(buf, sh, sems, m):
    def come(src, i, j):
        remote(src, src, sems.at[i - 1, j], sems.at[i, j], sibling()).wait_recv()

    @pl.when(m == 0)
    def _():
        pm, hm = place(0)
        come(buf.at[pm, :, hm, share(sh, False)], 1, 0)

    @pl.when(m == 1)
    def _():
        for j in (1, 2):
            pj, hj = place(j)
            come(buf.at[pj, :, hj, share(sh, True)], 1, j)
            relay_copy(buf, sh, sems, j).start()
            forward_copy(buf, sh, sems, j, True).start()

    @pl.when(m == 3)
    def _():
        pj, hj = place(3)
        for j in (1, 2):
            come(buf.at[pj, j - 1, hj, share(sh, True)], 9, j)
        forward_copy(buf, sh, sems, 3, True).start()

    @pl.when(m > 0)
    def _():
        forward_copy(buf, sh, sems, m, False).wait_recv()


def end_gather(buf, sh, sems):
    gather_copy(buf, sh, sems, 0, sibling()).wait_send()
    for m in (1, 2):
        gather_copy(buf, sh, sems, m, peer(m)).wait_send()
        relay_copy(buf, sh, sems, m).wait_send()
    for m in (1, 2, 3):
        forward_copy(buf, sh, sems, m, True).wait_send()


def sum_copy(ys, yr, sems, m, half):
    return remote(ys.at[m, half], yr.at[m, half], sems.at[6, 2 * half + m - 1], sems.at[7, 2 * half + m - 1], peer(m))


def relay_sum_copy(ys, yr, sems, half):
    return remote(ys.at[3, half], yr.at[3, half], sems.at[10, half], sems.at[11, half], peer(half + 1))


def scatter(part, xr, ys, yr, sh, sems, m):
    across = remote(
        part.at[m, :, share(sh, False)], xr.at[m], sems.at[4, m], sems.at[5, m], sibling()
    )
    across.start()
    across.wait_recv()
    both = part[m, :, share(sh, True)] + xr[m]
    xr[m] = both
    ys[m] = both.astype(bf16)

    @pl.when(m == 3)
    def _():
        for half in (0, 1):
            relay_sum_copy(ys, yr, sems, half).start()

    for j in (1, 2):

        @pl.when(m == j)
        def _():
            sum_copy(ys, yr, sems, j, j - 1).start()


def end_scatter(part, xr, ys, yr, sh, sems):
    for half in (0, 1):
        m = 2 - half
        relay_sum_copy(ys, yr, sems, half).wait_recv()
        ys[m, half] = (xr[m, half] + yr[3, half].astype(f32)).astype(bf16)
        sum_copy(ys, yr, sems, m, half).start()
    total = xr[0]
    for m in (1, 2):
        for half in (0, 1):
            sum_copy(ys, yr, sems, m, half).wait_recv()
        total = total + yr[m].astype(f32)
    for half in (0, 1):
        relay_sum_copy(ys, yr, sems, half).wait_send()
        for m in (1, 2):
            sum_copy(ys, yr, sems, m, half).wait_send()
    for m in range(4):
        remote(
            part.at[m, :, share(sh, False)], xr.at[m], sems.at[4, m], sems.at[5, m], sibling()
        ).wait_send()
    return total


def rms(x):
    return lax.rsqrt(jnp.mean(x * x, axis=-1, keepdims=True) + epsilon)


def put_own(buf, sh, value):
    pm, hm = place(0)
    buf[pm, :, hm, share(sh, True)] = value.astype(bf16)


def norm_own(x_ref, gain_ref):
    x = x_ref[...]
    return x * rms(x) * gain_ref[...]


def norm_back(n, x_ref, gain_ref, grad_ref, out_ref, gain_out):
    x = x_ref[...]
    q = rms(x)
    scaled = n * gain_ref[...]
    dots = jnp.mean(scaled * x, axis=-1, keepdims=True)
    out_ref[...] = grad_ref[...] + scaled * q - x * (q * q * q) * dots
    gain_out[...] = jnp.sum(n * x * q, axis=(0, 1))[None]


def flat(x):
    return x.reshape(x.shape[0] * x.shape[1], x.shape[2])


def tiles(width):
    return [(a, min(256, width - a)) for a in range(0, width, 256)]


def padded(width):
    return -(-width // 128) * 128


def load_copies(w_ref, wbuf, wide, sem):
    return [
        pltpu.make_async_copy(
            w_ref.at[c, pl.ds(g * wide, wide)], wbuf.at[g, pl.ds(c * wide, wide)], sem.at[c * 3 + g]
        )
        for c in range(w_ref.shape[0])
        for g in range(3)
    ]


def zero_pad(wbuf, used):
    if wbuf.shape[1] > used:
        wbuf[:, used:] = jnp.zeros((3, wbuf.shape[1] - used, wbuf.shape[2]), bf16)


def ffn_forward_kernel(sh, wide, x_ref, gain_ref, w_ref, out_ref, n_ref, gu_ref,
                       buf, wbuf, gu, hid, part, xr, ys, yr, sems, wsem, osem):
    loads = load_copies(w_ref, wbuf, wide, wsem)
    for copy in loads:
        copy.start()
    zero_pad(wbuf, w_ref.shape[0] * wide)
    put_own(buf, sh, norm_own(x_ref, gain_ref))
    greet()
    start_gather(buf, sh, sems)
    for copy in loads:
        copy.wait()
    width = wbuf.shape[1]

    def step(m, carry):
        arrive(buf, sh, sems, m)
        pm, hm = place(m)
        x = flat(buf[pm, :, hm])
        for a, n in tiles(width):
            g = dot(x, wbuf[0, a : a + n], 1, 1)
            u = dot(x, wbuf[1, a : a + n], 1, 1)
            gu[m, 0, :, a : a + n] = g
            gu[m, 1, :, a : a + n] = u
            hid[:, a : a + n] = (g * jax.nn.sigmoid(g) * u).astype(bf16)
        pltpu.make_async_copy(gu.at[m], gu_ref.at[m], osem.at[m]).start()
        for a, n in tiles(D):
            y = dot(hid[...], wbuf[2, :, a : a + n], 1, 0)
            part[m, :, :, a : a + n] = y.reshape(part.shape[1], part.shape[2], n)
        scatter(part, xr, ys, yr, sh, sems, m)
        return carry

    lax.fori_loop(0, 4, step, 0)
    save = pltpu.make_async_copy(buf, n_ref, osem.at[4])
    save.start()
    out_ref[...] = x_ref[...] + end_scatter(part, xr, ys, yr, sh, sems)
    end_gather(buf, sh, sems)
    for m in range(4):
        pltpu.make_async_copy(gu.at[m], gu_ref.at[m], osem.at[m]).wait()
    save.wait()


def ffn_backward_kernel(sh, wide, grad_ref, x_ref, gain_ref, w_ref, n_ref, gu_ref,
                        out_ref, gain_out, dw_ref,
                        buf, nbuf, wbuf, gu, hid, dw, part, xr, ys, yr, sems, wsem, osem):
    cols = w_ref.shape[0]
    gloads = [pltpu.make_async_copy(gu_ref.at[m], gu.at[m], osem.at[m]) for m in range(4)]
    nload = pltpu.make_async_copy(n_ref, nbuf, osem.at[4])
    loads = load_copies(w_ref, wbuf, wide, wsem)
    for copy in loads + gloads + [nload]:
        copy.start()
    zero_pad(wbuf, cols * wide)
    put_own(buf, sh, grad_ref[...])
    greet()
    start_gather(buf, sh, sems)
    for copy in loads + gloads:
        copy.wait()
    width = wbuf.shape[1]

    def step(m, carry):
        arrive(buf, sh, sems, m)
        pm, hm = place(m)
        gg = flat(buf[pm, :, hm])
        for a, n in tiles(width):
            gh = dot(gg, wbuf[2, a : a + n], 1, 1)
            g = gu[m, 0, :, a : a + n]
            u = gu[m, 1, :, a : a + n]
            s = jax.nn.sigmoid(g)
            silu = g * s
            shape = (part.shape[1], part.shape[2], n)
            hid[0, pm, :, hm, :, a : a + n] = (gh * u * (s * (1.0 + g * (1.0 - s)))).astype(bf16).reshape(shape)
            hid[1, pm, :, hm, :, a : a + n] = (gh * silu).astype(bf16).reshape(shape)
            hid[2, pm, :, hm, :, a : a + n] = (silu * u).astype(bf16).reshape(shape)
        for a, n in tiles(D):
            y = dot(flat(hid[0, pm, :, hm]), wbuf[0, :, a : a + n], 1, 0)
            y = y + dot(flat(hid[1, pm, :, hm]), wbuf[1, :, a : a + n], 1, 0)
            part[m, :, :, a : a + n] = y.reshape(part.shape[1], part.shape[2], n)
        scatter(part, xr, ys, yr, sh, sems, m)
        return carry

    lax.fori_loop(0, 4, step, 0)
    nload.wait()
    tokens = 8 * buf.shape[3]

    def grads(other, g):
        def one(i, carry):
            at = pl.ds(pl.multiple_of(i * 128, 128), 128)
            left = hid[g, :, :, :, :, at].reshape(tokens, 128)
            dw[g, at] = dot(left, other[...].reshape(tokens, D), 0, 0).astype(bf16)
            return carry

        lax.fori_loop(0, width // 128, one, 0)

    grads(nbuf, 0)
    grads(nbuf, 1)
    grads(buf, 2)
    stores = [
        pltpu.make_async_copy(
            dw.at[g, pl.ds(c * wide, wide)], dw_ref.at[c, pl.ds(g * wide, wide)], wsem.at[c * 3 + g]
        )
        for c in range(cols)
        for g in range(3)
    ]
    for copy in stores:
        copy.start()
    n = end_scatter(part, xr, ys, yr, sh, sems)
    norm_back(n, x_ref, gain_ref, grad_ref, out_ref, gain_out)
    end_gather(buf, sh, sems)
    for copy in stores:
        copy.wait()


def shape(dims, kind):
    return jax.ShapeDtypeStruct(dims, kind)


def scatter_scratch(seqs, sh):
    return [
        pltpu.VMEM((4, seqs, 2 * sh, D), f32),
        pltpu.VMEM((4, seqs, sh, D), f32),
        pltpu.VMEM((4, seqs, sh, D), bf16),
        pltpu.VMEM((4, seqs, sh, D), bf16),
    ]


def call(kernel, name, cid, outs, out_specs, in_specs, scratch, args, flops=46 * 10**9, limit=60):
    return pl.pallas_call(
        kernel,
        name=name,
        out_shape=outs,
        in_specs=in_specs,
        out_specs=out_specs,
        scratch_shapes=scratch,
        cost_estimate=pl.CostEstimate(flops=flops, bytes_accessed=10**7, transcendentals=0),
        compiler_params=pltpu.CompilerParams(
            collective_id=cid, has_side_effects=True, vmem_limit_bytes=limit << 20
        ),
    )(*args)


DMA = pltpu.SemaphoreType.DMA


def ffn_forward(cid, x, gain, w, wide):
    seqs, sh, _ = x.shape
    cols = w.shape[0]
    width = padded(cols * wide)
    full = (2, seqs, 2, 2 * sh, D)
    rows = seqs * 2 * sh
    return call(
        functools.partial(ffn_forward_kernel, sh, wide), "ffn_forward", cid,
        (shape(x.shape, f32), shape(full, bf16), shape((4, 2, rows, width), f32)),
        (VMEM, ANY, ANY), (VMEM, VMEM, ANY),
        [
            pltpu.VMEM(full, bf16), pltpu.VMEM((3, width, D), bf16),
            pltpu.VMEM((4, 2, rows, width), f32), pltpu.VMEM((rows, width), bf16),
        ] + scatter_scratch(seqs, sh) + [DMA((12, 4)), DMA((3 * cols,)), DMA((5,))],
        (x, gain, w),
    )


def ffn_backward(cid, grad, x, gain, w, n, gu, wide):
    seqs, sh, _ = x.shape
    cols = w.shape[0]
    width = padded(cols * wide)
    full = (2, seqs, 2, 2 * sh, D)
    rows = seqs * 2 * sh
    return call(
        functools.partial(ffn_backward_kernel, sh, wide), "ffn_backward", cid,
        (shape(x.shape, f32), shape((1, D), f32), shape(w.shape, bf16)),
        (VMEM, VMEM, ANY), (VMEM, VMEM, VMEM, ANY, ANY, ANY),
        [
            pltpu.VMEM(full, bf16), pltpu.VMEM(full, bf16), pltpu.VMEM((3, width, D), bf16),
            pltpu.VMEM((4, 2, rows, width), f32), pltpu.VMEM((3,) + full[:4] + (width,), bf16),
            pltpu.VMEM((3, width, D), bf16),
        ] + scatter_scratch(seqs, sh) + [DMA((12, 4)), DMA((3 * cols,)), DMA((5,))],
        (grad, x, gain, w, n, gu),
    )


def greet_all():
    barrier = pltpu.get_barrier_semaphore()
    count = lax.axis_size("cols")
    c = lax.axis_index("cols")
    for to in [sibling()] + [peer(m) for m in (1, 2, 3)]:
        pl.semaphore_signal(barrier, inc=1, device_id=to, device_id_type=MESH)
    for i in range(1, count):
        to = {"cols": lax.rem(c + i, count)}
        pl.semaphore_signal(barrier, inc=1, device_id=to, device_id_type=MESH)
    pl.semaphore_wait(barrier, 3 + count)


def out_copy(stage, dest, sems, m, i):
    pm, hm = place(m)
    c = lax.axis_index("cols")
    s = pm * stage.shape[1] + i
    return s, remote(
        stage.at[m, i], dest.at[c, hm], sems.at[0, m * 2 + i], sems.at[1, c * 2 + hm], {"cols": s}
    )


def send_out(stage, dest, sems, m):
    pm, hm = place(m)
    c = lax.axis_index("cols")
    for i in range(stage.shape[1]):
        s, copy = out_copy(stage, dest, sems, m, i)

        @pl.when(s == c)
        def _():
            dest[c, hm] = stage[m, i]

        @pl.when(s != c)
        def _():
            copy.start()


def wait_out(stage, dest, sems):
    c = lax.axis_index("cols")
    for z in range(dest.shape[0]):
        for h in range(2):

            @pl.when(z != c)
            def _():
                got = dest.at[z, h]
                remote(got, got, sems.at[0, z * 2 + h], sems.at[1, z * 2 + h], {"cols": z}).wait_recv()


def end_out(stage, dest, sems):
    c = lax.axis_index("cols")
    for m in range(4):
        for i in range(stage.shape[1]):
            s, copy = out_copy(stage, dest, sems, m, i)

            @pl.when(s != c)
            def _():
                copy.wait_send()


def back_copy(stage, dest, sems, i):
    c = lax.axis_index("cols")
    seqs = dest.shape[1]
    return remote(
        stage.at[i], dest.at[c // seqs, lax.rem(c, seqs)], sems.at[2, i], sems.at[3, c], {"cols": i}
    )


def send_back(stage, dest, sems, i):
    c = lax.axis_index("cols")
    seqs = dest.shape[1]

    @pl.when(i == c)
    def _():
        dest[c // seqs, lax.rem(c, seqs)] = stage[i]

    @pl.when(i != c)
    def _():
        back_copy(stage, dest, sems, i).start()


def wait_back(stage, dest, sems):
    c = lax.axis_index("cols")
    seqs = dest.shape[1]
    for s in range(stage.shape[0]):

        @pl.when(s != c)
        def _():
            got = dest.at[s // seqs, s % seqs]
            remote(got, got, sems.at[2, s], sems.at[3, s], {"cols": s}).wait_recv()
            back_copy(stage, dest, sems, s).wait_send()


def low_lanes(x):
    return lax.broadcasted_iota(jnp.int32, x.shape, x.ndim - 1) < HD


def per_head(x):
    low = low_lanes(x)
    a = jnp.sum(jnp.where(low, x, 0.0), axis=-1, keepdims=True)
    b = jnp.sum(jnp.where(low, 0.0, x), axis=-1, keepdims=True)
    return jnp.where(low, a, b) * (1.0 / HD)


def partner(x):
    lane = lax.rem(lax.broadcasted_iota(jnp.int32, x.shape, x.ndim - 1), HD)
    return jnp.where(lane < HD // 2, pltpu.roll(x, 2 * HD - HD // 2, axis=1), pltpu.roll(x, HD // 2, axis=1))


def swap(x):
    return pltpu.roll(x, HD, axis=1)


def rope_forward(x, gain, cos, sin):
    y = x * lax.rsqrt(per_head(x * x) + epsilon) * gain
    return y * cos + partner(y) * sin


def rope_backward(x, gain, cos, sin, grad):
    inv = lax.rsqrt(per_head(x * x) + epsilon)
    g = grad * cos - partner(grad) * sin
    scaled = g * gain
    out = scaled * inv - x * (inv * inv * inv) * per_head(scaled * x)
    return out, jnp.sum(g * x * inv, axis=0, keepdims=True)


def split_heads(x, upper):
    x = x.astype(f32)
    low = low_lanes(x)
    if upper:
        return jnp.where(low, 0.0, swap(x)).astype(bf16), jnp.where(low, 0.0, x).astype(bf16)
    return jnp.where(low, x, 0.0).astype(bf16), jnp.where(low, swap(x), 0.0).astype(bf16)


def probabilities(q, keys, first, length):
    s = dot(q, keys, 1, 1)
    at = lax.broadcasted_iota(jnp.int32, s.shape, 1)
    row = lax.broadcasted_iota(jnp.int32, s.shape, 0) + first
    s = jnp.where((at <= row) & (at < length), s, -1e30)
    e = jnp.exp(s - jnp.max(s, axis=1, keepdims=True))
    return e * (1.0 / jnp.sum(e, axis=1, keepdims=True))


def key_bound(i, slots):
    return min(-(-(i + 1) * slots // 128) * 128, 4 * slots)


def attention_forward_kernel(sh, x_ref, gain_ref, w_ref, wo_ref, cos_ref, sin_ref, gq_ref, gk_ref, len_ref,
                             out_ref, n_ref, raw_ref, seq_ref, att_ref,
                             buf, stage, q2, kv, o, back, part, xr, ys, yr, sems, zsems, osem):
    c = lax.axis_index("cols")
    slots = 4 * sh
    put_own(buf, sh, norm_own(x_ref, gain_ref))
    greet_all()
    start_gather(buf, sh, sems)
    low = low_lanes(gq_ref[...])

    def step(m, carry):
        arrive(buf, sh, sems, m)
        pm, hm = place(m)
        y = dot(flat(buf[pm, :, hm]), w_ref[...], 1, 1)
        raw_ref[pm, :, hm] = y.reshape(raw_ref.shape[1], 2 * sh, 4 * HD)
        for i in range(stage.shape[1]):
            rows = slice(i * 2 * sh, (i + 1) * 2 * sh)
            cos, sin = cos_ref[hm], sin_ref[hm]
            q = rope_forward(y[rows, : 2 * HD], gq_ref[...], cos, sin) * (HD**-0.5)
            raw = y[rows, 2 * HD :]
            k = rope_forward(raw, gk_ref[...], cos, sin)
            stage[m, i, :, : 2 * HD] = q.astype(bf16)
            stage[m, i, :, 2 * HD :] = jnp.where(low, k, raw).astype(bf16)
        send_out(stage, seq_ref, zsems, m)
        return carry

    lax.fori_loop(0, 4, step, 0)
    save = pltpu.make_async_copy(buf, n_ref, osem.at[0])
    save.start()
    wait_out(stage, seq_ref, zsems)
    for i in range(4):
        for h in range(2):
            kv[i, h] = seq_ref[i, h, :, 2 * HD :]
            a, b = split_heads(seq_ref[i, h, :, : 2 * HD], False)
            q2[i, 0, h], q2[i, 1, h] = a, b
    length = len_ref[0]
    for i in range(4):
        bound = key_bound(i, slots)

        def tile(u, carry, i=i, bound=bound):
            head, h = u // 2, lax.rem(u, 2)
            keys = kv[...].reshape(4 * slots, 2 * HD)[:bound]
            p = probabilities(q2[i, head, h], keys, i * slots + h * 2 * sh, length)
            o[head, h] = dot(p.astype(bf16), keys, 1, 0)
            return carry

        lax.fori_loop(0, 4, tile, 0)
        for h in range(2):
            back[i, h] = jnp.where(low, swap(o[0, h]), o[1, h]).astype(bf16)
        send_back(back, att_ref, zsems, i)
    wait_back(back, att_ref, zsems)

    def merge_step(i, carry):
        m = 3 - i
        pm, hm = place(m)
        y = flat(att_ref[pm, :, hm])
        for a, n in tiles(D):
            z = dot(y, wo_ref[:, a : a + n], 1, 0)
            part[m, :, :, a : a + n] = z.reshape(part.shape[1], part.shape[2], n)
        scatter(part, xr, ys, yr, sh, sems, m)
        return carry

    lax.fori_loop(0, 4, merge_step, 0)
    out_ref[...] = x_ref[...] + end_scatter(part, xr, ys, yr, sh, sems)
    end_gather(buf, sh, sems)
    end_out(stage, seq_ref, zsems)
    save.wait()


def attention_backward_kernel(sh, grad_ref, x_ref, gain_ref, w_ref, wo_ref, cos_ref, sin_ref, gq_ref, gk_ref, len_ref,
                              n_ref, raw_ref, seq_ref, att_ref,
                              out_ref, gain_out, head_out, dw_ref,
                              buf, nbuf, stage, dseq, q2, do2, kv, dq, dkv, back, dproj, gproj,
                              part, xr, ys, yr, sems, zsems, osem):
    c = lax.axis_index("cols")
    slots = 4 * sh
    tokens = 8 * buf.shape[3]
    nload = pltpu.make_async_copy(n_ref, nbuf, osem.at[0])
    nload.start()
    put_own(buf, sh, grad_ref[...])
    greet_all()
    start_gather(buf, sh, sems)
    low = low_lanes(gq_ref[...])
    for i in range(4):
        for h in range(2):
            kv[i, h] = seq_ref[i, h, :, 2 * HD :]
            a, b = split_heads(seq_ref[i, h, :, : 2 * HD], False)
            q2[i, 0, h], q2[i, 1, h] = a, b
    dkv[...] = jnp.zeros_like(dkv)
    head_out[...] = jnp.zeros_like(head_out)

    def step(m, carry):
        arrive(buf, sh, sems, m)
        pm, hm = place(m)
        y = dot(flat(buf[pm, :, hm]), wo_ref[...], 1, 1).astype(bf16)
        stage[m] = y.reshape(stage.shape[1], 2 * sh, 2 * HD)
        send_out(stage, dseq, zsems, m)
        return carry

    lax.fori_loop(0, 4, step, 0)
    wait_out(stage, dseq, zsems)
    length = len_ref[0]
    for i in range(4):
        for h in range(2):
            a, b = split_heads(dseq[i, h], True)
            do2[i, 0, h], do2[i, 1, h] = a, b
    for i in range(4):
        bound = key_bound(i, slots)

        def tile(u, carry, i=i, bound=bound):
            head, h = u // 2, lax.rem(u, 2)
            keys = kv[...].reshape(4 * slots, 2 * HD)[:bound]
            q, do = q2[i, head, h], do2[i, head, h]
            p = probabilities(q, keys, i * slots + h * 2 * sh, length)
            dp = dot(do, keys, 1, 1)
            ds = (p * (dp - jnp.sum(p * dp, axis=1, keepdims=True))).astype(bf16)
            dq[head, h] = dot(ds, keys, 1, 0) * (HD**-0.5)
            dkv[:, :bound] += dot(q, ds, 0, 0) + dot(do, p.astype(bf16), 0, 0)
            return carry

        lax.fori_loop(0, 4, tile, 0)
        for h in range(2):
            back[i, h, :, : 2 * HD] = jnp.where(low, dq[0, h], swap(dq[1, h])).astype(bf16)
    grads = dkv[...].T.reshape(4, 2, 2 * sh, 2 * HD)
    for i in range(4):
        back[i, :, :, 2 * HD :] = grads[i].astype(bf16)
        send_back(back, dproj, zsems, i)
    wait_back(back, dproj, zsems)

    def merge_step(t, carry):
        m = 3 - t
        pm, hm = place(m)
        for i in range(stage.shape[1]):
            cos, sin = cos_ref[hm], sin_ref[hm]
            g = dproj[pm, i, hm].astype(f32)
            raw = raw_ref[pm, i, hm]
            a, ga = rope_backward(raw[:, : 2 * HD], gq_ref[...], cos, sin, g[:, : 2 * HD])
            b, gb = rope_backward(raw[:, 2 * HD :], gk_ref[...], cos, sin, g[:, 2 * HD :])
            gproj[pm, i, hm, :, : 2 * HD] = a.astype(bf16)
            gproj[pm, i, hm, :, 2 * HD :] = jnp.where(low, b, g[:, 2 * HD :]).astype(bf16)
            head_out[0:1] += ga
            head_out[1:2] += gb
        y = flat(gproj[pm, :, hm])
        for a, n in tiles(D):
            z = dot(y, w_ref[:, a : a + n], 1, 0)
            part[m, :, :, a : a + n] = z.reshape(part.shape[1], part.shape[2], n)
        scatter(part, xr, ys, yr, sh, sems, m)
        return carry

    lax.fori_loop(0, 4, merge_step, 0)
    nload.wait()
    left = gproj[...].reshape(tokens, 4 * HD)
    dw_ref[: 4 * HD] = dot(left, nbuf[...].reshape(tokens, D), 0, 0).astype(bf16)
    left = att_ref[...].reshape(tokens, 2 * HD)
    dw_ref[4 * HD :] = dot(left, buf[...].reshape(tokens, D), 0, 0).astype(bf16)
    n = end_scatter(part, xr, ys, yr, sh, sems)
    norm_back(n, x_ref, gain_ref, grad_ref, out_ref, gain_out)
    end_gather(buf, sh, sems)
    end_out(stage, dseq, zsems)


SMEM = pl.BlockSpec(memory_space=pltpu.SMEM)


def attention_forward(cid, x, gain, w, wo, tables, length):
    seqs, sh, _ = x.shape
    full = (2, seqs, 2, 2 * sh)
    zshape = (4, 2, 2 * sh)
    return call(
        functools.partial(attention_forward_kernel, sh), "attention_forward", cid,
        (shape(x.shape, f32), shape(full + (D,), bf16), shape(full + (4 * HD,), f32),
         shape(zshape + (4 * HD,), bf16), shape(full + (2 * HD,), bf16)),
        (VMEM, ANY, VMEM, VMEM, VMEM), (VMEM,) * 8 + (SMEM,),
        [
            pltpu.VMEM(full + (D,), bf16), pltpu.VMEM((4, seqs, 2 * sh, 4 * HD), bf16),
            pltpu.VMEM((4, 2, 2, 2 * sh, 2 * HD), bf16), pltpu.VMEM(zshape + (2 * HD,), bf16),
            pltpu.VMEM((2, 2, 2 * sh, 2 * HD), f32), pltpu.VMEM(zshape + (2 * HD,), bf16),
        ] + scatter_scratch(seqs, sh) + [DMA((12, 4)), DMA((4, 8)), DMA((1,))],
        (x, gain, w, wo) + tables + (length,), limit=48,
    )


def attention_backward(cid, grad, x, gain, w, wo, tables, length, n, raw, seq, att):
    seqs, sh, _ = x.shape
    full = (2, seqs, 2, 2 * sh)
    zshape = (4, 2, 2 * sh)
    return call(
        functools.partial(attention_backward_kernel, sh), "attention_backward", cid,
        (shape(x.shape, f32), shape((1, D), f32), shape((2, 2 * HD), f32), shape((6 * HD, D), bf16)),
        (VMEM,) * 4, (VMEM,) * 9 + (SMEM, ANY, VMEM, VMEM, VMEM),
        [
            pltpu.VMEM(full + (D,), bf16), pltpu.VMEM(full + (D,), bf16),
            pltpu.VMEM((4, seqs, 2 * sh, 2 * HD), bf16), pltpu.VMEM(zshape + (2 * HD,), bf16),
            pltpu.VMEM((4, 2, 2, 2 * sh, 2 * HD), bf16), pltpu.VMEM((4, 2, 2, 2 * sh, 2 * HD), bf16),
            pltpu.VMEM(zshape + (2 * HD,), bf16), pltpu.VMEM((2, 2, 2 * sh, 2 * HD), f32),
            pltpu.VMEM((2 * HD, 16 * sh), f32), pltpu.VMEM(zshape + (4 * HD,), bf16),
            pltpu.VMEM(full + (4 * HD,), bf16), pltpu.VMEM(full + (4 * HD,), bf16),
        ] + scatter_scratch(seqs, sh) + [DMA((12, 4)), DMA((4, 8)), DMA((1,))],
        (grad, x, gain, w, wo) + tables + (length, n, raw, seq, att), limit=58,
    )


def edge_copy(src, dst, sems, step, recv):
    c = lax.axis_index("cols")
    to = c - step if recv else c + step
    return remote(src, dst, sems.at[0], sems.at[1], {"cols": to})


def exchange_edge(src, dst, sems, step):
    c = lax.axis_index("cols")
    count = lax.axis_size("cols")
    sends = c < count - 1 if step > 0 else c > 0
    gets = c > 0 if step > 0 else c < count - 1

    @pl.when(sends)
    def _():
        edge_copy(src, dst, sems, step, False).start()

    @pl.when(gets)
    def _():
        edge_copy(src, dst, sems, step, True).wait_recv()

    @pl.when(jnp.logical_not(gets))
    def _():
        dst[...] = jnp.zeros(dst.shape, f32)

    @pl.when(sends)
    def _():
        edge_copy(src, dst, sems, step, False).wait_send()


def window(ref, s, hm, rows):
    return ref[s, pl.ds(pl.multiple_of(hm * rows, 8), rows + 8)]


def convolve(taps, ext, rows):
    return sum(taps[k : k + 1] * ext[8 - (CONV - 1) + k : 8 - (CONV - 1) + k + rows] for k in range(CONV))


def conv_forward_kernel(sh, x_ref, gain_ref, w_ref, wo_ref, taps_ref,
                        out_ref, n_ref, mixed_ref, prod_ref,
                        buf, cmix, part, xr, ys, yr, sems, zsems, osem):
    seqs, rows = buf.shape[1], 2 * sh
    ch = wo_ref.shape[0]
    slots = 2 * rows
    put_own(buf, sh, norm_own(x_ref, gain_ref))
    greet_all()
    start_gather(buf, sh, sems)

    def step(m, carry):
        arrive(buf, sh, sems, m)
        pm, hm = place(m)
        y = dot(flat(buf[pm, :, hm]), w_ref[...], 1, 1)
        mixed_ref[pm, :, hm] = y.reshape(seqs, rows, 3 * ch)
        for i in range(seqs):
            z = y[i * rows : (i + 1) * rows]
            at = pl.ds(pl.multiple_of(8 + hm * rows, 8), rows)
            prod_ref[pm * seqs + i, at] = z[:, :ch] * z[:, 2 * ch :]
        return carry

    lax.fori_loop(0, 4, step, 0)
    save = pltpu.make_async_copy(buf, n_ref, osem.at[0])
    save.start()
    exchange_edge(prod_ref.at[:, pl.ds(slots, 8)], prod_ref.at[:, pl.ds(0, 8)], zsems, 1)
    taps = taps_ref[...]

    def merge_step(t, carry):
        m = 3 - t
        pm, hm = place(m)
        for i in range(seqs):
            conv = convolve(taps, window(prod_ref, pm * seqs + i, hm, rows), rows)
            cmix[i] = (mixed_ref[pm, i, hm, :, ch : 2 * ch] * conv).astype(bf16)
        y = flat(cmix[...])
        for a, n in tiles(D):
            z = dot(y, wo_ref[:, a : a + n], 1, 0)
            part[m, :, :, a : a + n] = z.reshape(seqs, rows, n)
        scatter(part, xr, ys, yr, sh, sems, m)
        return carry

    lax.fori_loop(0, 4, merge_step, 0)
    out_ref[...] = x_ref[...] + end_scatter(part, xr, ys, yr, sh, sems)
    end_gather(buf, sh, sems)
    save.wait()


def conv_backward_kernel(sh, grad_ref, x_ref, gain_ref, w_ref, wo_ref, taps_ref, n_ref, mixed_ref, prod_ref,
                         out_ref, gain_out, taps_out, dw_ref,
                         buf, nbuf, gext, gmix, gin, cmix, part, xr, ys, yr, sems, zsems, osem):
    seqs, rows = buf.shape[1], 2 * sh
    ch = wo_ref.shape[0]
    slots = 2 * rows
    tokens = 8 * rows
    nload = pltpu.make_async_copy(n_ref, nbuf, osem.at[0])
    nload.start()
    put_own(buf, sh, grad_ref[...])
    greet_all()
    start_gather(buf, sh, sems)
    taps_out[...] = jnp.zeros_like(taps_out)

    def step(m, carry):
        arrive(buf, sh, sems, m)
        pm, hm = place(m)
        y = dot(flat(buf[pm, :, hm]), wo_ref[...], 1, 1)
        for i in range(seqs):
            z = y[i * rows : (i + 1) * rows]
            gmix[pm, i, hm] = z
            at = pl.ds(pl.multiple_of(hm * rows, 8), rows)
            gext[pm * seqs + i, at] = z * mixed_ref[pm, i, hm, :, ch : 2 * ch]
        return carry

    lax.fori_loop(0, 4, step, 0)
    exchange_edge(gext.at[:, pl.ds(0, 8)], gext.at[:, pl.ds(slots, 8)], zsems, -1)
    taps = taps_ref[...]

    def merge_step(t, carry):
        m = 3 - t
        pm, hm = place(m)
        for i in range(seqs):
            ext = window(prod_ref, pm * seqs + i, hm, rows)
            conv = convolve(taps, ext, rows)
            g = window(gext, pm * seqs + i, hm, rows)
            gprod = sum(taps[k : k + 1] * g[CONV - 1 - k : CONV - 1 - k + rows] for k in range(CONV))
            for k in range(CONV):
                shifted = ext[8 - (CONV - 1) + k : 8 - (CONV - 1) + k + rows]
                taps_out[k : k + 1] += jnp.sum(g[:rows] * shifted, axis=0, keepdims=True)
            mix = mixed_ref[pm, i, hm]
            gin[pm, i, hm, :, :ch] = (gprod * mix[:, 2 * ch :]).astype(bf16)
            gin[pm, i, hm, :, ch : 2 * ch] = (gmix[pm, i, hm] * conv).astype(bf16)
            gin[pm, i, hm, :, 2 * ch :] = (gprod * mix[:, :ch]).astype(bf16)
            cmix[pm, i, hm] = (mix[:, ch : 2 * ch] * conv).astype(bf16)
        y = flat(gin[pm, :, hm])
        for a, n in tiles(D):
            z = dot(y, w_ref[:, a : a + n], 1, 0)
            part[m, :, :, a : a + n] = z.reshape(seqs, rows, n)
        scatter(part, xr, ys, yr, sh, sems, m)
        return carry

    lax.fori_loop(0, 4, merge_step, 0)
    nload.wait()
    left = gin[...].reshape(tokens, 3 * ch)
    dw_ref[: 3 * ch] = dot(left, nbuf[...].reshape(tokens, D), 0, 0).astype(bf16)
    left = cmix[...].reshape(tokens, ch)
    dw_ref[3 * ch :] = dot(left, buf[...].reshape(tokens, D), 0, 0).astype(bf16)
    n = end_scatter(part, xr, ys, yr, sh, sems)
    norm_back(n, x_ref, gain_ref, grad_ref, out_ref, gain_out)
    end_gather(buf, sh, sems)


def conv_forward(cid, x, gain, w, wo, taps):
    seqs, sh, _ = x.shape
    full = (2, seqs, 2, 2 * sh)
    ch = wo.shape[0]
    return call(
        functools.partial(conv_forward_kernel, sh), "conv_forward", cid,
        (shape(x.shape, f32), shape(full + (D,), bf16), shape(full + (3 * ch,), f32),
         shape((2 * seqs, 4 * sh + 8, ch), f32)),
        (VMEM, ANY, VMEM, VMEM), (VMEM,) * 5,
        [pltpu.VMEM(full + (D,), bf16), pltpu.VMEM((seqs, 2 * sh, ch), bf16)]
        + scatter_scratch(seqs, sh) + [DMA((12, 4)), DMA((2,)), DMA((1,))],
        (x, gain, w, wo, taps), limit=40,
    )


def conv_backward(cid, grad, x, gain, w, wo, taps, n, mixed, prod):
    seqs, sh, _ = x.shape
    full = (2, seqs, 2, 2 * sh)
    ch = wo.shape[0]
    return call(
        functools.partial(conv_backward_kernel, sh), "conv_backward", cid,
        (shape(x.shape, f32), shape((1, D), f32), shape((CONV, ch), f32), shape((4 * ch, D), bf16)),
        (VMEM,) * 4, (VMEM,) * 6 + (ANY, VMEM, VMEM),
        [
            pltpu.VMEM(full + (D,), bf16), pltpu.VMEM(full + (D,), bf16),
            pltpu.VMEM((2 * seqs, 4 * sh + 8, ch), f32), pltpu.VMEM(full + (ch,), f32),
            pltpu.VMEM(full + (3 * ch,), bf16), pltpu.VMEM(full + (ch,), bf16),
        ] + scatter_scratch(seqs, sh) + [DMA((12, 4)), DMA((2,)), DMA((1,))],
        (grad, x, gain, w, wo, taps, n, mixed, prod), limit=52,
    )


def band(ref, i, width):
    return ref.at[..., pl.ds(pl.multiple_of(i * width, 128), width)]


def row_pieces(kind, src, dst, here, there):
    rows = lax.axis_size("rows")
    if kind == "weights":
        return src.at[there], band(dst, here, src.shape[2])
    if kind == "tokens":
        sh = src.shape[1] // rows
        return src.at[:, pl.ds(pl.multiple_of(there * sh, 8), sh)], band(dst, here, src.shape[2])
    if kind == "gains":
        return src, band(dst, here, src.shape[1])
    sh = src.shape[1]
    return band(src, there, dst.shape[2]), dst.at[:, pl.ds(pl.multiple_of(here * sh, 8), sh)]


def row_copies(kind, src, dst, sems, i):
    rows = lax.axis_size("rows")
    r = lax.axis_index("rows")
    sends, gets = [], []
    for k in range(1, rows):
        to, come = lax.rem(r + k, rows), lax.rem(r + rows - k, rows)
        a, b = row_pieces(kind, src, dst, r, to)
        sends.append(remote(a, b, sems.at[0, i, k], sems.at[1, i, k], {"rows": to}))
        a, b = row_pieces(kind, src, dst, come, r)
        gets.append(remote(a, b, sems.at[0, i, k], sems.at[1, i, k], {"rows": to}))
    a, b = row_pieces(kind, src, dst, r, r)
    return sends, gets, pltpu.make_async_copy(a, b, sems.at[0, i, 0])


def line_copies(axis, src, dst, sems, i):
    count = lax.axis_size(axis) if axis == "cols" else 2
    at = lax.axis_index(axis)
    low = lax.rem(at, count)
    base = at - low
    sends, gets = [], []
    for k in range(1, count):
        to, come = lax.rem(low + k, count), lax.rem(low + count - k, count)
        sends.append(remote(src, dst.at[low], sems.at[0, i, k], sems.at[1, i, k], {axis: base + to}))
        gets.append(remote(src, dst.at[come], sems.at[0, i, k], sems.at[1, i, k], {axis: base + to}))
    return sends, gets, pltpu.make_async_copy(src, dst.at[low], sems.at[0, i, 0])


def greet_lines(cols, pair):
    barrier = pltpu.get_barrier_semaphore()
    rows = lax.axis_size("rows")
    to = [{"rows": lax.rem(lax.axis_index("rows") + k, rows)} for k in range(1, rows)]
    if cols:
        count = lax.axis_size("cols")
        to += [{"cols": lax.rem(lax.axis_index("cols") + k, count)} for k in range(1, count)]
    if pair:
        d = lax.axis_index("dp")
        to += [{"dp": d + 1 - 2 * lax.rem(d, 2)}]
    for device in to:
        pl.semaphore_signal(barrier, inc=1, device_id=device, device_id_type=MESH)
    pl.semaphore_wait(barrier, len(to))


def greet_box(pairs):
    barrier = pltpu.get_barrier_semaphore()
    rows, cols = lax.axis_size("rows"), lax.axis_size("cols")
    d, r, c = lax.axis_index("dp"), lax.axis_index("rows"), lax.axis_index("cols")
    for p in range(pairs):
        for i in range(rows):
            for j in range(cols):
                if p + i + j > 0:
                    to = {"dp": d if p == 0 else d + 1 - 2 * lax.rem(d, 2),
                          "rows": lax.rem(r + i, rows), "cols": lax.rem(c + j, cols)}
                    pl.semaphore_signal(barrier, inc=1, device_id=to, device_id_type=MESH)
    pl.semaphore_wait(barrier, pairs * rows * cols - 1)


def attention_spread(src, dst, sems, i):
    halves, cols, _, width = src.shape
    rows = lax.axis_size("rows")
    r, c = lax.axis_index("rows"), lax.axis_index("cols")
    pair = lax.rem(lax.axis_index("dp"), 2)
    holds = pair == halves * c // rows
    first = lax.rem(halves * c, rows)
    origin = (pair * rows + r) // halves

    def to_others(act, local):
        for h in range(halves):
            for z in range(cols):
                own = (first + h == r) & (z == c)
                here = band(dst, r, width)

                @pl.when(holds & jnp.logical_not(own))
                def _():
                    act(remote(src.at[h, z], here, sems.at[0, h * cols + z], sems.at[1, r],
                               {"rows": first + h, "cols": z}))

                @pl.when(holds & own)
                def _():
                    local(pltpu.make_async_copy(src.at[h, z], here, sems.at[0, h * cols + z]))

    def start():
        to_others(lambda copy: copy.start(), lambda copy: copy.start())

    def end():
        for k in range(rows):
            @pl.when(jnp.logical_not((origin == c) & (k == r)))
            def _():
                got = band(dst, k, width)
                remote(got, got, sems.at[0, 0], sems.at[1, k], {"rows": k, "cols": origin}).wait_recv()
        to_others(lambda copy: copy.wait_send(), lambda copy: copy.wait())

    return start, end


def exchange_kernel(kinds, *refs):
    n = len(kinds)
    ins, outs, sems = refs[:n], refs[n : 2 * n], refs[2 * n]
    if "attention" in kinds:
        greet_box(1)
    else:
        greet_lines("taps" in kinds, "lengths" in kinds)
    if "attention" in kinds:
        at = kinds.index("attention")
        start, end = attention_spread(ins[at], outs[at], refs[2 * n + 1], at)
        start()
    work = []
    for i, kind in enumerate(kinds):
        if kind == "attention":
            continue
        if kind == "taps":
            work.append(line_copies("cols", ins[i], outs[i], sems, i))
        elif kind == "lengths":
            work.append(line_copies("dp", ins[i], outs[i], sems, i))
        else:
            work.append(row_copies(kind, ins[i], outs[i], sems, i))
    for sends, _, local in work:
        for copy in sends:
            copy.start()
        local.start()
    for sends, gets, local in work:
        for copy in gets:
            copy.wait_recv()
        for copy in sends:
            copy.wait_send()
        local.wait()
    if "attention" in kinds:
        end()


def exchange(cid, name, kinds, arrays, rows, cols):
    outs = []
    for kind, x in zip(kinds, arrays):
        dims = {
            "weights": lambda: (x.shape[1], rows * x.shape[2]),
            "tokens": lambda: (x.shape[0], x.shape[1] // rows, rows * x.shape[2]),
            "gains": lambda: (x.shape[0], rows * x.shape[1]),
            "attention": lambda: (x.shape[2], rows * x.shape[3]),
            "taps": lambda: (cols,) + x.shape,
            "lengths": lambda: (2,) + x.shape,
        }[kind]()
        outs.append(shape(dims, x.dtype))
    n = len(kinds)
    return call(
        functools.partial(exchange_kernel, kinds), name, cid, tuple(outs), (ANY,) * n, (ANY,) * n,
        [DMA((2, n, 4))] + ([DMA((2, 8))] if "attention" in kinds else []), tuple(arrays), limit=8,
    )


def plane_peer(j):
    pm, hm = place(j // 2)
    d, r = lax.axis_index("dp"), lax.axis_index("rows")
    row = hm * 2 + lax.rem(lax.rem(r, 2) + j % 2, 2)
    return pm, row, {"dp": d - lax.rem(d, 2) + pm, "rows": row}


def plane_copies(src, dst, sems, i):
    rows = lax.axis_size("rows")
    width = dst.shape[2]
    pair, r = lax.rem(lax.axis_index("dp"), 2), lax.axis_index("rows")
    sends, gets = [], []
    for j in range(1, 8):
        pm, row, to = plane_peer(j)
        here = band(src, row, width)
        sends.append(remote(here, dst.at[pair * rows + r], sems.at[0, i, j], sems.at[1, i, j], to))
        gets.append(remote(here, dst.at[pm * rows + row], sems.at[0, i, j], sems.at[1, i, j], to))
    return sends, gets, pltpu.make_async_copy(band(src, r, width), dst.at[pair * rows + r], sems.at[0, i, 0])


def greet_plane(cols):
    barrier = pltpu.get_barrier_semaphore()
    to = [plane_peer(j)[2] for j in range(1, 8)]
    if cols:
        count = lax.axis_size("cols")
        to += [{"cols": lax.rem(lax.axis_index("cols") + k, count)} for k in range(1, count)]
    for device in to:
        pl.semaphore_signal(barrier, inc=1, device_id=device, device_id_type=MESH)
    pl.semaphore_wait(barrier, len(to))


def begin_all(work):
    sends, _, local = work
    for copy in sends:
        copy.start()
    local.start()


def end_all(work):
    sends, gets, local = work
    for copy in gets:
        copy.wait_recv()
    for copy in sends:
        copy.wait_send()
    local.wait()


def collect_kernel(per_col, f_ref, a_ref, t_ref, fo_ref, ao_ref, to_ref, sems, rsems):
    rows, cols = lax.axis_size("rows"), lax.axis_size("cols")
    d, r, c = lax.axis_index("dp"), lax.axis_index("rows"), lax.axis_index("cols")
    pair = lax.rem(d, 2)
    me = pair * rows + r
    width = ao_ref.shape[3]
    greet_box(2)
    owner, half = me // per_col, lax.rem(me, per_col)

    def attn_each(act, local):
        for p in range(2):
            for k in range(rows):
                own = (p == pair) & (k == r) & (owner == c)
                here = band(a_ref, k, width)

                @pl.when(jnp.logical_not(own))
                def _():
                    act(remote(here, ao_ref.at[half, c], sems.at[0, 1, p * rows + k], sems.at[2, half, c],
                               {"dp": d - pair + p, "rows": k, "cols": owner}))

                @pl.when(own)
                def _():
                    local(pltpu.make_async_copy(here, ao_ref.at[half, c], sems.at[0, 1, p * rows + k]))

    attn_each(lambda copy: copy.start(), lambda copy: copy.start())
    tok = row_copies("back", t_ref, to_ref, rsems, 0)
    ffn = plane_copies(f_ref, fo_ref, sems, 0)
    begin_all(tok)
    begin_all(ffn)
    for h in range(per_col):
        source = c * per_col + h
        for z in range(cols):

            @pl.when(jnp.logical_not((source == me) & (z == c)))
            def _():
                got = ao_ref.at[h, z]
                to = {"dp": d - pair + source // rows, "rows": lax.rem(source, rows), "cols": z}
                remote(got, got, sems.at[0, 1, 0], sems.at[2, h, z], to).wait_recv()

    attn_each(lambda copy: copy.wait_send(), lambda copy: copy.wait())
    end_all(tok)
    end_all(ffn)


def finish_kernel(f_ref, c_ref, s_ref, t_ref, fo_ref, co_ref, so_ref, to_ref,
                  crecv, csum, srecv, ssum, precv, sems, rsems, lsems):
    cols = c_ref.shape[0]
    c = lax.axis_index("cols")
    greet_plane(True)
    small = line_copies("cols", s_ref, srecv, lsems, 0)
    begin_all(small)
    sends, gets = [], []
    for k in range(1, cols):
        to, come = lax.rem(c + k, cols), lax.rem(c + cols - k, cols)
        sends.append(remote(c_ref.at[to], crecv.at[c], lsems.at[0, 1, k], lsems.at[1, 1, k], {"cols": to}))
        gets.append(remote(c_ref.at[c], crecv.at[come], lsems.at[0, 1, k], lsems.at[1, 1, k], {"cols": to}))
    conv = (sends, gets, pltpu.make_async_copy(c_ref.at[c], crecv.at[c], lsems.at[0, 1, 0]))
    begin_all(conv)
    tok = row_copies("back", t_ref, to_ref, rsems, 0)
    begin_all(tok)
    ffn = plane_copies(f_ref, fo_ref, sems, 0)
    begin_all(ffn)
    end_all(small)
    ssum[...] = jnp.sum(srecv[...], axis=0)
    rows = lax.axis_size("rows")
    me = lax.rem(lax.axis_index("dp"), 2) * rows + lax.axis_index("rows")
    for j in range(1, 8):
        to = plane_peer(j)[2]
        remote(ssum, precv.at[me], sems.at[0, 2, j], sems.at[1, 2, j], to).start()
    precv[me] = ssum[...]
    end_all(conv)
    csum[...] = jnp.sum(crecv[...].astype(f32), axis=0).astype(bf16)
    last = plane_copies(csum, co_ref, sems, 1)
    begin_all(last)
    for j in range(1, 8):
        pm, row, to = plane_peer(j)
        copy = remote(ssum, precv.at[pm * rows + row], sems.at[0, 2, j], sems.at[1, 2, j], to)
        copy.wait_recv()
        copy.wait_send()
    so_ref[...] = jnp.sum(precv[...], axis=0)
    end_all(tok)
    end_all(ffn)
    end_all(last)


def collect(cid, f, a, t, per_col, rows, cols):
    feat = D // rows
    return call(
        functools.partial(collect_kernel, per_col), "collect", cid,
        (shape((8, f.shape[0], feat), bf16), shape((per_col, cols, a.shape[0], feat), bf16),
         shape((t.shape[0], t.shape[1] * rows, feat), f32)),
        (ANY,) * 3, (ANY,) * 3, [DMA((3, 2, 8)), DMA((2, 1, 4))], (f, a, t), limit=8,
    )


def finish(cid, f, c, s, t, rows):
    feat = D // rows
    cols, n, _ = c.shape
    return call(
        finish_kernel, "finish", cid,
        (shape((8, f.shape[0], feat), bf16), shape((8, n, feat), bf16), shape(s.shape, f32),
         shape((t.shape[0], t.shape[1] * rows, feat), f32)),
        (ANY, ANY, VMEM, ANY), (ANY, ANY, VMEM, ANY),
        [pltpu.VMEM(c.shape, bf16), pltpu.VMEM((n, D), bf16), pltpu.VMEM((cols,) + s.shape, f32),
         pltpu.VMEM(s.shape, f32), pltpu.VMEM((8,) + s.shape, f32),
         DMA((2, 3, 8)), DMA((2, 1, 4)), DMA((2, 2, 4))],
        (f, c, s, t), limit=16,
    )


def per_device(
    hidden_in, lengths, conv_norm, conv_in, conv_kernel, conv_out, conv_ffn_norm, conv_ffn_in,
    conv_ffn_out, attn_norm, attn_q, attn_kv, q_gain, k_gain, attn_out, attn_ffn_norm,
    attn_ffn_in, attn_ffn_out, grad_out,
):
    rows, cols, dps = lax.axis_size("rows"), lax.axis_size("cols"), lax.axis_size("dp")
    tp = 2 * rows
    r, c, d = lax.axis_index("rows"), lax.axis_index("cols"), lax.axis_index("dp")
    pair = lax.rem(d, 2)
    me = pair * rows + r
    slots, seqs, feat = hidden_in.shape
    sh = slots // rows

    def halves(x, axis):
        return lax.dynamic_slice_in_dim(x, pair * rows, rows, axis)

    def cut_in(w):
        parts, width = w.shape[1], w.shape[2] // tp
        x = w.astype(bf16).transpose(1, 2, 0).reshape(parts, tp, width, feat)
        return halves(x, 1).transpose(1, 0, 2, 3).reshape(rows, parts * width, feat)

    def cut_out(w):
        return halves(w.astype(bf16).reshape(tp, -1, feat), 0)

    def cut(w_in, w_out):
        return jnp.concatenate([cut_in(w_in), cut_out(w_out)], axis=1)

    def over_cols(x):
        return lax.all_gather(x, "cols", axis=0)

    def after(x, y):
        return lax.optimization_barrier((x, y))[0]

    wide = conv_ffn_in.shape[2] // tp
    chan = conv_in.shape[2] // tp
    slot_ids = c * slots + jnp.arange(slots, dtype=jnp.int32)
    keep = (slot_ids[None, :] < lengths[:, None]).astype(f32)[:, :, None]
    gains_own = jnp.stack([conv_norm, conv_ffn_norm, attn_norm, attn_ffn_norm])
    conv_cut, begin, ffn1_cut, gains, taps, lens = exchange(
        1, "start", ("weights", "tokens", "weights", "gains", "taps", "lengths"),
        (
            cut(conv_in, conv_out),
            hidden_in.transpose(1, 0, 2) * keep,
            cut(conv_ffn_in, conv_ffn_out),
            jnp.pad(gains_own, ((0, 4), (0, 0))),
            jnp.pad(conv_kernel, ((0, 8 - CONV), (0, 0))),
            jnp.pad(lengths[None], ((0, 7), (0, 128 - seqs))),
        ),
        rows, cols,
    )
    conv_all = over_cols(conv_cut)
    w_conv = conv_all[:, : 3 * chan].reshape(cols, 3, chan, D).transpose(1, 0, 2, 3)
    w_conv = w_conv.reshape(3 * cols * chan, D)
    w_cout = conv_all[:, 3 * chan :].reshape(cols * chan, D)
    gains = gains[:4, None]
    kern = lax.dynamic_slice_in_dim(taps[:, :CONV], me * chan, chan, 2)
    kern = kern.transpose(1, 0, 2).reshape(CONV, cols * chan)
    len_here = lens[:, 0, :seqs].reshape(2 * seqs)
    length = lax.dynamic_slice_in_dim(len_here, c, 1)
    w_ffn1 = over_cols(after(ffn1_cut, conv_all))

    per_col = tp // cols
    q_w = attn_q.shape[1] // per_col
    kv_w = attn_kv.shape[2] // per_col
    parts = jnp.concatenate(
        [
            attn_q.astype(bf16).T.reshape(per_col, q_w, feat),
            attn_kv[:, 0].astype(bf16).T.reshape(per_col, kv_w, feat),
            attn_kv[:, 1].astype(bf16).T.reshape(per_col, kv_w, feat),
            attn_out.astype(bf16).reshape(per_col, q_w, feat),
        ],
        axis=1,
    )
    pieces = parts.reshape(per_col, cols, -1, feat)
    attn_cut, ffn2_cut, grad_final = exchange(
        2, "second", ("attention", "weights", "tokens"),
        (after(pieces, begin), cut(attn_ffn_in, attn_ffn_out), grad_out.transpose(1, 0, 2) * keep),
        rows, cols,
    )
    attn_all = over_cols(after(attn_cut, w_ffn1)).reshape(-1, D)
    w_qkv = attn_all[: q_w + 2 * kv_w]
    w_aout = attn_all[q_w + 2 * kv_w :]
    w_ffn2 = over_cols(after(ffn2_cut, attn_all))

    channels = cols * chan
    after_conv, n_conv, mixed, product = conv_forward(3, begin, gains[0], w_conv, w_cout, kern)
    after_ffn, n_1, gu_1 = ffn_forward(4, after_conv, gains[1], w_ffn1, wide)
    frequency = jnp.power(rope_base, -(jnp.arange(HD // 2, dtype=f32) * 2.0) / HD)
    angles = slot_ids.astype(f32)[:, None] * frequency[None, :]
    cos, sin = jnp.cos(angles), jnp.sin(angles)
    tables = (
        jnp.concatenate([cos] * 4, axis=1).reshape(2, 2 * sh, 2 * HD),
        jnp.concatenate([-sin, sin] * 2, axis=1).reshape(2, 2 * sh, 2 * HD),
        jnp.tile(q_gain, 2)[None],
        jnp.tile(k_gain, 2)[None],
    )
    after_attn, n_attn, raw, seq, attended = attention_forward(
        5, after_ffn, gains[2], w_qkv, w_aout, tables, length
    )
    final, n_2, gu_2 = ffn_forward(6, after_attn, gains[3], w_ffn2, wide)

    def over_pairs(x):
        return x if dps == 2 else lax.psum(x * jnp.asarray(0.5, x.dtype), "dp")

    def native_in(x, count):
        x = x.astype(f32).reshape(tp, count, -1, feat)
        return x.transpose(3, 1, 0, 2).reshape(feat, count, -1)

    def native_out(x):
        return x.astype(f32).reshape(-1, feat)

    grad_attn_res, gain_p3, packed2 = ffn_backward(
        7, grad_final, after_attn, gains[3], w_ffn2, n_2, gu_2, wide
    )
    sum2 = lax.psum_scatter(after(packed2, w_ffn2), "cols", scatter_dimension=0)
    grad_after_ffn, gain_p2, head_parts, grad_attn = attention_backward(
        8, grad_attn_res, after_ffn, gains[2], w_qkv, w_aout, tables, length, n_attn, raw, seq, attended
    )
    sum_attn = lax.psum_scatter(
        after(grad_attn, sum2).reshape(cols, -1, D), "cols", scatter_dimension=0
    )
    grad_after_conv, gain_p1, packed1 = ffn_backward(
        9, grad_after_ffn, after_conv, gains[1], w_ffn1, n_1, gu_1, wide
    )
    sum1 = lax.psum_scatter(after(packed1, sum_attn), "cols", scatter_dimension=0)
    grad_begin, gain_p0, kern_part, grad_conv = conv_backward(
        10, grad_after_conv, begin, gains[0], w_conv, w_cout, kern, n_conv, mixed, product
    )
    got2, got_a, final_here = collect(11, sum2, sum_attn, after(final, grad_begin), per_col, rows, cols)
    got2, got_a = over_pairs(got2), over_pairs(got_a).reshape(per_col, -1, feat)
    output = (final_here * keep).transpose(1, 0, 2)
    g_attn_ffn_in, g_attn_ffn_out = native_in(got2[:, : 2 * wide], 2), native_out(got2[:, 2 * wide :])
    g_q = got_a[:, :q_w].astype(f32).reshape(-1, feat).T
    g_kv = jnp.stack(
        [
            got_a[:, q_w : q_w + kv_w].astype(f32).reshape(-1, feat).T,
            got_a[:, q_w + kv_w : q_w + 2 * kv_w].astype(f32).reshape(-1, feat).T,
        ],
        axis=1,
    )
    g_aout = native_out(got_a[:, q_w + 2 * kv_w :])

    grad_cin = grad_conv[: 3 * channels].reshape(3, cols, chan, D).transpose(1, 0, 2, 3)
    packed0 = jnp.concatenate(
        [grad_cin.reshape(cols, 3 * chan, D), grad_conv[3 * channels :].reshape(cols, chan, D)], axis=1
    )
    zero = jnp.zeros((), jnp.int32)
    kern_full = lax.dynamic_update_slice(
        jnp.zeros((CONV, cols, tp, chan), f32),
        kern_part.reshape(CONV, cols, 1, chan),
        (zero, zero, me, zero),
    )
    heads = jnp.stack([head_parts[0, :HD] + head_parts[0, HD:], head_parts[1, :HD]])
    small = jnp.concatenate(
        [gain_p0, gain_p1, gain_p2, gain_p3, kern_full.reshape(CONV, D), jnp.pad(heads.reshape(1, -1), ((0, 0), (0, D - 2 * HD)))]
    )
    got1, got0, sums, grad_here = finish(12, sum1, packed0, small, grad_begin, rows)
    got1, got0, sums = over_pairs(got1), over_pairs(got0), over_pairs(sums)
    grad_in = (grad_here * keep).transpose(1, 0, 2)
    g_conv_ffn_in, g_conv_ffn_out = native_in(got1[:, : 2 * wide], 2), native_out(got1[:, 2 * wide :])
    g_conv_in, g_conv_out = native_in(got0[:, : 3 * chan], 3), native_out(got0[:, 3 * chan :])
    g_gain = lax.dynamic_slice(sums, (zero, r * feat), (4, feat))
    g_kern = lax.dynamic_slice(sums[4 : 4 + CONV], (zero, c * conv_kernel.shape[1]), conv_kernel.shape)
    return (
        output, grad_in, g_gain[0], g_conv_in, g_kern, g_conv_out, g_gain[1],
        g_conv_ffn_in, g_conv_ffn_out, g_gain[2], g_q, g_kv, sums[7, :HD], sums[7, HD : 2 * HD], g_aout,
        g_gain[3], g_attn_ffn_in, g_attn_ffn_out,
    )


def solution(mesh):
    tokens, vec, mat = P("cols", "dp", "rows"), P("rows"), P("rows", "cols")
    mat3, out, taps = P("rows", None, "cols"), P("cols", "rows"), P(None, "cols")
    weights = (vec, mat3, taps, out, vec, mat3, out, vec, mat, mat3, P(), P(), out, vec, mat3, out)
    return jax.shard_map(
        per_device,
        mesh=mesh,
        in_specs=(tokens, P("dp")) + weights + (tokens,),
        out_specs=(tokens, tokens) + weights,
        check_vma=False,
    )
```

```python
import functools

import jax
import jax.numpy as jnp
from jax import lax
from jax.experimental import pallas as pl
from jax.experimental.pallas import tpu as pltpu
from jax.sharding import PartitionSpec as P

D = 1024
HD = 64
CONV = 3
epsilon = 1e-05
rope_base = 1000000.0
bf16 = jnp.bfloat16
f32 = jnp.float32
MESH = pl.DeviceIdType.MESH
SECOND_ROWS = (160, 48, 48, 80)
SECOND_BACK = (64, 128, 128, 112)
FIRST_BACK = (256, 96, 80)
ANY = pl.BlockSpec(memory_space=pl.ANY)
VMEM = pl.BlockSpec(memory_space=pltpu.VMEM)


def dot(a, b, ca, cb):
    return lax.dot_general(a, b, (((ca,), (cb,)), ((), ())), preferred_element_type=f32)


def place(m):
    d, r = lax.axis_index("dp"), lax.axis_index("rows")
    pair, half = lax.rem(d, 2), r // 2
    return lax.rem(pair + lax.rem(m, 2), 2), lax.rem(half + m // 2, 2)


def peer(m):
    d, r = lax.axis_index("dp"), lax.axis_index("rows")
    pm, hm = place(m)
    return {"dp": d - lax.rem(d, 2) + pm, "rows": hm * 2 + lax.rem(r, 2)}


def sibling():
    r = lax.axis_index("rows")
    return {"rows": r + 1 - 2 * lax.rem(r, 2)}


def remote(src, dst, send, recv, to):
    return pltpu.make_async_remote_copy(
        src_ref=src, dst_ref=dst, send_sem=send, recv_sem=recv, device_id=to, device_id_type=MESH
    )


def share(sh, mine):
    k = lax.rem(lax.axis_index("rows"), 2)
    k = k if mine else 1 - k
    return pl.ds(pl.multiple_of(k * sh, 16), sh)


def greet():
    barrier = pltpu.get_barrier_semaphore()
    rows, cols = lax.axis_size("rows"), lax.axis_size("cols")
    r, c = lax.axis_index("rows"), lax.axis_index("cols")
    to = [peer(1), peer(3)] + [{"rows": lax.rem(r + k, rows)} for k in range(1, rows)]
    to += [{"cols": lax.rem(c + k, cols)} for k in range(1, cols)]
    for device in to:
        pl.semaphore_signal(barrier, inc=1, device_id=device, device_id_type=MESH)
    pl.semaphore_wait(barrier, len(to))


def gather_copy(buf, sh, sems, m, to):
    pm, hm = place(0)
    own = buf.at[pm, :, hm, share(sh, True)]
    return remote(own, own, sems.at[0, m], sems.at[1, m], to)


def relay_copy(buf, sh, sems, m):
    pm, hm = place(m)
    part = buf.at[pm, m - 1, hm, share(sh, True)]
    return remote(part, part, sems.at[8, m], sems.at[9, m], peer(3 - m))


def start_gather(buf, sh, sems):
    gather_copy(buf, sh, sems, 0, sibling()).start()
    for m in (1, 2):
        gather_copy(buf, sh, sems, m, peer(m)).start()


def forward_copy(buf, sh, sems, m, mine):
    pm, hm = place(m)
    part = buf.at[pm, :, hm, share(sh, mine)]
    return remote(part, part, sems.at[2, m], sems.at[3, m], sibling())


def arrive(buf, sh, sems, m):
    def come(src, i, j):
        remote(src, src, sems.at[i - 1, j], sems.at[i, j], sibling()).wait_recv()

    @pl.when(m == 0)
    def _():
        pm, hm = place(0)
        come(buf.at[pm, :, hm, share(sh, False)], 1, 0)

    @pl.when(m == 1)
    def _():
        for j in (1, 2):
            pj, hj = place(j)
            come(buf.at[pj, :, hj, share(sh, True)], 1, j)
            relay_copy(buf, sh, sems, j).start()
            forward_copy(buf, sh, sems, j, True).start()

    @pl.when(m == 3)
    def _():
        pj, hj = place(3)
        for j in (1, 2):
            come(buf.at[pj, j - 1, hj, share(sh, True)], 9, j)
        forward_copy(buf, sh, sems, 3, True).start()

    @pl.when(m > 0)
    def _():
        forward_copy(buf, sh, sems, m, False).wait_recv()


def end_gather(buf, sh, sems):
    gather_copy(buf, sh, sems, 0, sibling()).wait_send()
    for m in (1, 2):
        gather_copy(buf, sh, sems, m, peer(m)).wait_send()
        relay_copy(buf, sh, sems, m).wait_send()
    for m in (1, 2, 3):
        forward_copy(buf, sh, sems, m, True).wait_send()


def sum_copy(ys, yr, sems, m, half):
    return remote(ys.at[m, half], yr.at[m, half], sems.at[6, 2 * half + m - 1], sems.at[7, 2 * half + m - 1], peer(m))


def relay_sum_copy(ys, yr, sems, half):
    return remote(ys.at[3, half], yr.at[3, half], sems.at[10, half], sems.at[11, half], peer(half + 1))


def across_copy(part, xr, sh, sems, m):
    return remote(
        part.at[m, :, share(sh, False)], xr.at[m], sems.at[4, m], sems.at[5, m], sibling()
    )


def scatter(part, xr, ys, yr, sh, sems, m):
    across_copy(part, xr, sh, sems, m).wait_recv()
    both = part[m, :, share(sh, True)] + xr[m]
    xr[m] = both
    ys[m] = both.astype(bf16)

    @pl.when(m == 3)
    def _():
        for half in (0, 1):
            relay_sum_copy(ys, yr, sems, half).start()

    for j in (1, 2):

        @pl.when(m == j)
        def _():
            sum_copy(ys, yr, sems, j, j - 1).start()


def end_scatter(part, xr, ys, yr, sh, sems):
    for half in (0, 1):
        m = 2 - half
        relay_sum_copy(ys, yr, sems, half).wait_recv()
        ys[m, half] = (xr[m, half] + yr[3, half].astype(f32)).astype(bf16)
        sum_copy(ys, yr, sems, m, half).start()
    total = xr[0]
    for m in (1, 2):
        for half in (0, 1):
            sum_copy(ys, yr, sems, m, half).wait_recv()
        total = total + yr[m].astype(f32)
    for half in (0, 1):
        relay_sum_copy(ys, yr, sems, half).wait_send()
        for m in (1, 2):
            sum_copy(ys, yr, sems, m, half).wait_send()
    for m in range(4):
        across_copy(part, xr, sh, sems, m).wait_send()
    return total


def lines(src_of, dst_of, sems):
    count, c = lax.axis_size("cols"), lax.axis_index("cols")
    sends, gets = [], []
    for k in range(1, count):
        to, come = lax.rem(c + k, count), lax.rem(c + count - k, count)
        sends.append(remote(src_of(to), dst_of(c), sems.at[0, k], sems.at[1, k], {"cols": to}))
        gets.append(remote(src_of(c), dst_of(come), sems.at[0, k], sems.at[1, k], {"cols": to}))
    return sends, gets, pltpu.make_async_copy(src_of(c), dst_of(c), sems.at[0, 0])


class Gather:
    def __init__(self, array, lo, n, phase=0):
        self.args = (array,)
        self.phase = phase
        self.lo, self.n = lo, n
        self.relayed = False
        assert lax.axis_size("cols") == 4
        self.outs = ((shape((4, n, D), array.dtype), ANY),)
        self.scratch = [DMA((2, 5))]

    def bind(self, ins, outs, scratch):
        self.src, self.slot, self.sems = ins[0].at[pl.ds(self.lo, self.n)], lambda z: outs[0].at[z], scratch[0]

    @classmethod
    def of(cls, src, slot, sems):
        self = cls.__new__(cls)
        self.relayed = False
        self.src, self.slot, self.sems = src, slot, sems
        return self

    def send(self, t):
        c = lax.axis_index("cols")
        return remote(self.src, self.slot(c), self.sems.at[0, t], self.sems.at[1, c], {"cols": t})

    def pass_on(self):
        c = lax.axis_index("cols")
        part = self.slot(6 - 3 * c)
        return remote(part, part, self.sems.at[0, 4], self.sems.at[1, 6 - 3 * c], {"cols": 3 * c - 3})

    def local(self):
        return pltpu.make_async_copy(self.src, self.slot(lax.axis_index("cols")), self.sems.at[1, 4])

    def each(self, act):
        c = lax.axis_index("cols")
        for off in (2, -2, 1, -1):
            t = c + off

            @pl.when((t >= 0) & (t < 4))
            def _():
                act(self.send(t))

    def start(self):
        self.each(lambda copy: copy.start())
        self.local().start()

    def relay(self):
        self.relayed = True
        c = lax.axis_index("cols")

        @pl.when((c == 1) | (c == 2))
        def _():
            self.pass_on().wait_recv()
            self.pass_on().start()

    def finish(self):
        if not self.relayed:
            self.relay()
        c = lax.axis_index("cols")
        for s in range(4):

            @pl.when((s != c) & (s + 3 * c != 6))
            def _():
                part = self.slot(s)
                remote(part, part, self.sems.at[0, s], self.sems.at[1, s], {"cols": s}).wait_recv()

        self.each(lambda copy: copy.wait_send())

        @pl.when((c == 1) | (c == 2))
        def _():
            self.pass_on().wait_send()

        self.local().wait()


class Reduce:
    def __init__(self, array, lo, n, phase=0):
        self.args = (array,)
        self.phase = phase
        self.lo, self.n = lo, n
        self.relayed = False
        self.outs = ((shape((n, D), array.dtype), VMEM),)
        self.scratch = self.buffers(n)

    @staticmethod
    def buffers(n):
        return [pltpu.VMEM((4, n, D), bf16), pltpu.VMEM((n, D), bf16), pltpu.VMEM((n, D), bf16), DMA((2, 6))]

    def bind(self, ins, outs, scratch):
        self.out = outs[0]
        self.got, self.far, self.own, self.sems = scratch
        self.src = ins[0].at[:, pl.ds(self.lo, self.n)]

    @classmethod
    def of(cls, src, out, scratch):
        self = cls.__new__(cls)
        self.relayed = False
        self.src, self.out, self.n = src, out, out.shape[0]
        self.got, self.far, self.own, self.sems = scratch
        return self

    def send(self, off):
        c = lax.axis_index("cols")
        t = c + off
        if abs(off) == 3:
            return remote(self.src.at[t], self.far, self.sems.at[0, t], self.sems.at[1, 4], {"cols": c + off // 3})
        return remote(self.src.at[t], self.got.at[c], self.sems.at[0, t], self.sems.at[1, c], {"cols": t})

    def send_sum(self):
        c = lax.axis_index("cols")
        t = 6 - 3 * c
        return remote(self.own, self.got.at[c], self.sems.at[0, t], self.sems.at[1, c], {"cols": t})

    def each(self, act, offs):
        c = lax.axis_index("cols")
        for off in offs:
            t = c + off
            ok = (t >= 0) & (t < 4)
            if abs(off) == 2:
                ok = ok & (c != (1 if off == 2 else 2))

            @pl.when(ok)
            def _():
                act(self.send(off))

    def local(self):
        c = lax.axis_index("cols")
        return pltpu.make_async_copy(self.src.at[c], self.got.at[c], self.sems.at[0, 4])

    def load(self):
        c = lax.axis_index("cols")
        return pltpu.make_async_copy(self.src.at[6 - 3 * c], self.own, self.sems.at[0, 5])

    def start(self):
        self.start_far()
        self.start_near()

    def start_far(self):
        self.each(lambda copy: copy.start(), (3, -3))

    def start_near(self):
        c = lax.axis_index("cols")
        self.each(lambda copy: copy.start(), (2, -2, 1, -1))
        self.local().start()

        @pl.when((c == 1) | (c == 2))
        def _():
            self.load().start()

        @pl.when((c == 0) | (c == 3))
        def _():
            self.got[3 - c] = jnp.zeros((self.n, D), bf16)

    def blocks(self):
        return [slice(a, min(a + 48, self.n)) for a in range(0, self.n, 48)]

    def relay(self):
        self.relayed = True
        c = lax.axis_index("cols")

        @pl.when((c == 1) | (c == 2))
        def _():
            self.load().wait()
            remote(self.far, self.far, self.sems.at[0, 0], self.sems.at[1, 4], {"cols": 1}).wait_recv()
            for at in self.blocks():
                self.own[at] = (self.own[at].astype(f32) + self.far[at].astype(f32)).astype(bf16)

            self.send_sum().start()

    def finish(self):
        if not self.relayed:
            self.relay()
        c = lax.axis_index("cols")
        for s in range(4):

            @pl.when((s != c) & (s - c < 3) & (c - s < 3))
            def _():
                part = self.got.at[s]
                remote(part, part, self.sems.at[0, s], self.sems.at[1, s], {"cols": s}).wait_recv()

        self.local().wait()
        for at in self.blocks():
            self.out[at] = jnp.sum(self.got[:, at].astype(f32), axis=0).astype(bf16)
        self.each(lambda copy: copy.wait_send(), (3, -3, 2, -2, 1, -1))

        @pl.when((c == 1) | (c == 2))
        def _():
            self.send_sum().wait_send()


class Rows:
    def __init__(self, kind, array, phase=0):
        self.args = (array,)
        self.phase = phase
        self.kind = kind
        rows = lax.axis_size("rows")
        a, b, f = array.shape
        dims = (a, b // rows, f * rows) if kind == "tokens" else (a, b * rows, f // rows)
        self.outs = ((shape(dims, array.dtype), ANY),)
        self.scratch = [DMA((2, 1, 4))]

    def relay(self):
        pass

    def bind(self, ins, outs, scratch):
        self.work = row_copies(self.kind, ins[0], outs[0], scratch[0], 0)

    def start(self):
        begin_all(self.work)

    def finish(self):
        end_all(self.work)


def begin_all(work):
    sends, _, local = work
    for copy in sends:
        copy.start()
    local.start()


def end_all(work):
    sends, gets, local = work
    for copy in gets:
        copy.wait_recv()
    for copy in sends:
        copy.wait_send()
    local.wait()


def start_sides(sides, phase=0):
    for side in sides:
        if side.phase == phase:
            side.start()


def relay_sides(sides, phase=0):
    for side in sides:
        if side.phase == phase:
            side.relay()


def finish_sides(sides):
    for side in sides:
        side.finish()


def rms(x):
    return lax.rsqrt(jnp.mean(x * x, axis=-1, keepdims=True) + epsilon)


def put_own(buf, sh, value):
    pm, hm = place(0)
    buf[pm, :, hm, share(sh, True)] = value.astype(bf16)


def norm_own(x_ref, gain_ref):
    x = x_ref[...]
    return x * rms(x) * gain_ref[...]


def norm_back(n, x_ref, gain_ref, grad_ref, out_ref, gain_out):
    x = x_ref[...]
    q = rms(x)
    scaled = n * gain_ref[...]
    dots = jnp.mean(scaled * x, axis=-1, keepdims=True)
    out_ref[...] = grad_ref[...] + scaled * q - x * (q * q * q) * dots
    gain_out[...] = jnp.sum(n * x * q, axis=(0, 1))[None]


def flat(x):
    return x.reshape(x.shape[0] * x.shape[1], x.shape[2])


def tiles(width):
    return [(a, min(256, width - a)) for a in range(0, width, 256)]


def padded(width):
    return -(-width // 128) * 128


def segments(lo, n, wide):
    cuts = []
    for g in range(lo // wide, -(-(lo + n) // wide)):
        a, b = max(lo, g * wide), min(lo + n, (g + 1) * wide)
        cuts.append((g, a - g * wide, a - lo, b - a))
    return cuts


def first_rows(arrays, axis):
    return [sum(x.shape[axis] for x in arrays[:i]) for i in range(len(arrays))]


def load_copies(parts, wbuf, wide, sem):
    copies = []
    for ref, lo in zip(parts, first_rows(parts, 1)):
        for g, at, here, n in segments(lo, ref.shape[1], wide):
            for c in range(ref.shape[0]):
                copies.append(pltpu.make_async_copy(
                    ref.at[c, pl.ds(here, n)], wbuf.at[g, pl.ds(c * wide + at, n)], sem.at[len(copies)]
                ))
    return copies


def zero_pad(wbuf, used):
    if wbuf.shape[1] > used:
        wbuf[:, used:] = jnp.zeros((3, wbuf.shape[1] - used, wbuf.shape[2]), bf16)


def ffn_forward_kernel(sh, wide, count, last, sides, x_ref, gain_ref, *refs):
    parts, refs = refs[:count], refs[count:]
    if last:
        tail_ref, refs = refs[0], refs[1:]
    out_ref, n_ref, gu_ref, save_ref, buf, wbuf, gu, hid, part, xr, ys, yr, sems, wsem, osem, gsem = refs
    cols = parts[0].shape[0]
    loads = load_copies(parts, wbuf, wide, wsem)
    for copy in loads:
        copy.start()
    zero_pad(wbuf, cols * wide)
    put_own(buf, sh, norm_own(x_ref, gain_ref))
    greet()
    start_gather(buf, sh, sems)
    if last:
        tail = Gather.of(
            tail_ref.at[pl.ds(3 * wide - last, last)],
            lambda z: wbuf.at[2, pl.ds(pl.multiple_of(z * wide + wide - last, 16), last)],
            gsem,
        )
        tail.start()
    start_sides(sides)
    for copy in loads:
        copy.wait()
    width = wbuf.shape[1]

    def step(m, carry):
        arrive(buf, sh, sems, m)
        if last:
            pl.when(m == 2)(tail.relay)
        pl.when(m == 3)(lambda: relay_sides(sides))
        pm, hm = place(m)
        x = flat(buf[pm, :, hm])
        for a, n in tiles(width):
            g = dot(x, wbuf[0, a : a + n], 1, 1)
            u = dot(x, wbuf[1, a : a + n], 1, 1)
            gu[m, 0, :, a : a + n] = g
            gu[m, 1, :, a : a + n] = u
            hid[m, :, a : a + n] = (g * jax.nn.sigmoid(g) * u).astype(bf16)
        pltpu.make_async_copy(gu.at[m], gu_ref.at[m], osem.at[m]).start()
        return carry

    lax.fori_loop(0, 4, step, 0)
    if last:
        tail.finish()
    save = pltpu.make_async_copy(wbuf, save_ref, osem.at[5])
    save.start()
    keep_n = pltpu.make_async_copy(buf, n_ref, osem.at[4])
    keep_n.start()

    def merge_step(t, carry):
        m = 3 - t
        for a, n in tiles(D):
            y = dot(hid[m], wbuf[2, :, a : a + n], 1, 0)
            part[m, :, :, a : a + n] = y.reshape(part.shape[1], part.shape[2], n)
        across_copy(part, xr, sh, sems, m).start()

        @pl.when(m < 3)
        def _():
            scatter(part, xr, ys, yr, sh, sems, m + 1)

        return carry

    lax.fori_loop(0, 4, merge_step, 0)
    scatter(part, xr, ys, yr, sh, sems, 0)
    out_ref[...] = x_ref[...] + end_scatter(part, xr, ys, yr, sh, sems)
    end_gather(buf, sh, sems)
    for m in range(4):
        pltpu.make_async_copy(gu.at[m], gu_ref.at[m], osem.at[m]).wait()
    keep_n.wait()
    save.wait()
    finish_sides(sides)


def ffn_backward_kernel(sh, wide, sides, grad_ref, x_ref, gain_ref, w_ref, n_ref, gu_ref,
                        out_ref, gain_out, dw_ref,
                        buf, nbuf, wbuf, gu, hid, dw, part, xr, ys, yr, sems, wsem, osem):
    cols = dw_ref.shape[0]
    gloads = [pltpu.make_async_copy(gu_ref.at[m], gu.at[m], osem.at[m]) for m in range(4)]
    nload = pltpu.make_async_copy(n_ref, nbuf, osem.at[4])
    loads = [pltpu.make_async_copy(w_ref, wbuf, osem.at[5])]
    for copy in loads + gloads + [nload]:
        copy.start()
    put_own(buf, sh, grad_ref[...])
    greet()
    start_gather(buf, sh, sems)
    start_sides(sides)
    for copy in loads + gloads:
        copy.wait()
    width = wbuf.shape[1]

    def step(m, carry):
        arrive(buf, sh, sems, m)
        pl.when(m == 3)(lambda: relay_sides(sides))
        pm, hm = place(m)
        gg = flat(buf[pm, :, hm])
        for a, n in tiles(width):
            gh = dot(gg, wbuf[2, a : a + n], 1, 1)
            g = gu[m, 0, :, a : a + n]
            u = gu[m, 1, :, a : a + n]
            s = jax.nn.sigmoid(g)
            silu = g * s
            shape = (part.shape[1], part.shape[2], n)
            hid[0, pm, :, hm, :, a : a + n] = (gh * u * (s * (1.0 + g * (1.0 - s)))).astype(bf16).reshape(shape)
            hid[1, pm, :, hm, :, a : a + n] = (gh * silu).astype(bf16).reshape(shape)
            hid[2, pm, :, hm, :, a : a + n] = (silu * u).astype(bf16).reshape(shape)
        for a, n in tiles(D):
            y = dot(flat(hid[0, pm, :, hm]), wbuf[0, :, a : a + n], 1, 0)
            y = y + dot(flat(hid[1, pm, :, hm]), wbuf[1, :, a : a + n], 1, 0)
            part[m, :, :, a : a + n] = y.reshape(part.shape[1], part.shape[2], n)
        across_copy(part, xr, sh, sems, m).start()

        @pl.when(m > 0)
        def _():
            scatter(part, xr, ys, yr, sh, sems, m - 1)

        return carry

    lax.fori_loop(0, 4, step, 0)
    scatter(part, xr, ys, yr, sh, sems, 3)
    nload.wait()
    tokens = 8 * buf.shape[3]

    def grads(other, g):
        def one(i, carry):
            at = pl.ds(pl.multiple_of(i * 128, 128), 128)
            left = hid[g, :, :, :, :, at].reshape(tokens, 128)
            dw[g, at] = dot(left, other[...].reshape(tokens, D), 0, 0).astype(bf16)
            return carry

        lax.fori_loop(0, width // 128, one, 0)

    grads(nbuf, 0)
    grads(nbuf, 1)
    grads(buf, 2)
    stores = [
        pltpu.make_async_copy(
            dw.at[g, pl.ds(c * wide, wide)], dw_ref.at[c, pl.ds(g * wide, wide)], wsem.at[c * 3 + g]
        )
        for c in range(cols)
        for g in range(3)
    ]
    for copy in stores:
        copy.start()
    n = end_scatter(part, xr, ys, yr, sh, sems)
    norm_back(n, x_ref, gain_ref, grad_ref, out_ref, gain_out)
    end_gather(buf, sh, sems)
    for copy in stores:
        copy.wait()
    finish_sides(sides)


def shape(dims, kind):
    return jax.ShapeDtypeStruct(dims, kind)


def scatter_scratch(seqs, sh):
    return [
        pltpu.VMEM((4, seqs, 2 * sh, D), f32),
        pltpu.VMEM((4, seqs, sh, D), f32),
        pltpu.VMEM((4, seqs, sh, D), bf16),
        pltpu.VMEM((4, seqs, sh, D), bf16),
    ]


def call(kernel, name, cid, outs, out_specs, in_specs, scratch, args, flops=46 * 10**9, limit=60, sides=()):
    n_in, n_out, n_scratch = len(args), len(outs), len(scratch)
    side_in = [x for side in sides for x in side.args]
    side_out = [x for side in sides for x in side.outs]
    side_scratch = [x for side in sides for x in side.scratch]

    def body(*refs):
        ins, rest = refs[:n_in], refs[n_in:]
        extra_in, rest = rest[: len(side_in)], rest[len(side_in) :]
        out, rest = rest[:n_out], rest[n_out:]
        extra_out, rest = rest[: len(side_out)], rest[len(side_out) :]
        own, extra_scratch = rest[:n_scratch], rest[n_scratch:]
        for side in sides:
            a, b, s = len(side.args), len(side.outs), len(side.scratch)
            side.bind(extra_in[:a], extra_out[:b], extra_scratch[:s])
            extra_in, extra_out, extra_scratch = extra_in[a:], extra_out[b:], extra_scratch[s:]
        kernel(*((sides,) if sides is not None else ()), *ins, *out, *own)

    got = pl.pallas_call(
        body,
        name=name,
        out_shape=tuple(outs) + tuple(x[0] for x in side_out),
        in_specs=tuple(in_specs) + (ANY,) * len(side_in),
        out_specs=tuple(out_specs) + tuple(x[1] for x in side_out),
        scratch_shapes=list(scratch) + side_scratch,
        cost_estimate=pl.CostEstimate(flops=flops, bytes_accessed=10**7, transcendentals=0),
        compiler_params=pltpu.CompilerParams(
            collective_id=cid, has_side_effects=True, vmem_limit_bytes=limit << 20
        ),
    )(*args, *side_in)
    return got


DMA = pltpu.SemaphoreType.DMA


def ffn_forward(cid, x, gain, parts, wide, sides=(), tail=None):
    seqs, sh, _ = x.shape
    cols = parts[0].shape[0]
    width = padded(cols * wide)
    full = (2, seqs, 2, 2 * sh, D)
    rows = seqs * 2 * sh
    last = 3 * wide - sum(p.shape[1] for p in parts)
    assert 0 <= last <= wide and (last == 0 or tail is not None)
    args = (x, gain) + tuple(parts) + ((tail,) if last else ())
    return call(
        functools.partial(ffn_forward_kernel, sh, wide, len(parts), last), "ffn_forward", cid,
        (shape(x.shape, f32), shape(full, bf16), shape((4, 2, rows, width), f32), shape((3, width, D), bf16)),
        (VMEM, ANY, ANY, ANY), (VMEM, VMEM) + (ANY,) * (len(args) - 2),
        [
            pltpu.VMEM(full, bf16), pltpu.VMEM((3, width, D), bf16),
            pltpu.VMEM((4, 2, rows, width), f32), pltpu.VMEM((4, rows, width), bf16),
        ] + scatter_scratch(seqs, sh)
        + [DMA((12, 4)), DMA((cols * (len(parts) + 2),)), DMA((6,)), DMA((2, 5))],
        args, sides=sides,
    )


def ffn_backward(cid, grad, x, gain, w, n, gu, wide, cols, sides=()):
    seqs, sh, _ = x.shape
    width = w.shape[1]
    full = (2, seqs, 2, 2 * sh, D)
    rows = seqs * 2 * sh
    return call(
        functools.partial(ffn_backward_kernel, sh, wide), "ffn_backward", cid,
        (shape(x.shape, f32), shape((1, D), f32), shape((cols, 3 * wide, D), bf16)),
        (VMEM, VMEM, ANY), (VMEM, VMEM, VMEM, ANY, ANY, ANY),
        [
            pltpu.VMEM(full, bf16), pltpu.VMEM(full, bf16), pltpu.VMEM((3, width, D), bf16),
            pltpu.VMEM((4, 2, rows, width), f32), pltpu.VMEM((3,) + full[:4] + (width,), bf16),
            pltpu.VMEM((3, width, D), bf16),
        ] + scatter_scratch(seqs, sh) + [DMA((12, 4)), DMA((3 * cols,)), DMA((6,))],
        (grad, x, gain, w, n, gu), sides=sides,
    )


def out_copy(stage, dest, sems, m, i):
    pm, hm = place(m)
    c = lax.axis_index("cols")
    s = pm * stage.shape[1] + i
    return s, remote(
        stage.at[m, i], dest.at[c, hm], sems.at[0, m * 2 + i], sems.at[1, c * 2 + hm], {"cols": s}
    )


def send_out(stage, dest, sems, m):
    pm, hm = place(m)
    c = lax.axis_index("cols")
    for i in range(stage.shape[1]):
        s, copy = out_copy(stage, dest, sems, m, i)

        @pl.when(s == c)
        def _():
            dest[c, hm] = stage[m, i]

        @pl.when(s != c)
        def _():
            copy.start()


def wait_out(stage, dest, sems):
    c = lax.axis_index("cols")
    for z in range(dest.shape[0]):
        for h in range(2):

            @pl.when(z != c)
            def _():
                got = dest.at[z, h]
                remote(got, got, sems.at[0, z * 2 + h], sems.at[1, z * 2 + h], {"cols": z}).wait_recv()


def end_out(stage, dest, sems):
    c = lax.axis_index("cols")
    for m in range(4):
        for i in range(stage.shape[1]):
            s, copy = out_copy(stage, dest, sems, m, i)

            @pl.when(s != c)
            def _():
                copy.wait_send()


def back_copy(stage, dest, sems, i):
    c = lax.axis_index("cols")
    seqs = dest.shape[1]
    return remote(
        stage.at[i], dest.at[c // seqs, lax.rem(c, seqs)], sems.at[2, i], sems.at[3, c], {"cols": i}
    )


def send_back(stage, dest, sems, i):
    c = lax.axis_index("cols")
    seqs = dest.shape[1]

    @pl.when(i == c)
    def _():
        dest[c // seqs, lax.rem(c, seqs)] = stage[i]

    @pl.when(i != c)
    def _():
        back_copy(stage, dest, sems, i).start()


def wait_back(stage, dest, sems):
    c = lax.axis_index("cols")
    seqs = dest.shape[1]
    for s in range(stage.shape[0]):

        @pl.when(s != c)
        def _():
            got = dest.at[s // seqs, s % seqs]
            remote(got, got, sems.at[2, s], sems.at[3, s], {"cols": s}).wait_recv()
            back_copy(stage, dest, sems, s).wait_send()


def low_lanes(x):
    return lax.broadcasted_iota(jnp.int32, x.shape, x.ndim - 1) < HD


def per_head(x):
    low = low_lanes(x)
    a = jnp.sum(jnp.where(low, x, 0.0), axis=-1, keepdims=True)
    b = jnp.sum(jnp.where(low, 0.0, x), axis=-1, keepdims=True)
    return jnp.where(low, a, b) * (1.0 / HD)


def partner(x):
    lane = lax.rem(lax.broadcasted_iota(jnp.int32, x.shape, x.ndim - 1), HD)
    return jnp.where(lane < HD // 2, pltpu.roll(x, 2 * HD - HD // 2, axis=1), pltpu.roll(x, HD // 2, axis=1))


def swap(x):
    return pltpu.roll(x, HD, axis=1)


def rope_forward(x, gain, cos, sin):
    y = x * lax.rsqrt(per_head(x * x) + epsilon) * gain
    return y * cos + partner(y) * sin


def rope_backward(x, gain, cos, sin, grad):
    inv = lax.rsqrt(per_head(x * x) + epsilon)
    g = grad * cos - partner(grad) * sin
    scaled = g * gain
    out = scaled * inv - x * (inv * inv * inv) * per_head(scaled * x)
    return out, jnp.sum(g * x * inv, axis=0, keepdims=True)


def split_heads(x, upper):
    x = x.astype(f32)
    low = low_lanes(x)
    if upper:
        return jnp.where(low, 0.0, swap(x)).astype(bf16), jnp.where(low, 0.0, x).astype(bf16)
    return jnp.where(low, x, 0.0).astype(bf16), jnp.where(low, swap(x), 0.0).astype(bf16)


def probabilities(q, keys, first, length):
    s = dot(q, keys, 1, 1)
    at = lax.broadcasted_iota(jnp.int32, s.shape, 1)
    row = lax.broadcasted_iota(jnp.int32, s.shape, 0) + first
    s = jnp.where((at <= row) & (at < length), s, -1e30)
    e = jnp.exp(s - jnp.max(s, axis=1, keepdims=True))
    return e * (1.0 / jnp.sum(e, axis=1, keepdims=True))


def key_bound(i, slots):
    return min(-(-(i + 1) * slots // 128) * 128, 4 * slots)


def attention_forward_kernel(sh, sides, x_ref, gain_ref, w_ref, wo_ref, cos_ref, sin_ref, gq_ref, gk_ref, len_ref,
                             out_ref, n_ref, raw_ref, seq_ref, att_ref,
                             buf, stage, q2, kv, o, back, part, xr, ys, yr, sems, zsems, osem):
    c = lax.axis_index("cols")
    slots = 4 * sh
    put_own(buf, sh, norm_own(x_ref, gain_ref))
    greet()
    start_gather(buf, sh, sems)
    start_sides(sides)
    low = low_lanes(gq_ref[...])

    def step(m, carry):
        arrive(buf, sh, sems, m)
        pm, hm = place(m)
        y = dot(flat(buf[pm, :, hm]), w_ref[...], 1, 1)
        raw_ref[pm, :, hm] = y.reshape(raw_ref.shape[1], 2 * sh, 4 * HD)
        for i in range(stage.shape[1]):
            rows = slice(i * 2 * sh, (i + 1) * 2 * sh)
            cos, sin = cos_ref[hm], sin_ref[hm]
            q = rope_forward(y[rows, : 2 * HD], gq_ref[...], cos, sin) * (HD**-0.5)
            raw = y[rows, 2 * HD :]
            k = rope_forward(raw, gk_ref[...], cos, sin)
            stage[m, i, :, : 2 * HD] = q.astype(bf16)
            stage[m, i, :, 2 * HD :] = jnp.where(low, k, raw).astype(bf16)
        send_out(stage, seq_ref, zsems, m)
        return carry

    lax.fori_loop(0, 4, step, 0)
    save = pltpu.make_async_copy(buf, n_ref, osem.at[0])
    save.start()
    wait_out(stage, seq_ref, zsems)
    relay_sides(sides, 0)
    start_sides(sides, 1)
    for i in range(4):
        for h in range(2):
            kv[i, h] = seq_ref[i, h, :, 2 * HD :]
            a, b = split_heads(seq_ref[i, h, :, : 2 * HD], False)
            q2[i, 0, h], q2[i, 1, h] = a, b
    length = len_ref[0]
    for i in range(4):
        bound = key_bound(i, slots)

        def tile(u, carry, i=i, bound=bound):
            head, h = u // 2, lax.rem(u, 2)
            keys = kv[...].reshape(4 * slots, 2 * HD)[:bound]
            p = probabilities(q2[i, head, h], keys, i * slots + h * 2 * sh, length)
            o[head, h] = dot(p.astype(bf16), keys, 1, 0)
            return carry

        lax.fori_loop(0, 4, tile, 0)
        for h in range(2):
            back[i, h] = jnp.where(low, swap(o[0, h]), o[1, h]).astype(bf16)
        send_back(back, att_ref, zsems, i)
    wait_back(back, att_ref, zsems)
    relay_sides(sides, 1)
    start_sides(sides, 2)

    def merge_step(i, carry):
        m = 3 - i
        pm, hm = place(m)
        pl.when(i == 3)(lambda: relay_sides(sides, 2))
        y = flat(att_ref[pm, :, hm])
        for a, n in tiles(D):
            z = dot(y, wo_ref[:, a : a + n], 1, 0)
            part[m, :, :, a : a + n] = z.reshape(part.shape[1], part.shape[2], n)
        across_copy(part, xr, sh, sems, m).start()

        @pl.when(m < 3)
        def _():
            scatter(part, xr, ys, yr, sh, sems, m + 1)

        return carry

    lax.fori_loop(0, 4, merge_step, 0)
    scatter(part, xr, ys, yr, sh, sems, 0)
    out_ref[...] = x_ref[...] + end_scatter(part, xr, ys, yr, sh, sems)
    end_gather(buf, sh, sems)
    end_out(stage, seq_ref, zsems)
    save.wait()
    finish_sides(sides)


def attention_backward_kernel(sh, sides, grad_ref, x_ref, gain_ref, w_ref, wo_ref, cos_ref, sin_ref, gq_ref, gk_ref, len_ref,
                              n_ref, raw_ref, seq_ref, att_ref,
                              out_ref, gain_out, head_out, dw_ref,
                              buf, nbuf, stage, dseq, q2, do2, kv, dq, dkv, back, dproj, gproj,
                              part, xr, ys, yr, sems, zsems, osem):
    c = lax.axis_index("cols")
    slots = 4 * sh
    tokens = 8 * buf.shape[3]
    nload = pltpu.make_async_copy(n_ref, nbuf, osem.at[0])
    nload.start()
    put_own(buf, sh, grad_ref[...])
    greet()
    start_gather(buf, sh, sems)
    start_sides(sides)
    low = low_lanes(gq_ref[...])
    for i in range(4):
        for h in range(2):
            kv[i, h] = seq_ref[i, h, :, 2 * HD :]
            a, b = split_heads(seq_ref[i, h, :, : 2 * HD], False)
            q2[i, 0, h], q2[i, 1, h] = a, b
    dkv[...] = jnp.zeros_like(dkv)
    head_out[...] = jnp.zeros_like(head_out)

    def step(m, carry):
        arrive(buf, sh, sems, m)
        pm, hm = place(m)
        y = dot(flat(buf[pm, :, hm]), wo_ref[...], 1, 1).astype(bf16)
        stage[m] = y.reshape(stage.shape[1], 2 * sh, 2 * HD)
        send_out(stage, dseq, zsems, m)
        return carry

    lax.fori_loop(0, 4, step, 0)
    wait_out(stage, dseq, zsems)
    relay_sides(sides, 0)
    start_sides(sides, 1)
    length = len_ref[0]
    for i in range(4):
        for h in range(2):
            a, b = split_heads(dseq[i, h], True)
            do2[i, 0, h], do2[i, 1, h] = a, b
    for i in range(4):
        bound = key_bound(i, slots)

        def tile(u, carry, i=i, bound=bound):
            head, h = u // 2, lax.rem(u, 2)
            keys = kv[...].reshape(4 * slots, 2 * HD)[:bound]
            q, do = q2[i, head, h], do2[i, head, h]
            p = probabilities(q, keys, i * slots + h * 2 * sh, length)
            dp = dot(do, keys, 1, 1)
            ds = (p * (dp - jnp.sum(p * dp, axis=1, keepdims=True))).astype(bf16)
            dq[head, h] = dot(ds, keys, 1, 0) * (HD**-0.5)
            dkv[:, :bound] += dot(q, ds, 0, 0) + dot(do, p.astype(bf16), 0, 0)
            return carry

        lax.fori_loop(0, 4, tile, 0)
        for h in range(2):
            back[i, h, :, : 2 * HD] = jnp.where(low, dq[0, h], swap(dq[1, h])).astype(bf16)
    grads = dkv[...].T.reshape(4, 2, 2 * sh, 2 * HD)
    for i in range(4):
        back[i, :, :, 2 * HD :] = grads[i].astype(bf16)
        send_back(back, dproj, zsems, i)
    wait_back(back, dproj, zsems)
    relay_sides(sides, 1)
    start_sides(sides, 2)

    def merge_step(t, carry):
        m = 3 - t
        pm, hm = place(m)
        pl.when(t == 3)(lambda: relay_sides(sides, 2))
        for i in range(stage.shape[1]):
            cos, sin = cos_ref[hm], sin_ref[hm]
            g = dproj[pm, i, hm].astype(f32)
            raw = raw_ref[pm, i, hm]
            a, ga = rope_backward(raw[:, : 2 * HD], gq_ref[...], cos, sin, g[:, : 2 * HD])
            b, gb = rope_backward(raw[:, 2 * HD :], gk_ref[...], cos, sin, g[:, 2 * HD :])
            gproj[pm, i, hm, :, : 2 * HD] = a.astype(bf16)
            gproj[pm, i, hm, :, 2 * HD :] = jnp.where(low, b, g[:, 2 * HD :]).astype(bf16)
            head_out[0:1] += ga
            head_out[1:2] += gb
        y = flat(gproj[pm, :, hm])
        for a, n in tiles(D):
            z = dot(y, w_ref[:, a : a + n], 1, 0)
            part[m, :, :, a : a + n] = z.reshape(part.shape[1], part.shape[2], n)
        across_copy(part, xr, sh, sems, m).start()

        @pl.when(m < 3)
        def _():
            scatter(part, xr, ys, yr, sh, sems, m + 1)

        return carry

    lax.fori_loop(0, 4, merge_step, 0)
    scatter(part, xr, ys, yr, sh, sems, 0)
    nload.wait()
    left = gproj[...].reshape(tokens, 4 * HD)
    dw_ref[: 4 * HD] = dot(left, nbuf[...].reshape(tokens, D), 0, 0).astype(bf16)
    left = att_ref[...].reshape(tokens, 2 * HD)
    dw_ref[4 * HD :] = dot(left, buf[...].reshape(tokens, D), 0, 0).astype(bf16)
    n = end_scatter(part, xr, ys, yr, sh, sems)
    norm_back(n, x_ref, gain_ref, grad_ref, out_ref, gain_out)
    end_gather(buf, sh, sems)
    end_out(stage, dseq, zsems)
    finish_sides(sides)


SMEM = pl.BlockSpec(memory_space=pltpu.SMEM)


def attention_forward(cid, x, gain, w, wo, tables, length, sides=()):
    seqs, sh, _ = x.shape
    full = (2, seqs, 2, 2 * sh)
    zshape = (4, 2, 2 * sh)
    return call(
        functools.partial(attention_forward_kernel, sh), "attention_forward", cid,
        (shape(x.shape, f32), shape(full + (D,), bf16), shape(full + (4 * HD,), f32),
         shape(zshape + (4 * HD,), bf16), shape(full + (2 * HD,), bf16)),
        (VMEM, ANY, VMEM, VMEM, VMEM), (VMEM,) * 8 + (SMEM,),
        [
            pltpu.VMEM(full + (D,), bf16), pltpu.VMEM((4, seqs, 2 * sh, 4 * HD), bf16),
            pltpu.VMEM((4, 2, 2, 2 * sh, 2 * HD), bf16), pltpu.VMEM(zshape + (2 * HD,), bf16),
            pltpu.VMEM((2, 2, 2 * sh, 2 * HD), f32), pltpu.VMEM(zshape + (2 * HD,), bf16),
        ] + scatter_scratch(seqs, sh) + [DMA((12, 4)), DMA((4, 8)), DMA((1,))],
        (x, gain, w, wo) + tables + (length,), limit=48, sides=sides,
    )


def attention_backward(cid, grad, x, gain, w, wo, tables, length, n, raw, seq, att, sides=()):
    seqs, sh, _ = x.shape
    full = (2, seqs, 2, 2 * sh)
    zshape = (4, 2, 2 * sh)
    return call(
        functools.partial(attention_backward_kernel, sh), "attention_backward", cid,
        (shape(x.shape, f32), shape((1, D), f32), shape((2, 2 * HD), f32), shape((6 * HD, D), bf16)),
        (VMEM,) * 4, (VMEM,) * 9 + (SMEM, ANY, VMEM, VMEM, VMEM),
        [
            pltpu.VMEM(full + (D,), bf16), pltpu.VMEM(full + (D,), bf16),
            pltpu.VMEM((4, seqs, 2 * sh, 2 * HD), bf16), pltpu.VMEM(zshape + (2 * HD,), bf16),
            pltpu.VMEM((4, 2, 2, 2 * sh, 2 * HD), bf16), pltpu.VMEM((4, 2, 2, 2 * sh, 2 * HD), bf16),
            pltpu.VMEM(zshape + (2 * HD,), bf16), pltpu.VMEM((2, 2, 2 * sh, 2 * HD), f32),
            pltpu.VMEM((2 * HD, 16 * sh), f32), pltpu.VMEM(zshape + (4 * HD,), bf16),
            pltpu.VMEM(full + (4 * HD,), bf16), pltpu.VMEM(full + (4 * HD,), bf16),
        ] + scatter_scratch(seqs, sh) + [DMA((12, 4)), DMA((4, 8)), DMA((1,))],
        (grad, x, gain, w, wo) + tables + (length, n, raw, seq, att), limit=58, sides=sides,
    )


def edge_send(buf, edge, sh, sems, way, p, i):
    d, c = lax.axis_index("dp"), lax.axis_index("cols")
    pm, hm = place(0)
    at = share(sh, True).start + (sh - 16 if way == 0 else 0)
    to = {"dp": d - lax.rem(d, 2) + p, "rows": i, "cols": c + 1 if way == 0 else c - 1}
    return remote(
        buf.at[pm, :, hm, pl.ds(pl.multiple_of(at, 16), 16)], edge.at[way, pm],
        sems.at[0, way * 8 + p * 4 + i], sems.at[1, way * 8 + pm], to,
    )


def edge_senders(way):
    r, c = lax.axis_index("rows"), lax.axis_index("cols")
    rows, cols = lax.axis_size("rows"), lax.axis_size("cols")
    return (r == rows - 1) & (c < cols - 1) if way == 0 else (r == 0) & (c > 0)


def edges_each(buf, edge, sh, sems, way, act):
    @pl.when(edge_senders(way))
    def _():
        for p in range(2):
            for i in range(4):
                act(edge_send(buf, edge, sh, sems, way, p, i))


def wait_edges(edge, sems, way):
    c = lax.axis_index("cols")
    gets = c > 0 if way == 0 else c < lax.axis_size("cols") - 1

    @pl.when(gets)
    def _():
        for p in range(2):
            part = edge.at[way, p]
            remote(part, part, sems.at[0, way * 8 + p], sems.at[1, way * 8 + p], sibling()).wait_recv()

    @pl.when(jnp.logical_not(gets))
    def _():
        edge[way] = jnp.zeros(edge.shape[1:], bf16)


def window(ref, s, hm, rows):
    return ref[s, pl.ds(pl.multiple_of(hm * rows, 8), rows + 8)]


def convolve(taps, ext, rows):
    return sum(taps[k : k + 1] * ext[8 - (CONV - 1) + k : 8 - (CONV - 1) + k + rows] for k in range(CONV))


def conv_forward_kernel(sh, sides, x_ref, gain_ref, w_ref, wo_ref, taps_ref,
                        out_ref, n_ref, mixed_ref, prod_ref, gate_ref,
                        buf, cmix, edge, part, xr, ys, yr, sems, zsems, osem):
    seqs, rows = buf.shape[1], 2 * sh
    ch = wo_ref.shape[0]
    slots = 2 * rows
    put_own(buf, sh, norm_own(x_ref, gain_ref))
    greet_box(2)
    for way in (0, 1):
        edges_each(buf, edge, sh, zsems, way, lambda copy: copy.start())
    start_gather(buf, sh, sems)
    start_sides(sides)

    def step(m, carry):
        arrive(buf, sh, sems, m)
        pm, hm = place(m)
        y = dot(flat(buf[pm, :, hm]), w_ref[...], 1, 1)
        mixed_ref[pm, :, hm] = y.reshape(seqs, rows, 3 * ch)
        for i in range(seqs):
            z = y[i * rows : (i + 1) * rows]
            at = pl.ds(pl.multiple_of(8 + hm * rows, 8), rows)
            prod_ref[pm * seqs + i, at] = z[:, :ch] * z[:, 2 * ch :]
        return carry

    lax.fori_loop(0, 4, step, 0)
    save = pltpu.make_async_copy(buf, n_ref, osem.at[0])
    save.start()
    for way in (0, 1):
        wait_edges(edge, zsems, way)
    y = dot(edge[...].reshape(4 * seqs * 16, D), w_ref[...], 1, 1).reshape(2, 2 * seqs, 16, 3 * ch)
    prod_ref[:, :8] = y[0, :, 8:, :ch] * y[0, :, 8:, 2 * ch :]
    gate_ref[...] = y[1, :, :8, ch : 2 * ch]
    taps = taps_ref[...]

    def merge_step(t, carry):
        m = 3 - t
        pm, hm = place(m)
        for i in range(seqs):
            conv = convolve(taps, window(prod_ref, pm * seqs + i, hm, rows), rows)
            cmix[i] = (mixed_ref[pm, i, hm, :, ch : 2 * ch] * conv).astype(bf16)
        y = flat(cmix[...])
        for a, n in tiles(D):
            z = dot(y, wo_ref[:, a : a + n], 1, 0)
            part[m, :, :, a : a + n] = z.reshape(seqs, rows, n)
        across_copy(part, xr, sh, sems, m).start()

        @pl.when(m < 3)
        def _():
            scatter(part, xr, ys, yr, sh, sems, m + 1)

        return carry

    lax.fori_loop(0, 4, merge_step, 0)
    scatter(part, xr, ys, yr, sh, sems, 0)
    out_ref[...] = x_ref[...] + end_scatter(part, xr, ys, yr, sh, sems)
    end_gather(buf, sh, sems)
    for way in (0, 1):
        edges_each(buf, edge, sh, zsems, way, lambda copy: copy.wait_send())
    save.wait()
    finish_sides(sides)


def conv_backward_kernel(sh, sides, grad_ref, x_ref, gain_ref, w_ref, wo_ref, taps_ref, n_ref, mixed_ref, prod_ref, gate_ref,
                         out_ref, gain_out, taps_out, dw_ref,
                         buf, nbuf, gext, gmix, gin, cmix, edge, part, xr, ys, yr, sems, zsems, osem):
    seqs, rows = buf.shape[1], 2 * sh
    ch = wo_ref.shape[0]
    slots = 2 * rows
    tokens = 8 * rows
    nload = pltpu.make_async_copy(n_ref, nbuf, osem.at[0])
    nload.start()
    put_own(buf, sh, grad_ref[...])
    greet_box(2)
    edges_each(buf, edge, sh, zsems, 1, lambda copy: copy.start())
    start_gather(buf, sh, sems)
    start_sides(sides)
    taps_out[...] = jnp.zeros_like(taps_out)

    def step(m, carry):
        arrive(buf, sh, sems, m)
        pm, hm = place(m)
        y = dot(flat(buf[pm, :, hm]), wo_ref[...], 1, 1)
        for i in range(seqs):
            z = y[i * rows : (i + 1) * rows]
            gmix[pm, i, hm] = z
            at = pl.ds(pl.multiple_of(hm * rows, 8), rows)
            gext[pm * seqs + i, at] = z * mixed_ref[pm, i, hm, :, ch : 2 * ch]
        return carry

    lax.fori_loop(0, 4, step, 0)
    wait_edges(edge, zsems, 1)
    y = dot(edge[1].reshape(2 * seqs * 16, D), wo_ref[...], 1, 1).reshape(2 * seqs, 16, ch)
    gext[:, slots:] = y[:, :8] * gate_ref[...]
    taps = taps_ref[...]

    def merge_step(t, carry):
        m = 3 - t
        pm, hm = place(m)
        pl.when(t == 1)(lambda: relay_sides(sides))
        for i in range(seqs):
            ext = window(prod_ref, pm * seqs + i, hm, rows)
            conv = convolve(taps, ext, rows)
            g = window(gext, pm * seqs + i, hm, rows)
            gprod = sum(taps[k : k + 1] * g[CONV - 1 - k : CONV - 1 - k + rows] for k in range(CONV))
            for k in range(CONV):
                shifted = ext[8 - (CONV - 1) + k : 8 - (CONV - 1) + k + rows]
                taps_out[k : k + 1] += jnp.sum(g[:rows] * shifted, axis=0, keepdims=True)
            mix = mixed_ref[pm, i, hm]
            gin[pm, i, hm, :, :ch] = (gprod * mix[:, 2 * ch :]).astype(bf16)
            gin[pm, i, hm, :, ch : 2 * ch] = (gmix[pm, i, hm] * conv).astype(bf16)
            gin[pm, i, hm, :, 2 * ch :] = (gprod * mix[:, :ch]).astype(bf16)
            cmix[pm, i, hm] = (mix[:, ch : 2 * ch] * conv).astype(bf16)
        y = flat(gin[pm, :, hm])
        for a, n in tiles(D):
            z = dot(y, w_ref[:, a : a + n], 1, 0)
            part[m, :, :, a : a + n] = z.reshape(seqs, rows, n)
        across_copy(part, xr, sh, sems, m).start()

        @pl.when(m < 3)
        def _():
            scatter(part, xr, ys, yr, sh, sems, m + 1)

        return carry

    lax.fori_loop(0, 4, merge_step, 0)
    scatter(part, xr, ys, yr, sh, sems, 0)
    nload.wait()
    left = gin[...].reshape(tokens, 3 * ch)
    dw_ref[: 3 * ch] = dot(left, nbuf[...].reshape(tokens, D), 0, 0).astype(bf16)
    left = cmix[...].reshape(tokens, ch)
    dw_ref[3 * ch :] = dot(left, buf[...].reshape(tokens, D), 0, 0).astype(bf16)
    n = end_scatter(part, xr, ys, yr, sh, sems)
    norm_back(n, x_ref, gain_ref, grad_ref, out_ref, gain_out)
    end_gather(buf, sh, sems)
    edges_each(buf, edge, sh, zsems, 1, lambda copy: copy.wait_send())
    finish_sides(sides)


def conv_forward(cid, x, gain, w, wo, taps, sides=()):
    seqs, sh, _ = x.shape
    full = (2, seqs, 2, 2 * sh)
    ch = wo.shape[0]
    return call(
        functools.partial(conv_forward_kernel, sh), "conv_forward", cid,
        (shape(x.shape, f32), shape(full + (D,), bf16), shape(full + (3 * ch,), f32),
         shape((2 * seqs, 4 * sh + 8, ch), f32), shape((2 * seqs, 8, ch), f32)),
        (VMEM, ANY, VMEM, VMEM, VMEM), (VMEM,) * 5,
        [pltpu.VMEM(full + (D,), bf16), pltpu.VMEM((seqs, 2 * sh, ch), bf16), pltpu.VMEM((2, 2, seqs, 16, D), bf16)]
        + scatter_scratch(seqs, sh) + [DMA((12, 4)), DMA((2, 16)), DMA((1,))],
        (x, gain, w, wo, taps), limit=40, sides=sides,
    )


def conv_backward(cid, grad, x, gain, w, wo, taps, n, mixed, prod, gate, sides=()):
    seqs, sh, _ = x.shape
    full = (2, seqs, 2, 2 * sh)
    ch = wo.shape[0]
    return call(
        functools.partial(conv_backward_kernel, sh), "conv_backward", cid,
        (shape(x.shape, f32), shape((1, D), f32), shape((CONV, ch), f32), shape((4 * ch, D), bf16)),
        (VMEM,) * 4, (VMEM,) * 6 + (ANY, VMEM, VMEM, VMEM),
        [
            pltpu.VMEM(full + (D,), bf16), pltpu.VMEM(full + (D,), bf16),
            pltpu.VMEM((2 * seqs, 4 * sh + 8, ch), f32), pltpu.VMEM(full + (ch,), f32),
            pltpu.VMEM(full + (3 * ch,), bf16), pltpu.VMEM(full + (ch,), bf16), pltpu.VMEM((2, 2, seqs, 16, D), bf16),
        ] + scatter_scratch(seqs, sh) + [DMA((12, 4)), DMA((2, 16)), DMA((1,))],
        (grad, x, gain, w, wo, taps, n, mixed, prod, gate), limit=52, sides=sides,
    )


def band(ref, i, width):
    return ref.at[..., pl.ds(pl.multiple_of(i * width, 128), width)]


def row_pieces(kind, src, dst, here, there):
    rows = lax.axis_size("rows")
    if kind == "weights":
        return src.at[there], band(dst, here, src.shape[2])
    if kind == "tokens":
        sh = src.shape[1] // rows
        return src.at[:, pl.ds(pl.multiple_of(there * sh, 8), sh)], band(dst, here, src.shape[2])
    if kind == "gains":
        return src, band(dst, here, src.shape[1])
    sh = src.shape[1]
    return band(src, there, dst.shape[2]), dst.at[:, pl.ds(pl.multiple_of(here * sh, 8), sh)]


def row_copies(kind, src, dst, sems, i):
    rows = lax.axis_size("rows")
    r = lax.axis_index("rows")
    sends, gets = [], []
    for k in range(1, rows):
        to, come = lax.rem(r + k, rows), lax.rem(r + rows - k, rows)
        a, b = row_pieces(kind, src, dst, r, to)
        sends.append(remote(a, b, sems.at[0, i, k], sems.at[1, i, k], {"rows": to}))
        a, b = row_pieces(kind, src, dst, come, r)
        gets.append(remote(a, b, sems.at[0, i, k], sems.at[1, i, k], {"rows": to}))
    a, b = row_pieces(kind, src, dst, r, r)
    return sends, gets, pltpu.make_async_copy(a, b, sems.at[0, i, 0])


def line_copies(axis, src, dst, sems, i):
    count = lax.axis_size(axis) if axis == "cols" else 2
    at = lax.axis_index(axis)
    low = lax.rem(at, count)
    base = at - low
    sends, gets = [], []
    for k in range(1, count):
        to, come = lax.rem(low + k, count), lax.rem(low + count - k, count)
        sends.append(remote(src, dst.at[low], sems.at[0, i, k], sems.at[1, i, k], {axis: base + to}))
        gets.append(remote(src, dst.at[come], sems.at[0, i, k], sems.at[1, i, k], {axis: base + to}))
    return sends, gets, pltpu.make_async_copy(src, dst.at[low], sems.at[0, i, 0])


def greet_box(pairs):
    barrier = pltpu.get_barrier_semaphore()
    rows, cols = lax.axis_size("rows"), lax.axis_size("cols")
    d, r, c = lax.axis_index("dp"), lax.axis_index("rows"), lax.axis_index("cols")
    for p in range(pairs):
        for i in range(rows):
            for j in range(cols):
                if p + i + j > 0:
                    to = {"dp": d if p == 0 else d + 1 - 2 * lax.rem(d, 2),
                          "rows": lax.rem(r + i, rows), "cols": lax.rem(c + j, cols)}
                    pl.semaphore_signal(barrier, inc=1, device_id=to, device_id_type=MESH)
    pl.semaphore_wait(barrier, pairs * rows * cols - 1)


def attention_spread(src, dst, sems):
    halves, cols, _, width = src.shape
    rows = lax.axis_size("rows")
    r, c = lax.axis_index("rows"), lax.axis_index("cols")
    pair = lax.rem(lax.axis_index("dp"), 2)
    holds = pair == halves * c // rows
    first = lax.rem(halves * c, rows)
    origin = (pair * rows + r) // halves

    def to_all(act, local):
        for h in range(halves):
            for z in range(cols):
                own = (first + h == r) & (z == c)
                here = band(dst, r, width)

                @pl.when(holds & jnp.logical_not(own))
                def _():
                    act(remote(src.at[h, z], here, sems.at[0, h * cols + z], sems.at[1, r],
                               {"rows": first + h, "cols": z}))

                @pl.when(holds & own)
                def _():
                    local(pltpu.make_async_copy(src.at[h, z], here, sems.at[0, h * cols + z]))

    def start():
        to_all(lambda copy: copy.start(), lambda copy: copy.start())

    def end():
        for k in range(rows):
            @pl.when(jnp.logical_not((origin == c) & (k == r)))
            def _():
                got = band(dst, k, width)
                remote(got, got, sems.at[0, 0], sems.at[1, k], {"rows": k, "cols": origin}).wait_recv()
        to_all(lambda copy: copy.wait_send(), lambda copy: copy.wait())

    return start, end


def start_kernel(sides, conv_ref, tok_ref, ffn_ref, gain_ref, tap_ref, len_ref,
                 conv_out, tok_out, ffn_out, gain_out, tap_out, len_out, conv_cut, rsems, lsems, zsems):
    barrier = pltpu.get_barrier_semaphore()
    rows, cols = lax.axis_size("rows"), lax.axis_size("cols")
    d, r, c = lax.axis_index("dp"), lax.axis_index("rows"), lax.axis_index("cols")
    to = [{"rows": lax.rem(r + k, rows)} for k in range(1, rows)]
    to += [{"cols": lax.rem(c + k, cols)} for k in range(1, cols)]
    to += [{"dp": d + 1 - 2 * lax.rem(d, 2)}]
    for device in to:
        pl.semaphore_signal(barrier, inc=1, device_id=device, device_id_type=MESH)
    pl.semaphore_wait(barrier, len(to))
    conv = row_copies("weights", conv_ref, conv_cut, rsems, 0)
    small = [
        row_copies("gains", gain_ref, gain_out, rsems, 1),
        line_copies("cols", tap_ref, tap_out, lsems, 0),
        line_copies("dp", len_ref, len_out, lsems, 1),
    ]
    begin_all(conv)
    for work in small:
        begin_all(work)
    tok = row_copies("tokens", tok_ref, tok_out, rsems, 2)
    begin_all(tok)
    end_all(conv)
    conv = lines(lambda z: conv_cut, lambda z: conv_out.at[z], zsems)
    begin_all(conv)
    ffn = row_copies("weights", ffn_ref, ffn_out, rsems, 3)
    begin_all(ffn)
    for work in small + [tok, ffn, conv]:
        end_all(work)


def second_kernel(sides, attn_ref, ffn_ref, attn_out, ffn_out, asems, rsems):
    greet_box(1)
    begin, end = attention_spread(attn_ref, attn_out, asems)
    start_sides(sides)
    begin()
    ffn = row_copies("weights", ffn_ref, ffn_out, rsems, 0)
    begin_all(ffn)
    end()
    end_all(ffn)
    finish_sides(sides)


def start_exchange(cid, conv, tok, ffn, gain, tap, length, rows, cols):
    outs = (
        shape((cols, conv.shape[1], D), bf16), shape((tok.shape[0], tok.shape[1] // rows, D), f32),
        shape((ffn.shape[1], D), bf16), shape((8, D), f32), shape((cols,) + tap.shape, f32),
        shape((2,) + length.shape, length.dtype),
    )
    return call(
        start_kernel, "start", cid, outs, (ANY,) * 6, (ANY,) * 6,
        [pltpu.VMEM((conv.shape[1], D), bf16), DMA((2, 4, 4)), DMA((2, 2, 4)), DMA((2, 4))],
        (conv, tok, ffn, gain, tap, length), limit=8,
    )


def second_exchange(cid, attn, ffn, sides):
    return call(
        second_kernel, "second", cid,
        (shape((attn.shape[2], D), bf16), shape((ffn.shape[1], D), bf16)), (ANY,) * 2, (ANY,) * 2,
        [DMA((2, 8)), DMA((2, 1, 4))], (attn, ffn), limit=8, sides=sides,
    )


def plane_peer(j):
    pm, hm = place(j // 2)
    d, r = lax.axis_index("dp"), lax.axis_index("rows")
    row = hm * 2 + lax.rem(lax.rem(r, 2) + j % 2, 2)
    return pm, row, {"dp": d - lax.rem(d, 2) + pm, "rows": row}


class Plane:
    def __init__(self, src, dst, lo, w, sems):
        rows = lax.axis_size("rows")
        d, r = lax.axis_index("dp"), lax.axis_index("rows")
        pair = lax.rem(d, 2)
        n, width = src.shape[0], dst.shape[2]
        other = {"dp": d + 1 - 2 * pair}
        self.steps, self.gets = [], []
        for i, (g, at, here, n) in enumerate(segments(lo, src.shape[0], w)):

            def block(p, row, g=g, at=at, n=n):
                return dst.at[g, pl.ds(pl.multiple_of((p * rows + row) * w + at, 16), n)]

            def piece(row, here=here, n=n):
                return band(src.at[pl.ds(here, n)], row, width)

            sem = sems.at[i]
            local = pltpu.make_async_copy(piece(r), block(pair, r), sem.at[0, 0])
            sends = [local]
            turns = [(local, True, remote(block(pair, r), block(pair, r), sem.at[2, 0], sem.at[3, 0], other))]
            self.gets.append(
                remote(block(1 - pair, r), block(1 - pair, r), sem.at[2, 0], sem.at[3, 0], other)
            )
            for k in range(1, rows):
                to, come = lax.rem(r + k, rows), lax.rem(r + rows - k, rows)
                send = remote(piece(to), block(pair, r), sem.at[0, k], sem.at[1, k], {"rows": to})
                get = remote(piece(to), block(pair, come), sem.at[0, k], sem.at[1, k], {"rows": to})
                on = remote(block(pair, come), block(pair, come), sem.at[2, k], sem.at[3, k], other)
                sends.append(send)
                turns.append((get, False, on))
                self.gets.append(
                    remote(block(1 - pair, come), block(1 - pair, come), sem.at[2, k], sem.at[3, k], other)
                )
            self.steps.append((sends, turns))

    def start(self):
        for sends, _ in self.steps:
            for copy in sends:
                copy.start()

    def turn(self):
        for _, turns in self.steps:
            for get, local, on in turns:
                if local:
                    get.wait()
                else:
                    get.wait_recv()
                on.start()

    def finish(self):
        for copy in self.gets:
            copy.wait_recv()
        for sends, turns in self.steps:
            for copy in sends[1:]:
                copy.wait_send()
            for _, _, on in turns:
                on.wait_send()


class AttentionReturn:
    def __init__(self, src, dst, sems, per_col):
        self.src, self.dst, self.sems, self.per_col = src, dst, sems, per_col
        self.rows, self.cols = lax.axis_size("rows"), lax.axis_size("cols")
        self.d, self.r, self.c = lax.axis_index("dp"), lax.axis_index("rows"), lax.axis_index("cols")
        self.pair = lax.rem(self.d, 2)
        self.me = self.pair * self.rows + self.r
        self.gets_direct = per_col * self.c // self.rows == self.pair

    def each(self, act, local):
        owner, half = self.me // self.per_col, lax.rem(self.me, self.per_col)
        width = self.dst.shape[3]
        for k in range(self.rows):
            own = (k == self.r) & (owner == self.c)
            here, there = band(self.src, k, width), self.dst.at[half, self.c]

            @pl.when(jnp.logical_not(own))
            def _():
                act(remote(here, there, self.sems.at[0, k], self.sems.at[1, half * self.cols + self.c],
                           {"rows": k, "cols": owner}))

            @pl.when(own)
            def _():
                local(pltpu.make_async_copy(here, there, self.sems.at[0, k]))

    def start(self):
        self.each(lambda copy: copy.start(), lambda copy: copy.start())

    def on(self, h, z):
        part = self.dst.at[h, z]
        i = h * self.cols + z
        return remote(part, part, self.sems.at[2, i], self.sems.at[3, i], {"dp": self.d + 1 - 2 * self.pair})

    def turn(self):
        for h in range(self.per_col):
            source = self.c * self.per_col + h
            for z in range(self.cols):
                part = self.dst.at[h, z]
                mine = (source == self.me) & (z == self.c)

                @pl.when(self.gets_direct & jnp.logical_not(mine))
                def _():
                    to = {"rows": lax.rem(source, self.rows), "cols": z}
                    remote(part, part, self.sems.at[0, 0], self.sems.at[1, h * self.cols + z], to).wait_recv()

                @pl.when(mine)
                def _():
                    here = band(self.src, self.r, self.dst.shape[3])
                    pltpu.make_async_copy(here, part, self.sems.at[0, self.r]).wait()

                @pl.when(self.gets_direct)
                def _():
                    self.on(h, z).start()

    def finish(self):
        for h in range(self.per_col):
            for z in range(self.cols):

                @pl.when(self.gets_direct)
                def _():
                    self.on(h, z).wait_send()

                @pl.when(jnp.logical_not(self.gets_direct))
                def _():
                    self.on(h, z).wait_recv()

        self.each(lambda copy: copy.wait_send(), lambda copy: None)


def finish_kernel(per_col, wide, chan, los, chunks, sides, *refs):
    count = len(los)
    arrays, refs = refs[:count], refs[count:]
    attn_ref, ffn_ref, conv_ref, small_ref, tok_ref, o2_ref, o1_ref, oc_ref, oa_ref, os_ref, ot_ref = refs[:11]
    srecv, ssum, precv, psems, asems, rsems, ssems = refs[11:18]
    scratch = refs[18:]
    rows = lax.axis_size("rows")
    me = lax.rem(lax.axis_index("dp"), 2) * rows + lax.axis_index("rows")
    greet_box(2)
    small = line_copies("cols", small_ref, srecv, ssems, 0)
    begin_all(small)
    work = [(conv_ref, oc_ref, 0, chan)]
    work += [(ffn_ref.at[:, pl.ds(lo, n)], o1_ref, lo, wide) for lo, n in chunks]
    sums = []
    for i, (src, out, lo, w) in enumerate(work):
        own = scratch[5 * i : 5 * i + 5]
        sums.append(Reduce.of(src, own[0], own[1:]))
    for one in sums:
        one.start_far()
    for one in sums:
        one.start_near()
    outs = (o2_ref, o1_ref)
    planes = [Plane(a, outs[o], lo, wide, psems.at[i]) for i, (a, (o, lo)) in enumerate(zip(arrays, los))]
    heads = AttentionReturn(attn_ref, oa_ref, asems, per_col)
    heads.start()
    for plane in planes:
        plane.start()
    tok = row_copies("back", tok_ref, ot_ref, rsems, 0)
    begin_all(tok)
    for plane in planes:
        plane.turn()
    end_all(small)
    ssum[...] = jnp.sum(srecv[...], axis=0)
    precv[me] = ssum[...]
    for j in range(1, 8):
        to = plane_peer(j)[2]
        remote(ssum, precv.at[me], ssems.at[2, 0, j], ssems.at[3, 0, j], to).start()
    last = []
    for i, (src, out, lo, w) in enumerate(work):
        if i == 0:
            for one in sums:
                one.relay()
        sums[i].finish()
        if last:
            last[-1].turn()
        last.append(Plane(sums[i].out, out, lo, w, psems.at[count + i]))
        last[-1].start()
    last[-1].turn()
    heads.turn()
    for j in range(1, 8):
        pm, row, to = plane_peer(j)
        copy = remote(ssum, precv.at[pm * rows + row], ssems.at[2, 0, j], ssems.at[3, 0, j], to)
        copy.wait_recv()
        copy.wait_send()
    os_ref[...] = jnp.sum(precv[...], axis=0)
    heads.finish()
    end_all(tok)
    for plane in planes + last:
        plane.finish()


def finish_exchange(cid, arrays, los, attn, ffn, chunks, conv, small, tok, wide, chan, per_col, rows):
    feat = D // rows
    cols, nc, _ = conv.shape
    outs = (
        shape((3, 8 * wide, feat), bf16), shape((3, 8 * wide, feat), bf16),
        shape((nc // chan, 8 * chan, feat), bf16), shape((per_col, cols, attn.shape[0], feat), bf16),
        shape(small.shape, f32), shape((tok.shape[0], tok.shape[1] * rows, feat), f32),
    )
    scratch = [
        pltpu.VMEM((cols,) + small.shape, f32), pltpu.VMEM(small.shape, f32), pltpu.VMEM((8,) + small.shape, f32),
        DMA((len(arrays) + len(chunks) + 1, 4, 4, 4)), DMA((4, 8)), DMA((2, 1, 4)), DMA((4, 1, 8)),
    ]
    for n in [nc] + [n for _, n in chunks]:
        scratch += [pltpu.VMEM((n, D), bf16)] + Reduce.buffers(n)
    return call(
        functools.partial(finish_kernel, per_col, wide, chan, los, chunks), "finish", cid, outs,
        (ANY,) * 4 + (VMEM, ANY), (ANY,) * (len(arrays) + 3) + (VMEM, ANY), scratch,
        tuple(arrays) + (attn, ffn, conv, small, tok), limit=24,
    )


def per_device(
    hidden_in, lengths, conv_norm, conv_in, conv_kernel, conv_out, conv_ffn_norm, conv_ffn_in,
    conv_ffn_out, attn_norm, attn_q, attn_kv, q_gain, k_gain, attn_out, attn_ffn_norm,
    attn_ffn_in, attn_ffn_out, grad_out,
):
    rows, cols, dps = lax.axis_size("rows"), lax.axis_size("cols"), lax.axis_size("dp")
    tp = 2 * rows
    r, c, d = lax.axis_index("rows"), lax.axis_index("cols"), lax.axis_index("dp")
    pair = lax.rem(d, 2)
    me = pair * rows + r
    slots, seqs, feat = hidden_in.shape
    sh = slots // rows

    def halves(x, axis):
        return lax.dynamic_slice_in_dim(x, pair * rows, rows, axis)

    def cut_in(w):
        parts, width = w.shape[1], w.shape[2] // tp
        x = w.astype(bf16).transpose(1, 2, 0).reshape(parts, tp, width, feat)
        return halves(x, 1).transpose(1, 0, 2, 3).reshape(rows, parts * width, feat)

    def cut_out(w):
        return halves(w.astype(bf16).reshape(tp, -1, feat), 0)

    def cut(w_in, w_out):
        return jnp.concatenate([cut_in(w_in), cut_out(w_out)], axis=1)

    wide = conv_ffn_in.shape[2] // tp
    chan = conv_in.shape[2] // tp
    channels = cols * chan
    slot_ids = c * slots + jnp.arange(slots, dtype=jnp.int32)
    keep = (slot_ids[None, :] < lengths[:, None]).astype(f32)[:, :, None]
    gains_own = jnp.stack([conv_norm, conv_ffn_norm, attn_norm, attn_ffn_norm])
    conv_all, begin, ffn1_cut, gains, taps, lens = start_exchange(
        1, cut(conv_in, conv_out), hidden_in.transpose(1, 0, 2) * keep, cut(conv_ffn_in, conv_ffn_out),
        jnp.pad(gains_own, ((0, 4), (0, 0))), jnp.pad(conv_kernel, ((0, 8 - CONV), (0, 0))),
        jnp.pad(lengths[None], ((0, 7), (0, 128 - seqs))), rows, cols,
    )
    w_conv = conv_all[:, : 3 * chan].reshape(cols, 3, chan, D).transpose(1, 0, 2, 3)
    w_conv = w_conv.reshape(3 * channels, D)
    w_cout = conv_all[:, 3 * chan :].reshape(channels, D)
    gains = gains[:4, None]
    kern = lax.dynamic_slice_in_dim(taps[:, :CONV], me * chan, chan, 2)
    kern = kern.transpose(1, 0, 2).reshape(CONV, channels)
    length = lax.dynamic_slice_in_dim(lens[:, 0, :seqs].reshape(2 * seqs), c, 1)

    per_col = tp // cols
    q_w = attn_q.shape[1] // per_col
    kv_w = attn_kv.shape[2] // per_col
    parts = jnp.concatenate(
        [
            attn_q.astype(bf16).T.reshape(per_col, q_w, feat),
            attn_kv[:, 0].astype(bf16).T.reshape(per_col, kv_w, feat),
            attn_kv[:, 1].astype(bf16).T.reshape(per_col, kv_w, feat),
            attn_out.astype(bf16).reshape(per_col, q_w, feat),
        ],
        axis=1,
    )
    w_ffn1 = lax.all_gather(ffn1_cut, "cols", axis=0)

    def after(x, y):
        return lax.optimization_barrier((x, y))[0]

    after_conv, n_conv, mixed, product, gate_edge = conv_forward(3, begin, gains[0], w_conv, w_cout, kern)
    attn_cut, ffn2_cut = second_exchange(
        2, after(parts, after_conv).reshape(per_col, cols, -1, feat), cut(attn_ffn_in, attn_ffn_out), ()
    )
    f2_rows = SECOND_ROWS
    f2_at = [sum(f2_rows[:i]) for i in range(4)]
    after_ffn, n_1, gu_1, w_1, attn_all, f2_a = ffn_forward(
        4, after_conv, gains[1], (w_ffn1,), wide,
        [Gather(attn_cut, 0, attn_cut.shape[0]), Gather(ffn2_cut, f2_at[0], f2_rows[0])],
    )
    attn_all = attn_all.reshape(-1, D)
    w_qkv = attn_all[: q_w + 2 * kv_w]
    w_aout = attn_all[q_w + 2 * kv_w :]
    frequency = jnp.power(rope_base, -(jnp.arange(HD // 2, dtype=f32) * 2.0) / HD)
    angles = slot_ids.astype(f32)[:, None] * frequency[None, :]
    cos, sin = jnp.cos(angles), jnp.sin(angles)
    tables = (
        jnp.concatenate([cos] * 4, axis=1).reshape(2, 2 * sh, 2 * HD),
        jnp.concatenate([-sin, sin] * 2, axis=1).reshape(2, 2 * sh, 2 * HD),
        jnp.tile(q_gain, 2)[None],
        jnp.tile(k_gain, 2)[None],
    )
    after_attn, n_attn, raw, seq, attended, grad_final, f2_b, f2_c, f2_d = attention_forward(
        5, after_ffn, gains[2], w_qkv, w_aout, tables, length,
        [
            Rows("tokens", grad_out.transpose(1, 0, 2) * keep, 1),
            Gather(ffn2_cut, f2_at[1], f2_rows[1], 0), Gather(ffn2_cut, f2_at[2], f2_rows[2], 1),
            Gather(ffn2_cut, f2_at[3], f2_rows[3], 2),
        ],
    )
    final, n_2, gu_2, w_2 = ffn_forward(6, after_attn, gains[3], (f2_a, f2_b, f2_c, f2_d), wide, (), ffn2_cut)

    def over_pairs(x):
        return x if dps == 2 else lax.psum(x * jnp.asarray(0.5, x.dtype), "dp")

    def native(x):
        return x[:-1].transpose(2, 0, 1).astype(f32), x[-1].astype(f32)

    grad_attn_res, gain_p3, dw_2 = ffn_backward(
        7, grad_final, after_attn, gains[3], w_2, n_2, gu_2, wide, cols
    )
    b2_rows, b1_rows = SECOND_BACK, FIRST_BACK
    b2_at = [sum(b2_rows[:i]) for i in range(4)]
    grad_after_ffn, gain_p2, head_parts, grad_attn, final_here, r2_a, r2_b, r2_c = attention_backward(
        8, grad_attn_res, after_ffn, gains[2], w_qkv, w_aout, tables, length, n_attn, raw, seq, attended,
        [Rows("back", final, 1), Reduce(dw_2, 0, b2_rows[0], 0),
         Reduce(dw_2, b2_at[1], b2_rows[1], 1), Reduce(dw_2, b2_at[2], b2_rows[2], 2)],
    )
    grad_attn = grad_attn.reshape(cols, -1, D)
    grad_after_conv, gain_p1, dw_1, r_attn, r2_d = ffn_backward(
        9, grad_after_ffn, after_conv, gains[1], w_1, n_1, gu_1, wide, cols,
        [Reduce(grad_attn, 0, grad_attn.shape[1]), Reduce(dw_2, b2_at[3], b2_rows[3])],
    )
    grad_begin, gain_p0, kern_part, grad_conv, r1_a = conv_backward(
        10, grad_after_conv, begin, gains[0], w_conv, w_cout, kern, n_conv, mixed, product, gate_edge,
        [Reduce(dw_1, 0, b1_rows[0])],
    )
    output = (final_here * keep).transpose(1, 0, 2)
    grad_cin = grad_conv[: 3 * channels].reshape(3, cols, chan, D).transpose(1, 0, 2, 3)
    packed0 = jnp.concatenate(
        [grad_cin.reshape(cols, 3 * chan, D), grad_conv[3 * channels :].reshape(cols, chan, D)], axis=1
    )
    zero = jnp.zeros((), jnp.int32)
    kern_full = lax.dynamic_update_slice(
        jnp.zeros((CONV, cols, tp, chan), f32),
        kern_part.reshape(CONV, cols, 1, chan),
        (zero, zero, me, zero),
    )
    heads = jnp.stack([head_parts[0, :HD] + head_parts[0, HD:], head_parts[1, :HD]])
    small = jnp.concatenate(
        [gain_p0, gain_p1, gain_p2, gain_p3, kern_full.reshape(CONV, D),
         jnp.pad(heads.reshape(1, -1), ((0, 0), (0, D - 2 * HD)))]
    )
    chunks = [(sum(b1_rows[:i]), n) for i, n in enumerate(b1_rows)][1:]
    got2, got1, got0, got_a, sums, grad_here = finish_exchange(
        11, (r2_a, r2_b, r2_c, r2_d, r1_a), [(0, at) for at in b2_at] + [(1, 0)], r_attn, dw_1, chunks,
        packed0, small, grad_begin, wide, chan, per_col, rows,
    )
    got2, got1, got0, got_a, sums = (over_pairs(x) for x in (got2, got1, got0, got_a, sums))
    got_a = got_a.reshape(per_col, -1, feat)
    g_attn_ffn_in, g_attn_ffn_out = native(got2)
    g_q = got_a[:, :q_w].astype(f32).reshape(-1, feat).T
    g_kv = jnp.stack(
        [
            got_a[:, q_w : q_w + kv_w].astype(f32).reshape(-1, feat).T,
            got_a[:, q_w + kv_w : q_w + 2 * kv_w].astype(f32).reshape(-1, feat).T,
        ],
        axis=1,
    )
    g_aout = got_a[:, q_w + 2 * kv_w :].astype(f32).reshape(-1, feat)
    grad_in = (grad_here * keep).transpose(1, 0, 2)
    g_conv_ffn_in, g_conv_ffn_out = native(got1)
    g_conv_in, g_conv_out = native(got0)
    g_gain = lax.dynamic_slice(sums, (zero, r * feat), (4, feat))
    g_kern = lax.dynamic_slice(sums[4 : 4 + CONV], (zero, c * conv_kernel.shape[1]), conv_kernel.shape)
    return (
        output, grad_in, g_gain[0], g_conv_in, g_kern, g_conv_out, g_gain[1],
        g_conv_ffn_in, g_conv_ffn_out, g_gain[2], g_q, g_kv, sums[7, :HD], sums[7, HD : 2 * HD], g_aout,
        g_gain[3], g_attn_ffn_in, g_attn_ffn_out,
    )


def solution(mesh):
    tokens, vec, mat = P("cols", "dp", "rows"), P("rows"), P("rows", "cols")
    mat3, out, taps = P("rows", None, "cols"), P("cols", "rows"), P(None, "cols")
    weights = (vec, mat3, taps, out, vec, mat3, out, vec, mat, mat3, P(), P(), out, vec, mat3, out)
    return jax.shard_map(
        per_device,
        mesh=mesh,
        in_specs=(tokens, P("dp")) + weights + (tokens,),
        out_specs=(tokens, tokens) + weights,
        check_vma=False,
    )
```

```python
import functools

import jax
import jax.numpy as jnp
from jax import lax
from jax.experimental import pallas as pl
from jax.experimental.pallas import tpu as pltpu
from jax.sharding import PartitionSpec as P

D = 1024
HD = 64
CONV = 3
epsilon = 1e-05
rope_base = 1000000.0
bf16 = jnp.bfloat16
f32 = jnp.float32
MESH = pl.DeviceIdType.MESH
LIMIT = 62
SECOND_ROWS = (160, 48, 48, 80)
SECOND_BACK = (64, 128, 128, 112)
FIRST_BACK = (208, 128, 96)
ANY = pl.BlockSpec(memory_space=pl.ANY)
VMEM = pl.BlockSpec(memory_space=pltpu.VMEM)


def dot(a, b, ca, cb):
    return lax.dot_general(a, b, (((ca,), (cb,)), ((), ())), preferred_element_type=f32)


def place(m):
    d, r = lax.axis_index("dp"), lax.axis_index("rows")
    pair, half = lax.rem(d, 2), r // 2
    return lax.rem(pair + lax.rem(m, 2), 2), lax.rem(half + m // 2, 2)


def peer(m):
    d, r = lax.axis_index("dp"), lax.axis_index("rows")
    pm, hm = place(m)
    return {"dp": d - lax.rem(d, 2) + pm, "rows": hm * 2 + lax.rem(r, 2)}


def sibling():
    r = lax.axis_index("rows")
    return {"rows": r + 1 - 2 * lax.rem(r, 2)}


def remote(src, dst, send, recv, to):
    return pltpu.make_async_remote_copy(
        src_ref=src, dst_ref=dst, send_sem=send, recv_sem=recv, device_id=to, device_id_type=MESH
    )


def share(sh, mine):
    k = lax.rem(lax.axis_index("rows"), 2)
    k = k if mine else 1 - k
    return pl.ds(pl.multiple_of(k * sh, 16), sh)


def greet():
    barrier = pltpu.get_barrier_semaphore()
    rows, cols = lax.axis_size("rows"), lax.axis_size("cols")
    r, c = lax.axis_index("rows"), lax.axis_index("cols")
    to = [peer(1), peer(3)] + [{"rows": lax.rem(r + k, rows)} for k in range(1, rows)]
    to += [{"cols": lax.rem(c + k, cols)} for k in range(1, cols)]
    for device in to:
        pl.semaphore_signal(barrier, inc=1, device_id=device, device_id_type=MESH)
    pl.semaphore_wait(barrier, len(to))


def gather_copy(buf, sh, sems, m, to):
    pm, hm = place(0)
    own = buf.at[pm, :, hm, share(sh, True)]
    return remote(own, own, sems.at[0, m], sems.at[1, m], to)


def relay_copy(buf, sh, sems, m):
    pm, hm = place(m)
    part = buf.at[pm, m - 1, hm, share(sh, True)]
    return remote(part, part, sems.at[8, m], sems.at[9, m], peer(3 - m))


def start_gather(buf, sh, sems):
    gather_copy(buf, sh, sems, 0, sibling()).start()
    for m in (1, 2):
        gather_copy(buf, sh, sems, m, peer(m)).start()


def forward_copy(buf, sh, sems, m, mine):
    pm, hm = place(m)
    part = buf.at[pm, :, hm, share(sh, mine)]
    return remote(part, part, sems.at[2, m], sems.at[3, m], sibling())


def arrive(buf, sh, sems, m):
    def come(src, i, j):
        remote(src, src, sems.at[i - 1, j], sems.at[i, j], sibling()).wait_recv()

    @pl.when(m == 0)
    def _():
        pm, hm = place(0)
        come(buf.at[pm, :, hm, share(sh, False)], 1, 0)

    @pl.when(m == 1)
    def _():
        for j in (1, 2):
            pj, hj = place(j)
            come(buf.at[pj, :, hj, share(sh, True)], 1, j)
            relay_copy(buf, sh, sems, j).start()
            forward_copy(buf, sh, sems, j, True).start()

    @pl.when(m == 3)
    def _():
        pj, hj = place(3)
        for j in (1, 2):
            come(buf.at[pj, j - 1, hj, share(sh, True)], 9, j)
        forward_copy(buf, sh, sems, 3, True).start()

    @pl.when(m > 0)
    def _():
        forward_copy(buf, sh, sems, m, False).wait_recv()


def end_gather(buf, sh, sems):
    gather_copy(buf, sh, sems, 0, sibling()).wait_send()
    for m in (1, 2):
        gather_copy(buf, sh, sems, m, peer(m)).wait_send()
        relay_copy(buf, sh, sems, m).wait_send()
    for m in (1, 2, 3):
        forward_copy(buf, sh, sems, m, True).wait_send()


def sum_copy(ys, yr, sems, m, half):
    return remote(ys.at[m, half], yr.at[m, half], sems.at[6, 2 * half + m - 1], sems.at[7, 2 * half + m - 1], peer(m))


def relay_sum_copy(ys, yr, sems, half):
    return remote(ys.at[3, half], yr.at[3, half], sems.at[10, half], sems.at[11, half], peer(half + 1))


def across_copy(part, xr, sh, sems, m):
    return remote(
        part.at[m, :, share(sh, False)], xr.at[m], sems.at[4, m], sems.at[5, m], sibling()
    )


def scatter(part, xr, ys, yr, sh, sems, m):
    across_copy(part, xr, sh, sems, m).wait_recv()
    both = part[m, :, share(sh, True)] + xr[m]
    xr[m] = both
    ys[m] = both.astype(bf16)

    @pl.when(m == 3)
    def _():
        for half in (0, 1):
            relay_sum_copy(ys, yr, sems, half).start()

    for j in (1, 2):

        @pl.when(m == j)
        def _():
            sum_copy(ys, yr, sems, j, j - 1).start()


def end_scatter(part, xr, ys, yr, sh, sems):
    for half in (0, 1):
        m = 2 - half
        relay_sum_copy(ys, yr, sems, half).wait_recv()
        ys[m, half] = (xr[m, half] + yr[3, half].astype(f32)).astype(bf16)
        sum_copy(ys, yr, sems, m, half).start()
    total = xr[0]
    for m in (1, 2):
        for half in (0, 1):
            sum_copy(ys, yr, sems, m, half).wait_recv()
        total = total + yr[m].astype(f32)
    for half in (0, 1):
        relay_sum_copy(ys, yr, sems, half).wait_send()
        for m in (1, 2):
            sum_copy(ys, yr, sems, m, half).wait_send()
    for m in range(4):
        across_copy(part, xr, sh, sems, m).wait_send()
    return total


def lines(src_of, dst_of, sems):
    count, c = lax.axis_size("cols"), lax.axis_index("cols")
    sends, gets = [], []
    for k in range(1, count):
        to, come = lax.rem(c + k, count), lax.rem(c + count - k, count)
        sends.append(remote(src_of(to), dst_of(c), sems.at[0, k], sems.at[1, k], {"cols": to}))
        gets.append(remote(src_of(c), dst_of(come), sems.at[0, k], sems.at[1, k], {"cols": to}))
    return sends, gets, pltpu.make_async_copy(src_of(c), dst_of(c), sems.at[0, 0])


class Side:
    def relay(self):
        pass


class Gather(Side):
    def __init__(self, array, lo, n, phase=0):
        self.args = (array,)
        self.phase = phase
        self.lo, self.n = lo, n
        self.relayed = False
        assert lax.axis_size("cols") == 4
        self.outs = ((shape((4, n, D), array.dtype), ANY),)
        self.scratch = [DMA((2, 5))]

    def bind(self, ins, outs, scratch):
        self.src, self.slot, self.sems = ins[0].at[pl.ds(self.lo, self.n)], lambda z: outs[0].at[z], scratch[0]

    @classmethod
    def of(cls, src, slot, sems):
        self = cls.__new__(cls)
        self.relayed = False
        self.src, self.slot, self.sems = src, slot, sems
        return self

    def send(self, t):
        c = lax.axis_index("cols")
        return remote(self.src, self.slot(c), self.sems.at[0, t], self.sems.at[1, c], {"cols": t})

    def pass_on(self):
        c = lax.axis_index("cols")
        part = self.slot(6 - 3 * c)
        return remote(part, part, self.sems.at[0, 4], self.sems.at[1, 6 - 3 * c], {"cols": 3 * c - 3})

    def local(self):
        return pltpu.make_async_copy(self.src, self.slot(lax.axis_index("cols")), self.sems.at[1, 4])

    def each(self, act):
        c = lax.axis_index("cols")
        for off in (2, -2, 1, -1):
            t = c + off

            @pl.when((t >= 0) & (t < 4))
            def _():
                act(self.send(t))

    def start(self):
        self.each(lambda copy: copy.start())
        self.local().start()

    def relay(self):
        self.relayed = True
        c = lax.axis_index("cols")

        @pl.when((c == 1) | (c == 2))
        def _():
            self.pass_on().wait_recv()
            self.pass_on().start()

    def finish(self):
        if not self.relayed:
            self.relay()
        c = lax.axis_index("cols")
        for s in range(4):

            @pl.when((s != c) & (s + 3 * c != 6))
            def _():
                part = self.slot(s)
                remote(part, part, self.sems.at[0, s], self.sems.at[1, s], {"cols": s}).wait_recv()

        self.each(lambda copy: copy.wait_send())

        @pl.when((c == 1) | (c == 2))
        def _():
            self.pass_on().wait_send()

        self.local().wait()


class Reduce(Side):
    def __init__(self, array, lo, n, phase=0):
        self.args = (array,)
        self.phase = phase
        self.lo, self.n = lo, n
        self.relayed = False
        self.outs = ((shape((n, D), array.dtype), VMEM),)
        self.scratch = self.buffers(n)

    @staticmethod
    def buffers(n):
        return [pltpu.VMEM((4, n, D), bf16), pltpu.VMEM((n, D), bf16), pltpu.VMEM((n, D), bf16), DMA((2, 6))]

    def bind(self, ins, outs, scratch):
        self.out = outs[0]
        self.got, self.far, self.own, self.sems = scratch
        self.src = ins[0].at[:, pl.ds(self.lo, self.n)]

    @classmethod
    def of(cls, src, out, scratch):
        self = cls.__new__(cls)
        self.relayed = False
        self.src, self.out, self.n = src, out, out.shape[0]
        self.got, self.far, self.own, self.sems = scratch
        return self

    def send(self, off):
        c = lax.axis_index("cols")
        t = c + off
        if abs(off) == 3:
            return remote(self.src.at[t], self.far, self.sems.at[0, t], self.sems.at[1, 4], {"cols": c + off // 3})
        return remote(self.src.at[t], self.got.at[c], self.sems.at[0, t], self.sems.at[1, c], {"cols": t})

    def send_sum(self):
        c = lax.axis_index("cols")
        t = 6 - 3 * c
        return remote(self.own, self.got.at[c], self.sems.at[0, t], self.sems.at[1, c], {"cols": t})

    def each(self, act, offs):
        c = lax.axis_index("cols")
        for off in offs:
            t = c + off
            ok = (t >= 0) & (t < 4)
            if abs(off) == 2:
                ok = ok & (c != (1 if off == 2 else 2))

            @pl.when(ok)
            def _():
                act(self.send(off))

    def local(self):
        c = lax.axis_index("cols")
        return pltpu.make_async_copy(self.src.at[c], self.got.at[c], self.sems.at[0, 4])

    def load(self):
        c = lax.axis_index("cols")
        return pltpu.make_async_copy(self.src.at[6 - 3 * c], self.own, self.sems.at[0, 5])

    def start(self):
        self.start_far()
        self.start_near()

    def start_far(self):
        self.each(lambda copy: copy.start(), (3, -3))

    def start_near(self):
        c = lax.axis_index("cols")
        self.each(lambda copy: copy.start(), (2, -2, 1, -1))
        self.local().start()

        @pl.when((c == 1) | (c == 2))
        def _():
            self.load().start()

        @pl.when((c == 0) | (c == 3))
        def _():
            self.got[3 - c] = jnp.zeros((self.n, D), bf16)

    def blocks(self):
        return [slice(a, min(a + 48, self.n)) for a in range(0, self.n, 48)]

    def relay(self):
        self.relayed = True
        c = lax.axis_index("cols")

        @pl.when((c == 1) | (c == 2))
        def _():
            self.load().wait()
            remote(self.far, self.far, self.sems.at[0, 0], self.sems.at[1, 4], {"cols": 1}).wait_recv()
            for at in self.blocks():
                self.own[at] = (self.own[at].astype(f32) + self.far[at].astype(f32)).astype(bf16)

            self.send_sum().start()

    def finish(self):
        if not self.relayed:
            self.relay()
        c = lax.axis_index("cols")
        for s in range(4):

            @pl.when((s != c) & (s - c < 3) & (c - s < 3))
            def _():
                part = self.got.at[s]
                remote(part, part, self.sems.at[0, s], self.sems.at[1, s], {"cols": s}).wait_recv()

        self.local().wait()
        for at in self.blocks():
            self.out[at] = jnp.sum(self.got[:, at].astype(f32), axis=0).astype(bf16)
        self.each(lambda copy: copy.wait_send(), (3, -3, 2, -2, 1, -1))

        @pl.when((c == 1) | (c == 2))
        def _():
            self.send_sum().wait_send()


class Rows(Side):
    def __init__(self, kind, array, phase=0):
        self.args = (array,)
        self.phase = phase
        self.kind = kind
        rows = lax.axis_size("rows")
        a, b, f = array.shape
        dims = (a, b // rows, f * rows) if kind == "tokens" else (a, b * rows, f // rows)
        self.outs = ((shape(dims, array.dtype), ANY),)
        self.scratch = [DMA((2, 1, 4))]

    def bind(self, ins, outs, scratch):
        self.work = row_copies(self.kind, ins[0], outs[0], scratch[0], 0)

    def start(self):
        begin_all(self.work)

    def finish(self):
        end_all(self.work)


class AttentionReturn:
    def __init__(self, src, dst, sems, per_col):
        self.src, self.dst, self.sems, self.per_col = src, dst, sems, per_col
        self.rows, self.cols = lax.axis_size("rows"), lax.axis_size("cols")
        self.d, self.r, self.c = lax.axis_index("dp"), lax.axis_index("rows"), lax.axis_index("cols")
        self.pair = lax.rem(self.d, 2)
        self.me = self.pair * self.rows + self.r
        self.gets_direct = per_col * self.c // self.rows == self.pair

    def each(self, act, local):
        owner, half = self.me // self.per_col, lax.rem(self.me, self.per_col)
        width = self.dst.shape[3]
        for k in range(self.rows):
            own = (k == self.r) & (owner == self.c)
            here, there = band(self.src, k, width), self.dst.at[half, self.c]

            @pl.when(jnp.logical_not(own))
            def _():
                act(remote(here, there, self.sems.at[0, k], self.sems.at[1, half * self.cols + self.c],
                           {"rows": k, "cols": owner}))

            @pl.when(own)
            def _():
                local(pltpu.make_async_copy(here, there, self.sems.at[0, k]))

    def start(self):
        self.each(lambda copy: copy.start(), lambda copy: copy.start())

    def finish(self):
        for h in range(self.per_col):
            source = self.c * self.per_col + h
            for z in range(self.cols):
                part = self.dst.at[h, z]
                mine = (source == self.me) & (z == self.c)

                @pl.when(self.gets_direct & jnp.logical_not(mine))
                def _():
                    to = {"rows": lax.rem(source, self.rows), "cols": z}
                    remote(part, part, self.sems.at[0, 0], self.sems.at[1, h * self.cols + z], to).wait_recv()

        self.each(lambda copy: copy.wait_send(), lambda copy: copy.wait())


class PairShare(Side):
    def __init__(self, array, per_col, phase=0):
        self.args = (array,)
        self.phase = phase
        self.per_col = per_col
        self.outs = ((shape(array.shape, array.dtype), ANY),)
        self.scratch = [DMA((3,))]

    def bind(self, ins, outs, scratch):
        d, c = lax.axis_index("dp"), lax.axis_index("cols")
        pair = lax.rem(d, 2)
        self.holds = self.per_col * c // lax.axis_size("rows") == pair
        self.copy = remote(ins[0], outs[0], scratch[0].at[0], scratch[0].at[1], {"dp": d + 1 - 2 * pair})
        self.local = pltpu.make_async_copy(ins[0], outs[0], scratch[0].at[2])

    def start(self):
        @pl.when(self.holds)
        def _():
            self.copy.start()
            self.local.start()

    def finish(self):
        @pl.when(self.holds)
        def _():
            self.copy.wait_send()
            self.local.wait()

        @pl.when(jnp.logical_not(self.holds))
        def _():
            self.copy.wait_recv()


class Return(Side):
    def __init__(self, array, per_col, phase=0):
        n, rows = array.shape[0], lax.axis_size("rows")
        self.args = (array,)
        self.phase = phase
        self.per_col = per_col
        self.outs = ((shape((per_col, 4, n, D // rows), array.dtype), ANY),)
        self.scratch = [DMA((4, 8))]

    def bind(self, ins, outs, scratch):
        self.back = AttentionReturn(ins[0], outs[0], scratch[0], self.per_col)

    def start(self):
        self.back.start()

    def finish(self):
        self.back.finish()


def begin_all(work):
    sends, _, local = work
    for copy in sends:
        copy.start()
    local.start()


def end_all(work):
    sends, gets, local = work
    for copy in gets:
        copy.wait_recv()
    for copy in sends:
        copy.wait_send()
    local.wait()


def start_sides(sides, phase=0):
    for side in sides:
        if side.phase == phase:
            side.start()


def relay_sides(sides, phase=0):
    for side in sides:
        if side.phase == phase:
            side.relay()


def finish_sides(sides):
    for side in sides:
        side.finish()


def rms(x):
    return lax.rsqrt(jnp.mean(x * x, axis=-1, keepdims=True) + epsilon)


def put_own(buf, sh, value):
    pm, hm = place(0)
    buf[pm, :, hm, share(sh, True)] = value.astype(bf16)


def norm_own(x_ref, gain_ref):
    x = x_ref[...]
    return x * rms(x) * gain_ref[...]


def norm_back(n, x_ref, gain_ref, grad_ref, out_ref, gain_out):
    x = x_ref[...]
    q = rms(x)
    scaled = n * gain_ref[...]
    dots = jnp.mean(scaled * x, axis=-1, keepdims=True)
    out_ref[...] = grad_ref[...] + scaled * q - x * (q * q * q) * dots
    gain_out[...] = jnp.sum(n * x * q, axis=(0, 1))[None]


def flat(x):
    return x.reshape(x.shape[0] * x.shape[1], x.shape[2])


def tiles(width):
    return [(a, min(256, width - a)) for a in range(0, width, 256)]


def columns(width, act):
    def one(j, carry):
        act(pl.ds(pl.multiple_of(j * 256, 256), 256))
        return carry

    lax.fori_loop(0, width // 256, one, 0)


def padded(width):
    return -(-width // 128) * 128


def segments(lo, n, wide):
    cuts = []
    for g in range(lo // wide, -(-(lo + n) // wide)):
        a, b = max(lo, g * wide), min(lo + n, (g + 1) * wide)
        cuts.append((g, a - g * wide, a - lo, b - a))
    return cuts


def first_rows(arrays, axis):
    return [sum(x.shape[axis] for x in arrays[:i]) for i in range(len(arrays))]


def load_copies(parts, wbuf, wide, sem):
    copies = []
    for ref, lo in zip(parts, first_rows(parts, 1)):
        for g, at, here, n in segments(lo, ref.shape[1], wide):
            for c in range(ref.shape[0]):
                copies.append(pltpu.make_async_copy(
                    ref.at[c, pl.ds(here, n)], wbuf.at[g, pl.ds(c * wide + at, n)], sem.at[len(copies)]
                ))
    return copies


def zero_pad(wbuf, used):
    if wbuf.shape[1] > used:
        wbuf[:, used:] = jnp.zeros((3, wbuf.shape[1] - used, wbuf.shape[2]), bf16)


def ffn_forward_kernel(sh, wide, count, last, sides, x_ref, gain_ref, *refs):
    parts, refs = refs[:count], refs[count:]
    if last:
        tail_ref, refs = refs[0], refs[1:]
    out_ref, n_ref, gu_ref, save_ref, buf, wbuf, gu, hid, part, xr, ys, yr, sems, wsem, osem, gsem = refs
    cols = parts[0].shape[0]
    loads = load_copies(parts, wbuf, wide, wsem)
    for copy in loads:
        copy.start()
    zero_pad(wbuf, cols * wide)
    put_own(buf, sh, norm_own(x_ref, gain_ref))
    greet()
    start_gather(buf, sh, sems)
    if last:
        tail = Gather.of(
            tail_ref.at[pl.ds(3 * wide - last, last)],
            lambda z: wbuf.at[2, pl.ds(pl.multiple_of(z * wide + wide - last, 16), last)],
            gsem,
        )
        tail.start()
    start_sides(sides)
    for copy in loads:
        copy.wait()
    width = wbuf.shape[1]

    def step(m, carry):
        arrive(buf, sh, sems, m)
        if last:
            pl.when(m == 2)(tail.relay)
        pl.when(m == 3)(lambda: relay_sides(sides))
        pm, hm = place(m)
        x = flat(buf[pm, :, hm])
        for a, n in tiles(width):
            g = dot(x, wbuf[0, a : a + n], 1, 1)
            u = dot(x, wbuf[1, a : a + n], 1, 1)
            gu[m, 0, :, a : a + n] = g
            gu[m, 1, :, a : a + n] = u
            hid[m, :, a : a + n] = (g * jax.nn.sigmoid(g) * u).astype(bf16)
        pltpu.make_async_copy(gu.at[m], gu_ref.at[m], osem.at[m]).start()
        return carry

    lax.fori_loop(0, 4, step, 0)
    if last:
        tail.finish()
    save = pltpu.make_async_copy(wbuf, save_ref, osem.at[5])
    save.start()
    keep_n = pltpu.make_async_copy(buf, n_ref, osem.at[4])
    keep_n.start()

    def merge_step(t, carry):
        m = 3 - t

        def down(at):
            part[m, :, :, at] = dot(hid[m], wbuf[2, :, at], 1, 0).reshape(part.shape[1], part.shape[2], 256)

        columns(D, down)
        across_copy(part, xr, sh, sems, m).start()

        @pl.when(m < 3)
        def _():
            scatter(part, xr, ys, yr, sh, sems, m + 1)

        return carry

    lax.fori_loop(0, 4, merge_step, 0)
    scatter(part, xr, ys, yr, sh, sems, 0)
    out_ref[...] = x_ref[...] + end_scatter(part, xr, ys, yr, sh, sems)
    end_gather(buf, sh, sems)
    for m in range(4):
        pltpu.make_async_copy(gu.at[m], gu_ref.at[m], osem.at[m]).wait()
    keep_n.wait()
    save.wait()
    finish_sides(sides)


def ffn_backward_kernel(sh, wide, sides, grad_ref, x_ref, gain_ref, w_ref, n_ref, gu_ref,
                        out_ref, gain_out, dw_ref,
                        buf, nbuf, wbuf, gu, hid, dw, part, xr, ys, yr, sems, wsem, osem):
    cols = dw_ref.shape[0]
    gloads = [pltpu.make_async_copy(gu_ref.at[m], gu.at[m], osem.at[m]) for m in range(4)]
    nload = pltpu.make_async_copy(n_ref, nbuf, osem.at[4])
    loads = [pltpu.make_async_copy(w_ref, wbuf, osem.at[5])]
    for copy in loads + gloads + [nload]:
        copy.start()
    put_own(buf, sh, grad_ref[...])
    greet()
    start_gather(buf, sh, sems)
    start_sides(sides)
    for copy in loads + gloads:
        copy.wait()
    width = wbuf.shape[1]

    def step(m, carry):
        arrive(buf, sh, sems, m)
        pl.when(m == 3)(lambda: relay_sides(sides))
        pm, hm = place(m)
        gg = flat(buf[pm, :, hm])
        for a, n in tiles(width):
            gh = dot(gg, wbuf[2, a : a + n], 1, 1)
            g = gu[m, 0, :, a : a + n]
            u = gu[m, 1, :, a : a + n]
            s = jax.nn.sigmoid(g)
            silu = g * s
            shape = (part.shape[1], part.shape[2], n)
            hid[0, pm, :, hm, :, a : a + n] = (gh * u * (s * (1.0 + g * (1.0 - s)))).astype(bf16).reshape(shape)
            hid[1, pm, :, hm, :, a : a + n] = (gh * silu).astype(bf16).reshape(shape)
            hid[2, pm, :, hm, :, a : a + n] = (silu * u).astype(bf16).reshape(shape)

        def back(at):
            y = dot(flat(hid[0, pm, :, hm]), wbuf[0, :, at], 1, 0) + dot(flat(hid[1, pm, :, hm]), wbuf[1, :, at], 1, 0)
            part[m, :, :, at] = y.reshape(part.shape[1], part.shape[2], 256)

        columns(D, back)
        across_copy(part, xr, sh, sems, m).start()

        @pl.when(m > 0)
        def _():
            scatter(part, xr, ys, yr, sh, sems, m - 1)

        return carry

    lax.fori_loop(0, 4, step, 0)
    scatter(part, xr, ys, yr, sh, sems, 3)
    nload.wait()
    tokens = 8 * buf.shape[3]

    def grads(other, g):
        def one(i, carry):
            at = pl.ds(pl.multiple_of(i * 128, 128), 128)
            left = hid[g, :, :, :, :, at].reshape(tokens, 128)
            dw[g, at] = dot(left, other[...].reshape(tokens, D), 0, 0).astype(bf16)
            return carry

        lax.fori_loop(0, width // 128, one, 0)

    grads(nbuf, 0)
    grads(nbuf, 1)
    grads(buf, 2)
    stores = [
        pltpu.make_async_copy(
            dw.at[g, pl.ds(c * wide, wide)], dw_ref.at[c, pl.ds(g * wide, wide)], wsem.at[c * 3 + g]
        )
        for c in range(cols)
        for g in range(3)
    ]
    for copy in stores:
        copy.start()
    n = end_scatter(part, xr, ys, yr, sh, sems)
    norm_back(n, x_ref, gain_ref, grad_ref, out_ref, gain_out)
    end_gather(buf, sh, sems)
    for copy in stores:
        copy.wait()
    finish_sides(sides)


def ffn_both_kernel(sh, wide, count, last, sides, x_ref, gain_ref, grad_ref, *refs):
    parts, refs = refs[:count], refs[count:]
    if last:
        tail_ref, refs = refs[0], refs[1:]
    out_ref, grad_out, gain_out, dw_ref, buf, gbuf, wbuf, gu, hid, dw = refs[:10]
    one, two = refs[10:14] + refs[18:19], refs[14:18] + refs[19:20]
    wsem, dsem, gsem = refs[20:]
    cols = dw_ref.shape[0]
    sems, gsems = one[4], two[4]
    loads = load_copies(parts, wbuf, wide, wsem)
    for copy in loads:
        copy.start()
    zero_pad(wbuf, cols * wide)
    put_own(buf, sh, norm_own(x_ref, gain_ref))
    put_own(gbuf, sh, grad_ref[...])
    greet()
    start_gather(buf, sh, sems)
    if last:
        tail = Gather.of(
            tail_ref.at[pl.ds(3 * wide - last, last)],
            lambda z: wbuf.at[2, pl.ds(pl.multiple_of(z * wide + wide - last, 16), last)],
            gsem,
        )
        tail.start()
    start_gather(gbuf, sh, gsems)
    start_sides(sides)
    for copy in loads:
        copy.wait()
    width = wbuf.shape[1]
    tokens = 8 * buf.shape[3]

    def out(state):
        part, xr, ys, yr, sem = state
        return part, xr, ys, yr, sh, sem

    def step(m, carry):
        arrive(buf, sh, sems, m)
        if last:
            pl.when(m == 2)(tail.relay)
        pm, hm = place(m)
        x = flat(buf[pm, :, hm])
        for a, n in tiles(width):
            g = dot(x, wbuf[0, a : a + n], 1, 1)
            u = dot(x, wbuf[1, a : a + n], 1, 1)
            gu[m, 0, :, a : a + n] = g
            gu[m, 1, :, a : a + n] = u
            h = (g * jax.nn.sigmoid(g) * u).astype(bf16)
            hid[2, pm, :, hm, :, a : a + n] = h.reshape(buf.shape[1], buf.shape[3], n)
        return carry

    lax.fori_loop(0, 4, step, 0)
    if last:
        tail.finish()

    def merge_step(t, carry):
        m = 3 - t
        pm, hm = place(m)
        part = one[0]

        def down(at):
            y = dot(flat(hid[2, pm, :, hm]), wbuf[2, :, at], 1, 0)
            part[m, :, :, at] = y.reshape(part.shape[1], part.shape[2], 256)

        columns(D, down)
        across_copy(part, one[1], sh, sems, m).start()

        @pl.when(m < 3)
        def _():
            scatter(*out(one), m + 1)

        return carry

    lax.fori_loop(0, 4, merge_step, 0)
    scatter(*out(one), 0)

    def back_step(m, carry):
        arrive(gbuf, sh, gsems, m)

        @pl.when(m == 2)
        def _():
            out_ref[...] = x_ref[...] + end_scatter(*out(one))

        pm, hm = place(m)
        part = two[0]
        gg = flat(gbuf[pm, :, hm])
        for a, n in tiles(width):
            gh = dot(gg, wbuf[2, a : a + n], 1, 1)
            g = gu[m, 0, :, a : a + n]
            u = gu[m, 1, :, a : a + n]
            s = jax.nn.sigmoid(g)
            size = (part.shape[1], part.shape[2], n)
            hid[0, pm, :, hm, :, a : a + n] = (gh * u * (s * (1.0 + g * (1.0 - s)))).astype(bf16).reshape(size)
            hid[1, pm, :, hm, :, a : a + n] = (gh * (g * s)).astype(bf16).reshape(size)

        def back(at):
            y = dot(flat(hid[0, pm, :, hm]), wbuf[0, :, at], 1, 0) + dot(flat(hid[1, pm, :, hm]), wbuf[1, :, at], 1, 0)
            part[m, :, :, at] = y.reshape(part.shape[1], part.shape[2], 256)

        columns(D, back)
        across_copy(part, two[1], sh, gsems, m).start()

        @pl.when(m > 0)
        def _():
            scatter(*out(two), m - 1)

        return carry

    lax.fori_loop(0, 4, back_step, 0)
    scatter(*out(two), 3)

    def grads(other, g):
        def rows(i, carry):
            at = pl.ds(pl.multiple_of(i * 128, 128), 128)
            left = hid[g, :, :, :, :, at].reshape(tokens, 128)
            dw[g, at] = dot(left, other[...].reshape(tokens, D), 0, 0).astype(bf16)
            return carry

        lax.fori_loop(0, width // 128, rows, 0)

    grads(buf, 0)
    grads(buf, 1)
    grads(gbuf, 2)
    stores = [
        pltpu.make_async_copy(
            dw.at[g, pl.ds(c * wide, wide)], dw_ref.at[c, pl.ds(g * wide, wide)], dsem.at[c * 3 + g]
        )
        for c in range(cols)
        for g in range(3)
    ]
    for copy in stores:
        copy.start()
    norm_back(end_scatter(*out(two)), x_ref, gain_ref, grad_ref, grad_out, gain_out)
    end_gather(buf, sh, sems)
    end_gather(gbuf, sh, gsems)
    for copy in stores:
        copy.wait()
    finish_sides(sides)


def shape(dims, kind):
    return jax.ShapeDtypeStruct(dims, kind)


def save_all(sem, *pairs, first=0):
    copies = [pltpu.make_async_copy(a, b, sem.at[first + i]) for i, (a, b) in enumerate(pairs)]
    for copy in copies:
        copy.start()
    return copies


def scatter_scratch(seqs, sh):
    return [
        pltpu.VMEM((4, seqs, 2 * sh, D), f32),
        pltpu.VMEM((4, seqs, sh, D), f32),
        pltpu.VMEM((4, seqs, sh, D), bf16),
        pltpu.VMEM((4, seqs, sh, D), bf16),
    ]


def call(kernel, name, cid, outs, out_specs, in_specs, scratch, args, flops=46 * 10**9, limit=LIMIT, sides=()):
    n_in, n_out, n_scratch = len(args), len(outs), len(scratch)
    side_in = [x for side in sides for x in side.args]
    side_out = [x for side in sides for x in side.outs]
    side_scratch = [x for side in sides for x in side.scratch]

    def body(*refs):
        ins, rest = refs[:n_in], refs[n_in:]
        extra_in, rest = rest[: len(side_in)], rest[len(side_in) :]
        out, rest = rest[:n_out], rest[n_out:]
        extra_out, rest = rest[: len(side_out)], rest[len(side_out) :]
        own, extra_scratch = rest[:n_scratch], rest[n_scratch:]
        for side in sides:
            a, b, s = len(side.args), len(side.outs), len(side.scratch)
            side.bind(extra_in[:a], extra_out[:b], extra_scratch[:s])
            extra_in, extra_out, extra_scratch = extra_in[a:], extra_out[b:], extra_scratch[s:]
        kernel(*((sides,) if sides is not None else ()), *ins, *out, *own)

    got = pl.pallas_call(
        body,
        name=name,
        out_shape=tuple(outs) + tuple(x[0] for x in side_out),
        in_specs=tuple(in_specs) + (ANY,) * len(side_in),
        out_specs=tuple(out_specs) + tuple(x[1] for x in side_out),
        scratch_shapes=list(scratch) + side_scratch,
        cost_estimate=pl.CostEstimate(flops=flops, bytes_accessed=10**7, transcendentals=0),
        compiler_params=pltpu.CompilerParams(
            collective_id=cid, has_side_effects=True, vmem_limit_bytes=limit << 20
        ),
    )(*args, *side_in)
    return got


DMA = pltpu.SemaphoreType.DMA


def ffn_forward(cid, x, gain, parts, wide, sides=(), tail=None):
    seqs, sh, _ = x.shape
    cols = parts[0].shape[0]
    width = padded(cols * wide)
    full = (2, seqs, 2, 2 * sh, D)
    rows = seqs * 2 * sh
    last = 3 * wide - sum(p.shape[1] for p in parts)
    assert 0 <= last <= wide and (last == 0 or tail is not None)
    args = (x, gain) + tuple(parts) + ((tail,) if last else ())
    return call(
        functools.partial(ffn_forward_kernel, sh, wide, len(parts), last), "ffn_forward", cid,
        (shape(x.shape, f32), shape(full, bf16), shape((4, 2, rows, width), f32), shape((3, width, D), bf16)),
        (VMEM, ANY, ANY, ANY), (VMEM, VMEM) + (ANY,) * (len(args) - 2),
        [
            pltpu.VMEM(full, bf16), pltpu.VMEM((3, width, D), bf16),
            pltpu.VMEM((4, 2, rows, width), f32), pltpu.VMEM((4, rows, width), bf16),
        ] + scatter_scratch(seqs, sh)
        + [DMA((12, 4)), DMA((cols * (len(parts) + 2),)), DMA((6,)), DMA((2, 5))],
        args, sides=sides,
    )


def ffn_both(cid, x, gain, grad, parts, wide, tail, sides=()):
    seqs, sh, _ = x.shape
    cols = parts[0].shape[0]
    width = padded(cols * wide)
    full = (2, seqs, 2, 2 * sh, D)
    rows = seqs * 2 * sh
    last = 3 * wide - sum(p.shape[1] for p in parts)
    assert 0 <= last <= wide
    args = (x, gain, grad) + tuple(parts) + ((tail,) if last else ())
    return call(
        functools.partial(ffn_both_kernel, sh, wide, len(parts), last), "ffn_both", cid,
        (shape(x.shape, f32), shape(x.shape, f32), shape((1, D), f32), shape((cols, 3 * wide, D), bf16)),
        (VMEM, VMEM, VMEM, ANY), (VMEM, VMEM, VMEM) + (ANY,) * (len(args) - 3),
        [
            pltpu.VMEM(full, bf16), pltpu.VMEM(full, bf16), pltpu.VMEM((3, width, D), bf16),
            pltpu.VMEM((4, 2, rows, width), f32), pltpu.VMEM((3,) + full[:4] + (width,), bf16),
            pltpu.VMEM((3, width, D), bf16),
        ] + scatter_scratch(seqs, sh) + scatter_scratch(seqs, sh)
        + [DMA((12, 4)), DMA((12, 4)), DMA((cols * (len(parts) + 2),)), DMA((3 * cols,)), DMA((2, 5))],
        args, sides=sides,
    )


def ffn_backward(cid, grad, x, gain, w, n, gu, wide, cols, sides=()):
    seqs, sh, _ = x.shape
    width = w.shape[1]
    full = (2, seqs, 2, 2 * sh, D)
    rows = seqs * 2 * sh
    return call(
        functools.partial(ffn_backward_kernel, sh, wide), "ffn_backward", cid,
        (shape(x.shape, f32), shape((1, D), f32), shape((cols, 3 * wide, D), bf16)),
        (VMEM, VMEM, ANY), (VMEM, VMEM, VMEM, ANY, ANY, ANY),
        [
            pltpu.VMEM(full, bf16), pltpu.VMEM(full, bf16), pltpu.VMEM((3, width, D), bf16),
            pltpu.VMEM((4, 2, rows, width), f32), pltpu.VMEM((3,) + full[:4] + (width,), bf16),
            pltpu.VMEM((3, width, D), bf16),
        ] + scatter_scratch(seqs, sh) + [DMA((12, 4)), DMA((3 * cols,)), DMA((6,))],
        (grad, x, gain, w, n, gu), sides=sides,
    )


def out_copy(stage, dest, sems, m, i):
    pm, hm = place(m)
    c = lax.axis_index("cols")
    s = pm * stage.shape[1] + i
    return s, remote(
        stage.at[m, i], dest.at[c, hm], sems.at[0, m * 2 + i], sems.at[1, c * 2 + hm], {"cols": s}
    )


def send_out(stage, dest, sems, m):
    pm, hm = place(m)
    c = lax.axis_index("cols")
    for i in range(stage.shape[1]):
        s, copy = out_copy(stage, dest, sems, m, i)

        @pl.when(s == c)
        def _():
            dest[c, hm] = stage[m, i]

        @pl.when(s != c)
        def _():
            copy.start()


def wait_out(stage, dest, sems):
    c = lax.axis_index("cols")
    for z in range(dest.shape[0]):
        for h in range(2):

            @pl.when(z != c)
            def _():
                got = dest.at[z, h]
                remote(got, got, sems.at[0, z * 2 + h], sems.at[1, z * 2 + h], {"cols": z}).wait_recv()


def end_out(stage, dest, sems):
    c = lax.axis_index("cols")
    for m in range(4):
        for i in range(stage.shape[1]):
            s, copy = out_copy(stage, dest, sems, m, i)

            @pl.when(s != c)
            def _():
                copy.wait_send()


def back_copy(stage, dest, sems, i, row=2):
    c = lax.axis_index("cols")
    seqs = dest.shape[1]
    return remote(
        stage.at[i], dest.at[c // seqs, lax.rem(c, seqs)], sems.at[row, i], sems.at[row + 1, c], {"cols": i}
    )


def send_back(stage, dest, sems, i, row=2):
    c = lax.axis_index("cols")
    seqs = dest.shape[1]

    @pl.when(i == c)
    def _():
        dest[c // seqs, lax.rem(c, seqs)] = stage[i]

    @pl.when(i != c)
    def _():
        back_copy(stage, dest, sems, i, row).start()


def wait_back(stage, dest, sems, row=2):
    c = lax.axis_index("cols")
    seqs = dest.shape[1]
    for s in range(stage.shape[0]):

        @pl.when(s != c)
        def _():
            got = dest.at[s // seqs, s % seqs]
            remote(got, got, sems.at[row, s], sems.at[row + 1, s], {"cols": s}).wait_recv()
            back_copy(stage, dest, sems, s, row).wait_send()


def low_lanes(x):
    return lax.broadcasted_iota(jnp.int32, x.shape, x.ndim - 1) < HD


def per_head(x):
    low = low_lanes(x)
    a = jnp.sum(jnp.where(low, x, 0.0), axis=-1, keepdims=True)
    b = jnp.sum(jnp.where(low, 0.0, x), axis=-1, keepdims=True)
    return jnp.where(low, a, b) * (1.0 / HD)


def partner(x):
    lane = lax.rem(lax.broadcasted_iota(jnp.int32, x.shape, x.ndim - 1), HD)
    return jnp.where(lane < HD // 2, pltpu.roll(x, 2 * HD - HD // 2, axis=1), pltpu.roll(x, HD // 2, axis=1))


def swap(x):
    return pltpu.roll(x, HD, axis=1)


def rope_forward(x, gain, cos, sin):
    y = x * lax.rsqrt(per_head(x * x) + epsilon) * gain
    return y * cos + partner(y) * sin


def rope_backward(x, gain, cos, sin, grad):
    inv = lax.rsqrt(per_head(x * x) + epsilon)
    g = grad * cos - partner(grad) * sin
    scaled = g * gain
    out = scaled * inv - x * (inv * inv * inv) * per_head(scaled * x)
    return out, jnp.sum(g * x * inv, axis=0, keepdims=True)


def split_heads(x, upper):
    x = x.astype(f32)
    low = low_lanes(x)
    if upper:
        return jnp.where(low, 0.0, swap(x)).astype(bf16), jnp.where(low, 0.0, x).astype(bf16)
    return jnp.where(low, x, 0.0).astype(bf16), jnp.where(low, swap(x), 0.0).astype(bf16)


def probabilities(q, keys, first, length):
    s = dot(q, keys, 1, 1)
    at = lax.broadcasted_iota(jnp.int32, s.shape, 1)
    row = lax.broadcasted_iota(jnp.int32, s.shape, 0) + first
    s = jnp.where((at <= row) & (at < length), s, -1e30)
    e = jnp.exp(s - jnp.max(s, axis=1, keepdims=True))
    return e * (1.0 / jnp.sum(e, axis=1, keepdims=True))


def key_bound(i, slots):
    return min(-(-(i + 1) * slots // 128) * 128, 4 * slots)


def attention_forward_kernel(sh, sides, x_ref, gain_ref, w_all, cos_ref, sin_ref, gq_ref, gk_ref, len_ref,
                             out_ref, n_out, raw_out, seq_out, att_out,
                             raw_ref, seq_ref, att_ref, buf, stage, q2, kv, o, back, part, xr, ys, yr, sems, zsems, osem):
    c = lax.axis_index("cols")
    slots = 4 * sh
    w_ref, wo_ref = w_all.at[pl.ds(0, 4 * HD)], w_all.at[pl.ds(4 * HD, 2 * HD)]
    put_own(buf, sh, norm_own(x_ref, gain_ref))
    greet()
    start_gather(buf, sh, sems)
    start_sides(sides)
    low = low_lanes(gq_ref[...])

    def step(m, carry):
        arrive(buf, sh, sems, m)
        pm, hm = place(m)
        y = dot(flat(buf[pm, :, hm]), w_ref[...], 1, 1)
        raw_ref[pm, :, hm] = y.reshape(raw_ref.shape[1], 2 * sh, 4 * HD)
        for i in range(stage.shape[1]):
            rows = slice(i * 2 * sh, (i + 1) * 2 * sh)
            cos, sin = cos_ref[hm], sin_ref[hm]
            q = rope_forward(y[rows, : 2 * HD], gq_ref[...], cos, sin) * (HD**-0.5)
            raw = y[rows, 2 * HD :]
            k = rope_forward(raw, gk_ref[...], cos, sin)
            stage[m, i, :, : 2 * HD] = q.astype(bf16)
            stage[m, i, :, 2 * HD :] = jnp.where(low, k, raw).astype(bf16)
        send_out(stage, seq_ref, zsems, m)
        return carry

    lax.fori_loop(0, 4, step, 0)
    saves = save_all(osem, (buf, n_out), (raw_ref, raw_out))
    wait_out(stage, seq_ref, zsems)
    relay_sides(sides, 0)
    start_sides(sides, 1)
    for i in range(4):
        for h in range(2):
            kv[i, h] = seq_ref[i, h, :, 2 * HD :]
            a, b = split_heads(seq_ref[i, h, :, : 2 * HD], False)
            q2[i, 0, h], q2[i, 1, h] = a, b
    length = len_ref[0]
    for i in range(4):
        bound = key_bound(i, slots)

        def tile(u, carry, i=i, bound=bound):
            head, h = u // 2, lax.rem(u, 2)
            keys = kv[...].reshape(4 * slots, 2 * HD)[:bound]
            p = probabilities(q2[i, head, h], keys, i * slots + h * 2 * sh, length)
            o[head, h] = dot(p.astype(bf16), keys, 1, 0)
            return carry

        lax.fori_loop(0, 4, tile, 0)
        for h in range(2):
            back[i, h] = jnp.where(low, swap(o[0, h]), o[1, h]).astype(bf16)
        send_back(back, att_ref, zsems, i)
    wait_back(back, att_ref, zsems)
    saves += save_all(osem, (seq_ref, seq_out), (att_ref, att_out), first=2)
    relay_sides(sides, 1)
    start_sides(sides, 2)

    def merge_step(i, carry):
        m = 3 - i
        pm, hm = place(m)
        pl.when(i == 3)(lambda: relay_sides(sides, 2))
        y = flat(att_ref[pm, :, hm])

        def multiply(at):
            part[m, :, :, at] = dot(y, wo_ref[:, at], 1, 0).reshape(part.shape[1], part.shape[2], 256)

        columns(D, multiply)
        across_copy(part, xr, sh, sems, m).start()

        @pl.when(m < 3)
        def _():
            scatter(part, xr, ys, yr, sh, sems, m + 1)

        return carry

    lax.fori_loop(0, 4, merge_step, 0)
    scatter(part, xr, ys, yr, sh, sems, 0)
    out_ref[...] = x_ref[...] + end_scatter(part, xr, ys, yr, sh, sems)
    end_gather(buf, sh, sems)
    end_out(stage, seq_ref, zsems)
    for copy in saves:
        copy.wait()
    finish_sides(sides)


def attention_backward_kernel(sh, sides, grad_ref, x_ref, gain_ref, w_all, cos_ref, sin_ref, gq_ref, gk_ref, len_ref,
                              n_in, raw_in, seq_in, att_in,
                              out_ref, gain_out, head_out, dw_ref,
                              raw_ref, seq_ref, att_ref, buf, nbuf, stage, dseq, q2, do2, kv, dq, dkv, back_q, back_k, dproj_q, dproj_k, gproj,
                              part, xr, ys, yr, sems, zsems, osem):
    c = lax.axis_index("cols")
    slots = 4 * sh
    w_ref, wo_ref = w_all.at[pl.ds(0, 4 * HD)], w_all.at[pl.ds(4 * HD, 2 * HD)]
    tokens = 8 * buf.shape[3]
    loads = save_all(osem, (seq_in, seq_ref), (raw_in, raw_ref), (att_in, att_ref), (n_in, nbuf))
    put_own(buf, sh, grad_ref[...])
    greet()
    start_gather(buf, sh, sems)
    start_sides(sides)
    for copy in loads[:3]:
        copy.wait()
    low = low_lanes(gq_ref[...])
    for i in range(4):
        for h in range(2):
            kv[i, h] = seq_ref[i, h, :, 2 * HD :]
            a, b = split_heads(seq_ref[i, h, :, : 2 * HD], False)
            q2[i, 0, h], q2[i, 1, h] = a, b
    dkv[...] = jnp.zeros_like(dkv)
    head_out[...] = jnp.zeros_like(head_out)

    def step(m, carry):
        arrive(buf, sh, sems, m)
        pm, hm = place(m)
        y = dot(flat(buf[pm, :, hm]), wo_ref[...], 1, 1).astype(bf16)
        stage[m] = y.reshape(stage.shape[1], 2 * sh, 2 * HD)
        send_out(stage, dseq, zsems, m)
        return carry

    lax.fori_loop(0, 4, step, 0)
    wait_out(stage, dseq, zsems)
    relay_sides(sides, 0)
    start_sides(sides, 1)
    length = len_ref[0]
    for i in range(4):
        for h in range(2):
            a, b = split_heads(dseq[i, h], True)
            do2[i, 0, h], do2[i, 1, h] = a, b
    for i in range(4):
        bound = key_bound(i, slots)

        def tile(u, carry, i=i, bound=bound):
            head, h = u // 2, lax.rem(u, 2)
            keys = kv[...].reshape(4 * slots, 2 * HD)[:bound]
            q, do = q2[i, head, h], do2[i, head, h]
            p = probabilities(q, keys, i * slots + h * 2 * sh, length)
            dp = dot(do, keys, 1, 1)
            ds = (p * (dp - jnp.sum(p * dp, axis=1, keepdims=True))).astype(bf16)
            dq[head, h] = dot(ds, keys, 1, 0) * (HD**-0.5)
            dkv[:, :bound] += dot(q, ds, 0, 0) + dot(do, p.astype(bf16), 0, 0)
            return carry

        lax.fori_loop(0, 4, tile, 0)
        for h in range(2):
            back_q[i, h] = jnp.where(low, dq[0, h], swap(dq[1, h])).astype(bf16)
        send_back(back_q, dproj_q, zsems, i)
    grads = dkv[...].T.reshape(4, 2, 2 * sh, 2 * HD)
    for i in range(4):
        back_k[i] = grads[i].astype(bf16)
        send_back(back_k, dproj_k, zsems, i, 4)
    wait_back(back_q, dproj_q, zsems)
    wait_back(back_k, dproj_k, zsems, 4)
    relay_sides(sides, 1)
    start_sides(sides, 2)

    def merge_step(t, carry):
        m = 3 - t
        pm, hm = place(m)
        pl.when(t == 3)(lambda: relay_sides(sides, 2))
        for i in range(stage.shape[1]):
            cos, sin = cos_ref[hm], sin_ref[hm]
            g_q, g_k = dproj_q[pm, i, hm].astype(f32), dproj_k[pm, i, hm].astype(f32)
            raw = raw_ref[pm, i, hm]
            a, ga = rope_backward(raw[:, : 2 * HD], gq_ref[...], cos, sin, g_q)
            b, gb = rope_backward(raw[:, 2 * HD :], gk_ref[...], cos, sin, g_k)
            gproj[pm, i, hm, :, : 2 * HD] = a.astype(bf16)
            gproj[pm, i, hm, :, 2 * HD :] = jnp.where(low, b, g_k).astype(bf16)
            head_out[0:1] += ga
            head_out[1:2] += gb
        y = flat(gproj[pm, :, hm])

        def multiply(at):
            part[m, :, :, at] = dot(y, w_ref[:, at], 1, 0).reshape(part.shape[1], part.shape[2], 256)

        columns(D, multiply)
        across_copy(part, xr, sh, sems, m).start()

        @pl.when(m < 3)
        def _():
            scatter(part, xr, ys, yr, sh, sems, m + 1)

        return carry

    lax.fori_loop(0, 4, merge_step, 0)
    scatter(part, xr, ys, yr, sh, sems, 0)
    loads[3].wait()
    left = gproj[...].reshape(tokens, 4 * HD)
    dw_ref[: 4 * HD] = dot(left, nbuf[...].reshape(tokens, D), 0, 0).astype(bf16)
    left = att_ref[...].reshape(tokens, 2 * HD)
    dw_ref[4 * HD :] = dot(left, buf[...].reshape(tokens, D), 0, 0).astype(bf16)
    n = end_scatter(part, xr, ys, yr, sh, sems)
    norm_back(n, x_ref, gain_ref, grad_ref, out_ref, gain_out)
    end_gather(buf, sh, sems)
    end_out(stage, dseq, zsems)
    finish_sides(sides)


SMEM = pl.BlockSpec(memory_space=pltpu.SMEM)


def attention_forward(cid, x, gain, w, tables, length, sides=()):
    seqs, sh, _ = x.shape
    full = (2, seqs, 2, 2 * sh)
    zshape = (4, 2, 2 * sh)
    return call(
        functools.partial(attention_forward_kernel, sh), "attention_forward", cid,
        (shape(x.shape, f32), shape(full + (D,), bf16), shape(full + (4 * HD,), f32),
         shape(zshape + (4 * HD,), bf16), shape(full + (2 * HD,), bf16)),
        (VMEM, ANY, ANY, ANY, ANY), (VMEM,) * 7 + (SMEM,),
        [
            pltpu.VMEM(full + (4 * HD,), f32), pltpu.VMEM(zshape + (4 * HD,), bf16), pltpu.VMEM(full + (2 * HD,), bf16),
            pltpu.VMEM(full + (D,), bf16), pltpu.VMEM((4, seqs, 2 * sh, 4 * HD), bf16),
            pltpu.VMEM((4, 2, 2, 2 * sh, 2 * HD), bf16), pltpu.VMEM(zshape + (2 * HD,), bf16),
            pltpu.VMEM((2, 2, 2 * sh, 2 * HD), f32), pltpu.VMEM(zshape + (2 * HD,), bf16),
        ] + scatter_scratch(seqs, sh) + [DMA((12, 4)), DMA((4, 8)), DMA((4,))],
        (x, gain, w) + tables + (length,), sides=sides,
    )


def attention_backward(cid, grad, x, gain, w, tables, length, n, raw, seq, att, sides=()):
    seqs, sh, _ = x.shape
    full = (2, seqs, 2, 2 * sh)
    zshape = (4, 2, 2 * sh)
    return call(
        functools.partial(attention_backward_kernel, sh), "attention_backward", cid,
        (shape(x.shape, f32), shape((1, D), f32), shape((2, 2 * HD), f32), shape((6 * HD, D), bf16)),
        (VMEM,) * 4, (VMEM,) * 8 + (SMEM, ANY, ANY, ANY, ANY),
        [
            pltpu.VMEM(full + (4 * HD,), f32), pltpu.VMEM(zshape + (4 * HD,), bf16), pltpu.VMEM(full + (2 * HD,), bf16),
            pltpu.VMEM(full + (D,), bf16), pltpu.VMEM(full + (D,), bf16),
            pltpu.VMEM((4, seqs, 2 * sh, 2 * HD), bf16), pltpu.VMEM(zshape + (2 * HD,), bf16),
            pltpu.VMEM((4, 2, 2, 2 * sh, 2 * HD), bf16), pltpu.VMEM((4, 2, 2, 2 * sh, 2 * HD), bf16),
            pltpu.VMEM(zshape + (2 * HD,), bf16), pltpu.VMEM((2, 2, 2 * sh, 2 * HD), f32),
            pltpu.VMEM((2 * HD, 16 * sh), f32), pltpu.VMEM(zshape + (2 * HD,), bf16), pltpu.VMEM(zshape + (2 * HD,), bf16),
            pltpu.VMEM(full + (2 * HD,), bf16), pltpu.VMEM(full + (2 * HD,), bf16), pltpu.VMEM(full + (4 * HD,), bf16),
        ] + scatter_scratch(seqs, sh) + [DMA((12, 4)), DMA((6, 8)), DMA((4,))],
        (grad, x, gain, w) + tables + (length, n, raw, seq, att), sides=sides,
    )


def edge_send(buf, edge, sh, sems, way, p, i):
    d, c = lax.axis_index("dp"), lax.axis_index("cols")
    pm, hm = place(0)
    at = share(sh, True).start + (sh - 16 if way == 0 else 0)
    to = {"dp": d - lax.rem(d, 2) + p, "rows": i, "cols": c + 1 if way == 0 else c - 1}
    return remote(
        buf.at[pm, :, hm, pl.ds(pl.multiple_of(at, 16), 16)], edge.at[way, pm],
        sems.at[0, way * 8 + p * 4 + i], sems.at[1, way * 8 + pm], to,
    )


def edge_senders(way):
    r, c = lax.axis_index("rows"), lax.axis_index("cols")
    rows, cols = lax.axis_size("rows"), lax.axis_size("cols")
    return (r == rows - 1) & (c < cols - 1) if way == 0 else (r == 0) & (c > 0)


def edges_each(buf, edge, sh, sems, way, act):
    @pl.when(edge_senders(way))
    def _():
        for p in range(2):
            for i in range(4):
                act(edge_send(buf, edge, sh, sems, way, p, i))


def wait_edges(edge, sems, way):
    c = lax.axis_index("cols")
    gets = c > 0 if way == 0 else c < lax.axis_size("cols") - 1

    @pl.when(gets)
    def _():
        for p in range(2):
            part = edge.at[way, p]
            remote(part, part, sems.at[0, way * 8 + p], sems.at[1, way * 8 + p], sibling()).wait_recv()

    @pl.when(jnp.logical_not(gets))
    def _():
        edge[way] = jnp.zeros(edge.shape[1:], bf16)


def window(ref, s, hm, rows):
    return ref[s, pl.ds(pl.multiple_of(hm * rows, 8), rows + 8)]


def convolve(taps, ext, rows):
    return sum(taps[k : k + 1] * ext[8 - (CONV - 1) + k : 8 - (CONV - 1) + k + rows] for k in range(CONV))


def conv_forward_kernel(sh, sides, x_ref, gain_ref, w_in, taps_ref,
                        out_ref, n_out, mixed_out, prod_out, gate_out,
                        wall, wsem, mixed_ref, prod_ref, gate_ref, buf, cmix, edge, part, xr, ys, yr, sems, zsems, osem):
    seqs, rows = buf.shape[1], 2 * sh
    ch = wall.shape[0] // 4
    chan = ch // w_in.shape[0]
    wloads = [
        pltpu.make_async_copy(
            w_in.at[c, pl.ds(g * chan, chan)], wall.at[pl.ds(g * ch + c * chan, chan)], wsem.at[4 * c + g]
        )
        for c in range(w_in.shape[0])
        for g in range(4)
    ]
    for copy in wloads:
        copy.start()
    w_ref, wo_ref = wall.at[pl.ds(0, 3 * ch)], wall.at[pl.ds(3 * ch, ch)]
    slots = 2 * rows
    put_own(buf, sh, norm_own(x_ref, gain_ref))
    greet_box(2)
    for way in (0, 1):
        edges_each(buf, edge, sh, zsems, way, lambda copy: copy.start())
    start_gather(buf, sh, sems)
    start_sides(sides)
    for copy in wloads:
        copy.wait()

    def step(m, carry):
        arrive(buf, sh, sems, m)
        pm, hm = place(m)
        y = dot(flat(buf[pm, :, hm]), w_ref[...], 1, 1)
        mixed_ref[pm, :, hm] = y.reshape(seqs, rows, 3 * ch)
        for i in range(seqs):
            z = y[i * rows : (i + 1) * rows]
            at = pl.ds(pl.multiple_of(8 + hm * rows, 8), rows)
            prod_ref[pm * seqs + i, at] = z[:, :ch] * z[:, 2 * ch :]
        return carry

    lax.fori_loop(0, 4, step, 0)
    saves = save_all(osem, (buf, n_out), (mixed_ref, mixed_out))
    for way in (0, 1):
        wait_edges(edge, zsems, way)
    y = dot(edge[...].reshape(4 * seqs * 16, D), w_ref[...], 1, 1).reshape(2, 2 * seqs, 16, 3 * ch)
    prod_ref[:, :8] = y[0, :, 8:, :ch] * y[0, :, 8:, 2 * ch :]
    gate_ref[...] = y[1, :, :8, ch : 2 * ch]
    saves += save_all(osem, (prod_ref, prod_out), (gate_ref, gate_out), first=2)
    taps = taps_ref[...]

    def merge_step(t, carry):
        m = 3 - t
        pm, hm = place(m)
        for i in range(seqs):
            conv = convolve(taps, window(prod_ref, pm * seqs + i, hm, rows), rows)
            cmix[i] = (mixed_ref[pm, i, hm, :, ch : 2 * ch] * conv).astype(bf16)
        y = flat(cmix[...])

        def multiply(at):
            part[m, :, :, at] = dot(y, wo_ref[:, at], 1, 0).reshape(seqs, rows, 256)

        columns(D, multiply)
        across_copy(part, xr, sh, sems, m).start()

        @pl.when(m < 3)
        def _():
            scatter(part, xr, ys, yr, sh, sems, m + 1)

        return carry

    lax.fori_loop(0, 4, merge_step, 0)
    scatter(part, xr, ys, yr, sh, sems, 0)
    out_ref[...] = x_ref[...] + end_scatter(part, xr, ys, yr, sh, sems)
    end_gather(buf, sh, sems)
    for way in (0, 1):
        edges_each(buf, edge, sh, zsems, way, lambda copy: copy.wait_send())
    for copy in saves:
        copy.wait()
    finish_sides(sides)


def conv_backward_kernel(sh, sides, grad_ref, x_ref, gain_ref, w_in, taps_ref, n_in, mixed_in, prod_in, gate_in,
                         out_ref, gain_out, taps_out, dw_ref,
                         wall, wsem, mixed_ref, prod_ref, gate_ref, buf, nbuf, gext, gmix, gin, cmix, edge, part, xr, ys, yr, sems, zsems, osem):
    seqs, rows = buf.shape[1], 2 * sh
    ch = wall.shape[0] // 4
    chan = ch // w_in.shape[0]
    wloads = [
        pltpu.make_async_copy(
            w_in.at[c, pl.ds(g * chan, chan)], wall.at[pl.ds(g * ch + c * chan, chan)], wsem.at[4 * c + g]
        )
        for c in range(w_in.shape[0])
        for g in range(4)
    ]
    for copy in wloads:
        copy.start()
    w_ref, wo_ref = wall.at[pl.ds(0, 3 * ch)], wall.at[pl.ds(3 * ch, ch)]
    slots = 2 * rows
    tokens = 8 * rows
    loads = save_all(osem, (mixed_in, mixed_ref), (prod_in, prod_ref), (gate_in, gate_ref), (n_in, nbuf))
    put_own(buf, sh, grad_ref[...])
    greet_box(2)
    edges_each(buf, edge, sh, zsems, 1, lambda copy: copy.start())
    start_gather(buf, sh, sems)
    start_sides(sides)
    taps_out[...] = jnp.zeros_like(taps_out)
    for copy in loads[:3] + wloads:
        copy.wait()

    def step(m, carry):
        arrive(buf, sh, sems, m)
        pm, hm = place(m)
        y = dot(flat(buf[pm, :, hm]), wo_ref[...], 1, 1)
        for i in range(seqs):
            z = y[i * rows : (i + 1) * rows]
            gmix[pm, i, hm] = z
            at = pl.ds(pl.multiple_of(hm * rows, 8), rows)
            gext[pm * seqs + i, at] = z * mixed_ref[pm, i, hm, :, ch : 2 * ch]
        return carry

    lax.fori_loop(0, 4, step, 0)
    wait_edges(edge, zsems, 1)
    y = dot(edge[1].reshape(2 * seqs * 16, D), wo_ref[...], 1, 1).reshape(2 * seqs, 16, ch)
    gext[:, slots:] = y[:, :8] * gate_ref[...]
    taps = taps_ref[...]

    def merge_step(t, carry):
        m = 3 - t
        pm, hm = place(m)
        pl.when(t == 1)(lambda: relay_sides(sides))
        for i in range(seqs):
            ext = window(prod_ref, pm * seqs + i, hm, rows)
            conv = convolve(taps, ext, rows)
            g = window(gext, pm * seqs + i, hm, rows)
            gprod = sum(taps[k : k + 1] * g[CONV - 1 - k : CONV - 1 - k + rows] for k in range(CONV))
            for k in range(CONV):
                shifted = ext[8 - (CONV - 1) + k : 8 - (CONV - 1) + k + rows]
                taps_out[k : k + 1] += jnp.sum(g[:rows] * shifted, axis=0, keepdims=True)
            mix = mixed_ref[pm, i, hm]
            gin[pm, i, hm, :, :ch] = (gprod * mix[:, 2 * ch :]).astype(bf16)
            gin[pm, i, hm, :, ch : 2 * ch] = (gmix[pm, i, hm] * conv).astype(bf16)
            gin[pm, i, hm, :, 2 * ch :] = (gprod * mix[:, :ch]).astype(bf16)
            cmix[pm, i, hm] = (mix[:, ch : 2 * ch] * conv).astype(bf16)
        y = flat(gin[pm, :, hm])

        def multiply(at):
            part[m, :, :, at] = dot(y, w_ref[:, at], 1, 0).reshape(seqs, rows, 256)

        columns(D, multiply)
        across_copy(part, xr, sh, sems, m).start()

        @pl.when(m < 3)
        def _():
            scatter(part, xr, ys, yr, sh, sems, m + 1)

        return carry

    lax.fori_loop(0, 4, merge_step, 0)
    scatter(part, xr, ys, yr, sh, sems, 0)
    loads[3].wait()
    left = gin[...].reshape(tokens, 3 * ch)
    dw_ref[: 3 * ch] = dot(left, nbuf[...].reshape(tokens, D), 0, 0).astype(bf16)
    left = cmix[...].reshape(tokens, ch)
    dw_ref[3 * ch :] = dot(left, buf[...].reshape(tokens, D), 0, 0).astype(bf16)
    n = end_scatter(part, xr, ys, yr, sh, sems)
    norm_back(n, x_ref, gain_ref, grad_ref, out_ref, gain_out)
    end_gather(buf, sh, sems)
    edges_each(buf, edge, sh, zsems, 1, lambda copy: copy.wait_send())
    finish_sides(sides)


def conv_forward(cid, x, gain, w, taps, sides=()):
    seqs, sh, _ = x.shape
    full = (2, seqs, 2, 2 * sh)
    ch = w.shape[0] * w.shape[1] // 4
    own = [pltpu.VMEM((4 * ch, D), bf16), DMA((4 * w.shape[0],))]
    return call(
        functools.partial(conv_forward_kernel, sh), "conv_forward", cid,
        (shape(x.shape, f32), shape(full + (D,), bf16), shape(full + (3 * ch,), f32),
         shape((2 * seqs, 4 * sh + 8, ch), f32), shape((2 * seqs, 8, ch), f32)),
        (VMEM, ANY, ANY, ANY, ANY), (VMEM, VMEM, ANY, VMEM),
        own + [pltpu.VMEM(full + (3 * ch,), f32), pltpu.VMEM((2 * seqs, 4 * sh + 8, ch), f32),
         pltpu.VMEM((2 * seqs, 8, ch), f32),
         pltpu.VMEM(full + (D,), bf16), pltpu.VMEM((seqs, 2 * sh, ch), bf16), pltpu.VMEM((2, 2, seqs, 16, D), bf16)]
        + scatter_scratch(seqs, sh) + [DMA((12, 4)), DMA((2, 16)), DMA((4,))],
        (x, gain, w, taps), sides=sides,
    )


def conv_backward(cid, grad, x, gain, w, taps, n, mixed, prod, gate, sides=()):
    seqs, sh, _ = x.shape
    full = (2, seqs, 2, 2 * sh)
    ch = w.shape[0] * w.shape[1] // 4
    own = [pltpu.VMEM((4 * ch, D), bf16), DMA((4 * w.shape[0],))]
    return call(
        functools.partial(conv_backward_kernel, sh), "conv_backward", cid,
        (shape(x.shape, f32), shape((1, D), f32), shape((CONV, ch), f32), shape((4 * ch, D), bf16)),
        (VMEM,) * 4, (VMEM, VMEM, VMEM, ANY, VMEM) + (ANY,) * 4,
        own + [
            pltpu.VMEM(full + (3 * ch,), f32), pltpu.VMEM((2 * seqs, 4 * sh + 8, ch), f32),
            pltpu.VMEM((2 * seqs, 8, ch), f32),
            pltpu.VMEM(full + (D,), bf16), pltpu.VMEM(full + (D,), bf16),
            pltpu.VMEM((2 * seqs, 4 * sh + 8, ch), f32), pltpu.VMEM(full + (ch,), f32),
            pltpu.VMEM(full + (3 * ch,), bf16), pltpu.VMEM(full + (ch,), bf16), pltpu.VMEM((2, 2, seqs, 16, D), bf16),
        ] + scatter_scratch(seqs, sh) + [DMA((12, 4)), DMA((2, 16)), DMA((4,))],
        (grad, x, gain, w, taps, n, mixed, prod, gate), sides=sides,
    )


def band(ref, i, width):
    return ref.at[..., pl.ds(pl.multiple_of(i * width, 128), width)]


def row_pieces(kind, src, dst, here, there):
    rows = lax.axis_size("rows")
    if kind == "weights":
        return src.at[there], band(dst, here, src.shape[2])
    if kind == "tokens":
        sh = src.shape[1] // rows
        return src.at[:, pl.ds(pl.multiple_of(there * sh, 8), sh)], band(dst, here, src.shape[2])
    if kind == "gains":
        return src, band(dst, here, src.shape[1])
    sh = src.shape[1]
    return band(src, there, dst.shape[2]), dst.at[:, pl.ds(pl.multiple_of(here * sh, 8), sh)]


def row_copies(kind, src, dst, sems, i):
    rows = lax.axis_size("rows")
    r = lax.axis_index("rows")
    sends, gets = [], []
    for k in range(1, rows):
        to, come = lax.rem(r + k, rows), lax.rem(r + rows - k, rows)
        a, b = row_pieces(kind, src, dst, r, to)
        sends.append(remote(a, b, sems.at[0, i, k], sems.at[1, i, k], {"rows": to}))
        a, b = row_pieces(kind, src, dst, come, r)
        gets.append(remote(a, b, sems.at[0, i, k], sems.at[1, i, k], {"rows": to}))
    a, b = row_pieces(kind, src, dst, r, r)
    return sends, gets, pltpu.make_async_copy(a, b, sems.at[0, i, 0])


def line_copies(axis, src, dst, sems, i):
    count = lax.axis_size(axis) if axis == "cols" else 2
    at = lax.axis_index(axis)
    low = lax.rem(at, count)
    base = at - low
    sends, gets = [], []
    for k in range(1, count):
        to, come = lax.rem(low + k, count), lax.rem(low + count - k, count)
        sends.append(remote(src, dst.at[low], sems.at[0, i, k], sems.at[1, i, k], {axis: base + to}))
        gets.append(remote(src, dst.at[come], sems.at[0, i, k], sems.at[1, i, k], {axis: base + to}))
    return sends, gets, pltpu.make_async_copy(src, dst.at[low], sems.at[0, i, 0])


def greet_box(pairs):
    barrier = pltpu.get_barrier_semaphore()
    rows, cols = lax.axis_size("rows"), lax.axis_size("cols")
    d, r, c = lax.axis_index("dp"), lax.axis_index("rows"), lax.axis_index("cols")
    for p in range(pairs):
        for i in range(rows):
            for j in range(cols):
                if p + i + j > 0:
                    to = {"dp": d if p == 0 else d + 1 - 2 * lax.rem(d, 2),
                          "rows": lax.rem(r + i, rows), "cols": lax.rem(c + j, cols)}
                    pl.semaphore_signal(barrier, inc=1, device_id=to, device_id_type=MESH)
    pl.semaphore_wait(barrier, pairs * rows * cols - 1)


def attention_spread(src, dst, sems):
    halves, cols, _, width = src.shape
    rows = lax.axis_size("rows")
    r, c = lax.axis_index("rows"), lax.axis_index("cols")
    pair = lax.rem(lax.axis_index("dp"), 2)
    holds = pair == halves * c // rows
    first = lax.rem(halves * c, rows)
    origin = (pair * rows + r) // halves

    def to_all(act, local):
        for h in range(halves):
            for z in range(cols):
                own = (first + h == r) & (z == c)
                here = band(dst, r, width)

                @pl.when(holds & jnp.logical_not(own))
                def _():
                    act(remote(src.at[h, z], here, sems.at[0, h * cols + z], sems.at[1, r],
                               {"rows": first + h, "cols": z}))

                @pl.when(holds & own)
                def _():
                    local(pltpu.make_async_copy(src.at[h, z], here, sems.at[0, h * cols + z]))

    def start():
        to_all(lambda copy: copy.start(), lambda copy: copy.start())

    def end():
        for k in range(rows):
            @pl.when(jnp.logical_not((origin == c) & (k == r)))
            def _():
                got = band(dst, k, width)
                remote(got, got, sems.at[0, 0], sems.at[1, k], {"rows": k, "cols": origin}).wait_recv()
        to_all(lambda copy: copy.wait_send(), lambda copy: copy.wait())

    return start, end


def start_kernel(sides, conv_ref, tok_ref, ffn_ref, gain_ref, tap_ref, len_ref,
                 conv_out, tok_out, ffn_out, gain_out, tap_out, len_out, conv_cut, rsems, lsems, zsems):
    barrier = pltpu.get_barrier_semaphore()
    rows, cols = lax.axis_size("rows"), lax.axis_size("cols")
    d, r, c = lax.axis_index("dp"), lax.axis_index("rows"), lax.axis_index("cols")
    to = [{"rows": lax.rem(r + k, rows)} for k in range(1, rows)]
    to += [{"cols": lax.rem(c + k, cols)} for k in range(1, cols)]
    to += [{"dp": d + 1 - 2 * lax.rem(d, 2)}]
    for device in to:
        pl.semaphore_signal(barrier, inc=1, device_id=device, device_id_type=MESH)
    pl.semaphore_wait(barrier, len(to))
    conv = row_copies("weights", conv_ref, conv_cut, rsems, 0)
    small = [
        row_copies("gains", gain_ref, gain_out, rsems, 1),
        line_copies("cols", tap_ref, tap_out, lsems, 0),
        line_copies("dp", len_ref, len_out, lsems, 1),
    ]
    begin_all(conv)
    for work in small:
        begin_all(work)
    tok = row_copies("tokens", tok_ref, tok_out, rsems, 2)
    begin_all(tok)
    end_all(conv)
    conv = Gather.of(conv_cut, lambda z: conv_out.at[z], zsems)
    conv.start()
    ffn = row_copies("weights", ffn_ref, ffn_out, rsems, 3)
    begin_all(ffn)
    for work in small + [tok]:
        end_all(work)
    conv.relay()
    end_all(ffn)
    conv.finish()


def second_kernel(sides, attn_ref, ffn_ref, attn_out, ffn_out, asems, rsems):
    greet_box(1)
    begin, end = attention_spread(attn_ref, attn_out, asems)
    start_sides(sides)
    begin()
    ffn = row_copies("weights", ffn_ref, ffn_out, rsems, 0)
    begin_all(ffn)
    end()
    end_all(ffn)
    finish_sides(sides)


def start_exchange(cid, conv, tok, ffn, gain, tap, length, rows, cols):
    outs = (
        shape((cols, conv.shape[1], D), bf16), shape((tok.shape[0], tok.shape[1] // rows, D), f32),
        shape((ffn.shape[1], D), bf16), shape((8, D), f32), shape((cols,) + tap.shape, f32),
        shape((2,) + length.shape, length.dtype),
    )
    return call(
        start_kernel, "start", cid, outs, (ANY,) * 6, (ANY,) * 6,
        [pltpu.VMEM((conv.shape[1], D), bf16), DMA((2, 4, 4)), DMA((2, 2, 4)), DMA((2, 5))],
        (conv, tok, ffn, gain, tap, length),
    )


def second_exchange(cid, attn, ffn, sides):
    return call(
        second_kernel, "second", cid,
        (shape((attn.shape[2], D), bf16), shape((ffn.shape[1], D), bf16)), (ANY,) * 2, (ANY,) * 2,
        [DMA((2, 8)), DMA((2, 1, 4))], (attn, ffn), sides=sides,
    )


def plane_peer(j):
    pm, hm = place(j // 2)
    d, r = lax.axis_index("dp"), lax.axis_index("rows")
    row = hm * 2 + lax.rem(lax.rem(r, 2) + j % 2, 2)
    return pm, row, {"dp": d - lax.rem(d, 2) + pm, "rows": row}


class Plane:
    def __init__(self, src, dst, lo, w, sems):
        rows = lax.axis_size("rows")
        d, r = lax.axis_index("dp"), lax.axis_index("rows")
        pair = lax.rem(d, 2)
        n, width = src.shape[0], dst.shape[2]
        other = {"dp": d + 1 - 2 * pair}
        self.steps, self.gets = [], []
        for i, (g, at, here, n) in enumerate(segments(lo, src.shape[0], w)):

            def block(p, row, g=g, at=at, n=n):
                return dst.at[g, pl.ds(pl.multiple_of((p * rows + row) * w + at, 16), n)]

            def piece(row, here=here, n=n):
                return band(src.at[pl.ds(here, n)], row, width)

            sem = sems.at[i]
            local = pltpu.make_async_copy(piece(r), block(pair, r), sem.at[0, 0])
            sends = [local]
            turns = [(local, True, remote(block(pair, r), block(pair, r), sem.at[2, 0], sem.at[3, 0], other))]
            self.gets.append(
                remote(block(1 - pair, r), block(1 - pair, r), sem.at[2, 0], sem.at[3, 0], other)
            )
            for k in range(1, rows):
                to, come = lax.rem(r + k, rows), lax.rem(r + rows - k, rows)
                send = remote(piece(to), block(pair, r), sem.at[0, k], sem.at[1, k], {"rows": to})
                get = remote(piece(to), block(pair, come), sem.at[0, k], sem.at[1, k], {"rows": to})
                on = remote(block(pair, come), block(pair, come), sem.at[2, k], sem.at[3, k], other)
                sends.append(send)
                turns.append((get, False, on))
                self.gets.append(
                    remote(block(1 - pair, come), block(1 - pair, come), sem.at[2, k], sem.at[3, k], other)
                )
            self.steps.append((sends, turns))

    def start(self):
        for sends, _ in self.steps:
            for copy in sends:
                copy.start()

    def turn(self):
        for _, turns in self.steps:
            for get, local, on in turns:
                if local:
                    get.wait()
                else:
                    get.wait_recv()
                on.start()

    def finish(self):
        for copy in self.gets:
            copy.wait_recv()
        for sends, turns in self.steps:
            for copy in sends[1:]:
                copy.wait_send()
            for _, _, on in turns:
                on.wait_send()


def finish_kernel(wide, chan, los, chunks, sides, *refs):
    count = len(los)
    arrays, refs = refs[:count], refs[count:]
    ffn_ref, conv_ref, small_ref, tok_ref, o2_ref, o1_ref, oc_ref, os_ref, ot_ref = refs[:9]
    srecv, ssum, precv, psems, rsems, ssems = refs[9:15]
    scratch = refs[15:]
    rows = lax.axis_size("rows")
    me = lax.rem(lax.axis_index("dp"), 2) * rows + lax.axis_index("rows")
    greet_box(2)
    small = line_copies("cols", small_ref, srecv, ssems, 0)
    begin_all(small)
    start_sides(sides)
    work = [(conv_ref, oc_ref, 0, chan)]
    work += [(ffn_ref.at[:, pl.ds(lo, n)], o1_ref, lo, wide) for lo, n in chunks]
    sums = []
    for i, (src, out, lo, w) in enumerate(work):
        own = scratch[5 * i : 5 * i + 5]
        sums.append(Reduce.of(src, own[0], own[1:]))
    for one in sums:
        one.start_far()
    for one in sums:
        one.start_near()
    outs = (o2_ref, o1_ref)
    planes = [Plane(a, outs[o], lo, wide, psems.at[i]) for i, (a, (o, lo)) in enumerate(zip(arrays, los))]
    for plane in planes:
        plane.start()
    tok = row_copies("back", tok_ref, ot_ref, rsems, 0)
    begin_all(tok)
    for plane in planes:
        plane.turn()
    end_all(small)
    ssum[...] = jnp.sum(srecv[...], axis=0)
    precv[me] = ssum[...]
    for j in range(1, 8):
        to = plane_peer(j)[2]
        remote(ssum, precv.at[me], ssems.at[2, 0, j], ssems.at[3, 0, j], to).start()
    last = []
    for i, (src, out, lo, w) in enumerate(work):
        if i == 0:
            for one in sums:
                one.relay()
        sums[i].finish()
        if last:
            last[-1].turn()
        last.append(Plane(sums[i].out, out, lo, w, psems.at[count + i]))
        last[-1].start()
    last[-1].turn()
    for j in range(1, 8):
        pm, row, to = plane_peer(j)
        copy = remote(ssum, precv.at[pm * rows + row], ssems.at[2, 0, j], ssems.at[3, 0, j], to)
        copy.wait_recv()
        copy.wait_send()
    os_ref[...] = jnp.sum(precv[...], axis=0)
    end_all(tok)
    for plane in planes + last:
        plane.finish()
    finish_sides(sides)


def finish_exchange(cid, arrays, los, ffn, chunks, conv, small, tok, wide, chan, rows, sides):
    feat = D // rows
    cols, nc, _ = conv.shape
    outs = (
        shape((3, 8 * wide, feat), bf16), shape((3, 8 * wide, feat), bf16),
        shape((nc // chan, 8 * chan, feat), bf16), shape(small.shape, f32), shape((tok.shape[0], tok.shape[1] * rows, feat), f32),
    )
    scratch = [
        pltpu.VMEM((cols,) + small.shape, f32), pltpu.VMEM(small.shape, f32), pltpu.VMEM((8,) + small.shape, f32),
        DMA((len(arrays) + len(chunks) + 1, 4, 4, 4)), DMA((2, 1, 4)), DMA((4, 1, 8)),
    ]
    for n in [nc] + [n for _, n in chunks]:
        scratch += [pltpu.VMEM((n, D), bf16)] + Reduce.buffers(n)
    return call(
        functools.partial(finish_kernel, wide, chan, los, chunks), "finish", cid, outs,
        (ANY,) * 3 + (VMEM, ANY), (ANY,) * (len(arrays) + 2) + (VMEM, ANY), scratch,
        tuple(arrays) + (ffn, conv, small, tok), sides=sides,
    )


def turn_kernel(x_ref, in_ref, out_ref):
    for a in range(0, x_ref.shape[1], 128):
        at = slice(a, a + 128)
        for g in range(2):
            in_ref[:, g, at] = x_ref[g, at].astype(f32).T
        out_ref[at] = x_ref[2, at].astype(f32)


def turn(x):
    _, n, feat = x.shape
    return pl.pallas_call(
        turn_kernel, name="turn", out_shape=(shape((feat, 2, n), f32), shape((n, feat), f32)),
        in_specs=[VMEM], out_specs=(VMEM, VMEM),
        compiler_params=pltpu.CompilerParams(vmem_limit_bytes=LIMIT << 20),
    )(x)


def per_device(
    hidden_in, lengths, conv_norm, conv_in, conv_kernel, conv_out, conv_ffn_norm, conv_ffn_in,
    conv_ffn_out, attn_norm, attn_q, attn_kv, q_gain, k_gain, attn_out, attn_ffn_norm,
    attn_ffn_in, attn_ffn_out, grad_out,
):
    rows, cols, dps = lax.axis_size("rows"), lax.axis_size("cols"), lax.axis_size("dp")
    tp = 2 * rows
    r, c, d = lax.axis_index("rows"), lax.axis_index("cols"), lax.axis_index("dp")
    pair = lax.rem(d, 2)
    me = pair * rows + r
    slots, seqs, feat = hidden_in.shape
    sh = slots // rows

    def halves(x, axis):
        return lax.dynamic_slice_in_dim(x, pair * rows, rows, axis)

    def cut_in(w):
        parts, width = w.shape[1], w.shape[2] // tp
        x = w.astype(bf16).transpose(1, 2, 0).reshape(parts, tp, width, feat)
        return halves(x, 1).transpose(1, 0, 2, 3).reshape(rows, parts * width, feat)

    def cut_out(w):
        return halves(w.astype(bf16).reshape(tp, -1, feat), 0)

    def cut(w_in, w_out):
        return jnp.concatenate([cut_in(w_in), cut_out(w_out)], axis=1)

    wide = conv_ffn_in.shape[2] // tp
    chan = conv_in.shape[2] // tp
    channels = cols * chan
    slot_ids = c * slots + jnp.arange(slots, dtype=jnp.int32)
    keep = (slot_ids[None, :] < lengths[:, None]).astype(f32)[:, :, None]
    gains_own = jnp.stack([conv_norm, conv_ffn_norm, attn_norm, attn_ffn_norm])
    conv_all, begin, ffn1_cut, gains, taps, lens = start_exchange(
        1, cut(conv_in, conv_out), hidden_in.transpose(1, 0, 2) * keep, cut(conv_ffn_in, conv_ffn_out),
        jnp.pad(gains_own, ((0, 4), (0, 0))), jnp.pad(conv_kernel, ((0, 8 - CONV), (0, 0))),
        jnp.pad(lengths[None], ((0, 7), (0, 128 - seqs))), rows, cols,
    )
    gains = gains[:4, None]
    kern = lax.dynamic_slice_in_dim(taps[:, :CONV], me * chan, chan, 2)
    kern = kern.transpose(1, 0, 2).reshape(CONV, channels)
    length = lax.dynamic_slice_in_dim(lens[:, 0, :seqs].reshape(2 * seqs), c, 1)

    per_col = tp // cols
    q_w = attn_q.shape[1] // per_col
    kv_w = attn_kv.shape[2] // per_col
    parts = jnp.concatenate(
        [
            attn_q.astype(bf16).T.reshape(per_col, q_w, feat),
            attn_kv[:, 0].astype(bf16).T.reshape(per_col, kv_w, feat),
            attn_kv[:, 1].astype(bf16).T.reshape(per_col, kv_w, feat),
            attn_out.astype(bf16).reshape(per_col, q_w, feat),
        ],
        axis=1,
    )
    w_ffn1 = lax.all_gather(ffn1_cut, "cols", axis=0)

    def after(x, y):
        return lax.optimization_barrier((x, y))[0]

    after_conv, n_conv, mixed, product, gate_edge = conv_forward(3, begin, gains[0], conv_all, kern)
    attn_cut, ffn2_cut = second_exchange(
        2, after(parts, after_conv).reshape(per_col, cols, -1, feat), cut(after(attn_ffn_in, after_conv), after(attn_ffn_out, after_conv)), ()
    )
    f2_rows = SECOND_ROWS
    f2_at = [sum(f2_rows[:i]) for i in range(4)]
    after_ffn, n_1, gu_1, w_1, attn_all, f2_a = ffn_forward(
        4, after_conv, gains[1], (w_ffn1,), wide,
        [Gather(attn_cut, 0, attn_cut.shape[0]), Gather(ffn2_cut, f2_at[0], f2_rows[0])],
    )
    attn_all = attn_all.reshape(-1, D)
    frequency = jnp.power(rope_base, -(jnp.arange(HD // 2, dtype=f32) * 2.0) / HD)
    angles = slot_ids.astype(f32)[:, None] * frequency[None, :]
    cos, sin = jnp.cos(angles), jnp.sin(angles)
    tables = (
        jnp.concatenate([cos] * 4, axis=1).reshape(2, 2 * sh, 2 * HD),
        jnp.concatenate([-sin, sin] * 2, axis=1).reshape(2, 2 * sh, 2 * HD),
        jnp.tile(q_gain, 2)[None],
        jnp.tile(k_gain, 2)[None],
    )
    after_attn, n_attn, raw, seq, attended, grad_final, f2_b, f2_c, f2_d = attention_forward(
        5, after_ffn, gains[2], attn_all, tables, length,
        [
            Rows("tokens", grad_out.transpose(1, 0, 2) * keep, 1),
            Gather(ffn2_cut, f2_at[1], f2_rows[1], 0), Gather(ffn2_cut, f2_at[2], f2_rows[2], 1),
            Gather(ffn2_cut, f2_at[3], f2_rows[3], 2),
        ],
    )
    final, grad_attn_res, gain_p3, dw_2 = ffn_both(
        6, after_attn, gains[3], grad_final, (f2_a, f2_b, f2_c, f2_d), wide, ffn2_cut
    )

    def over_pairs(x):
        return x if dps == 2 else lax.psum(x * jnp.asarray(0.5, x.dtype), "dp")

    def native(x):
        return x[:-1].transpose(2, 0, 1).astype(f32), x[-1].astype(f32)

    b2_rows, b1_rows = SECOND_BACK, FIRST_BACK
    b2_at = [sum(b2_rows[:i]) for i in range(4)]
    grad_after_ffn, gain_p2, head_parts, grad_attn, final_here, r2_a, r2_b, r2_c = attention_backward(
        8, grad_attn_res, after_ffn, gains[2], attn_all, tables, length, n_attn, raw, seq, attended,
        [Rows("back", final, 1), Reduce(dw_2, 0, b2_rows[0], 0),
         Reduce(dw_2, b2_at[1], b2_rows[1], 1), Reduce(dw_2, b2_at[2], b2_rows[2], 2)],
    )
    grad_attn = grad_attn.reshape(cols, -1, D)
    grad_after_conv, gain_p1, dw_1, r_attn, r2_d = ffn_backward(
        9, grad_after_ffn, after_conv, gains[1], w_1, n_1, gu_1, wide, cols,
        [Reduce(grad_attn, 0, grad_attn.shape[1]), Reduce(dw_2, b2_at[3], b2_rows[3])],
    )
    grad_begin, gain_p0, kern_part, grad_conv, back_a, r1_a = conv_backward(
        10, grad_after_conv, begin, gains[0], conv_all, kern, n_conv, mixed, product, gate_edge,
        [Return(r_attn, per_col), Reduce(dw_1, 0, b1_rows[0])],
    )
    output = (final_here * keep).transpose(1, 0, 2)
    grad_cin = grad_conv[: 3 * channels].reshape(3, cols, chan, D).transpose(1, 0, 2, 3)
    packed0 = jnp.concatenate(
        [grad_cin.reshape(cols, 3 * chan, D), grad_conv[3 * channels :].reshape(cols, chan, D)], axis=1
    )
    zero = jnp.zeros((), jnp.int32)
    kern_full = lax.dynamic_update_slice(
        jnp.zeros((CONV, cols, tp, chan), f32),
        kern_part.reshape(CONV, cols, 1, chan),
        (zero, zero, me, zero),
    )
    heads = jnp.stack([head_parts[0, :HD] + head_parts[0, HD:], head_parts[1, :HD]])
    small = jnp.concatenate(
        [gain_p0, gain_p1, gain_p2, gain_p3, kern_full.reshape(CONV, D),
         jnp.pad(heads.reshape(1, -1), ((0, 0), (0, D - 2 * HD)))]
    )
    chunks = [(sum(b1_rows[:i]), n) for i, n in enumerate(b1_rows)][1:]
    got2, got1, got0, sums, grad_here, got_a = finish_exchange(
        11, (r2_a, r2_b, r2_c, r2_d, r1_a), [(0, at) for at in b2_at] + [(1, 0)], dw_1, chunks,
        packed0, small, grad_begin, wide, chan, rows, [PairShare(back_a, per_col)],
    )
    got2, got1, got0, got_a, sums = (over_pairs(x) for x in (got2, got1, got0, got_a, sums))
    got_a = got_a.reshape(per_col, -1, feat)
    g_attn_ffn_in, g_attn_ffn_out = turn(got2)
    g_q = got_a[:, :q_w].astype(f32).reshape(-1, feat).T
    g_kv = jnp.stack(
        [
            got_a[:, q_w : q_w + kv_w].astype(f32).reshape(-1, feat).T,
            got_a[:, q_w + kv_w : q_w + 2 * kv_w].astype(f32).reshape(-1, feat).T,
        ],
        axis=1,
    )
    g_aout = got_a[:, q_w + 2 * kv_w :].astype(f32).reshape(-1, feat)
    grad_in = (grad_here * keep).transpose(1, 0, 2)
    g_conv_ffn_in, g_conv_ffn_out = turn(got1)
    g_conv_in, g_conv_out = native(got0)
    g_gain = lax.dynamic_slice(sums, (zero, r * feat), (4, feat))
    g_kern = lax.dynamic_slice(sums[4 : 4 + CONV], (zero, c * conv_kernel.shape[1]), conv_kernel.shape)
    return (
        output, grad_in, g_gain[0], g_conv_in, g_kern, g_conv_out, g_gain[1],
        g_conv_ffn_in, g_conv_ffn_out, g_gain[2], g_q, g_kv, sums[7, :HD], sums[7, HD : 2 * HD], g_aout,
        g_gain[3], g_attn_ffn_in, g_attn_ffn_out,
    )


def solution(mesh):
    tokens, vec, mat = P("cols", "dp", "rows"), P("rows"), P("rows", "cols")
    mat3, out, taps = P("rows", None, "cols"), P("cols", "rows"), P(None, "cols")
    weights = (vec, mat3, taps, out, vec, mat3, out, vec, mat, mat3, P(), P(), out, vec, mat3, out)
    return jax.shard_map(
        per_device,
        mesh=mesh,
        in_specs=(tokens, P("dp")) + weights + (tokens,),
        out_specs=(tokens, tokens) + weights,
        check_vma=False,
    )
```

```python
import functools

import jax
import jax.numpy as jnp
from jax import lax
from jax.experimental import pallas as pl
from jax.experimental.pallas import tpu as pltpu
from jax.sharding import PartitionSpec as P

D = 1024
HD = 64
CONV = 3
epsilon = 1e-05
rope_base = 1000000.0
bf16 = jnp.bfloat16
f32 = jnp.float32
MESH = pl.DeviceIdType.MESH
LIMIT = 62
SECOND_ROWS = (160, 48, 48, 80)
SECOND_BACK = (64, 128, 128, 112)
FIRST_BACK = (208, 128, 96)
ANY = pl.BlockSpec(memory_space=pl.ANY)
VMEM = pl.BlockSpec(memory_space=pltpu.VMEM)


def dot(a, b, ca, cb):
    return lax.dot_general(a, b, (((ca,), (cb,)), ((), ())), preferred_element_type=f32)


def place(m):
    d, r = lax.axis_index("dp"), lax.axis_index("rows")
    pair, half = lax.rem(d, 2), r // 2
    return lax.rem(pair + lax.rem(m, 2), 2), lax.rem(half + m // 2, 2)


def peer(m):
    d, r = lax.axis_index("dp"), lax.axis_index("rows")
    pm, hm = place(m)
    return {"dp": d - lax.rem(d, 2) + pm, "rows": hm * 2 + lax.rem(r, 2)}


def sibling():
    r = lax.axis_index("rows")
    return {"rows": r + 1 - 2 * lax.rem(r, 2)}


def remote(src, dst, send, recv, to):
    return pltpu.make_async_remote_copy(
        src_ref=src, dst_ref=dst, send_sem=send, recv_sem=recv, device_id=to, device_id_type=MESH
    )


def share(sh, mine):
    k = lax.rem(lax.axis_index("rows"), 2)
    k = k if mine else 1 - k
    return pl.ds(pl.multiple_of(k * sh, 16), sh)


def greet():
    barrier = pltpu.get_barrier_semaphore()
    rows, cols = lax.axis_size("rows"), lax.axis_size("cols")
    r, c = lax.axis_index("rows"), lax.axis_index("cols")
    to = [peer(1), peer(3)] + [{"rows": lax.rem(r + k, rows)} for k in range(1, rows)]
    to += [{"cols": lax.rem(c + k, cols)} for k in range(1, cols)]
    for device in to:
        pl.semaphore_signal(barrier, inc=1, device_id=device, device_id_type=MESH)
    pl.semaphore_wait(barrier, len(to))


def gather_copy(buf, sh, sems, m, to):
    pm, hm = place(0)
    own = buf.at[pm, :, hm, share(sh, True)]
    return remote(own, own, sems.at[0, m], sems.at[1, m], to)


def relay_copy(buf, sh, sems, m):
    pm, hm = place(m)
    part = buf.at[pm, m - 1, hm, share(sh, True)]
    return remote(part, part, sems.at[8, m], sems.at[9, m], peer(3 - m))


def start_gather(buf, sh, sems):
    gather_copy(buf, sh, sems, 0, sibling()).start()
    for m in (1, 2):
        gather_copy(buf, sh, sems, m, peer(m)).start()


def forward_copy(buf, sh, sems, m, mine):
    pm, hm = place(m)
    part = buf.at[pm, :, hm, share(sh, mine)]
    return remote(part, part, sems.at[2, m], sems.at[3, m], sibling())


def arrive(buf, sh, sems, m):
    def come(src, i, j):
        remote(src, src, sems.at[i - 1, j], sems.at[i, j], sibling()).wait_recv()

    @pl.when(m == 0)
    def _():
        pm, hm = place(0)
        come(buf.at[pm, :, hm, share(sh, False)], 1, 0)

    @pl.when(m == 1)
    def _():
        for j in (1, 2):
            pj, hj = place(j)
            come(buf.at[pj, :, hj, share(sh, True)], 1, j)
            relay_copy(buf, sh, sems, j).start()
            forward_copy(buf, sh, sems, j, True).start()

    @pl.when(m == 3)
    def _():
        pj, hj = place(3)
        for j in (1, 2):
            come(buf.at[pj, j - 1, hj, share(sh, True)], 9, j)
        forward_copy(buf, sh, sems, 3, True).start()

    @pl.when(m > 0)
    def _():
        forward_copy(buf, sh, sems, m, False).wait_recv()


def end_gather(buf, sh, sems):
    gather_copy(buf, sh, sems, 0, sibling()).wait_send()
    for m in (1, 2):
        gather_copy(buf, sh, sems, m, peer(m)).wait_send()
        relay_copy(buf, sh, sems, m).wait_send()
    for m in (1, 2, 3):
        forward_copy(buf, sh, sems, m, True).wait_send()


def sum_copy(ys, yr, sems, m, half):
    return remote(ys.at[m, half], yr.at[m, half], sems.at[6, 2 * half + m - 1], sems.at[7, 2 * half + m - 1], peer(m))


def relay_sum_copy(ys, yr, sems, half):
    return remote(ys.at[3, half], yr.at[3, half], sems.at[10, half], sems.at[11, half], peer(half + 1))


def across_copy(part, xr, sh, sems, m):
    return remote(
        part.at[m, :, share(sh, False)], xr.at[m], sems.at[4, m], sems.at[5, m], sibling()
    )


def scatter(part, xr, ys, yr, sh, sems, m):
    across_copy(part, xr, sh, sems, m).wait_recv()
    both = part[m, :, share(sh, True)] + xr[m]
    xr[m] = both
    ys[m] = both.astype(bf16)

    @pl.when(m == 3)
    def _():
        for half in (0, 1):
            relay_sum_copy(ys, yr, sems, half).start()

    for j in (1, 2):

        @pl.when(m == j)
        def _():
            sum_copy(ys, yr, sems, j, j - 1).start()


def end_scatter(part, xr, ys, yr, sh, sems):
    for half in (0, 1):
        m = 2 - half
        relay_sum_copy(ys, yr, sems, half).wait_recv()
        ys[m, half] = (xr[m, half] + yr[3, half].astype(f32)).astype(bf16)
        sum_copy(ys, yr, sems, m, half).start()
    total = xr[0]
    for m in (1, 2):
        for half in (0, 1):
            sum_copy(ys, yr, sems, m, half).wait_recv()
        total = total + yr[m].astype(f32)
    for half in (0, 1):
        relay_sum_copy(ys, yr, sems, half).wait_send()
        for m in (1, 2):
            sum_copy(ys, yr, sems, m, half).wait_send()
    for m in range(4):
        across_copy(part, xr, sh, sems, m).wait_send()
    return total


def lines(src_of, dst_of, sems):
    count, c = lax.axis_size("cols"), lax.axis_index("cols")
    sends, gets = [], []
    for k in range(1, count):
        to, come = lax.rem(c + k, count), lax.rem(c + count - k, count)
        sends.append(remote(src_of(to), dst_of(c), sems.at[0, k], sems.at[1, k], {"cols": to}))
        gets.append(remote(src_of(c), dst_of(come), sems.at[0, k], sems.at[1, k], {"cols": to}))
    return sends, gets, pltpu.make_async_copy(src_of(c), dst_of(c), sems.at[0, 0])


class Side:
    def relay(self):
        pass


class Gather(Side):
    def __init__(self, array, lo, n, phase=0):
        self.args = (array,)
        self.phase = phase
        self.lo, self.n = lo, n
        self.relayed = False
        assert lax.axis_size("cols") == 4
        self.outs = ((shape((4, n, D), array.dtype), ANY),)
        self.scratch = [DMA((2, 5))]

    def bind(self, ins, outs, scratch):
        self.src, self.slot, self.sems = ins[0].at[pl.ds(self.lo, self.n)], lambda z: outs[0].at[z], scratch[0]

    @classmethod
    def of(cls, src, slot, sems):
        self = cls.__new__(cls)
        self.relayed = False
        self.src, self.slot, self.sems = src, slot, sems
        return self

    def send(self, t):
        c = lax.axis_index("cols")
        return remote(self.src, self.slot(c), self.sems.at[0, t], self.sems.at[1, c], {"cols": t})

    def pass_on(self):
        c = lax.axis_index("cols")
        part = self.slot(6 - 3 * c)
        return remote(part, part, self.sems.at[0, 4], self.sems.at[1, 6 - 3 * c], {"cols": 3 * c - 3})

    def local(self):
        return pltpu.make_async_copy(self.src, self.slot(lax.axis_index("cols")), self.sems.at[1, 4])

    def each(self, act):
        c = lax.axis_index("cols")
        for off in (2, -2, 1, -1):
            t = c + off

            @pl.when((t >= 0) & (t < 4))
            def _():
                act(self.send(t))

    def start(self):
        self.each(lambda copy: copy.start())
        self.local().start()

    def relay(self):
        self.relayed = True
        c = lax.axis_index("cols")

        @pl.when((c == 1) | (c == 2))
        def _():
            self.pass_on().wait_recv()
            self.pass_on().start()

    def finish(self):
        if not self.relayed:
            self.relay()
        c = lax.axis_index("cols")
        for s in range(4):

            @pl.when((s != c) & (s + 3 * c != 6))
            def _():
                part = self.slot(s)
                remote(part, part, self.sems.at[0, s], self.sems.at[1, s], {"cols": s}).wait_recv()

        self.each(lambda copy: copy.wait_send())

        @pl.when((c == 1) | (c == 2))
        def _():
            self.pass_on().wait_send()

        self.local().wait()


class Reduce(Side):
    def __init__(self, array, lo, n, phase=0):
        self.args = (array,)
        self.phase = phase
        self.lo, self.n = lo, n
        self.relayed = False
        self.outs = ((shape((n, D), array.dtype), VMEM),)
        self.scratch = self.buffers(n)

    @staticmethod
    def buffers(n):
        return [pltpu.VMEM((4, n, D), bf16), pltpu.VMEM((n, D), bf16), pltpu.VMEM((n, D), bf16), DMA((2, 6))]

    def bind(self, ins, outs, scratch):
        self.out = outs[0]
        self.got, self.far, self.own, self.sems = scratch
        self.src = ins[0].at[:, pl.ds(self.lo, self.n)]

    @classmethod
    def of(cls, src, out, scratch):
        self = cls.__new__(cls)
        self.relayed = False
        self.src, self.out, self.n = src, out, out.shape[0]
        self.got, self.far, self.own, self.sems = scratch
        return self

    def send(self, off):
        c = lax.axis_index("cols")
        t = c + off
        if abs(off) == 3:
            return remote(self.src.at[t], self.far, self.sems.at[0, t], self.sems.at[1, 4], {"cols": c + off // 3})
        return remote(self.src.at[t], self.got.at[c], self.sems.at[0, t], self.sems.at[1, c], {"cols": t})

    def send_sum(self):
        c = lax.axis_index("cols")
        t = 6 - 3 * c
        return remote(self.own, self.got.at[c], self.sems.at[0, t], self.sems.at[1, c], {"cols": t})

    def each(self, act, offs):
        c = lax.axis_index("cols")
        for off in offs:
            t = c + off
            ok = (t >= 0) & (t < 4)
            if abs(off) == 2:
                ok = ok & (c != (1 if off == 2 else 2))

            @pl.when(ok)
            def _():
                act(self.send(off))

    def local(self):
        c = lax.axis_index("cols")
        return pltpu.make_async_copy(self.src.at[c], self.got.at[c], self.sems.at[0, 4])

    def load(self):
        c = lax.axis_index("cols")
        return pltpu.make_async_copy(self.src.at[6 - 3 * c], self.own, self.sems.at[0, 5])

    def start(self):
        self.start_far()
        self.start_near()

    def start_far(self):
        self.each(lambda copy: copy.start(), (3, -3))

    def start_near(self):
        c = lax.axis_index("cols")
        self.each(lambda copy: copy.start(), (2, -2, 1, -1))
        self.local().start()

        @pl.when((c == 1) | (c == 2))
        def _():
            self.load().start()

        @pl.when((c == 0) | (c == 3))
        def _():
            self.got[3 - c] = jnp.zeros((self.n, D), bf16)

    def blocks(self):
        return [slice(a, min(a + 48, self.n)) for a in range(0, self.n, 48)]

    def relay(self):
        self.relayed = True
        c = lax.axis_index("cols")

        @pl.when((c == 1) | (c == 2))
        def _():
            self.load().wait()
            remote(self.far, self.far, self.sems.at[0, 0], self.sems.at[1, 4], {"cols": 1}).wait_recv()
            for at in self.blocks():
                self.own[at] = (self.own[at].astype(f32) + self.far[at].astype(f32)).astype(bf16)

            self.send_sum().start()

    def finish(self):
        if not self.relayed:
            self.relay()
        c = lax.axis_index("cols")
        for s in range(4):

            @pl.when((s != c) & (s - c < 3) & (c - s < 3))
            def _():
                part = self.got.at[s]
                remote(part, part, self.sems.at[0, s], self.sems.at[1, s], {"cols": s}).wait_recv()

        self.local().wait()
        for at in self.blocks():
            self.out[at] = jnp.sum(self.got[:, at].astype(f32), axis=0).astype(bf16)
        self.each(lambda copy: copy.wait_send(), (3, -3, 2, -2, 1, -1))

        @pl.when((c == 1) | (c == 2))
        def _():
            self.send_sum().wait_send()


class Rows(Side):
    def __init__(self, kind, array, phase=0):
        self.args = (array,)
        self.phase = phase
        self.kind = kind
        rows = lax.axis_size("rows")
        a, b, f = array.shape
        dims = (a, b // rows, f * rows) if kind == "tokens" else (a, b * rows, f // rows)
        self.outs = ((shape(dims, array.dtype), ANY),)
        self.scratch = [DMA((2, 1, 4))]

    def bind(self, ins, outs, scratch):
        self.work = row_copies(self.kind, ins[0], outs[0], scratch[0], 0)

    def start(self):
        begin_all(self.work)

    def finish(self):
        end_all(self.work)


class AttentionReturn:
    def __init__(self, src, dst, sems, per_col):
        self.src, self.dst, self.sems, self.per_col = src, dst, sems, per_col
        self.rows, self.cols = lax.axis_size("rows"), lax.axis_size("cols")
        self.d, self.r, self.c = lax.axis_index("dp"), lax.axis_index("rows"), lax.axis_index("cols")
        self.pair = lax.rem(self.d, 2)
        self.me = self.pair * self.rows + self.r
        self.gets_direct = per_col * self.c // self.rows == self.pair

    def each(self, act, local):
        owner, half = self.me // self.per_col, lax.rem(self.me, self.per_col)
        width = self.dst.shape[3]
        for k in range(self.rows):
            own = (k == self.r) & (owner == self.c)
            here, there = band(self.src, k, width), self.dst.at[half, self.c]

            @pl.when(jnp.logical_not(own))
            def _():
                act(remote(here, there, self.sems.at[0, k], self.sems.at[1, half * self.cols + self.c],
                           {"rows": k, "cols": owner}))

            @pl.when(own)
            def _():
                local(pltpu.make_async_copy(here, there, self.sems.at[0, k]))

    def start(self):
        self.each(lambda copy: copy.start(), lambda copy: copy.start())

    def finish(self):
        for h in range(self.per_col):
            source = self.c * self.per_col + h
            for z in range(self.cols):
                part = self.dst.at[h, z]
                mine = (source == self.me) & (z == self.c)

                @pl.when(self.gets_direct & jnp.logical_not(mine))
                def _():
                    to = {"rows": lax.rem(source, self.rows), "cols": z}
                    remote(part, part, self.sems.at[0, 0], self.sems.at[1, h * self.cols + z], to).wait_recv()

        self.each(lambda copy: copy.wait_send(), lambda copy: copy.wait())


def begin_all(work):
    sends, _, local = work
    for copy in sends:
        copy.start()
    local.start()


def end_all(work):
    sends, gets, local = work
    for copy in gets:
        copy.wait_recv()
    for copy in sends:
        copy.wait_send()
    local.wait()


def start_sides(sides, phase=0):
    for side in sides:
        if side.phase == phase:
            side.start()


def relay_sides(sides, phase=0):
    for side in sides:
        if side.phase == phase:
            side.relay()


def finish_sides(sides):
    for side in sides:
        side.finish()


def rms(x):
    return lax.rsqrt(jnp.mean(x * x, axis=-1, keepdims=True) + epsilon)


def put_own(buf, sh, value):
    pm, hm = place(0)
    buf[pm, :, hm, share(sh, True)] = value.astype(bf16)


def norm_own(x_ref, gain_ref):
    x = x_ref[...]
    return x * rms(x) * gain_ref[...]


def norm_back(n, x_ref, gain_ref, grad_ref, out_ref, gain_out):
    x = x_ref[...]
    q = rms(x)
    scaled = n * gain_ref[...]
    dots = jnp.mean(scaled * x, axis=-1, keepdims=True)
    out_ref[...] = grad_ref[...] + scaled * q - x * (q * q * q) * dots
    gain_out[...] = jnp.sum(n * x * q, axis=(0, 1))[None]


def flat(x):
    return x.reshape(x.shape[0] * x.shape[1], x.shape[2])


def tiles(width):
    return [(a, min(256, width - a)) for a in range(0, width, 256)]


def columns(width, act):
    def one(j, carry):
        act(pl.ds(pl.multiple_of(j * 256, 256), 256))
        return carry

    lax.fori_loop(0, width // 256, one, 0)


def padded(width):
    return -(-width // 128) * 128


def segments(lo, n, wide):
    cuts = []
    for g in range(lo // wide, -(-(lo + n) // wide)):
        a, b = max(lo, g * wide), min(lo + n, (g + 1) * wide)
        cuts.append((g, a - g * wide, a - lo, b - a))
    return cuts


def first_rows(arrays, axis):
    return [sum(x.shape[axis] for x in arrays[:i]) for i in range(len(arrays))]


def load_copies(parts, wbuf, wide, sem):
    copies = []
    for ref, lo in zip(parts, first_rows(parts, 1)):
        for g, at, here, n in segments(lo, ref.shape[1], wide):
            for c in range(ref.shape[0]):
                copies.append(pltpu.make_async_copy(
                    ref.at[c, pl.ds(here, n)], wbuf.at[g, pl.ds(c * wide + at, n)], sem.at[len(copies)]
                ))
    return copies


def zero_pad(wbuf, used):
    if wbuf.shape[1] > used:
        wbuf[:, used:] = jnp.zeros((3, wbuf.shape[1] - used, wbuf.shape[2]), bf16)


def ffn_forward_kernel(sh, wide, count, last, sides, x_ref, gain_ref, *refs):
    parts, refs = refs[:count], refs[count:]
    if last:
        tail_ref, refs = refs[0], refs[1:]
    out_ref, n_ref, gu_ref, save_ref, buf, wbuf, gu, hid, part, xr, ys, yr, sems, wsem, osem, gsem = refs
    cols = parts[0].shape[0]
    loads = load_copies(parts, wbuf, wide, wsem)
    for copy in loads:
        copy.start()
    zero_pad(wbuf, cols * wide)
    put_own(buf, sh, norm_own(x_ref, gain_ref))
    greet()
    start_gather(buf, sh, sems)
    if last:
        tail = Gather.of(
            tail_ref.at[pl.ds(3 * wide - last, last)],
            lambda z: wbuf.at[2, pl.ds(pl.multiple_of(z * wide + wide - last, 16), last)],
            gsem,
        )
        tail.start()
    start_sides(sides)
    for copy in loads:
        copy.wait()
    width = wbuf.shape[1]

    def step(m, carry):
        arrive(buf, sh, sems, m)
        if last:
            pl.when(m == 2)(tail.relay)
        pl.when(m == 3)(lambda: relay_sides(sides))
        pm, hm = place(m)
        x = flat(buf[pm, :, hm])
        for a, n in tiles(width):
            g = dot(x, wbuf[0, a : a + n], 1, 1)
            u = dot(x, wbuf[1, a : a + n], 1, 1)
            gu[m, 0, :, a : a + n] = g
            gu[m, 1, :, a : a + n] = u
            hid[m, :, a : a + n] = (g * jax.nn.sigmoid(g) * u).astype(bf16)
        pltpu.make_async_copy(gu.at[m], gu_ref.at[m], osem.at[m]).start()
        return carry

    lax.fori_loop(0, 4, step, 0)
    if last:
        tail.finish()
    save = pltpu.make_async_copy(wbuf, save_ref, osem.at[5])
    save.start()
    keep_n = pltpu.make_async_copy(buf, n_ref, osem.at[4])
    keep_n.start()

    def merge_step(t, carry):
        m = 3 - t

        def down(at):
            part[m, :, :, at] = dot(hid[m], wbuf[2, :, at], 1, 0).reshape(part.shape[1], part.shape[2], 256)

        columns(D, down)
        across_copy(part, xr, sh, sems, m).start()

        @pl.when(m < 3)
        def _():
            scatter(part, xr, ys, yr, sh, sems, m + 1)

        return carry

    lax.fori_loop(0, 4, merge_step, 0)
    scatter(part, xr, ys, yr, sh, sems, 0)
    out_ref[...] = x_ref[...] + end_scatter(part, xr, ys, yr, sh, sems)
    end_gather(buf, sh, sems)
    for m in range(4):
        pltpu.make_async_copy(gu.at[m], gu_ref.at[m], osem.at[m]).wait()
    keep_n.wait()
    save.wait()
    finish_sides(sides)


def ffn_backward_kernel(sh, wide, sides, grad_ref, x_ref, gain_ref, w_ref, n_ref, gu_ref,
                        out_ref, gain_out, dw_ref,
                        buf, nbuf, wbuf, gu, hid, dw, part, xr, ys, yr, sems, wsem, osem):
    cols = dw_ref.shape[0]
    gloads = [pltpu.make_async_copy(gu_ref.at[m], gu.at[m], osem.at[m]) for m in range(4)]
    nload = pltpu.make_async_copy(n_ref, nbuf, osem.at[4])
    loads = [pltpu.make_async_copy(w_ref, wbuf, osem.at[5])]
    for copy in loads + gloads + [nload]:
        copy.start()
    put_own(buf, sh, grad_ref[...])
    greet()
    start_gather(buf, sh, sems)
    start_sides(sides)
    for copy in loads + gloads:
        copy.wait()
    width = wbuf.shape[1]

    def step(m, carry):
        arrive(buf, sh, sems, m)
        pl.when(m == 3)(lambda: relay_sides(sides))
        pm, hm = place(m)
        gg = flat(buf[pm, :, hm])
        for a, n in tiles(width):
            gh = dot(gg, wbuf[2, a : a + n], 1, 1)
            g = gu[m, 0, :, a : a + n]
            u = gu[m, 1, :, a : a + n]
            s = jax.nn.sigmoid(g)
            silu = g * s
            shape = (part.shape[1], part.shape[2], n)
            hid[0, pm, :, hm, :, a : a + n] = (gh * u * (s * (1.0 + g * (1.0 - s)))).astype(bf16).reshape(shape)
            hid[1, pm, :, hm, :, a : a + n] = (gh * silu).astype(bf16).reshape(shape)
            hid[2, pm, :, hm, :, a : a + n] = (silu * u).astype(bf16).reshape(shape)

        def back(at):
            y = dot(flat(hid[0, pm, :, hm]), wbuf[0, :, at], 1, 0) + dot(flat(hid[1, pm, :, hm]), wbuf[1, :, at], 1, 0)
            part[m, :, :, at] = y.reshape(part.shape[1], part.shape[2], 256)

        columns(D, back)
        across_copy(part, xr, sh, sems, m).start()

        @pl.when(m > 0)
        def _():
            scatter(part, xr, ys, yr, sh, sems, m - 1)

        return carry

    lax.fori_loop(0, 4, step, 0)
    scatter(part, xr, ys, yr, sh, sems, 3)
    nload.wait()
    tokens = 8 * buf.shape[3]

    def grads(other, g):
        def one(i, carry):
            at = pl.ds(pl.multiple_of(i * 128, 128), 128)
            left = hid[g, :, :, :, :, at].reshape(tokens, 128)
            dw[g, at] = dot(left, other[...].reshape(tokens, D), 0, 0).astype(bf16)
            return carry

        lax.fori_loop(0, width // 128, one, 0)

    grads(nbuf, 0)
    grads(nbuf, 1)
    grads(buf, 2)
    stores = [
        pltpu.make_async_copy(
            dw.at[g, pl.ds(c * wide, wide)], dw_ref.at[c, pl.ds(g * wide, wide)], wsem.at[c * 3 + g]
        )
        for c in range(cols)
        for g in range(3)
    ]
    for copy in stores:
        copy.start()
    n = end_scatter(part, xr, ys, yr, sh, sems)
    norm_back(n, x_ref, gain_ref, grad_ref, out_ref, gain_out)
    end_gather(buf, sh, sems)
    for copy in stores:
        copy.wait()
    finish_sides(sides)


def ffn_both_kernel(sh, wide, count, last, sides, x_ref, gain_ref, grad_ref, *refs):
    parts, refs = refs[:count], refs[count:]
    if last:
        tail_ref, refs = refs[0], refs[1:]
    out_ref, grad_out, gain_out, dw_ref, buf, gbuf, wbuf, gu, hid, dw = refs[:10]
    one, two = refs[10:14] + refs[18:19], refs[14:18] + refs[19:20]
    wsem, dsem, gsem = refs[20:]
    cols = dw_ref.shape[0]
    sems, gsems = one[4], two[4]
    loads = load_copies(parts, wbuf, wide, wsem)
    for copy in loads:
        copy.start()
    zero_pad(wbuf, cols * wide)
    put_own(buf, sh, norm_own(x_ref, gain_ref))
    put_own(gbuf, sh, grad_ref[...])
    greet()
    start_gather(buf, sh, sems)
    if last:
        tail = Gather.of(
            tail_ref.at[pl.ds(3 * wide - last, last)],
            lambda z: wbuf.at[2, pl.ds(pl.multiple_of(z * wide + wide - last, 16), last)],
            gsem,
        )
        tail.start()
    start_gather(gbuf, sh, gsems)
    start_sides(sides)
    for copy in loads:
        copy.wait()
    width = wbuf.shape[1]
    tokens = 8 * buf.shape[3]

    def out(state):
        part, xr, ys, yr, sem = state
        return part, xr, ys, yr, sh, sem

    def step(m, carry):
        arrive(buf, sh, sems, m)
        if last:
            pl.when(m == 2)(tail.relay)
        pm, hm = place(m)
        x = flat(buf[pm, :, hm])
        for a, n in tiles(width):
            g = dot(x, wbuf[0, a : a + n], 1, 1)
            u = dot(x, wbuf[1, a : a + n], 1, 1)
            gu[m, 0, :, a : a + n] = g
            gu[m, 1, :, a : a + n] = u
            h = (g * jax.nn.sigmoid(g) * u).astype(bf16)
            hid[2, pm, :, hm, :, a : a + n] = h.reshape(buf.shape[1], buf.shape[3], n)
        return carry

    lax.fori_loop(0, 4, step, 0)
    if last:
        tail.finish()

    def merge_step(t, carry):
        m = 3 - t
        pm, hm = place(m)
        part = one[0]

        def down(at):
            y = dot(flat(hid[2, pm, :, hm]), wbuf[2, :, at], 1, 0)
            part[m, :, :, at] = y.reshape(part.shape[1], part.shape[2], 256)

        columns(D, down)
        across_copy(part, one[1], sh, sems, m).start()

        @pl.when(m < 3)
        def _():
            scatter(*out(one), m + 1)

        return carry

    lax.fori_loop(0, 4, merge_step, 0)
    scatter(*out(one), 0)

    def back_step(m, carry):
        arrive(gbuf, sh, gsems, m)

        @pl.when(m == 2)
        def _():
            out_ref[...] = x_ref[...] + end_scatter(*out(one))

        pm, hm = place(m)
        part = two[0]
        gg = flat(gbuf[pm, :, hm])
        for a, n in tiles(width):
            gh = dot(gg, wbuf[2, a : a + n], 1, 1)
            g = gu[m, 0, :, a : a + n]
            u = gu[m, 1, :, a : a + n]
            s = jax.nn.sigmoid(g)
            size = (part.shape[1], part.shape[2], n)
            hid[0, pm, :, hm, :, a : a + n] = (gh * u * (s * (1.0 + g * (1.0 - s)))).astype(bf16).reshape(size)
            hid[1, pm, :, hm, :, a : a + n] = (gh * (g * s)).astype(bf16).reshape(size)

        def back(at):
            y = dot(flat(hid[0, pm, :, hm]), wbuf[0, :, at], 1, 0) + dot(flat(hid[1, pm, :, hm]), wbuf[1, :, at], 1, 0)
            part[m, :, :, at] = y.reshape(part.shape[1], part.shape[2], 256)

        columns(D, back)
        across_copy(part, two[1], sh, gsems, m).start()

        @pl.when(m > 0)
        def _():
            scatter(*out(two), m - 1)

        return carry

    lax.fori_loop(0, 4, back_step, 0)
    scatter(*out(two), 3)

    def grads(other, g):
        def rows(i, carry):
            at = pl.ds(pl.multiple_of(i * 128, 128), 128)
            left = hid[g, :, :, :, :, at].reshape(tokens, 128)
            dw[g, at] = dot(left, other[...].reshape(tokens, D), 0, 0).astype(bf16)
            return carry

        lax.fori_loop(0, width // 128, rows, 0)

    grads(buf, 0)
    grads(buf, 1)
    grads(gbuf, 2)
    stores = [
        pltpu.make_async_copy(
            dw.at[g, pl.ds(c * wide, wide)], dw_ref.at[c, pl.ds(g * wide, wide)], dsem.at[c * 3 + g]
        )
        for c in range(cols)
        for g in range(3)
    ]
    for copy in stores:
        copy.start()
    norm_back(end_scatter(*out(two)), x_ref, gain_ref, grad_ref, grad_out, gain_out)
    end_gather(buf, sh, sems)
    end_gather(gbuf, sh, gsems)
    for copy in stores:
        copy.wait()
    finish_sides(sides)


def shape(dims, kind):
    return jax.ShapeDtypeStruct(dims, kind)


def save_all(sem, *pairs, first=0):
    copies = [pltpu.make_async_copy(a, b, sem.at[first + i]) for i, (a, b) in enumerate(pairs)]
    for copy in copies:
        copy.start()
    return copies


def scatter_scratch(seqs, sh):
    return [
        pltpu.VMEM((4, seqs, 2 * sh, D), f32),
        pltpu.VMEM((4, seqs, sh, D), f32),
        pltpu.VMEM((4, seqs, sh, D), bf16),
        pltpu.VMEM((4, seqs, sh, D), bf16),
    ]


def call(kernel, name, cid, outs, out_specs, in_specs, scratch, args, flops=46 * 10**9, limit=LIMIT, sides=()):
    n_in, n_out, n_scratch = len(args), len(outs), len(scratch)
    side_in = [x for side in sides for x in side.args]
    side_out = [x for side in sides for x in side.outs]
    side_scratch = [x for side in sides for x in side.scratch]

    def body(*refs):
        ins, rest = refs[:n_in], refs[n_in:]
        extra_in, rest = rest[: len(side_in)], rest[len(side_in) :]
        out, rest = rest[:n_out], rest[n_out:]
        extra_out, rest = rest[: len(side_out)], rest[len(side_out) :]
        own, extra_scratch = rest[:n_scratch], rest[n_scratch:]
        for side in sides:
            a, b, s = len(side.args), len(side.outs), len(side.scratch)
            side.bind(extra_in[:a], extra_out[:b], extra_scratch[:s])
            extra_in, extra_out, extra_scratch = extra_in[a:], extra_out[b:], extra_scratch[s:]
        kernel(*((sides,) if sides is not None else ()), *ins, *out, *own)

    got = pl.pallas_call(
        body,
        name=name,
        out_shape=tuple(outs) + tuple(x[0] for x in side_out),
        in_specs=tuple(in_specs) + (ANY,) * len(side_in),
        out_specs=tuple(out_specs) + tuple(x[1] for x in side_out),
        scratch_shapes=list(scratch) + side_scratch,
        cost_estimate=pl.CostEstimate(flops=flops, bytes_accessed=10**7, transcendentals=0),
        compiler_params=pltpu.CompilerParams(
            collective_id=cid, has_side_effects=True, vmem_limit_bytes=limit << 20
        ),
    )(*args, *side_in)
    return got


DMA = pltpu.SemaphoreType.DMA


def ffn_forward(cid, x, gain, parts, wide, sides=(), tail=None):
    seqs, sh, _ = x.shape
    cols = parts[0].shape[0]
    width = padded(cols * wide)
    full = (2, seqs, 2, 2 * sh, D)
    rows = seqs * 2 * sh
    last = 3 * wide - sum(p.shape[1] for p in parts)
    assert 0 <= last <= wide and (last == 0 or tail is not None)
    args = (x, gain) + tuple(parts) + ((tail,) if last else ())
    return call(
        functools.partial(ffn_forward_kernel, sh, wide, len(parts), last), "ffn_forward", cid,
        (shape(x.shape, f32), shape(full, bf16), shape((4, 2, rows, width), f32), shape((3, width, D), bf16)),
        (VMEM, ANY, ANY, ANY), (VMEM, VMEM) + (ANY,) * (len(args) - 2),
        [
            pltpu.VMEM(full, bf16), pltpu.VMEM((3, width, D), bf16),
            pltpu.VMEM((4, 2, rows, width), f32), pltpu.VMEM((4, rows, width), bf16),
        ] + scatter_scratch(seqs, sh)
        + [DMA((12, 4)), DMA((cols * (len(parts) + 2),)), DMA((6,)), DMA((2, 5))],
        args, sides=sides,
    )


def ffn_both(cid, x, gain, grad, parts, wide, tail, sides=()):
    seqs, sh, _ = x.shape
    cols = parts[0].shape[0]
    width = padded(cols * wide)
    full = (2, seqs, 2, 2 * sh, D)
    rows = seqs * 2 * sh
    last = 3 * wide - sum(p.shape[1] for p in parts)
    assert 0 <= last <= wide
    args = (x, gain, grad) + tuple(parts) + ((tail,) if last else ())
    return call(
        functools.partial(ffn_both_kernel, sh, wide, len(parts), last), "ffn_both", cid,
        (shape(x.shape, f32), shape(x.shape, f32), shape((1, D), f32), shape((cols, 3 * wide, D), bf16)),
        (VMEM, VMEM, VMEM, ANY), (VMEM, VMEM, VMEM) + (ANY,) * (len(args) - 3),
        [
            pltpu.VMEM(full, bf16), pltpu.VMEM(full, bf16), pltpu.VMEM((3, width, D), bf16),
            pltpu.VMEM((4, 2, rows, width), f32), pltpu.VMEM((3,) + full[:4] + (width,), bf16),
            pltpu.VMEM((3, width, D), bf16),
        ] + scatter_scratch(seqs, sh) + scatter_scratch(seqs, sh)
        + [DMA((12, 4)), DMA((12, 4)), DMA((cols * (len(parts) + 2),)), DMA((3 * cols,)), DMA((2, 5))],
        args, sides=sides,
    )


def ffn_backward(cid, grad, x, gain, w, n, gu, wide, cols, sides=()):
    seqs, sh, _ = x.shape
    width = w.shape[1]
    full = (2, seqs, 2, 2 * sh, D)
    rows = seqs * 2 * sh
    return call(
        functools.partial(ffn_backward_kernel, sh, wide), "ffn_backward", cid,
        (shape(x.shape, f32), shape((1, D), f32), shape((cols, 3 * wide, D), bf16)),
        (VMEM, VMEM, ANY), (VMEM, VMEM, VMEM, ANY, ANY, ANY),
        [
            pltpu.VMEM(full, bf16), pltpu.VMEM(full, bf16), pltpu.VMEM((3, width, D), bf16),
            pltpu.VMEM((4, 2, rows, width), f32), pltpu.VMEM((3,) + full[:4] + (width,), bf16),
            pltpu.VMEM((3, width, D), bf16),
        ] + scatter_scratch(seqs, sh) + [DMA((12, 4)), DMA((3 * cols,)), DMA((6,))],
        (grad, x, gain, w, n, gu), sides=sides,
    )


def out_copy(stage, dest, sems, m, i):
    pm, hm = place(m)
    c = lax.axis_index("cols")
    s = pm * stage.shape[1] + i
    return s, remote(
        stage.at[m, i], dest.at[c, hm], sems.at[0, m * 2 + i], sems.at[1, c * 2 + hm], {"cols": s}
    )


def send_out(stage, dest, sems, m):
    pm, hm = place(m)
    c = lax.axis_index("cols")
    for i in range(stage.shape[1]):
        s, copy = out_copy(stage, dest, sems, m, i)

        @pl.when(s == c)
        def _():
            dest[c, hm] = stage[m, i]

        @pl.when(s != c)
        def _():
            copy.start()


def wait_out(stage, dest, sems):
    c = lax.axis_index("cols")
    for z in range(dest.shape[0]):
        for h in range(2):

            @pl.when(z != c)
            def _():
                got = dest.at[z, h]
                remote(got, got, sems.at[0, z * 2 + h], sems.at[1, z * 2 + h], {"cols": z}).wait_recv()


def end_out(stage, dest, sems):
    c = lax.axis_index("cols")
    for m in range(4):
        for i in range(stage.shape[1]):
            s, copy = out_copy(stage, dest, sems, m, i)

            @pl.when(s != c)
            def _():
                copy.wait_send()


def back_copy(stage, dest, sems, i, row=2):
    c = lax.axis_index("cols")
    seqs = dest.shape[1]
    return remote(
        stage.at[i], dest.at[c // seqs, lax.rem(c, seqs)], sems.at[row, i], sems.at[row + 1, c], {"cols": i}
    )


def send_back(stage, dest, sems, i, row=2):
    c = lax.axis_index("cols")
    seqs = dest.shape[1]

    @pl.when(i == c)
    def _():
        dest[c // seqs, lax.rem(c, seqs)] = stage[i]

    @pl.when(i != c)
    def _():
        back_copy(stage, dest, sems, i, row).start()


def wait_back(stage, dest, sems, row=2):
    c = lax.axis_index("cols")
    seqs = dest.shape[1]
    for s in range(stage.shape[0]):

        @pl.when(s != c)
        def _():
            got = dest.at[s // seqs, s % seqs]
            remote(got, got, sems.at[row, s], sems.at[row + 1, s], {"cols": s}).wait_recv()
            back_copy(stage, dest, sems, s, row).wait_send()


def low_lanes(x):
    return lax.broadcasted_iota(jnp.int32, x.shape, x.ndim - 1) < HD


def per_head(x):
    low = low_lanes(x)
    a = jnp.sum(jnp.where(low, x, 0.0), axis=-1, keepdims=True)
    b = jnp.sum(jnp.where(low, 0.0, x), axis=-1, keepdims=True)
    return jnp.where(low, a, b) * (1.0 / HD)


def partner(x):
    lane = lax.rem(lax.broadcasted_iota(jnp.int32, x.shape, x.ndim - 1), HD)
    return jnp.where(lane < HD // 2, pltpu.roll(x, 2 * HD - HD // 2, axis=1), pltpu.roll(x, HD // 2, axis=1))


def swap(x):
    return pltpu.roll(x, HD, axis=1)


def rope_forward(x, gain, cos, sin):
    y = x * lax.rsqrt(per_head(x * x) + epsilon) * gain
    return y * cos + partner(y) * sin


def rope_backward(x, gain, cos, sin, grad):
    inv = lax.rsqrt(per_head(x * x) + epsilon)
    g = grad * cos - partner(grad) * sin
    scaled = g * gain
    out = scaled * inv - x * (inv * inv * inv) * per_head(scaled * x)
    return out, jnp.sum(g * x * inv, axis=0, keepdims=True)


def split_heads(x, upper):
    x = x.astype(f32)
    low = low_lanes(x)
    if upper:
        return jnp.where(low, 0.0, swap(x)).astype(bf16), jnp.where(low, 0.0, x).astype(bf16)
    return jnp.where(low, x, 0.0).astype(bf16), jnp.where(low, swap(x), 0.0).astype(bf16)


def probabilities(q, keys, first, length):
    s = dot(q, keys, 1, 1)
    at = lax.broadcasted_iota(jnp.int32, s.shape, 1)
    row = lax.broadcasted_iota(jnp.int32, s.shape, 0) + first
    s = jnp.where((at <= row) & (at < length), s, -1e30)
    e = jnp.exp(s - jnp.max(s, axis=1, keepdims=True))
    return e * (1.0 / jnp.sum(e, axis=1, keepdims=True))


def key_bound(i, slots):
    return min(-(-(i + 1) * slots // 128) * 128, 4 * slots)


def attention_forward_kernel(sh, sides, x_ref, gain_ref, w_all, cos_ref, sin_ref, gq_ref, gk_ref, len_ref,
                             out_ref, n_out, raw_out, seq_out, att_out,
                             raw_ref, seq_ref, att_ref, buf, stage, q2, kv, o, back, part, xr, ys, yr, sems, zsems, osem):
    c = lax.axis_index("cols")
    slots = 4 * sh
    w_ref, wo_ref = w_all.at[pl.ds(0, 4 * HD)], w_all.at[pl.ds(4 * HD, 2 * HD)]
    put_own(buf, sh, norm_own(x_ref, gain_ref))
    greet()
    start_gather(buf, sh, sems)
    start_sides(sides)
    low = low_lanes(gq_ref[...])

    def step(m, carry):
        arrive(buf, sh, sems, m)
        pm, hm = place(m)
        y = dot(flat(buf[pm, :, hm]), w_ref[...], 1, 1)
        raw_ref[pm, :, hm] = y.reshape(raw_ref.shape[1], 2 * sh, 4 * HD)
        for i in range(stage.shape[1]):
            rows = slice(i * 2 * sh, (i + 1) * 2 * sh)
            cos, sin = cos_ref[hm], sin_ref[hm]
            q = rope_forward(y[rows, : 2 * HD], gq_ref[...], cos, sin) * (HD**-0.5)
            raw = y[rows, 2 * HD :]
            k = rope_forward(raw, gk_ref[...], cos, sin)
            stage[m, i, :, : 2 * HD] = q.astype(bf16)
            stage[m, i, :, 2 * HD :] = jnp.where(low, k, raw).astype(bf16)
        send_out(stage, seq_ref, zsems, m)
        return carry

    lax.fori_loop(0, 4, step, 0)
    saves = save_all(osem, (buf, n_out), (raw_ref, raw_out))
    wait_out(stage, seq_ref, zsems)
    relay_sides(sides, 0)
    start_sides(sides, 1)
    for i in range(4):
        for h in range(2):
            kv[i, h] = seq_ref[i, h, :, 2 * HD :]
            a, b = split_heads(seq_ref[i, h, :, : 2 * HD], False)
            q2[i, 0, h], q2[i, 1, h] = a, b
    length = len_ref[0]
    for i in range(4):
        bound = key_bound(i, slots)

        def tile(u, carry, i=i, bound=bound):
            head, h = u // 2, lax.rem(u, 2)
            keys = kv[...].reshape(4 * slots, 2 * HD)[:bound]
            p = probabilities(q2[i, head, h], keys, i * slots + h * 2 * sh, length)
            o[head, h] = dot(p.astype(bf16), keys, 1, 0)
            return carry

        lax.fori_loop(0, 4, tile, 0)
        for h in range(2):
            back[i, h] = jnp.where(low, swap(o[0, h]), o[1, h]).astype(bf16)
        send_back(back, att_ref, zsems, i)
    wait_back(back, att_ref, zsems)
    saves += save_all(osem, (seq_ref, seq_out), (att_ref, att_out), first=2)
    relay_sides(sides, 1)
    start_sides(sides, 2)

    def merge_step(i, carry):
        m = 3 - i
        pm, hm = place(m)
        pl.when(i == 3)(lambda: relay_sides(sides, 2))
        y = flat(att_ref[pm, :, hm])

        def multiply(at):
            part[m, :, :, at] = dot(y, wo_ref[:, at], 1, 0).reshape(part.shape[1], part.shape[2], 256)

        columns(D, multiply)
        across_copy(part, xr, sh, sems, m).start()

        @pl.when(m < 3)
        def _():
            scatter(part, xr, ys, yr, sh, sems, m + 1)

        return carry

    lax.fori_loop(0, 4, merge_step, 0)
    scatter(part, xr, ys, yr, sh, sems, 0)
    out_ref[...] = x_ref[...] + end_scatter(part, xr, ys, yr, sh, sems)
    end_gather(buf, sh, sems)
    end_out(stage, seq_ref, zsems)
    for copy in saves:
        copy.wait()
    finish_sides(sides)


def attention_backward_kernel(sh, sides, grad_ref, x_ref, gain_ref, w_all, cos_ref, sin_ref, gq_ref, gk_ref, len_ref,
                              n_in, raw_in, seq_in, att_in,
                              out_ref, gain_out, head_out, dw_ref,
                              raw_ref, seq_ref, att_ref, buf, nbuf, stage, dseq, q2, do2, kv, dq, dkv, back_q, back_k, dproj_q, dproj_k, gproj,
                              part, xr, ys, yr, sems, zsems, osem):
    c = lax.axis_index("cols")
    slots = 4 * sh
    w_ref, wo_ref = w_all.at[pl.ds(0, 4 * HD)], w_all.at[pl.ds(4 * HD, 2 * HD)]
    tokens = 8 * buf.shape[3]
    loads = save_all(osem, (seq_in, seq_ref), (raw_in, raw_ref), (att_in, att_ref), (n_in, nbuf))
    put_own(buf, sh, grad_ref[...])
    greet()
    start_gather(buf, sh, sems)
    start_sides(sides)
    for copy in loads[:3]:
        copy.wait()
    low = low_lanes(gq_ref[...])
    for i in range(4):
        for h in range(2):
            kv[i, h] = seq_ref[i, h, :, 2 * HD :]
            a, b = split_heads(seq_ref[i, h, :, : 2 * HD], False)
            q2[i, 0, h], q2[i, 1, h] = a, b
    dkv[...] = jnp.zeros_like(dkv)
    head_out[...] = jnp.zeros_like(head_out)

    def step(m, carry):
        arrive(buf, sh, sems, m)
        pm, hm = place(m)
        y = dot(flat(buf[pm, :, hm]), wo_ref[...], 1, 1).astype(bf16)
        stage[m] = y.reshape(stage.shape[1], 2 * sh, 2 * HD)
        send_out(stage, dseq, zsems, m)
        return carry

    lax.fori_loop(0, 4, step, 0)
    wait_out(stage, dseq, zsems)
    relay_sides(sides, 0)
    start_sides(sides, 1)
    length = len_ref[0]
    for i in range(4):
        for h in range(2):
            a, b = split_heads(dseq[i, h], True)
            do2[i, 0, h], do2[i, 1, h] = a, b
    for i in range(4):
        bound = key_bound(i, slots)

        def tile(u, carry, i=i, bound=bound):
            head, h = u // 2, lax.rem(u, 2)
            keys = kv[...].reshape(4 * slots, 2 * HD)[:bound]
            q, do = q2[i, head, h], do2[i, head, h]
            p = probabilities(q, keys, i * slots + h * 2 * sh, length)
            dp = dot(do, keys, 1, 1)
            ds = (p * (dp - jnp.sum(p * dp, axis=1, keepdims=True))).astype(bf16)
            dq[head, h] = dot(ds, keys, 1, 0) * (HD**-0.5)
            dkv[:, :bound] += dot(q, ds, 0, 0) + dot(do, p.astype(bf16), 0, 0)
            return carry

        lax.fori_loop(0, 4, tile, 0)
        for h in range(2):
            back_q[i, h] = jnp.where(low, dq[0, h], swap(dq[1, h])).astype(bf16)
        send_back(back_q, dproj_q, zsems, i)
    grads = dkv[...].T.reshape(4, 2, 2 * sh, 2 * HD)
    for i in range(4):
        back_k[i] = grads[i].astype(bf16)
        send_back(back_k, dproj_k, zsems, i, 4)
    wait_back(back_q, dproj_q, zsems)
    wait_back(back_k, dproj_k, zsems, 4)
    relay_sides(sides, 1)
    start_sides(sides, 2)

    def merge_step(t, carry):
        m = 3 - t
        pm, hm = place(m)
        pl.when(t == 3)(lambda: relay_sides(sides, 2))
        for i in range(stage.shape[1]):
            cos, sin = cos_ref[hm], sin_ref[hm]
            g_q, g_k = dproj_q[pm, i, hm].astype(f32), dproj_k[pm, i, hm].astype(f32)
            raw = raw_ref[pm, i, hm]
            a, ga = rope_backward(raw[:, : 2 * HD], gq_ref[...], cos, sin, g_q)
            b, gb = rope_backward(raw[:, 2 * HD :], gk_ref[...], cos, sin, g_k)
            gproj[pm, i, hm, :, : 2 * HD] = a.astype(bf16)
            gproj[pm, i, hm, :, 2 * HD :] = jnp.where(low, b, g_k).astype(bf16)
            head_out[0:1] += ga
            head_out[1:2] += gb
        y = flat(gproj[pm, :, hm])

        def multiply(at):
            part[m, :, :, at] = dot(y, w_ref[:, at], 1, 0).reshape(part.shape[1], part.shape[2], 256)

        columns(D, multiply)
        across_copy(part, xr, sh, sems, m).start()

        @pl.when(m < 3)
        def _():
            scatter(part, xr, ys, yr, sh, sems, m + 1)

        return carry

    lax.fori_loop(0, 4, merge_step, 0)
    scatter(part, xr, ys, yr, sh, sems, 0)
    loads[3].wait()
    left = gproj[...].reshape(tokens, 4 * HD)
    dw_ref[: 4 * HD] = dot(left, nbuf[...].reshape(tokens, D), 0, 0).astype(bf16)
    left = att_ref[...].reshape(tokens, 2 * HD)
    dw_ref[4 * HD :] = dot(left, buf[...].reshape(tokens, D), 0, 0).astype(bf16)
    n = end_scatter(part, xr, ys, yr, sh, sems)
    norm_back(n, x_ref, gain_ref, grad_ref, out_ref, gain_out)
    end_gather(buf, sh, sems)
    end_out(stage, dseq, zsems)
    finish_sides(sides)


SMEM = pl.BlockSpec(memory_space=pltpu.SMEM)


def attention_forward(cid, x, gain, w, tables, length, sides=()):
    seqs, sh, _ = x.shape
    full = (2, seqs, 2, 2 * sh)
    zshape = (4, 2, 2 * sh)
    return call(
        functools.partial(attention_forward_kernel, sh), "attention_forward", cid,
        (shape(x.shape, f32), shape(full + (D,), bf16), shape(full + (4 * HD,), f32),
         shape(zshape + (4 * HD,), bf16), shape(full + (2 * HD,), bf16)),
        (VMEM, ANY, ANY, ANY, ANY), (VMEM,) * 7 + (SMEM,),
        [
            pltpu.VMEM(full + (4 * HD,), f32), pltpu.VMEM(zshape + (4 * HD,), bf16), pltpu.VMEM(full + (2 * HD,), bf16),
            pltpu.VMEM(full + (D,), bf16), pltpu.VMEM((4, seqs, 2 * sh, 4 * HD), bf16),
            pltpu.VMEM((4, 2, 2, 2 * sh, 2 * HD), bf16), pltpu.VMEM(zshape + (2 * HD,), bf16),
            pltpu.VMEM((2, 2, 2 * sh, 2 * HD), f32), pltpu.VMEM(zshape + (2 * HD,), bf16),
        ] + scatter_scratch(seqs, sh) + [DMA((12, 4)), DMA((4, 8)), DMA((4,))],
        (x, gain, w) + tables + (length,), sides=sides,
    )


def attention_backward(cid, grad, x, gain, w, tables, length, n, raw, seq, att, sides=()):
    seqs, sh, _ = x.shape
    full = (2, seqs, 2, 2 * sh)
    zshape = (4, 2, 2 * sh)
    return call(
        functools.partial(attention_backward_kernel, sh), "attention_backward", cid,
        (shape(x.shape, f32), shape((1, D), f32), shape((2, 2 * HD), f32), shape((6 * HD, D), bf16)),
        (VMEM,) * 4, (VMEM,) * 8 + (SMEM, ANY, ANY, ANY, ANY),
        [
            pltpu.VMEM(full + (4 * HD,), f32), pltpu.VMEM(zshape + (4 * HD,), bf16), pltpu.VMEM(full + (2 * HD,), bf16),
            pltpu.VMEM(full + (D,), bf16), pltpu.VMEM(full + (D,), bf16),
            pltpu.VMEM((4, seqs, 2 * sh, 2 * HD), bf16), pltpu.VMEM(zshape + (2 * HD,), bf16),
            pltpu.VMEM((4, 2, 2, 2 * sh, 2 * HD), bf16), pltpu.VMEM((4, 2, 2, 2 * sh, 2 * HD), bf16),
            pltpu.VMEM(zshape + (2 * HD,), bf16), pltpu.VMEM((2, 2, 2 * sh, 2 * HD), f32),
            pltpu.VMEM((2 * HD, 16 * sh), f32), pltpu.VMEM(zshape + (2 * HD,), bf16), pltpu.VMEM(zshape + (2 * HD,), bf16),
            pltpu.VMEM(full + (2 * HD,), bf16), pltpu.VMEM(full + (2 * HD,), bf16), pltpu.VMEM(full + (4 * HD,), bf16),
        ] + scatter_scratch(seqs, sh) + [DMA((12, 4)), DMA((6, 8)), DMA((4,))],
        (grad, x, gain, w) + tables + (length, n, raw, seq, att), sides=sides,
    )


def edge_send(buf, edge, sh, sems, way, p, i):
    d, c = lax.axis_index("dp"), lax.axis_index("cols")
    pm, hm = place(0)
    at = share(sh, True).start + (sh - 16 if way == 0 else 0)
    to = {"dp": d - lax.rem(d, 2) + p, "rows": i, "cols": c + 1 if way == 0 else c - 1}
    return remote(
        buf.at[pm, :, hm, pl.ds(pl.multiple_of(at, 16), 16)], edge.at[way, pm],
        sems.at[0, way * 8 + p * 4 + i], sems.at[1, way * 8 + pm], to,
    )


def edge_senders(way):
    r, c = lax.axis_index("rows"), lax.axis_index("cols")
    rows, cols = lax.axis_size("rows"), lax.axis_size("cols")
    return (r == rows - 1) & (c < cols - 1) if way == 0 else (r == 0) & (c > 0)


def edges_each(buf, edge, sh, sems, way, act):
    @pl.when(edge_senders(way))
    def _():
        for p in range(2):
            for i in range(4):
                act(edge_send(buf, edge, sh, sems, way, p, i))


def wait_edges(edge, sems, way):
    c = lax.axis_index("cols")
    gets = c > 0 if way == 0 else c < lax.axis_size("cols") - 1

    @pl.when(gets)
    def _():
        for p in range(2):
            part = edge.at[way, p]
            remote(part, part, sems.at[0, way * 8 + p], sems.at[1, way * 8 + p], sibling()).wait_recv()

    @pl.when(jnp.logical_not(gets))
    def _():
        edge[way] = jnp.zeros(edge.shape[1:], bf16)


def window(ref, s, hm, rows):
    return ref[s, pl.ds(pl.multiple_of(hm * rows, 8), rows + 8)]


def convolve(taps, ext, rows):
    return sum(taps[k : k + 1] * ext[8 - (CONV - 1) + k : 8 - (CONV - 1) + k + rows] for k in range(CONV))


def conv_forward_kernel(sh, sides, x_ref, gain_ref, w_in, taps_ref,
                        out_ref, n_out, mixed_out, prod_out, gate_out,
                        wall, wsem, mixed_ref, prod_ref, gate_ref, buf, cmix, edge, part, xr, ys, yr, sems, zsems, osem):
    seqs, rows = buf.shape[1], 2 * sh
    ch = wall.shape[0] // 4
    chan = ch // w_in.shape[0]
    wloads = [
        pltpu.make_async_copy(
            w_in.at[c, pl.ds(g * chan, chan)], wall.at[pl.ds(g * ch + c * chan, chan)], wsem.at[4 * c + g]
        )
        for c in range(w_in.shape[0])
        for g in range(4)
    ]
    for copy in wloads:
        copy.start()
    w_ref, wo_ref = wall.at[pl.ds(0, 3 * ch)], wall.at[pl.ds(3 * ch, ch)]
    slots = 2 * rows
    put_own(buf, sh, norm_own(x_ref, gain_ref))
    greet_box(2)
    for way in (0, 1):
        edges_each(buf, edge, sh, zsems, way, lambda copy: copy.start())
    start_gather(buf, sh, sems)
    start_sides(sides)
    for copy in wloads:
        copy.wait()

    def step(m, carry):
        arrive(buf, sh, sems, m)
        pm, hm = place(m)
        y = dot(flat(buf[pm, :, hm]), w_ref[...], 1, 1)
        mixed_ref[pm, :, hm] = y.reshape(seqs, rows, 3 * ch)
        for i in range(seqs):
            z = y[i * rows : (i + 1) * rows]
            at = pl.ds(pl.multiple_of(8 + hm * rows, 8), rows)
            prod_ref[pm * seqs + i, at] = z[:, :ch] * z[:, 2 * ch :]
        return carry

    lax.fori_loop(0, 4, step, 0)
    saves = save_all(osem, (buf, n_out), (mixed_ref, mixed_out))
    for way in (0, 1):
        wait_edges(edge, zsems, way)
    y = dot(edge[...].reshape(4 * seqs * 16, D), w_ref[...], 1, 1).reshape(2, 2 * seqs, 16, 3 * ch)
    prod_ref[:, :8] = y[0, :, 8:, :ch] * y[0, :, 8:, 2 * ch :]
    gate_ref[...] = y[1, :, :8, ch : 2 * ch]
    saves += save_all(osem, (prod_ref, prod_out), (gate_ref, gate_out), first=2)
    taps = taps_ref[...]

    def merge_step(t, carry):
        m = 3 - t
        pm, hm = place(m)
        for i in range(seqs):
            conv = convolve(taps, window(prod_ref, pm * seqs + i, hm, rows), rows)
            cmix[i] = (mixed_ref[pm, i, hm, :, ch : 2 * ch] * conv).astype(bf16)
        y = flat(cmix[...])

        def multiply(at):
            part[m, :, :, at] = dot(y, wo_ref[:, at], 1, 0).reshape(seqs, rows, 256)

        columns(D, multiply)
        across_copy(part, xr, sh, sems, m).start()

        @pl.when(m < 3)
        def _():
            scatter(part, xr, ys, yr, sh, sems, m + 1)

        return carry

    lax.fori_loop(0, 4, merge_step, 0)
    scatter(part, xr, ys, yr, sh, sems, 0)
    out_ref[...] = x_ref[...] + end_scatter(part, xr, ys, yr, sh, sems)
    end_gather(buf, sh, sems)
    for way in (0, 1):
        edges_each(buf, edge, sh, zsems, way, lambda copy: copy.wait_send())
    for copy in saves:
        copy.wait()
    finish_sides(sides)


def conv_backward_kernel(sh, hook, sides, grad_ref, x_ref, gain_ref, w_in, taps_ref, n_in, mixed_in, prod_in, gate_in,
                         out_ref, gain_out, taps_out, dw_ref,
                         wall, wsem, mixed_ref, prod_ref, gate_ref, buf, nbuf, gext, gmix, gin, cmix, edge, part, xr, ys, yr, sems, zsems, osem):
    seqs, rows = buf.shape[1], 2 * sh
    ch = wall.shape[0] // 4
    chan = ch // w_in.shape[0]
    wloads = [
        pltpu.make_async_copy(
            w_in.at[c, pl.ds(g * chan, chan)], wall.at[pl.ds(g * ch + c * chan, chan)], wsem.at[4 * c + g]
        )
        for c in range(w_in.shape[0])
        for g in range(4)
    ]
    for copy in wloads:
        copy.start()
    w_ref, wo_ref = wall.at[pl.ds(0, 3 * ch)], wall.at[pl.ds(3 * ch, ch)]
    slots = 2 * rows
    tokens = 8 * rows
    loads = save_all(osem, (mixed_in, mixed_ref), (prod_in, prod_ref), (gate_in, gate_ref), (n_in, nbuf))
    put_own(buf, sh, grad_ref[...])
    greet_box(2)
    edges_each(buf, edge, sh, zsems, 1, lambda copy: copy.start())
    start_gather(buf, sh, sems)
    start_sides(sides)
    taps_out[...] = jnp.zeros_like(taps_out)
    for copy in loads[:3] + wloads:
        copy.wait()

    def step(m, carry):
        arrive(buf, sh, sems, m)
        pm, hm = place(m)
        y = dot(flat(buf[pm, :, hm]), wo_ref[...], 1, 1)
        for i in range(seqs):
            z = y[i * rows : (i + 1) * rows]
            gmix[pm, i, hm] = z
            at = pl.ds(pl.multiple_of(hm * rows, 8), rows)
            gext[pm * seqs + i, at] = z * mixed_ref[pm, i, hm, :, ch : 2 * ch]
        return carry

    lax.fori_loop(0, 4, step, 0)
    wait_edges(edge, zsems, 1)
    y = dot(edge[1].reshape(2 * seqs * 16, D), wo_ref[...], 1, 1).reshape(2 * seqs, 16, ch)
    gext[:, slots:] = y[:, :8] * gate_ref[...]
    taps = taps_ref[...]

    def merge_step(t, carry):
        m = 3 - t
        pm, hm = place(m)
        pl.when(t == 1)(lambda: relay_sides(sides))
        for i in range(seqs):
            ext = window(prod_ref, pm * seqs + i, hm, rows)
            conv = convolve(taps, ext, rows)
            g = window(gext, pm * seqs + i, hm, rows)
            gprod = sum(taps[k : k + 1] * g[CONV - 1 - k : CONV - 1 - k + rows] for k in range(CONV))
            for k in range(CONV):
                shifted = ext[8 - (CONV - 1) + k : 8 - (CONV - 1) + k + rows]
                taps_out[k : k + 1] += jnp.sum(g[:rows] * shifted, axis=0, keepdims=True)
            mix = mixed_ref[pm, i, hm]
            gin[pm, i, hm, :, :ch] = (gprod * mix[:, 2 * ch :]).astype(bf16)
            gin[pm, i, hm, :, ch : 2 * ch] = (gmix[pm, i, hm] * conv).astype(bf16)
            gin[pm, i, hm, :, 2 * ch :] = (gprod * mix[:, :ch]).astype(bf16)
            cmix[pm, i, hm] = (mix[:, ch : 2 * ch] * conv).astype(bf16)
        y = flat(gin[pm, :, hm])

        def multiply(at):
            part[m, :, :, at] = dot(y, w_ref[:, at], 1, 0).reshape(seqs, rows, 256)

        columns(D, multiply)
        across_copy(part, xr, sh, sems, m).start()

        @pl.when(m < 3)
        def _():
            scatter(part, xr, ys, yr, sh, sems, m + 1)

        return carry

    lax.fori_loop(0, 4, merge_step, 0)
    scatter(part, xr, ys, yr, sh, sems, 0)
    loads[3].wait()
    left = gin[...].reshape(tokens, 3 * ch)
    dw_ref[: 3 * ch] = dot(left, nbuf[...].reshape(tokens, D), 0, 0).astype(bf16)
    left = cmix[...].reshape(tokens, ch)
    dw_ref[3 * ch :] = dot(left, buf[...].reshape(tokens, D), 0, 0).astype(bf16)
    hook()
    n = end_scatter(part, xr, ys, yr, sh, sems)
    norm_back(n, x_ref, gain_ref, grad_ref, out_ref, gain_out)
    end_gather(buf, sh, sems)
    edges_each(buf, edge, sh, zsems, 1, lambda copy: copy.wait_send())
    finish_sides(sides)


def conv_forward(cid, x, gain, w, taps, sides=()):
    seqs, sh, _ = x.shape
    full = (2, seqs, 2, 2 * sh)
    ch = w.shape[0] * w.shape[1] // 4
    own = [pltpu.VMEM((4 * ch, D), bf16), DMA((4 * w.shape[0],))]
    return call(
        functools.partial(conv_forward_kernel, sh), "conv_forward", cid,
        (shape(x.shape, f32), shape(full + (D,), bf16), shape(full + (3 * ch,), f32),
         shape((2 * seqs, 4 * sh + 8, ch), f32), shape((2 * seqs, 8, ch), f32)),
        (VMEM, ANY, ANY, ANY, ANY), (VMEM, VMEM, ANY, VMEM),
        own + [pltpu.VMEM(full + (3 * ch,), f32), pltpu.VMEM((2 * seqs, 4 * sh + 8, ch), f32),
         pltpu.VMEM((2 * seqs, 8, ch), f32),
         pltpu.VMEM(full + (D,), bf16), pltpu.VMEM((seqs, 2 * sh, ch), bf16), pltpu.VMEM((2, 2, seqs, 16, D), bf16)]
        + scatter_scratch(seqs, sh) + [DMA((12, 4)), DMA((2, 16)), DMA((4,))],
        (x, gain, w, taps), sides=sides,
    )


def band(ref, i, width):
    return ref.at[..., pl.ds(pl.multiple_of(i * width, 128), width)]


def row_pieces(kind, src, dst, here, there):
    rows = lax.axis_size("rows")
    if kind == "weights":
        return src.at[there], band(dst, here, src.shape[2])
    if kind == "tokens":
        sh = src.shape[1] // rows
        return src.at[:, pl.ds(pl.multiple_of(there * sh, 8), sh)], band(dst, here, src.shape[2])
    if kind == "gains":
        return src, band(dst, here, src.shape[1])
    sh = src.shape[1]
    return band(src, there, dst.shape[2]), dst.at[:, pl.ds(pl.multiple_of(here * sh, 8), sh)]


def row_copies(kind, src, dst, sems, i):
    rows = lax.axis_size("rows")
    r = lax.axis_index("rows")
    sends, gets = [], []
    for k in range(1, rows):
        to, come = lax.rem(r + k, rows), lax.rem(r + rows - k, rows)
        a, b = row_pieces(kind, src, dst, r, to)
        sends.append(remote(a, b, sems.at[0, i, k], sems.at[1, i, k], {"rows": to}))
        a, b = row_pieces(kind, src, dst, come, r)
        gets.append(remote(a, b, sems.at[0, i, k], sems.at[1, i, k], {"rows": to}))
    a, b = row_pieces(kind, src, dst, r, r)
    return sends, gets, pltpu.make_async_copy(a, b, sems.at[0, i, 0])


def line_copies(axis, src, dst, sems, i):
    count = lax.axis_size(axis) if axis == "cols" else 2
    at = lax.axis_index(axis)
    low = lax.rem(at, count)
    base = at - low
    sends, gets = [], []
    for k in range(1, count):
        to, come = lax.rem(low + k, count), lax.rem(low + count - k, count)
        sends.append(remote(src, dst.at[low], sems.at[0, i, k], sems.at[1, i, k], {axis: base + to}))
        gets.append(remote(src, dst.at[come], sems.at[0, i, k], sems.at[1, i, k], {axis: base + to}))
    return sends, gets, pltpu.make_async_copy(src, dst.at[low], sems.at[0, i, 0])


def greet_box(pairs):
    barrier = pltpu.get_barrier_semaphore()
    rows, cols = lax.axis_size("rows"), lax.axis_size("cols")
    d, r, c = lax.axis_index("dp"), lax.axis_index("rows"), lax.axis_index("cols")
    for p in range(pairs):
        for i in range(rows):
            for j in range(cols):
                if p + i + j > 0:
                    to = {"dp": d if p == 0 else d + 1 - 2 * lax.rem(d, 2),
                          "rows": lax.rem(r + i, rows), "cols": lax.rem(c + j, cols)}
                    pl.semaphore_signal(barrier, inc=1, device_id=to, device_id_type=MESH)
    pl.semaphore_wait(barrier, pairs * rows * cols - 1)


def attention_spread(src, dst, sems):
    halves, cols, _, width = src.shape
    rows = lax.axis_size("rows")
    r, c = lax.axis_index("rows"), lax.axis_index("cols")
    pair = lax.rem(lax.axis_index("dp"), 2)
    holds = pair == halves * c // rows
    first = lax.rem(halves * c, rows)
    origin = (pair * rows + r) // halves

    def to_all(act, local):
        for h in range(halves):
            for z in range(cols):
                own = (first + h == r) & (z == c)
                here = band(dst, r, width)

                @pl.when(holds & jnp.logical_not(own))
                def _():
                    act(remote(src.at[h, z], here, sems.at[0, h * cols + z], sems.at[1, r],
                               {"rows": first + h, "cols": z}))

                @pl.when(holds & own)
                def _():
                    local(pltpu.make_async_copy(src.at[h, z], here, sems.at[0, h * cols + z]))

    def start():
        to_all(lambda copy: copy.start(), lambda copy: copy.start())

    def end():
        for k in range(rows):
            @pl.when(jnp.logical_not((origin == c) & (k == r)))
            def _():
                got = band(dst, k, width)
                remote(got, got, sems.at[0, 0], sems.at[1, k], {"rows": k, "cols": origin}).wait_recv()
        to_all(lambda copy: copy.wait_send(), lambda copy: copy.wait())

    return start, end


def start_kernel(sides, conv_ref, tok_ref, ffn_ref, gain_ref, tap_ref, len_ref,
                 conv_out, tok_out, ffn_out, gain_out, tap_out, len_out, conv_cut, rsems, lsems, zsems):
    barrier = pltpu.get_barrier_semaphore()
    rows, cols = lax.axis_size("rows"), lax.axis_size("cols")
    d, r, c = lax.axis_index("dp"), lax.axis_index("rows"), lax.axis_index("cols")
    to = [{"rows": lax.rem(r + k, rows)} for k in range(1, rows)]
    to += [{"cols": lax.rem(c + k, cols)} for k in range(1, cols)]
    to += [{"dp": d + 1 - 2 * lax.rem(d, 2)}]
    for device in to:
        pl.semaphore_signal(barrier, inc=1, device_id=device, device_id_type=MESH)
    pl.semaphore_wait(barrier, len(to))
    conv = row_copies("weights", conv_ref, conv_cut, rsems, 0)
    small = [
        row_copies("gains", gain_ref, gain_out, rsems, 1),
        line_copies("cols", tap_ref, tap_out, lsems, 0),
        line_copies("dp", len_ref, len_out, lsems, 1),
    ]
    begin_all(conv)
    for work in small:
        begin_all(work)
    tok = row_copies("tokens", tok_ref, tok_out, rsems, 2)
    begin_all(tok)
    end_all(conv)
    conv = Gather.of(conv_cut, lambda z: conv_out.at[z], zsems)
    conv.start()
    ffn = row_copies("weights", ffn_ref, ffn_out, rsems, 3)
    begin_all(ffn)
    for work in small + [tok]:
        end_all(work)
    conv.relay()
    end_all(ffn)
    conv.finish()


def second_kernel(sides, attn_ref, ffn_ref, attn_out, ffn_out, asems, rsems):
    greet_box(1)
    begin, end = attention_spread(attn_ref, attn_out, asems)
    start_sides(sides)
    begin()
    ffn = row_copies("weights", ffn_ref, ffn_out, rsems, 0)
    begin_all(ffn)
    end()
    end_all(ffn)
    finish_sides(sides)


def start_exchange(cid, conv, tok, ffn, gain, tap, length, rows, cols):
    outs = (
        shape((cols, conv.shape[1], D), bf16), shape((tok.shape[0], tok.shape[1] // rows, D), f32),
        shape((ffn.shape[1], D), bf16), shape((8, D), f32), shape((cols,) + tap.shape, f32),
        shape((2,) + length.shape, length.dtype),
    )
    return call(
        start_kernel, "start", cid, outs, (ANY,) * 6, (ANY,) * 6,
        [pltpu.VMEM((conv.shape[1], D), bf16), DMA((2, 4, 4)), DMA((2, 2, 4)), DMA((2, 5))],
        (conv, tok, ffn, gain, tap, length),
    )


def second_exchange(cid, attn, ffn, sides):
    return call(
        second_kernel, "second", cid,
        (shape((attn.shape[2], D), bf16), shape((ffn.shape[1], D), bf16)), (ANY,) * 2, (ANY,) * 2,
        [DMA((2, 8)), DMA((2, 1, 4))], (attn, ffn), sides=sides,
    )


def plane_peer(j):
    pm, hm = place(j // 2)
    d, r = lax.axis_index("dp"), lax.axis_index("rows")
    row = hm * 2 + lax.rem(lax.rem(r, 2) + j % 2, 2)
    return pm, row, {"dp": d - lax.rem(d, 2) + pm, "rows": row}


class Plane:
    def __init__(self, src, dst, lo, w, sems):
        rows = lax.axis_size("rows")
        d, r = lax.axis_index("dp"), lax.axis_index("rows")
        pair = lax.rem(d, 2)
        n, width = src.shape[0], dst.shape[2]
        other = {"dp": d + 1 - 2 * pair}
        self.steps, self.gets = [], []
        for i, (g, at, here, n) in enumerate(segments(lo, src.shape[0], w)):

            def block(p, row, g=g, at=at, n=n):
                return dst.at[g, pl.ds(pl.multiple_of((p * rows + row) * w + at, 16), n)]

            def piece(row, here=here, n=n):
                return band(src.at[pl.ds(here, n)], row, width)

            sem = sems.at[i]
            local = pltpu.make_async_copy(piece(r), block(pair, r), sem.at[0, 0])
            sends = [local]
            turns = [(local, True, remote(block(pair, r), block(pair, r), sem.at[2, 0], sem.at[3, 0], other))]
            self.gets.append(
                remote(block(1 - pair, r), block(1 - pair, r), sem.at[2, 0], sem.at[3, 0], other)
            )
            for k in range(1, rows):
                to, come = lax.rem(r + k, rows), lax.rem(r + rows - k, rows)
                send = remote(piece(to), block(pair, r), sem.at[0, k], sem.at[1, k], {"rows": to})
                get = remote(piece(to), block(pair, come), sem.at[0, k], sem.at[1, k], {"rows": to})
                on = remote(block(pair, come), block(pair, come), sem.at[2, k], sem.at[3, k], other)
                sends.append(send)
                turns.append((get, False, on))
                self.gets.append(
                    remote(block(1 - pair, come), block(1 - pair, come), sem.at[2, k], sem.at[3, k], other)
                )
            self.steps.append((sends, turns))

    def start(self):
        for sends, _ in self.steps:
            for copy in sends:
                copy.start()

    def turn(self):
        for _, turns in self.steps:
            for get, local, on in turns:
                if local:
                    get.wait()
                else:
                    get.wait_recv()
                on.start()

    def finish(self):
        for copy in self.gets:
            copy.wait_recv()
        for sends, turns in self.steps:
            for copy in sends[1:]:
                copy.wait_send()
            for _, _, on in turns:
                on.wait_send()


def conv_finish_kernel(sh, wide, chan, los, chunks, per_col, sides, *refs):
    core, refs = refs[:9], refs[9:]
    gains_ref, heads_ref, ffn_ref, attn_ref = refs[:4]
    arrays, refs = refs[4 : 4 + len(los)], refs[4 + len(los) :]
    o2_ref, o1_ref, oc_ref, os_ref, taps_ref, ot_ref, mid_ref, oa_ref = refs[:8]
    grad_s, gain_s, taps_s, dw_s = refs[8:12]
    conv_scratch, refs = refs[12:31], refs[31:]
    pack, small, srecv, ssum, precv, psems, rsems, ssems, asems, msems = refs[:10]
    scratch = refs[10:]
    rows, cols = lax.axis_size("rows"), lax.axis_size("cols")
    d, c = lax.axis_index("dp"), lax.axis_index("cols")
    pair = lax.rem(d, 2)
    me = pair * rows + lax.axis_index("rows")
    work = [(ffn_ref.at[:, pl.ds(*chunks[0])], o1_ref, chunks[0][0], wide), (pack, oc_ref, 0, chan)]
    work += [(ffn_ref.at[:, pl.ds(lo, n)], o1_ref, lo, wide) for lo, n in chunks[1:]]
    sums = []
    for i, (src, _, _, _) in enumerate(work):
        own = scratch[5 * i : 5 * i + 5]
        sums.append(Reduce.of(src, own[0], own[1:]))
    heads = AttentionReturn(attn_ref, mid_ref, asems, per_col)

    class Ahead(Side):
        phase = 0

        def start(self):
            heads.start()
            sums[0].start()

        def relay(self):
            sums[0].relay()

        def finish(self):
            pass

    def hook():
        count = dw_s.shape[0] // (cols * chan)
        for g in range(count):
            for z in range(cols):
                pack[z, g * chan : (g + 1) * chan] = dw_s[(g * cols + z) * chan : (g * cols + z + 1) * chan]
        for one in sums[1:]:
            one.start_far()
        for one in sums[1:]:
            one.start_near()

    conv_backward_kernel(sh, hook, [Ahead()], *core, grad_s, gain_s, taps_s, dw_s, *conv_scratch)
    planes = [Plane(a, o2_ref, lo, wide, psems.at[i]) for i, (a, lo) in enumerate(zip(arrays, los))]
    count = len(planes)
    for plane in planes:
        plane.start()
    for one in sums[1:]:
        one.relay()
    small[0:1] = gain_s[...]
    small[1:4] = gains_ref[...]
    small[4:5] = heads_ref[...]
    small[5:8] = jnp.zeros((3, D), f32)
    small[5:8, : taps_s.shape[1]] = taps_s[...]
    line = line_copies("cols", small, srecv, ssems, 0)
    begin_all(line)
    tok = row_copies("back", grad_s, ot_ref, rsems, 0)
    begin_all(tok)
    sums[0].finish()
    last = [Plane(sums[0].out, o1_ref, chunks[0][0], wide, psems.at[count])]
    last[0].start()
    for plane in planes:
        plane.turn()
    heads.finish()
    holds = per_col * c // rows == pair
    share_copy = remote(mid_ref, oa_ref, msems.at[0], msems.at[1], {"dp": d + 1 - 2 * pair})
    keep_copy = pltpu.make_async_copy(mid_ref, oa_ref, msems.at[2])

    @pl.when(holds)
    def _():
        share_copy.start()
        keep_copy.start()

    for i in range(1, len(work)):
        sums[i].finish()
        last[-1].turn()
        last.append(Plane(sums[i].out, work[i][1], work[i][2], work[i][3], psems.at[count + i]))
        last[-1].start()
    end_all(line)
    ssum[...] = jnp.sum(srecv[...], axis=0)
    precv[me] = ssum[...]
    for j in range(1, 8):
        to = plane_peer(j)[2]
        remote(ssum, precv.at[me], ssems.at[2, 0, j], ssems.at[3, 0, j], to).start()
    last[-1].turn()
    for j in range(1, 8):
        pm, row, to = plane_peer(j)
        copy = remote(ssum, precv.at[pm * rows + row], ssems.at[2, 0, j], ssems.at[3, 0, j], to)
        copy.wait_recv()
        copy.wait_send()
    os_ref[...] = jnp.sum(precv[...], axis=0)
    taps_ref[...] = precv[:, :, : taps_s.shape[1]]
    end_all(tok)
    for plane in planes + last:
        plane.finish()

    @pl.when(holds)
    def _():
        share_copy.wait_send()
        keep_copy.wait()

    @pl.when(jnp.logical_not(holds))
    def _():
        share_copy.wait_recv()


def conv_finish(cid, core, gains, heads, ffn, attn, arrays, los, chunks, wide, chan, per_col):
    seqs, sh, _ = core[1].shape
    w = core[3]
    cols, rows = lax.axis_size("cols"), lax.axis_size("rows")
    feat = D // rows
    full = (2, seqs, 2, 2 * sh)
    ch = cols * chan
    nc = w.shape[1]
    quarter = (per_col, cols, attn.shape[0], feat)
    outs = (
        shape((3, 8 * wide, feat), bf16), shape((3, 8 * wide, feat), bf16), shape((nc // chan, 8 * chan, feat), bf16),
        shape((8, D), f32), shape((8, 8, ch), f32), shape((seqs, sh * rows, feat), f32),
        shape(quarter, bf16), shape(quarter, bf16),
    )
    scratch = [
        pltpu.VMEM((seqs, sh, D), f32), pltpu.VMEM((1, D), f32), pltpu.VMEM((CONV, ch), f32),
        pltpu.VMEM((4 * ch, D), bf16),
        pltpu.VMEM((4 * ch, D), bf16), DMA((4 * cols,)),
        pltpu.VMEM(full + (3 * ch,), f32), pltpu.VMEM((2 * seqs, 4 * sh + 8, ch), f32),
        pltpu.VMEM((2 * seqs, 8, ch), f32),
        pltpu.VMEM(full + (D,), bf16), pltpu.VMEM(full + (D,), bf16),
        pltpu.VMEM((2 * seqs, 4 * sh + 8, ch), f32), pltpu.VMEM(full + (ch,), f32),
        pltpu.VMEM(full + (3 * ch,), bf16), pltpu.VMEM(full + (ch,), bf16), pltpu.VMEM((2, 2, seqs, 16, D), bf16),
    ] + scatter_scratch(seqs, sh) + [DMA((12, 4)), DMA((2, 16)), DMA((4,))]
    scratch += [
        pltpu.VMEM((cols, nc, D), bf16), pltpu.VMEM((8, D), f32), pltpu.VMEM((cols, 8, D), f32),
        pltpu.VMEM((8, D), f32), pltpu.VMEM((8, 8, D), f32),
        DMA((len(arrays) + len(chunks) + 1, 4, 4, 4)), DMA((2, 1, 4)), DMA((4, 1, 8)), DMA((4, 8)), DMA((3,)),
    ]
    for n in [chunks[0][1], nc] + [n for _, n in chunks[1:]]:
        scratch += [pltpu.VMEM((n, D), bf16)] + Reduce.buffers(n)
    return call(
        functools.partial(conv_finish_kernel, sh, wide, chan, los, chunks, per_col), "conv_finish", cid, outs,
        (ANY, ANY, ANY, VMEM, VMEM, ANY, ANY, ANY),
        (VMEM, VMEM, VMEM, ANY, VMEM) + (ANY,) * 4 + (VMEM, VMEM) + (ANY,) * (2 + len(arrays)), scratch,
        tuple(core) + (gains, heads, ffn, attn) + tuple(arrays),
    )


def turn_kernel(x1_ref, x2_ref, in1_ref, out1_ref, in2_ref, out2_ref, x1, x2, in1, out1, in2, out2, sem):
    loads = save_all(sem, (x1_ref, x1), (x2_ref, x2))
    stores = []
    for k, (load, x, a, b, to_a, to_b) in enumerate(
        ((loads[0], x1, in1, out1, in1_ref, out1_ref), (loads[1], x2, in2, out2, in2_ref, out2_ref))
    ):
        load.wait()
        for lo in range(0, x.shape[1], 128):
            at = slice(lo, lo + 128)
            for g in range(2):
                a[:, g, at] = x[g, at].astype(f32).T
            b[at] = x[2, at].astype(f32)
        stores += save_all(sem, (a, to_a), (b, to_b), first=2 + 2 * k)
    for copy in stores:
        copy.wait()


def turn(x1, x2):
    _, n, feat = x1.shape
    out = (shape((feat, 2, n), f32), shape((n, feat), f32)) * 2
    return pl.pallas_call(
        turn_kernel, name="turn", out_shape=out, in_specs=[ANY, ANY], out_specs=(ANY,) * 4,
        scratch_shapes=[pltpu.VMEM(x1.shape, bf16)] * 2 + [pltpu.VMEM(x.shape, f32) for x in out] + [DMA((6,))],
        compiler_params=pltpu.CompilerParams(vmem_limit_bytes=LIMIT << 20),
    )(x1, x2)


def per_device(
    hidden_in, lengths, conv_norm, conv_in, conv_kernel, conv_out, conv_ffn_norm, conv_ffn_in,
    conv_ffn_out, attn_norm, attn_q, attn_kv, q_gain, k_gain, attn_out, attn_ffn_norm,
    attn_ffn_in, attn_ffn_out, grad_out,
):
    rows, cols, dps = lax.axis_size("rows"), lax.axis_size("cols"), lax.axis_size("dp")
    tp = 2 * rows
    r, c, d = lax.axis_index("rows"), lax.axis_index("cols"), lax.axis_index("dp")
    pair = lax.rem(d, 2)
    me = pair * rows + r
    slots, seqs, feat = hidden_in.shape
    sh = slots // rows

    def halves(x, axis):
        return lax.dynamic_slice_in_dim(x, pair * rows, rows, axis)

    def cut_in(w):
        parts, width = w.shape[1], w.shape[2] // tp
        x = w.astype(bf16).transpose(1, 2, 0).reshape(parts, tp, width, feat)
        return halves(x, 1).transpose(1, 0, 2, 3).reshape(rows, parts * width, feat)

    def cut_out(w):
        return halves(w.astype(bf16).reshape(tp, -1, feat), 0)

    def cut(w_in, w_out):
        return jnp.concatenate([cut_in(w_in), cut_out(w_out)], axis=1)

    wide = conv_ffn_in.shape[2] // tp
    chan = conv_in.shape[2] // tp
    channels = cols * chan
    slot_ids = c * slots + jnp.arange(slots, dtype=jnp.int32)
    keep = (slot_ids[None, :] < lengths[:, None]).astype(f32)[:, :, None]
    gains_own = jnp.stack([conv_norm, conv_ffn_norm, attn_norm, attn_ffn_norm])
    conv_all, begin, ffn1_cut, gains, taps, lens = start_exchange(
        1, cut(conv_in, conv_out), hidden_in.transpose(1, 0, 2) * keep, cut(conv_ffn_in, conv_ffn_out),
        jnp.pad(gains_own, ((0, 4), (0, 0))), jnp.pad(conv_kernel, ((0, 8 - CONV), (0, 0))),
        jnp.pad(lengths[None], ((0, 7), (0, 128 - seqs))), rows, cols,
    )
    gains = gains[:4, None]
    kern = lax.dynamic_slice_in_dim(taps[:, :CONV], me * chan, chan, 2)
    kern = kern.transpose(1, 0, 2).reshape(CONV, channels)
    length = lax.dynamic_slice_in_dim(lens[:, 0, :seqs].reshape(2 * seqs), c, 1)

    per_col = tp // cols
    q_w = attn_q.shape[1] // per_col
    kv_w = attn_kv.shape[2] // per_col
    parts = jnp.concatenate(
        [
            attn_q.astype(bf16).T.reshape(per_col, q_w, feat),
            attn_kv[:, 0].astype(bf16).T.reshape(per_col, kv_w, feat),
            attn_kv[:, 1].astype(bf16).T.reshape(per_col, kv_w, feat),
            attn_out.astype(bf16).reshape(per_col, q_w, feat),
        ],
        axis=1,
    )
    w_ffn1 = lax.all_gather(ffn1_cut, "cols", axis=0)

    def after(x, y):
        return lax.optimization_barrier((x, y))[0]

    after_conv, n_conv, mixed, product, gate_edge = conv_forward(3, begin, gains[0], conv_all, kern)
    attn_cut, ffn2_cut = second_exchange(
        2, after(parts, after_conv).reshape(per_col, cols, -1, feat), cut(after(attn_ffn_in, after_conv), after(attn_ffn_out, after_conv)), ()
    )
    f2_rows = SECOND_ROWS
    f2_at = [sum(f2_rows[:i]) for i in range(4)]
    after_ffn, n_1, gu_1, w_1, attn_all, f2_a = ffn_forward(
        4, after_conv, gains[1], (w_ffn1,), wide,
        [Gather(attn_cut, 0, attn_cut.shape[0]), Gather(ffn2_cut, f2_at[0], f2_rows[0])],
    )
    attn_all = attn_all.reshape(-1, D)
    frequency = jnp.power(rope_base, -(jnp.arange(HD // 2, dtype=f32) * 2.0) / HD)
    angles = slot_ids.astype(f32)[:, None] * frequency[None, :]
    cos, sin = jnp.cos(angles), jnp.sin(angles)
    tables = (
        jnp.concatenate([cos] * 4, axis=1).reshape(2, 2 * sh, 2 * HD),
        jnp.concatenate([-sin, sin] * 2, axis=1).reshape(2, 2 * sh, 2 * HD),
        jnp.tile(q_gain, 2)[None],
        jnp.tile(k_gain, 2)[None],
    )
    after_attn, n_attn, raw, seq, attended, grad_final, f2_b, f2_c, f2_d = attention_forward(
        5, after_ffn, gains[2], attn_all, tables, length,
        [
            Rows("tokens", grad_out.transpose(1, 0, 2) * keep, 1),
            Gather(ffn2_cut, f2_at[1], f2_rows[1], 0), Gather(ffn2_cut, f2_at[2], f2_rows[2], 1),
            Gather(ffn2_cut, f2_at[3], f2_rows[3], 2),
        ],
    )
    final, grad_attn_res, gain_p3, dw_2 = ffn_both(
        6, after_attn, gains[3], grad_final, (f2_a, f2_b, f2_c, f2_d), wide, ffn2_cut
    )

    def over_pairs(x):
        return x if dps == 2 else lax.psum(x * jnp.asarray(0.5, x.dtype), "dp")

    def native(x):
        return x[:-1].transpose(2, 0, 1).astype(f32), x[-1].astype(f32)

    b2_rows, b1_rows = SECOND_BACK, FIRST_BACK
    b2_at = [sum(b2_rows[:i]) for i in range(4)]
    grad_after_ffn, gain_p2, head_parts, grad_attn, final_here, r2_a, r2_b, r2_c = attention_backward(
        8, grad_attn_res, after_ffn, gains[2], attn_all, tables, length, n_attn, raw, seq, attended,
        [Rows("back", final, 1), Reduce(dw_2, 0, b2_rows[0], 0),
         Reduce(dw_2, b2_at[1], b2_rows[1], 1), Reduce(dw_2, b2_at[2], b2_rows[2], 2)],
    )
    grad_attn = grad_attn.reshape(cols, -1, D)
    grad_after_conv, gain_p1, dw_1, r_attn, r2_d = ffn_backward(
        9, grad_after_ffn, after_conv, gains[1], w_1, n_1, gu_1, wide, cols,
        [Reduce(grad_attn, 0, grad_attn.shape[1]), Reduce(dw_2, b2_at[3], b2_rows[3])],
    )
    output = (final_here * keep).transpose(1, 0, 2)
    zero = jnp.zeros((), jnp.int32)
    heads = jnp.concatenate([head_parts[:1, :HD] + head_parts[:1, HD:], head_parts[1:, :HD]], axis=1)
    got2, got1, got0, sums, taps_all, grad_here, _, got_a = conv_finish(
        10, (grad_after_conv, begin, gains[0], conv_all, kern, n_conv, mixed, product, gate_edge),
        jnp.concatenate([gain_p1, gain_p2, gain_p3]), jnp.pad(heads, ((0, 0), (0, D - 2 * HD))), dw_1, r_attn,
        (r2_a, r2_b, r2_c, r2_d), b2_at, [(sum(b1_rows[:i]), n) for i, n in enumerate(b1_rows)], wide, chan, per_col,
    )
    got2, got1, got0, got_a, sums, taps_all = (over_pairs(x) for x in (got2, got1, got0, got_a, sums, taps_all))
    got_a = got_a.reshape(per_col, -1, feat)
    g_attn_ffn_in, g_attn_ffn_out, g_conv_ffn_in, g_conv_ffn_out = turn(got2, got1)
    g_q = got_a[:, :q_w].astype(f32).reshape(-1, feat).T
    g_kv = jnp.stack(
        [
            got_a[:, q_w : q_w + kv_w].astype(f32).reshape(-1, feat).T,
            got_a[:, q_w + kv_w : q_w + 2 * kv_w].astype(f32).reshape(-1, feat).T,
        ],
        axis=1,
    )
    g_aout = got_a[:, q_w + 2 * kv_w :].astype(f32).reshape(-1, feat)
    grad_in = (grad_here * keep).transpose(1, 0, 2)
    g_conv_in, g_conv_out = native(got0)
    g_gain = lax.dynamic_slice(sums, (zero, r * feat), (4, feat))
    g_kern = lax.dynamic_slice(taps_all, (zero, jnp.int32(5), c * chan), (tp, CONV, chan))
    g_kern = g_kern.transpose(1, 0, 2).reshape(conv_kernel.shape)
    return (
        output, grad_in, g_gain[0], g_conv_in, g_kern, g_conv_out, g_gain[1],
        g_conv_ffn_in, g_conv_ffn_out, g_gain[2], g_q, g_kv, sums[4, :HD], sums[4, HD : 2 * HD], g_aout,
        g_gain[3], g_attn_ffn_in, g_attn_ffn_out,
    )


def solution(mesh):
    tokens, vec, mat = P("cols", "dp", "rows"), P("rows"), P("rows", "cols")
    mat3, out, taps = P("rows", None, "cols"), P("cols", "rows"), P(None, "cols")
    weights = (vec, mat3, taps, out, vec, mat3, out, vec, mat, mat3, P(), P(), out, vec, mat3, out)
    return jax.shard_map(
        per_device,
        mesh=mesh,
        in_specs=(tokens, P("dp")) + weights + (tokens,),
        out_specs=(tokens, tokens) + weights,
        check_vma=False,
    )
```

```python
import functools

import jax
import jax.numpy as jnp
from jax import lax
from jax.experimental import pallas as pl
from jax.experimental.pallas import tpu as pltpu
from jax.sharding import PartitionSpec as P

D = 1024
HD = 64
CONV = 3
epsilon = 1e-05
rope_base = 1000000.0
bf16 = jnp.bfloat16
f32 = jnp.float32
MESH = pl.DeviceIdType.MESH
LIMIT = 62
SECOND_ROWS = (160, 48, 48, 80)
SECOND_BACK = (64, 128, 128, 112)
FIRST_BACK = (208, 128, 96)
ANY = pl.BlockSpec(memory_space=pl.ANY)
VMEM = pl.BlockSpec(memory_space=pltpu.VMEM)


def dot(a, b, ca, cb):
    return lax.dot_general(a, b, (((ca,), (cb,)), ((), ())), preferred_element_type=f32)


def place(m):
    d, r = lax.axis_index("dp"), lax.axis_index("rows")
    pair, half = lax.rem(d, 2), r // 2
    return lax.rem(pair + lax.rem(m, 2), 2), lax.rem(half + m // 2, 2)


def peer(m):
    d, r = lax.axis_index("dp"), lax.axis_index("rows")
    pm, hm = place(m)
    return {"dp": d - lax.rem(d, 2) + pm, "rows": hm * 2 + lax.rem(r, 2)}


def sibling():
    r = lax.axis_index("rows")
    return {"rows": r + 1 - 2 * lax.rem(r, 2)}


def remote(src, dst, send, recv, to):
    return pltpu.make_async_remote_copy(
        src_ref=src, dst_ref=dst, send_sem=send, recv_sem=recv, device_id=to, device_id_type=MESH
    )


def share(sh, mine):
    k = lax.rem(lax.axis_index("rows"), 2)
    k = k if mine else 1 - k
    return pl.ds(pl.multiple_of(k * sh, 16), sh)


def greet():
    barrier = pltpu.get_barrier_semaphore()
    rows, cols = lax.axis_size("rows"), lax.axis_size("cols")
    r, c = lax.axis_index("rows"), lax.axis_index("cols")
    to = [peer(1), peer(3)] + [{"rows": lax.rem(r + k, rows)} for k in range(1, rows)]
    to += [{"cols": lax.rem(c + k, cols)} for k in range(1, cols)]
    for device in to:
        pl.semaphore_signal(barrier, inc=1, device_id=device, device_id_type=MESH)
    pl.semaphore_wait(barrier, len(to))


def gather_copy(buf, sh, sems, m, to):
    pm, hm = place(0)
    own = buf.at[pm, :, hm, share(sh, True)]
    return remote(own, own, sems.at[0, m], sems.at[1, m], to)


def relay_copy(buf, sh, sems, m):
    pm, hm = place(m)
    part = buf.at[pm, m - 1, hm, share(sh, True)]
    return remote(part, part, sems.at[8, m], sems.at[9, m], peer(3 - m))


def start_gather(buf, sh, sems):
    gather_copy(buf, sh, sems, 0, sibling()).start()
    for m in (1, 2):
        gather_copy(buf, sh, sems, m, peer(m)).start()


def forward_copy(buf, sh, sems, m, mine):
    pm, hm = place(m)
    part = buf.at[pm, :, hm, share(sh, mine)]
    return remote(part, part, sems.at[2, m], sems.at[3, m], sibling())


def arrive(buf, sh, sems, m):
    def come(src, i, j):
        remote(src, src, sems.at[i - 1, j], sems.at[i, j], sibling()).wait_recv()

    @pl.when(m == 0)
    def _():
        pm, hm = place(0)
        come(buf.at[pm, :, hm, share(sh, False)], 1, 0)

    @pl.when(m == 1)
    def _():
        for j in (1, 2):
            pj, hj = place(j)
            come(buf.at[pj, :, hj, share(sh, True)], 1, j)
            relay_copy(buf, sh, sems, j).start()
            forward_copy(buf, sh, sems, j, True).start()

    @pl.when(m == 3)
    def _():
        pj, hj = place(3)
        for j in (1, 2):
            come(buf.at[pj, j - 1, hj, share(sh, True)], 9, j)
        forward_copy(buf, sh, sems, 3, True).start()

    @pl.when(m > 0)
    def _():
        forward_copy(buf, sh, sems, m, False).wait_recv()


def end_gather(buf, sh, sems):
    gather_copy(buf, sh, sems, 0, sibling()).wait_send()
    for m in (1, 2):
        gather_copy(buf, sh, sems, m, peer(m)).wait_send()
        relay_copy(buf, sh, sems, m).wait_send()
    for m in (1, 2, 3):
        forward_copy(buf, sh, sems, m, True).wait_send()


def sum_copy(ys, yr, sems, m, half):
    return remote(ys.at[m, half], yr.at[m, half], sems.at[6, 2 * half + m - 1], sems.at[7, 2 * half + m - 1], peer(m))


def relay_sum_copy(ys, yr, sems, half):
    return remote(ys.at[3, half], yr.at[3, half], sems.at[10, half], sems.at[11, half], peer(half + 1))


def across_copy(part, xr, sh, sems, m):
    return remote(
        part.at[m, :, share(sh, False)], xr.at[m], sems.at[4, m], sems.at[5, m], sibling()
    )


def scatter(part, xr, ys, yr, sh, sems, m):
    across_copy(part, xr, sh, sems, m).wait_recv()
    both = part[m, :, share(sh, True)] + xr[m]
    xr[m] = both
    ys[m] = both.astype(bf16)

    @pl.when(m == 3)
    def _():
        for half in (0, 1):
            relay_sum_copy(ys, yr, sems, half).start()

    for j in (1, 2):

        @pl.when(m == j)
        def _():
            sum_copy(ys, yr, sems, j, j - 1).start()


def end_scatter(part, xr, ys, yr, sh, sems):
    for half in (0, 1):
        m = 2 - half
        relay_sum_copy(ys, yr, sems, half).wait_recv()
        ys[m, half] = (xr[m, half] + yr[3, half].astype(f32)).astype(bf16)
        sum_copy(ys, yr, sems, m, half).start()
    total = xr[0]
    for m in (1, 2):
        for half in (0, 1):
            sum_copy(ys, yr, sems, m, half).wait_recv()
        total = total + yr[m].astype(f32)
    for half in (0, 1):
        relay_sum_copy(ys, yr, sems, half).wait_send()
        for m in (1, 2):
            sum_copy(ys, yr, sems, m, half).wait_send()
    for m in range(4):
        across_copy(part, xr, sh, sems, m).wait_send()
    return total


def lines(src_of, dst_of, sems):
    count, c = lax.axis_size("cols"), lax.axis_index("cols")
    sends, gets = [], []
    for k in range(1, count):
        to, come = lax.rem(c + k, count), lax.rem(c + count - k, count)
        sends.append(remote(src_of(to), dst_of(c), sems.at[0, k], sems.at[1, k], {"cols": to}))
        gets.append(remote(src_of(c), dst_of(come), sems.at[0, k], sems.at[1, k], {"cols": to}))
    return sends, gets, pltpu.make_async_copy(src_of(c), dst_of(c), sems.at[0, 0])


class Side:
    def relay(self):
        pass


class Gather(Side):
    def __init__(self, array, lo, n, phase=0):
        self.args = (array,)
        self.phase = phase
        self.lo, self.n = lo, n
        self.relayed = False
        assert lax.axis_size("cols") == 4
        self.outs = ((shape((4, n, D), array.dtype), ANY),)
        self.scratch = [DMA((2, 5))]

    def bind(self, ins, outs, scratch):
        self.src, self.slot, self.sems = ins[0].at[pl.ds(self.lo, self.n)], lambda z: outs[0].at[z], scratch[0]

    @classmethod
    def of(cls, src, slot, sems):
        self = cls.__new__(cls)
        self.relayed = False
        self.src, self.slot, self.sems = src, slot, sems
        return self

    def send(self, t):
        c = lax.axis_index("cols")
        return remote(self.src, self.slot(c), self.sems.at[0, t], self.sems.at[1, c], {"cols": t})

    def pass_on(self):
        c = lax.axis_index("cols")
        part = self.slot(6 - 3 * c)
        return remote(part, part, self.sems.at[0, 4], self.sems.at[1, 6 - 3 * c], {"cols": 3 * c - 3})

    def local(self):
        return pltpu.make_async_copy(self.src, self.slot(lax.axis_index("cols")), self.sems.at[1, 4])

    def each(self, act):
        c = lax.axis_index("cols")
        for off in (2, -2, 1, -1):
            t = c + off

            @pl.when((t >= 0) & (t < 4))
            def _():
                act(self.send(t))

    def start(self):
        self.each(lambda copy: copy.start())
        self.local().start()

    def relay(self):
        self.relayed = True
        c = lax.axis_index("cols")

        @pl.when((c == 1) | (c == 2))
        def _():
            self.pass_on().wait_recv()
            self.pass_on().start()

    def finish(self):
        if not self.relayed:
            self.relay()
        c = lax.axis_index("cols")
        for s in range(4):

            @pl.when((s != c) & (s + 3 * c != 6))
            def _():
                part = self.slot(s)
                remote(part, part, self.sems.at[0, s], self.sems.at[1, s], {"cols": s}).wait_recv()

        self.each(lambda copy: copy.wait_send())

        @pl.when((c == 1) | (c == 2))
        def _():
            self.pass_on().wait_send()

        self.local().wait()


class Reduce(Side):
    def __init__(self, array, lo, n, phase=0):
        self.args = (array,)
        self.phase = phase
        self.lo, self.n = lo, n
        self.relayed = False
        self.outs = ((shape((n, D), array.dtype), VMEM),)
        self.scratch = self.buffers(n)

    @staticmethod
    def buffers(n):
        return [pltpu.VMEM((4, n, D), bf16), pltpu.VMEM((n, D), bf16), pltpu.VMEM((n, D), bf16), DMA((2, 6))]

    def bind(self, ins, outs, scratch):
        self.out = outs[0]
        self.got, self.far, self.own, self.sems = scratch
        self.src = ins[0].at[:, pl.ds(self.lo, self.n)]

    @classmethod
    def of(cls, src, out, scratch):
        self = cls.__new__(cls)
        self.relayed = False
        self.src, self.out, self.n = src, out, out.shape[0]
        self.got, self.far, self.own, self.sems = scratch
        return self

    def send(self, off):
        c = lax.axis_index("cols")
        t = c + off
        if abs(off) == 3:
            return remote(self.src.at[t], self.far, self.sems.at[0, t], self.sems.at[1, 4], {"cols": c + off // 3})
        return remote(self.src.at[t], self.got.at[c], self.sems.at[0, t], self.sems.at[1, c], {"cols": t})

    def send_sum(self):
        c = lax.axis_index("cols")
        t = 6 - 3 * c
        return remote(self.own, self.got.at[c], self.sems.at[0, t], self.sems.at[1, c], {"cols": t})

    def each(self, act, offs):
        c = lax.axis_index("cols")
        for off in offs:
            t = c + off
            ok = (t >= 0) & (t < 4)
            if abs(off) == 2:
                ok = ok & (c != (1 if off == 2 else 2))

            @pl.when(ok)
            def _():
                act(self.send(off))

    def local(self):
        c = lax.axis_index("cols")
        return pltpu.make_async_copy(self.src.at[c], self.got.at[c], self.sems.at[0, 4])

    def load(self):
        c = lax.axis_index("cols")
        return pltpu.make_async_copy(self.src.at[6 - 3 * c], self.own, self.sems.at[0, 5])

    def start(self):
        self.start_far()
        self.start_near()

    def start_far(self):
        self.each(lambda copy: copy.start(), (3, -3))

    def start_near(self):
        c = lax.axis_index("cols")
        self.each(lambda copy: copy.start(), (2, -2, 1, -1))
        self.local().start()

        @pl.when((c == 1) | (c == 2))
        def _():
            self.load().start()

        @pl.when((c == 0) | (c == 3))
        def _():
            self.got[3 - c] = jnp.zeros((self.n, D), bf16)

    def blocks(self):
        return [slice(a, min(a + 48, self.n)) for a in range(0, self.n, 48)]

    def relay(self):
        self.relayed = True
        c = lax.axis_index("cols")

        @pl.when((c == 1) | (c == 2))
        def _():
            self.load().wait()
            remote(self.far, self.far, self.sems.at[0, 0], self.sems.at[1, 4], {"cols": 1}).wait_recv()
            for at in self.blocks():
                self.own[at] = (self.own[at].astype(f32) + self.far[at].astype(f32)).astype(bf16)

            self.send_sum().start()

    def finish(self):
        if not self.relayed:
            self.relay()
        c = lax.axis_index("cols")
        for s in range(4):

            @pl.when((s != c) & (s - c < 3) & (c - s < 3))
            def _():
                part = self.got.at[s]
                remote(part, part, self.sems.at[0, s], self.sems.at[1, s], {"cols": s}).wait_recv()

        self.local().wait()
        for at in self.blocks():
            self.out[at] = jnp.sum(self.got[:, at].astype(f32), axis=0).astype(bf16)
        self.each(lambda copy: copy.wait_send(), (3, -3, 2, -2, 1, -1))

        @pl.when((c == 1) | (c == 2))
        def _():
            self.send_sum().wait_send()


class Rows(Side):
    def __init__(self, kind, array, phase=0):
        self.args = (array,)
        self.phase = phase
        self.kind = kind
        rows = lax.axis_size("rows")
        a, b, f = array.shape
        dims = (a, b // rows, f * rows) if kind == "tokens" else (a, b * rows, f // rows)
        self.outs = ((shape(dims, array.dtype), ANY),)
        self.scratch = [DMA((2, 1, 4))]

    def bind(self, ins, outs, scratch):
        self.work = row_copies(self.kind, ins[0], outs[0], scratch[0], 0)

    def start(self):
        begin_all(self.work)

    def finish(self):
        end_all(self.work)


class AttentionReturn:
    def __init__(self, src, dst, sems, per_col):
        self.src, self.dst, self.sems, self.per_col = src, dst, sems, per_col
        self.rows, self.cols = lax.axis_size("rows"), lax.axis_size("cols")
        self.d, self.r, self.c = lax.axis_index("dp"), lax.axis_index("rows"), lax.axis_index("cols")
        self.pair = lax.rem(self.d, 2)
        self.me = self.pair * self.rows + self.r
        self.gets_direct = per_col * self.c // self.rows == self.pair

    def each(self, act, local):
        owner, half = self.me // self.per_col, lax.rem(self.me, self.per_col)
        width = self.dst.shape[3]
        for k in range(self.rows):
            own = (k == self.r) & (owner == self.c)
            here, there = band(self.src, k, width), self.dst.at[half, self.c]

            @pl.when(jnp.logical_not(own))
            def _():
                act(remote(here, there, self.sems.at[0, k], self.sems.at[1, half * self.cols + self.c],
                           {"rows": k, "cols": owner}))

            @pl.when(own)
            def _():
                local(pltpu.make_async_copy(here, there, self.sems.at[0, k]))

    def start(self):
        self.each(lambda copy: copy.start(), lambda copy: copy.start())

    def finish(self):
        for h in range(self.per_col):
            source = self.c * self.per_col + h
            for z in range(self.cols):
                part = self.dst.at[h, z]
                mine = (source == self.me) & (z == self.c)

                @pl.when(self.gets_direct & jnp.logical_not(mine))
                def _():
                    to = {"rows": lax.rem(source, self.rows), "cols": z}
                    remote(part, part, self.sems.at[0, 0], self.sems.at[1, h * self.cols + z], to).wait_recv()

        self.each(lambda copy: copy.wait_send(), lambda copy: copy.wait())


def begin_all(work):
    sends, _, local = work
    for copy in sends:
        copy.start()
    local.start()


def end_all(work):
    sends, gets, local = work
    for copy in gets:
        copy.wait_recv()
    for copy in sends:
        copy.wait_send()
    local.wait()


def start_sides(sides, phase=0):
    for side in sides:
        if side.phase == phase:
            side.start()


def relay_sides(sides, phase=0):
    for side in sides:
        if side.phase == phase:
            side.relay()


def finish_sides(sides):
    for side in sides:
        side.finish()


def rms(x):
    return lax.rsqrt(jnp.mean(x * x, axis=-1, keepdims=True) + epsilon)


def put_own(buf, sh, value):
    pm, hm = place(0)
    buf[pm, :, hm, share(sh, True)] = value.astype(bf16)


def norm_own(x_ref, gain_ref):
    x = x_ref[...]
    return x * rms(x) * gain_ref[...]


def norm_back(n, x_ref, gain_ref, grad_ref, out_ref, gain_out):
    x = x_ref[...]
    q = rms(x)
    scaled = n * gain_ref[...]
    dots = jnp.mean(scaled * x, axis=-1, keepdims=True)
    out_ref[...] = grad_ref[...] + scaled * q - x * (q * q * q) * dots
    gain_out[...] = jnp.sum(n * x * q, axis=(0, 1))[None]


def flat(x):
    return x.reshape(x.shape[0] * x.shape[1], x.shape[2])


def tiles(width):
    return [(a, min(256, width - a)) for a in range(0, width, 256)]


def columns(width, act):
    def one(j, carry):
        act(pl.ds(pl.multiple_of(j * 256, 256), 256))
        return carry

    lax.fori_loop(0, width // 256, one, 0)


def padded(width):
    return -(-width // 128) * 128


def segments(lo, n, wide):
    cuts = []
    for g in range(lo // wide, -(-(lo + n) // wide)):
        a, b = max(lo, g * wide), min(lo + n, (g + 1) * wide)
        cuts.append((g, a - g * wide, a - lo, b - a))
    return cuts


def first_rows(arrays, axis):
    return [sum(x.shape[axis] for x in arrays[:i]) for i in range(len(arrays))]


def load_copies(parts, wbuf, wide, sem):
    copies = []
    for ref, lo in zip(parts, first_rows(parts, 1)):
        for g, at, here, n in segments(lo, ref.shape[1], wide):
            for c in range(ref.shape[0]):
                copies.append(pltpu.make_async_copy(
                    ref.at[c, pl.ds(here, n)], wbuf.at[g, pl.ds(c * wide + at, n)], sem.at[len(copies)]
                ))
    return copies


def zero_pad(wbuf, used):
    if wbuf.shape[1] > used:
        wbuf[:, used:] = jnp.zeros((3, wbuf.shape[1] - used, wbuf.shape[2]), bf16)


def ffn_forward_kernel(sh, wide, count, last, sides, x_ref, gain_ref, *refs):
    parts, refs = refs[:count], refs[count:]
    if last:
        tail_ref, refs = refs[0], refs[1:]
    out_ref, n_ref, gu_ref, save_ref, buf, wbuf, gu, hid, part, xr, ys, yr, sems, wsem, osem, gsem = refs
    cols = parts[0].shape[0]
    loads = load_copies(parts, wbuf, wide, wsem)
    for copy in loads:
        copy.start()
    zero_pad(wbuf, cols * wide)
    put_own(buf, sh, norm_own(x_ref, gain_ref))
    greet()
    start_gather(buf, sh, sems)
    if last:
        tail = Gather.of(
            tail_ref.at[pl.ds(3 * wide - last, last)],
            lambda z: wbuf.at[2, pl.ds(pl.multiple_of(z * wide + wide - last, 16), last)],
            gsem,
        )
        tail.start()
    start_sides(sides)
    for copy in loads:
        copy.wait()
    width = wbuf.shape[1]

    def step(m, carry):
        arrive(buf, sh, sems, m)
        if last:
            pl.when(m == 2)(tail.relay)
        pl.when(m == 3)(lambda: relay_sides(sides))
        pm, hm = place(m)
        x = flat(buf[pm, :, hm])
        for a, n in tiles(width):
            g = dot(x, wbuf[0, a : a + n], 1, 1)
            u = dot(x, wbuf[1, a : a + n], 1, 1)
            gu[m, 0, :, a : a + n] = g
            gu[m, 1, :, a : a + n] = u
            hid[m, :, a : a + n] = (g * jax.nn.sigmoid(g) * u).astype(bf16)
        pltpu.make_async_copy(gu.at[m], gu_ref.at[m], osem.at[m]).start()
        return carry

    lax.fori_loop(0, 4, step, 0)
    if last:
        tail.finish()
    save = pltpu.make_async_copy(wbuf, save_ref, osem.at[5])
    save.start()
    keep_n = pltpu.make_async_copy(buf, n_ref, osem.at[4])
    keep_n.start()

    def merge_step(t, carry):
        m = 3 - t

        def down(at):
            part[m, :, :, at] = dot(hid[m], wbuf[2, :, at], 1, 0).reshape(part.shape[1], part.shape[2], 256)

        columns(D, down)
        across_copy(part, xr, sh, sems, m).start()

        @pl.when(m < 3)
        def _():
            scatter(part, xr, ys, yr, sh, sems, m + 1)

        return carry

    lax.fori_loop(0, 4, merge_step, 0)
    scatter(part, xr, ys, yr, sh, sems, 0)
    out_ref[...] = x_ref[...] + end_scatter(part, xr, ys, yr, sh, sems)
    end_gather(buf, sh, sems)
    for m in range(4):
        pltpu.make_async_copy(gu.at[m], gu_ref.at[m], osem.at[m]).wait()
    keep_n.wait()
    save.wait()
    finish_sides(sides)


def ffn_backward_kernel(sh, wide, sides, grad_ref, x_ref, gain_ref, w_ref, n_ref, gu_ref,
                        out_ref, gain_out, dw_ref,
                        buf, nbuf, wbuf, gu, hid, dw, part, xr, ys, yr, sems, wsem, osem):
    cols = dw_ref.shape[0]
    gloads = [pltpu.make_async_copy(gu_ref.at[m], gu.at[m], osem.at[m]) for m in range(4)]
    nload = pltpu.make_async_copy(n_ref, nbuf, osem.at[4])
    loads = [pltpu.make_async_copy(w_ref, wbuf, osem.at[5])]
    for copy in loads + gloads + [nload]:
        copy.start()
    put_own(buf, sh, grad_ref[...])
    greet()
    start_gather(buf, sh, sems)
    start_sides(sides)
    for copy in loads + gloads:
        copy.wait()
    width = wbuf.shape[1]

    def step(m, carry):
        arrive(buf, sh, sems, m)
        pl.when(m == 3)(lambda: relay_sides(sides))
        pm, hm = place(m)
        gg = flat(buf[pm, :, hm])
        for a, n in tiles(width):
            gh = dot(gg, wbuf[2, a : a + n], 1, 1)
            g = gu[m, 0, :, a : a + n]
            u = gu[m, 1, :, a : a + n]
            s = jax.nn.sigmoid(g)
            silu = g * s
            shape = (part.shape[1], part.shape[2], n)
            hid[0, pm, :, hm, :, a : a + n] = (gh * u * (s * (1.0 + g * (1.0 - s)))).astype(bf16).reshape(shape)
            hid[1, pm, :, hm, :, a : a + n] = (gh * silu).astype(bf16).reshape(shape)
            hid[2, pm, :, hm, :, a : a + n] = (silu * u).astype(bf16).reshape(shape)

        def back(at):
            y = dot(flat(hid[0, pm, :, hm]), wbuf[0, :, at], 1, 0) + dot(flat(hid[1, pm, :, hm]), wbuf[1, :, at], 1, 0)
            part[m, :, :, at] = y.reshape(part.shape[1], part.shape[2], 256)

        columns(D, back)
        across_copy(part, xr, sh, sems, m).start()

        @pl.when(m > 0)
        def _():
            scatter(part, xr, ys, yr, sh, sems, m - 1)

        return carry

    lax.fori_loop(0, 4, step, 0)
    scatter(part, xr, ys, yr, sh, sems, 3)
    nload.wait()
    tokens = 8 * buf.shape[3]

    def grads(other, g):
        def one(i, carry):
            at = pl.ds(pl.multiple_of(i * 128, 128), 128)
            left = hid[g, :, :, :, :, at].reshape(tokens, 128)
            dw[g, at] = dot(left, other[...].reshape(tokens, D), 0, 0).astype(bf16)
            return carry

        lax.fori_loop(0, width // 128, one, 0)

    grads(nbuf, 0)
    grads(nbuf, 1)
    grads(buf, 2)
    stores = [
        pltpu.make_async_copy(
            dw.at[g, pl.ds(c * wide, wide)], dw_ref.at[c, pl.ds(g * wide, wide)], wsem.at[c * 3 + g]
        )
        for c in range(cols)
        for g in range(3)
    ]
    for copy in stores:
        copy.start()
    n = end_scatter(part, xr, ys, yr, sh, sems)
    norm_back(n, x_ref, gain_ref, grad_ref, out_ref, gain_out)
    end_gather(buf, sh, sems)
    for copy in stores:
        copy.wait()
    finish_sides(sides)


def ffn_both_kernel(sh, wide, count, last, sides, x_ref, gain_ref, grad_ref, *refs):
    parts, refs = refs[:count], refs[count:]
    if last:
        tail_ref, refs = refs[0], refs[1:]
    out_ref, grad_out, gain_out, dw_ref, buf, gbuf, wbuf, gu, hid, dw = refs[:10]
    one, two = refs[10:14] + refs[18:19], refs[14:18] + refs[19:20]
    wsem, dsem, gsem = refs[20:]
    cols = dw_ref.shape[0]
    sems, gsems = one[4], two[4]
    loads = load_copies(parts, wbuf, wide, wsem)
    for copy in loads:
        copy.start()
    zero_pad(wbuf, cols * wide)
    put_own(buf, sh, norm_own(x_ref, gain_ref))
    put_own(gbuf, sh, grad_ref[...])
    greet()
    start_gather(buf, sh, sems)
    if last:
        tail = Gather.of(
            tail_ref.at[pl.ds(3 * wide - last, last)],
            lambda z: wbuf.at[2, pl.ds(pl.multiple_of(z * wide + wide - last, 16), last)],
            gsem,
        )
        tail.start()
    start_gather(gbuf, sh, gsems)
    start_sides(sides)
    for copy in loads:
        copy.wait()
    width = wbuf.shape[1]
    tokens = 8 * buf.shape[3]

    def out(state):
        part, xr, ys, yr, sem = state
        return part, xr, ys, yr, sh, sem

    def step(m, carry):
        arrive(buf, sh, sems, m)
        if last:
            pl.when(m == 2)(tail.relay)
        pm, hm = place(m)
        x = flat(buf[pm, :, hm])
        for a, n in tiles(width):
            g = dot(x, wbuf[0, a : a + n], 1, 1)
            u = dot(x, wbuf[1, a : a + n], 1, 1)
            gu[m, 0, :, a : a + n] = g
            gu[m, 1, :, a : a + n] = u
            h = (g * jax.nn.sigmoid(g) * u).astype(bf16)
            hid[2, pm, :, hm, :, a : a + n] = h.reshape(buf.shape[1], buf.shape[3], n)
        return carry

    lax.fori_loop(0, 4, step, 0)
    if last:
        tail.finish()

    def merge_step(t, carry):
        m = 3 - t
        pm, hm = place(m)
        part = one[0]

        def down(at):
            y = dot(flat(hid[2, pm, :, hm]), wbuf[2, :, at], 1, 0)
            part[m, :, :, at] = y.reshape(part.shape[1], part.shape[2], 256)

        columns(D, down)
        across_copy(part, one[1], sh, sems, m).start()

        @pl.when(m < 3)
        def _():
            scatter(*out(one), m + 1)

        return carry

    lax.fori_loop(0, 4, merge_step, 0)
    scatter(*out(one), 0)

    def back_step(m, carry):
        arrive(gbuf, sh, gsems, m)

        @pl.when(m == 2)
        def _():
            out_ref[...] = x_ref[...] + end_scatter(*out(one))

        pm, hm = place(m)
        part = two[0]
        gg = flat(gbuf[pm, :, hm])
        for a, n in tiles(width):
            gh = dot(gg, wbuf[2, a : a + n], 1, 1)
            g = gu[m, 0, :, a : a + n]
            u = gu[m, 1, :, a : a + n]
            s = jax.nn.sigmoid(g)
            size = (part.shape[1], part.shape[2], n)
            hid[0, pm, :, hm, :, a : a + n] = (gh * u * (s * (1.0 + g * (1.0 - s)))).astype(bf16).reshape(size)
            hid[1, pm, :, hm, :, a : a + n] = (gh * (g * s)).astype(bf16).reshape(size)

        def back(at):
            y = dot(flat(hid[0, pm, :, hm]), wbuf[0, :, at], 1, 0) + dot(flat(hid[1, pm, :, hm]), wbuf[1, :, at], 1, 0)
            part[m, :, :, at] = y.reshape(part.shape[1], part.shape[2], 256)

        columns(D, back)
        across_copy(part, two[1], sh, gsems, m).start()

        @pl.when(m > 0)
        def _():
            scatter(*out(two), m - 1)

        return carry

    lax.fori_loop(0, 4, back_step, 0)
    scatter(*out(two), 3)

    def grads(other, g):
        def rows(i, carry):
            at = pl.ds(pl.multiple_of(i * 128, 128), 128)
            left = hid[g, :, :, :, :, at].reshape(tokens, 128)
            dw[g, at] = dot(left, other[...].reshape(tokens, D), 0, 0).astype(bf16)
            return carry

        lax.fori_loop(0, width // 128, rows, 0)

    grads(buf, 0)
    grads(buf, 1)
    grads(gbuf, 2)
    stores = [
        pltpu.make_async_copy(
            dw.at[g, pl.ds(c * wide, wide)], dw_ref.at[c, pl.ds(g * wide, wide)], dsem.at[c * 3 + g]
        )
        for c in range(cols)
        for g in range(3)
    ]
    for copy in stores:
        copy.start()
    norm_back(end_scatter(*out(two)), x_ref, gain_ref, grad_ref, grad_out, gain_out)
    end_gather(buf, sh, sems)
    end_gather(gbuf, sh, gsems)
    for copy in stores:
        copy.wait()
    finish_sides(sides)


def shape(dims, kind):
    return jax.ShapeDtypeStruct(dims, kind)


def save_all(sem, *pairs, first=0):
    copies = [pltpu.make_async_copy(a, b, sem.at[first + i]) for i, (a, b) in enumerate(pairs)]
    for copy in copies:
        copy.start()
    return copies


def scatter_scratch(seqs, sh):
    return [
        pltpu.VMEM((4, seqs, 2 * sh, D), f32),
        pltpu.VMEM((4, seqs, sh, D), f32),
        pltpu.VMEM((4, seqs, sh, D), bf16),
        pltpu.VMEM((4, seqs, sh, D), bf16),
    ]


def call(kernel, name, cid, outs, out_specs, in_specs, scratch, args, flops=46 * 10**9, limit=LIMIT, sides=()):
    n_in, n_out, n_scratch = len(args), len(outs), len(scratch)
    side_in = [x for side in sides for x in side.args]
    side_out = [x for side in sides for x in side.outs]
    side_scratch = [x for side in sides for x in side.scratch]

    def body(*refs):
        ins, rest = refs[:n_in], refs[n_in:]
        extra_in, rest = rest[: len(side_in)], rest[len(side_in) :]
        out, rest = rest[:n_out], rest[n_out:]
        extra_out, rest = rest[: len(side_out)], rest[len(side_out) :]
        own, extra_scratch = rest[:n_scratch], rest[n_scratch:]
        for side in sides:
            a, b, s = len(side.args), len(side.outs), len(side.scratch)
            side.bind(extra_in[:a], extra_out[:b], extra_scratch[:s])
            extra_in, extra_out, extra_scratch = extra_in[a:], extra_out[b:], extra_scratch[s:]
        kernel(*((sides,) if sides is not None else ()), *ins, *out, *own)

    got = pl.pallas_call(
        body,
        name=name,
        out_shape=tuple(outs) + tuple(x[0] for x in side_out),
        in_specs=tuple(in_specs) + (ANY,) * len(side_in),
        out_specs=tuple(out_specs) + tuple(x[1] for x in side_out),
        scratch_shapes=list(scratch) + side_scratch,
        cost_estimate=pl.CostEstimate(flops=flops, bytes_accessed=10**7, transcendentals=0),
        compiler_params=pltpu.CompilerParams(
            collective_id=cid, has_side_effects=True, vmem_limit_bytes=limit << 20
        ),
    )(*args, *side_in)
    return got


DMA = pltpu.SemaphoreType.DMA


def ffn_forward(cid, x, gain, parts, wide, sides=(), tail=None):
    seqs, sh, _ = x.shape
    cols = parts[0].shape[0]
    width = padded(cols * wide)
    full = (2, seqs, 2, 2 * sh, D)
    rows = seqs * 2 * sh
    last = 3 * wide - sum(p.shape[1] for p in parts)
    assert 0 <= last <= wide and (last == 0 or tail is not None)
    args = (x, gain) + tuple(parts) + ((tail,) if last else ())
    return call(
        functools.partial(ffn_forward_kernel, sh, wide, len(parts), last), "ffn_forward", cid,
        (shape(x.shape, f32), shape(full, bf16), shape((4, 2, rows, width), f32), shape((3, width, D), bf16)),
        (VMEM, ANY, ANY, ANY), (VMEM, VMEM) + (ANY,) * (len(args) - 2),
        [
            pltpu.VMEM(full, bf16), pltpu.VMEM((3, width, D), bf16),
            pltpu.VMEM((4, 2, rows, width), f32), pltpu.VMEM((4, rows, width), bf16),
        ] + scatter_scratch(seqs, sh)
        + [DMA((12, 4)), DMA((cols * (len(parts) + 2),)), DMA((6,)), DMA((2, 5))],
        args, sides=sides,
    )


def ffn_both(cid, x, gain, grad, parts, wide, tail, sides=()):
    seqs, sh, _ = x.shape
    cols = parts[0].shape[0]
    width = padded(cols * wide)
    full = (2, seqs, 2, 2 * sh, D)
    rows = seqs * 2 * sh
    last = 3 * wide - sum(p.shape[1] for p in parts)
    assert 0 <= last <= wide
    args = (x, gain, grad) + tuple(parts) + ((tail,) if last else ())
    return call(
        functools.partial(ffn_both_kernel, sh, wide, len(parts), last), "ffn_both", cid,
        (shape(x.shape, f32), shape(x.shape, f32), shape((1, D), f32), shape((cols, 3 * wide, D), bf16)),
        (VMEM, VMEM, VMEM, ANY), (VMEM, VMEM, VMEM) + (ANY,) * (len(args) - 3),
        [
            pltpu.VMEM(full, bf16), pltpu.VMEM(full, bf16), pltpu.VMEM((3, width, D), bf16),
            pltpu.VMEM((4, 2, rows, width), f32), pltpu.VMEM((3,) + full[:4] + (width,), bf16),
            pltpu.VMEM((3, width, D), bf16),
        ] + scatter_scratch(seqs, sh) + scatter_scratch(seqs, sh)
        + [DMA((12, 4)), DMA((12, 4)), DMA((cols * (len(parts) + 2),)), DMA((3 * cols,)), DMA((2, 5))],
        args, sides=sides,
    )


def ffn_backward(cid, grad, x, gain, w, n, gu, wide, cols, sides=()):
    seqs, sh, _ = x.shape
    width = w.shape[1]
    full = (2, seqs, 2, 2 * sh, D)
    rows = seqs * 2 * sh
    return call(
        functools.partial(ffn_backward_kernel, sh, wide), "ffn_backward", cid,
        (shape(x.shape, f32), shape((1, D), f32), shape((cols, 3 * wide, D), bf16)),
        (VMEM, VMEM, ANY), (VMEM, VMEM, VMEM, ANY, ANY, ANY),
        [
            pltpu.VMEM(full, bf16), pltpu.VMEM(full, bf16), pltpu.VMEM((3, width, D), bf16),
            pltpu.VMEM((4, 2, rows, width), f32), pltpu.VMEM((3,) + full[:4] + (width,), bf16),
            pltpu.VMEM((3, width, D), bf16),
        ] + scatter_scratch(seqs, sh) + [DMA((12, 4)), DMA((3 * cols,)), DMA((6,))],
        (grad, x, gain, w, n, gu), sides=sides,
    )


def out_copy(stage, dest, sems, m, i):
    pm, hm = place(m)
    c = lax.axis_index("cols")
    s = pm * stage.shape[1] + i
    return s, remote(
        stage.at[m, i], dest.at[c, hm], sems.at[0, m * 2 + i], sems.at[1, c * 2 + hm], {"cols": s}
    )


def send_out(stage, dest, sems, m):
    pm, hm = place(m)
    c = lax.axis_index("cols")
    for i in range(stage.shape[1]):
        s, copy = out_copy(stage, dest, sems, m, i)

        @pl.when(s == c)
        def _():
            dest[c, hm] = stage[m, i]

        @pl.when(s != c)
        def _():
            copy.start()


def wait_out(stage, dest, sems):
    c = lax.axis_index("cols")
    for z in range(dest.shape[0]):
        for h in range(2):

            @pl.when(z != c)
            def _():
                got = dest.at[z, h]
                remote(got, got, sems.at[0, z * 2 + h], sems.at[1, z * 2 + h], {"cols": z}).wait_recv()


def end_out(stage, dest, sems):
    c = lax.axis_index("cols")
    for m in range(4):
        for i in range(stage.shape[1]):
            s, copy = out_copy(stage, dest, sems, m, i)

            @pl.when(s != c)
            def _():
                copy.wait_send()


def back_copy(stage, dest, sems, i, row=2):
    c = lax.axis_index("cols")
    seqs = dest.shape[1]
    return remote(
        stage.at[i], dest.at[c // seqs, lax.rem(c, seqs)], sems.at[row, i], sems.at[row + 1, c], {"cols": i}
    )


def send_back(stage, dest, sems, i, row=2):
    c = lax.axis_index("cols")
    seqs = dest.shape[1]

    @pl.when(i == c)
    def _():
        dest[c // seqs, lax.rem(c, seqs)] = stage[i]

    @pl.when(i != c)
    def _():
        back_copy(stage, dest, sems, i, row).start()


def wait_back(stage, dest, sems, row=2):
    c = lax.axis_index("cols")
    seqs = dest.shape[1]
    for s in range(stage.shape[0]):

        @pl.when(s != c)
        def _():
            got = dest.at[s // seqs, s % seqs]
            remote(got, got, sems.at[row, s], sems.at[row + 1, s], {"cols": s}).wait_recv()
            back_copy(stage, dest, sems, s, row).wait_send()


def low_lanes(x):
    return lax.broadcasted_iota(jnp.int32, x.shape, x.ndim - 1) < HD


def per_head(x):
    low = low_lanes(x)
    a = jnp.sum(jnp.where(low, x, 0.0), axis=-1, keepdims=True)
    b = jnp.sum(jnp.where(low, 0.0, x), axis=-1, keepdims=True)
    return jnp.where(low, a, b) * (1.0 / HD)


def partner(x):
    lane = lax.rem(lax.broadcasted_iota(jnp.int32, x.shape, x.ndim - 1), HD)
    return jnp.where(lane < HD // 2, pltpu.roll(x, 2 * HD - HD // 2, axis=1), pltpu.roll(x, HD // 2, axis=1))


def swap(x):
    return pltpu.roll(x, HD, axis=1)


def rope_forward(x, gain, cos, sin):
    y = x * lax.rsqrt(per_head(x * x) + epsilon) * gain
    return y * cos + partner(y) * sin


def rope_backward(x, gain, cos, sin, grad):
    inv = lax.rsqrt(per_head(x * x) + epsilon)
    g = grad * cos - partner(grad) * sin
    scaled = g * gain
    out = scaled * inv - x * (inv * inv * inv) * per_head(scaled * x)
    return out, jnp.sum(g * x * inv, axis=0, keepdims=True)


def split_heads(x, upper):
    x = x.astype(f32)
    low = low_lanes(x)
    if upper:
        return jnp.where(low, 0.0, swap(x)).astype(bf16), jnp.where(low, 0.0, x).astype(bf16)
    return jnp.where(low, x, 0.0).astype(bf16), jnp.where(low, swap(x), 0.0).astype(bf16)


def probabilities(q, keys, first, length):
    s = dot(q, keys, 1, 1)
    at = lax.broadcasted_iota(jnp.int32, s.shape, 1)
    row = lax.broadcasted_iota(jnp.int32, s.shape, 0) + first
    s = jnp.where((at <= row) & (at < length), s, -1e30)
    e = jnp.exp(s - jnp.max(s, axis=1, keepdims=True))
    return e * (1.0 / jnp.sum(e, axis=1, keepdims=True))


def key_bound(i, slots):
    return min(-(-(i + 1) * slots // 128) * 128, 4 * slots)


def attention_forward_kernel(sh, sides, x_ref, gain_ref, w_all, cos_ref, sin_ref, gq_ref, gk_ref, len_ref,
                             out_ref, n_out, raw_out, seq_out, att_out,
                             raw_ref, seq_ref, att_ref, buf, stage, q2, kv, o, back, part, xr, ys, yr, sems, zsems, osem):
    c = lax.axis_index("cols")
    slots = 4 * sh
    w_ref, wo_ref = w_all.at[pl.ds(0, 4 * HD)], w_all.at[pl.ds(4 * HD, 2 * HD)]
    put_own(buf, sh, norm_own(x_ref, gain_ref))
    greet()
    start_gather(buf, sh, sems)
    start_sides(sides)
    low = low_lanes(gq_ref[...])

    def step(m, carry):
        arrive(buf, sh, sems, m)
        pm, hm = place(m)
        y = dot(flat(buf[pm, :, hm]), w_ref[...], 1, 1)
        raw_ref[pm, :, hm] = y.reshape(raw_ref.shape[1], 2 * sh, 4 * HD)
        for i in range(stage.shape[1]):
            rows = slice(i * 2 * sh, (i + 1) * 2 * sh)
            cos, sin = cos_ref[hm], sin_ref[hm]
            q = rope_forward(y[rows, : 2 * HD], gq_ref[...], cos, sin) * (HD**-0.5)
            raw = y[rows, 2 * HD :]
            k = rope_forward(raw, gk_ref[...], cos, sin)
            stage[m, i, :, : 2 * HD] = q.astype(bf16)
            stage[m, i, :, 2 * HD :] = jnp.where(low, k, raw).astype(bf16)
        send_out(stage, seq_ref, zsems, m)
        return carry

    lax.fori_loop(0, 4, step, 0)
    saves = save_all(osem, (buf, n_out), (raw_ref, raw_out))
    wait_out(stage, seq_ref, zsems)
    relay_sides(sides, 0)
    start_sides(sides, 1)
    for i in range(4):
        for h in range(2):
            kv[i, h] = seq_ref[i, h, :, 2 * HD :]
            a, b = split_heads(seq_ref[i, h, :, : 2 * HD], False)
            q2[i, 0, h], q2[i, 1, h] = a, b
    length = len_ref[0]
    for i in range(4):
        bound = key_bound(i, slots)

        def tile(u, carry, i=i, bound=bound):
            head, h = u // 2, lax.rem(u, 2)
            keys = kv[...].reshape(4 * slots, 2 * HD)[:bound]
            p = probabilities(q2[i, head, h], keys, i * slots + h * 2 * sh, length)
            o[head, h] = dot(p.astype(bf16), keys, 1, 0)
            return carry

        lax.fori_loop(0, 4, tile, 0)
        for h in range(2):
            back[i, h] = jnp.where(low, swap(o[0, h]), o[1, h]).astype(bf16)
        send_back(back, att_ref, zsems, i)
    wait_back(back, att_ref, zsems)
    saves += save_all(osem, (seq_ref, seq_out), (att_ref, att_out), first=2)
    relay_sides(sides, 1)
    start_sides(sides, 2)

    def merge_step(i, carry):
        m = 3 - i
        pm, hm = place(m)
        pl.when(i == 3)(lambda: relay_sides(sides, 2))
        y = flat(att_ref[pm, :, hm])

        def multiply(at):
            part[m, :, :, at] = dot(y, wo_ref[:, at], 1, 0).reshape(part.shape[1], part.shape[2], 256)

        columns(D, multiply)
        across_copy(part, xr, sh, sems, m).start()

        @pl.when(m < 3)
        def _():
            scatter(part, xr, ys, yr, sh, sems, m + 1)

        return carry

    lax.fori_loop(0, 4, merge_step, 0)
    scatter(part, xr, ys, yr, sh, sems, 0)
    out_ref[...] = x_ref[...] + end_scatter(part, xr, ys, yr, sh, sems)
    end_gather(buf, sh, sems)
    end_out(stage, seq_ref, zsems)
    for copy in saves:
        copy.wait()
    finish_sides(sides)


def attention_backward_kernel(sh, sides, grad_ref, x_ref, gain_ref, w_all, cos_ref, sin_ref, gq_ref, gk_ref, len_ref,
                              n_in, raw_in, seq_in, att_in,
                              out_ref, gain_out, head_out, dw_ref,
                              raw_ref, seq_ref, att_ref, buf, nbuf, stage, dseq, q2, do2, kv, dq, dkv, back_q, back_k, dproj_q, dproj_k, gproj,
                              part, xr, ys, yr, sems, zsems, osem):
    c = lax.axis_index("cols")
    slots = 4 * sh
    w_ref, wo_ref = w_all.at[pl.ds(0, 4 * HD)], w_all.at[pl.ds(4 * HD, 2 * HD)]
    tokens = 8 * buf.shape[3]
    loads = save_all(osem, (seq_in, seq_ref), (raw_in, raw_ref), (att_in, att_ref), (n_in, nbuf))
    put_own(buf, sh, grad_ref[...])
    greet()
    start_gather(buf, sh, sems)
    start_sides(sides)
    for copy in loads[:3]:
        copy.wait()
    low = low_lanes(gq_ref[...])
    for i in range(4):
        for h in range(2):
            kv[i, h] = seq_ref[i, h, :, 2 * HD :]
            a, b = split_heads(seq_ref[i, h, :, : 2 * HD], False)
            q2[i, 0, h], q2[i, 1, h] = a, b
    dkv[...] = jnp.zeros_like(dkv)
    head_out[...] = jnp.zeros_like(head_out)

    def step(m, carry):
        arrive(buf, sh, sems, m)
        pm, hm = place(m)
        y = dot(flat(buf[pm, :, hm]), wo_ref[...], 1, 1).astype(bf16)
        stage[m] = y.reshape(stage.shape[1], 2 * sh, 2 * HD)
        send_out(stage, dseq, zsems, m)
        return carry

    lax.fori_loop(0, 4, step, 0)
    wait_out(stage, dseq, zsems)
    relay_sides(sides, 0)
    start_sides(sides, 1)
    length = len_ref[0]
    for i in range(4):
        for h in range(2):
            a, b = split_heads(dseq[i, h], True)
            do2[i, 0, h], do2[i, 1, h] = a, b
    for i in range(4):
        bound = key_bound(i, slots)

        def tile(u, carry, i=i, bound=bound):
            head, h = u // 2, lax.rem(u, 2)
            keys = kv[...].reshape(4 * slots, 2 * HD)[:bound]
            q, do = q2[i, head, h], do2[i, head, h]
            p = probabilities(q, keys, i * slots + h * 2 * sh, length)
            dp = dot(do, keys, 1, 1)
            ds = (p * (dp - jnp.sum(p * dp, axis=1, keepdims=True))).astype(bf16)
            dq[head, h] = dot(ds, keys, 1, 0) * (HD**-0.5)
            dkv[:, :bound] += dot(q, ds, 0, 0) + dot(do, p.astype(bf16), 0, 0)
            return carry

        lax.fori_loop(0, 4, tile, 0)
        for h in range(2):
            back_q[i, h] = jnp.where(low, dq[0, h], swap(dq[1, h])).astype(bf16)
        send_back(back_q, dproj_q, zsems, i)
    grads = dkv[...].T.reshape(4, 2, 2 * sh, 2 * HD)
    for i in range(4):
        back_k[i] = grads[i].astype(bf16)
        send_back(back_k, dproj_k, zsems, i, 4)
    wait_back(back_q, dproj_q, zsems)
    wait_back(back_k, dproj_k, zsems, 4)
    relay_sides(sides, 1)
    start_sides(sides, 2)

    def merge_step(t, carry):
        m = 3 - t
        pm, hm = place(m)
        pl.when(t == 3)(lambda: relay_sides(sides, 2))
        for i in range(stage.shape[1]):
            cos, sin = cos_ref[hm], sin_ref[hm]
            g_q, g_k = dproj_q[pm, i, hm].astype(f32), dproj_k[pm, i, hm].astype(f32)
            raw = raw_ref[pm, i, hm]
            a, ga = rope_backward(raw[:, : 2 * HD], gq_ref[...], cos, sin, g_q)
            b, gb = rope_backward(raw[:, 2 * HD :], gk_ref[...], cos, sin, g_k)
            gproj[pm, i, hm, :, : 2 * HD] = a.astype(bf16)
            gproj[pm, i, hm, :, 2 * HD :] = jnp.where(low, b, g_k).astype(bf16)
            head_out[0:1] += ga
            head_out[1:2] += gb
        y = flat(gproj[pm, :, hm])

        def multiply(at):
            part[m, :, :, at] = dot(y, w_ref[:, at], 1, 0).reshape(part.shape[1], part.shape[2], 256)

        columns(D, multiply)
        across_copy(part, xr, sh, sems, m).start()

        @pl.when(m < 3)
        def _():
            scatter(part, xr, ys, yr, sh, sems, m + 1)

        return carry

    lax.fori_loop(0, 4, merge_step, 0)
    scatter(part, xr, ys, yr, sh, sems, 0)
    loads[3].wait()
    left = gproj[...].reshape(tokens, 4 * HD)
    dw_ref[: 4 * HD] = dot(left, nbuf[...].reshape(tokens, D), 0, 0).astype(bf16)
    left = att_ref[...].reshape(tokens, 2 * HD)
    dw_ref[4 * HD :] = dot(left, buf[...].reshape(tokens, D), 0, 0).astype(bf16)
    n = end_scatter(part, xr, ys, yr, sh, sems)
    norm_back(n, x_ref, gain_ref, grad_ref, out_ref, gain_out)
    end_gather(buf, sh, sems)
    end_out(stage, dseq, zsems)
    finish_sides(sides)


SMEM = pl.BlockSpec(memory_space=pltpu.SMEM)


def attention_forward(cid, x, gain, w, tables, length, sides=()):
    seqs, sh, _ = x.shape
    full = (2, seqs, 2, 2 * sh)
    zshape = (4, 2, 2 * sh)
    return call(
        functools.partial(attention_forward_kernel, sh), "attention_forward", cid,
        (shape(x.shape, f32), shape(full + (D,), bf16), shape(full + (4 * HD,), f32),
         shape(zshape + (4 * HD,), bf16), shape(full + (2 * HD,), bf16)),
        (VMEM, ANY, ANY, ANY, ANY), (VMEM,) * 7 + (SMEM,),
        [
            pltpu.VMEM(full + (4 * HD,), f32), pltpu.VMEM(zshape + (4 * HD,), bf16), pltpu.VMEM(full + (2 * HD,), bf16),
            pltpu.VMEM(full + (D,), bf16), pltpu.VMEM((4, seqs, 2 * sh, 4 * HD), bf16),
            pltpu.VMEM((4, 2, 2, 2 * sh, 2 * HD), bf16), pltpu.VMEM(zshape + (2 * HD,), bf16),
            pltpu.VMEM((2, 2, 2 * sh, 2 * HD), f32), pltpu.VMEM(zshape + (2 * HD,), bf16),
        ] + scatter_scratch(seqs, sh) + [DMA((12, 4)), DMA((4, 8)), DMA((4,))],
        (x, gain, w) + tables + (length,), sides=sides,
    )


def attention_backward(cid, grad, x, gain, w, tables, length, n, raw, seq, att, sides=()):
    seqs, sh, _ = x.shape
    full = (2, seqs, 2, 2 * sh)
    zshape = (4, 2, 2 * sh)
    return call(
        functools.partial(attention_backward_kernel, sh), "attention_backward", cid,
        (shape(x.shape, f32), shape((1, D), f32), shape((2, 2 * HD), f32), shape((6 * HD, D), bf16)),
        (VMEM,) * 4, (VMEM,) * 8 + (SMEM, ANY, ANY, ANY, ANY),
        [
            pltpu.VMEM(full + (4 * HD,), f32), pltpu.VMEM(zshape + (4 * HD,), bf16), pltpu.VMEM(full + (2 * HD,), bf16),
            pltpu.VMEM(full + (D,), bf16), pltpu.VMEM(full + (D,), bf16),
            pltpu.VMEM((4, seqs, 2 * sh, 2 * HD), bf16), pltpu.VMEM(zshape + (2 * HD,), bf16),
            pltpu.VMEM((4, 2, 2, 2 * sh, 2 * HD), bf16), pltpu.VMEM((4, 2, 2, 2 * sh, 2 * HD), bf16),
            pltpu.VMEM(zshape + (2 * HD,), bf16), pltpu.VMEM((2, 2, 2 * sh, 2 * HD), f32),
            pltpu.VMEM((2 * HD, 16 * sh), f32), pltpu.VMEM(zshape + (2 * HD,), bf16), pltpu.VMEM(zshape + (2 * HD,), bf16),
            pltpu.VMEM(full + (2 * HD,), bf16), pltpu.VMEM(full + (2 * HD,), bf16), pltpu.VMEM(full + (4 * HD,), bf16),
        ] + scatter_scratch(seqs, sh) + [DMA((12, 4)), DMA((6, 8)), DMA((4,))],
        (grad, x, gain, w) + tables + (length, n, raw, seq, att), sides=sides,
    )


def edge_send(buf, edge, sh, sems, way, p, i):
    d, c = lax.axis_index("dp"), lax.axis_index("cols")
    pm, hm = place(0)
    at = share(sh, True).start + (sh - 16 if way == 0 else 0)
    to = {"dp": d - lax.rem(d, 2) + p, "rows": i, "cols": c + 1 if way == 0 else c - 1}
    return remote(
        buf.at[pm, :, hm, pl.ds(pl.multiple_of(at, 16), 16)], edge.at[way, pm],
        sems.at[0, way * 8 + p * 4 + i], sems.at[1, way * 8 + pm], to,
    )


def edge_senders(way):
    r, c = lax.axis_index("rows"), lax.axis_index("cols")
    rows, cols = lax.axis_size("rows"), lax.axis_size("cols")
    return (r == rows - 1) & (c < cols - 1) if way == 0 else (r == 0) & (c > 0)


def edges_each(buf, edge, sh, sems, way, act):
    @pl.when(edge_senders(way))
    def _():
        for p in range(2):
            for i in range(4):
                act(edge_send(buf, edge, sh, sems, way, p, i))


def wait_edges(edge, sems, way):
    c = lax.axis_index("cols")
    gets = c > 0 if way == 0 else c < lax.axis_size("cols") - 1

    @pl.when(gets)
    def _():
        for p in range(2):
            part = edge.at[way, p]
            remote(part, part, sems.at[0, way * 8 + p], sems.at[1, way * 8 + p], sibling()).wait_recv()

    @pl.when(jnp.logical_not(gets))
    def _():
        edge[way] = jnp.zeros(edge.shape[1:], bf16)


def window(ref, s, hm, rows):
    return ref[s, pl.ds(pl.multiple_of(hm * rows, 8), rows + 8)]


def convolve(taps, ext, rows):
    return sum(taps[k : k + 1] * ext[8 - (CONV - 1) + k : 8 - (CONV - 1) + k + rows] for k in range(CONV))


def conv_forward_kernel(sh, sides, x_ref, gain_ref, w_in, taps_ref,
                        out_ref, n_out, mixed_out, prod_out, gate_out,
                        wall, wsem, mixed_ref, prod_ref, gate_ref, buf, cmix, edge, part, xr, ys, yr, sems, zsems, osem):
    seqs, rows = buf.shape[1], 2 * sh
    ch = wall.shape[0] // 4
    chan = ch // w_in.shape[0]
    wloads = [
        pltpu.make_async_copy(
            w_in.at[c, pl.ds(g * chan, chan)], wall.at[pl.ds(g * ch + c * chan, chan)], wsem.at[4 * c + g]
        )
        for c in range(w_in.shape[0])
        for g in range(4)
    ]
    for copy in wloads:
        copy.start()
    w_ref, wo_ref = wall.at[pl.ds(0, 3 * ch)], wall.at[pl.ds(3 * ch, ch)]
    slots = 2 * rows
    put_own(buf, sh, norm_own(x_ref, gain_ref))
    greet_box(2)
    for way in (0, 1):
        edges_each(buf, edge, sh, zsems, way, lambda copy: copy.start())
    start_gather(buf, sh, sems)
    start_sides(sides)
    for copy in wloads:
        copy.wait()

    def step(m, carry):
        arrive(buf, sh, sems, m)
        pm, hm = place(m)
        y = dot(flat(buf[pm, :, hm]), w_ref[...], 1, 1)
        mixed_ref[pm, :, hm] = y.reshape(seqs, rows, 3 * ch)
        for i in range(seqs):
            z = y[i * rows : (i + 1) * rows]
            at = pl.ds(pl.multiple_of(8 + hm * rows, 8), rows)
            prod_ref[pm * seqs + i, at] = z[:, :ch] * z[:, 2 * ch :]
        return carry

    lax.fori_loop(0, 4, step, 0)
    saves = save_all(osem, (buf, n_out), (mixed_ref, mixed_out))
    for way in (0, 1):
        wait_edges(edge, zsems, way)
    y = dot(edge[...].reshape(4 * seqs * 16, D), w_ref[...], 1, 1).reshape(2, 2 * seqs, 16, 3 * ch)
    prod_ref[:, :8] = y[0, :, 8:, :ch] * y[0, :, 8:, 2 * ch :]
    gate_ref[...] = y[1, :, :8, ch : 2 * ch]
    saves += save_all(osem, (prod_ref, prod_out), (gate_ref, gate_out), first=2)
    taps = taps_ref[...]

    def merge_step(t, carry):
        m = 3 - t
        pm, hm = place(m)
        for i in range(seqs):
            conv = convolve(taps, window(prod_ref, pm * seqs + i, hm, rows), rows)
            cmix[i] = (mixed_ref[pm, i, hm, :, ch : 2 * ch] * conv).astype(bf16)
        y = flat(cmix[...])

        def multiply(at):
            part[m, :, :, at] = dot(y, wo_ref[:, at], 1, 0).reshape(seqs, rows, 256)

        columns(D, multiply)
        across_copy(part, xr, sh, sems, m).start()

        @pl.when(m < 3)
        def _():
            scatter(part, xr, ys, yr, sh, sems, m + 1)

        return carry

    lax.fori_loop(0, 4, merge_step, 0)
    scatter(part, xr, ys, yr, sh, sems, 0)
    out_ref[...] = x_ref[...] + end_scatter(part, xr, ys, yr, sh, sems)
    end_gather(buf, sh, sems)
    for way in (0, 1):
        edges_each(buf, edge, sh, zsems, way, lambda copy: copy.wait_send())
    for copy in saves:
        copy.wait()
    finish_sides(sides)


def conv_backward_kernel(sh, hook, sides, grad_ref, x_ref, gain_ref, w_in, taps_ref, n_in, mixed_in, prod_in, gate_in,
                         out_ref, gain_out, taps_out, dw_ref,
                         wall, wsem, mixed_ref, prod_ref, gate_ref, buf, nbuf, gext, gmix, gin, cmix, edge, part, xr, ys, yr, sems, zsems, osem):
    seqs, rows = buf.shape[1], 2 * sh
    ch = wall.shape[0] // 4
    chan = ch // w_in.shape[0]
    wloads = [
        pltpu.make_async_copy(
            w_in.at[c, pl.ds(g * chan, chan)], wall.at[pl.ds(g * ch + c * chan, chan)], wsem.at[4 * c + g]
        )
        for c in range(w_in.shape[0])
        for g in range(4)
    ]
    for copy in wloads:
        copy.start()
    w_ref, wo_ref = wall.at[pl.ds(0, 3 * ch)], wall.at[pl.ds(3 * ch, ch)]
    slots = 2 * rows
    tokens = 8 * rows
    loads = save_all(osem, (mixed_in, mixed_ref), (prod_in, prod_ref), (gate_in, gate_ref), (n_in, nbuf))
    put_own(buf, sh, grad_ref[...])
    greet_box(2)
    edges_each(buf, edge, sh, zsems, 1, lambda copy: copy.start())
    start_gather(buf, sh, sems)
    start_sides(sides)
    taps_out[...] = jnp.zeros_like(taps_out)
    for copy in loads[:3] + wloads:
        copy.wait()

    def step(m, carry):
        arrive(buf, sh, sems, m)
        pm, hm = place(m)
        y = dot(flat(buf[pm, :, hm]), wo_ref[...], 1, 1)
        for i in range(seqs):
            z = y[i * rows : (i + 1) * rows]
            gmix[pm, i, hm] = z
            at = pl.ds(pl.multiple_of(hm * rows, 8), rows)
            gext[pm * seqs + i, at] = z * mixed_ref[pm, i, hm, :, ch : 2 * ch]
        return carry

    lax.fori_loop(0, 4, step, 0)
    wait_edges(edge, zsems, 1)
    y = dot(edge[1].reshape(2 * seqs * 16, D), wo_ref[...], 1, 1).reshape(2 * seqs, 16, ch)
    gext[:, slots:] = y[:, :8] * gate_ref[...]
    taps = taps_ref[...]

    def merge_step(t, carry):
        m = 3 - t
        pm, hm = place(m)
        pl.when(t == 1)(lambda: relay_sides(sides))
        for i in range(seqs):
            ext = window(prod_ref, pm * seqs + i, hm, rows)
            conv = convolve(taps, ext, rows)
            g = window(gext, pm * seqs + i, hm, rows)
            gprod = sum(taps[k : k + 1] * g[CONV - 1 - k : CONV - 1 - k + rows] for k in range(CONV))
            for k in range(CONV):
                shifted = ext[8 - (CONV - 1) + k : 8 - (CONV - 1) + k + rows]
                taps_out[k : k + 1] += jnp.sum(g[:rows] * shifted, axis=0, keepdims=True)
            mix = mixed_ref[pm, i, hm]
            gin[pm, i, hm, :, :ch] = (gprod * mix[:, 2 * ch :]).astype(bf16)
            gin[pm, i, hm, :, ch : 2 * ch] = (gmix[pm, i, hm] * conv).astype(bf16)
            gin[pm, i, hm, :, 2 * ch :] = (gprod * mix[:, :ch]).astype(bf16)
            cmix[pm, i, hm] = (mix[:, ch : 2 * ch] * conv).astype(bf16)
        y = flat(gin[pm, :, hm])

        def multiply(at):
            part[m, :, :, at] = dot(y, w_ref[:, at], 1, 0).reshape(seqs, rows, 256)

        columns(D, multiply)
        across_copy(part, xr, sh, sems, m).start()

        @pl.when(m < 3)
        def _():
            scatter(part, xr, ys, yr, sh, sems, m + 1)

        return carry

    lax.fori_loop(0, 4, merge_step, 0)
    scatter(part, xr, ys, yr, sh, sems, 0)
    loads[3].wait()
    left = gin[...].reshape(tokens, 3 * ch)
    dw_ref[: 3 * ch] = dot(left, nbuf[...].reshape(tokens, D), 0, 0).astype(bf16)
    left = cmix[...].reshape(tokens, ch)
    dw_ref[3 * ch :] = dot(left, buf[...].reshape(tokens, D), 0, 0).astype(bf16)
    hook()
    n = end_scatter(part, xr, ys, yr, sh, sems)
    norm_back(n, x_ref, gain_ref, grad_ref, out_ref, gain_out)
    end_gather(buf, sh, sems)
    edges_each(buf, edge, sh, zsems, 1, lambda copy: copy.wait_send())
    finish_sides(sides)


def conv_forward(cid, x, gain, w, taps, sides=()):
    seqs, sh, _ = x.shape
    full = (2, seqs, 2, 2 * sh)
    ch = w.shape[0] * w.shape[1] // 4
    own = [pltpu.VMEM((4 * ch, D), bf16), DMA((4 * w.shape[0],))]
    return call(
        functools.partial(conv_forward_kernel, sh), "conv_forward", cid,
        (shape(x.shape, f32), shape(full + (D,), bf16), shape(full + (3 * ch,), f32),
         shape((2 * seqs, 4 * sh + 8, ch), f32), shape((2 * seqs, 8, ch), f32)),
        (VMEM, ANY, ANY, ANY, ANY), (VMEM, VMEM, ANY, VMEM),
        own + [pltpu.VMEM(full + (3 * ch,), f32), pltpu.VMEM((2 * seqs, 4 * sh + 8, ch), f32),
         pltpu.VMEM((2 * seqs, 8, ch), f32),
         pltpu.VMEM(full + (D,), bf16), pltpu.VMEM((seqs, 2 * sh, ch), bf16), pltpu.VMEM((2, 2, seqs, 16, D), bf16)]
        + scatter_scratch(seqs, sh) + [DMA((12, 4)), DMA((2, 16)), DMA((4,))],
        (x, gain, w, taps), sides=sides,
    )


def band(ref, i, width):
    return ref.at[..., pl.ds(pl.multiple_of(i * width, 128), width)]


def row_pieces(kind, src, dst, here, there):
    rows = lax.axis_size("rows")
    if kind == "weights":
        return src.at[there], band(dst, here, src.shape[2])
    if kind == "tokens":
        sh = src.shape[1] // rows
        return src.at[:, pl.ds(pl.multiple_of(there * sh, 8), sh)], band(dst, here, src.shape[2])
    if kind == "gains":
        return src, band(dst, here, src.shape[1])
    sh = src.shape[1]
    return band(src, there, dst.shape[2]), dst.at[:, pl.ds(pl.multiple_of(here * sh, 8), sh)]


def row_copies(kind, src, dst, sems, i):
    rows = lax.axis_size("rows")
    r = lax.axis_index("rows")
    sends, gets = [], []
    for k in range(1, rows):
        to, come = lax.rem(r + k, rows), lax.rem(r + rows - k, rows)
        a, b = row_pieces(kind, src, dst, r, to)
        sends.append(remote(a, b, sems.at[0, i, k], sems.at[1, i, k], {"rows": to}))
        a, b = row_pieces(kind, src, dst, come, r)
        gets.append(remote(a, b, sems.at[0, i, k], sems.at[1, i, k], {"rows": to}))
    a, b = row_pieces(kind, src, dst, r, r)
    return sends, gets, pltpu.make_async_copy(a, b, sems.at[0, i, 0])


def line_copies(axis, src, dst, sems, i):
    count = lax.axis_size(axis) if axis == "cols" else 2
    at = lax.axis_index(axis)
    low = lax.rem(at, count)
    base = at - low
    sends, gets = [], []
    for k in range(1, count):
        to, come = lax.rem(low + k, count), lax.rem(low + count - k, count)
        sends.append(remote(src, dst.at[low], sems.at[0, i, k], sems.at[1, i, k], {axis: base + to}))
        gets.append(remote(src, dst.at[come], sems.at[0, i, k], sems.at[1, i, k], {axis: base + to}))
    return sends, gets, pltpu.make_async_copy(src, dst.at[low], sems.at[0, i, 0])


def greet_box(pairs):
    barrier = pltpu.get_barrier_semaphore()
    rows, cols = lax.axis_size("rows"), lax.axis_size("cols")
    d, r, c = lax.axis_index("dp"), lax.axis_index("rows"), lax.axis_index("cols")
    for p in range(pairs):
        for i in range(rows):
            for j in range(cols):
                if p + i + j > 0:
                    to = {"dp": d if p == 0 else d + 1 - 2 * lax.rem(d, 2),
                          "rows": lax.rem(r + i, rows), "cols": lax.rem(c + j, cols)}
                    pl.semaphore_signal(barrier, inc=1, device_id=to, device_id_type=MESH)
    pl.semaphore_wait(barrier, pairs * rows * cols - 1)


def attention_spread(src, dst, sems):
    halves, cols, _, width = src.shape
    rows = lax.axis_size("rows")
    r, c = lax.axis_index("rows"), lax.axis_index("cols")
    pair = lax.rem(lax.axis_index("dp"), 2)
    holds = pair == halves * c // rows
    first = lax.rem(halves * c, rows)
    origin = (pair * rows + r) // halves

    def to_all(act, local):
        for h in range(halves):
            for z in range(cols):
                own = (first + h == r) & (z == c)
                here = band(dst, r, width)

                @pl.when(holds & jnp.logical_not(own))
                def _():
                    act(remote(src.at[h, z], here, sems.at[0, h * cols + z], sems.at[1, r],
                               {"rows": first + h, "cols": z}))

                @pl.when(holds & own)
                def _():
                    local(pltpu.make_async_copy(src.at[h, z], here, sems.at[0, h * cols + z]))

    def start():
        to_all(lambda copy: copy.start(), lambda copy: copy.start())

    def end():
        for k in range(rows):
            @pl.when(jnp.logical_not((origin == c) & (k == r)))
            def _():
                got = band(dst, k, width)
                remote(got, got, sems.at[0, 0], sems.at[1, k], {"rows": k, "cols": origin}).wait_recv()
        to_all(lambda copy: copy.wait_send(), lambda copy: copy.wait())

    return start, end


def start_kernel(sides, conv_ref, tok_ref, ffn_ref, down_ref, gain_ref, tap_ref, len_ref,
                 conv_out, tok_out, ffn_out, gain_out, tap_out, len_out, conv_cut, rsems, lsems, zsems):
    barrier = pltpu.get_barrier_semaphore()
    rows, cols = lax.axis_size("rows"), lax.axis_size("cols")
    d, r, c = lax.axis_index("dp"), lax.axis_index("rows"), lax.axis_index("cols")
    to = [{"rows": lax.rem(r + k, rows)} for k in range(1, rows)]
    to += [{"cols": lax.rem(c + k, cols)} for k in range(1, cols)]
    to += [{"dp": d + 1 - 2 * lax.rem(d, 2)}]
    for device in to:
        pl.semaphore_signal(barrier, inc=1, device_id=device, device_id_type=MESH)
    pl.semaphore_wait(barrier, len(to))
    conv = row_copies("weights", conv_ref, conv_cut, rsems, 0)
    small = [
        row_copies("gains", gain_ref, gain_out, rsems, 1),
        line_copies("cols", tap_ref, tap_out, lsems, 0),
        line_copies("dp", len_ref, len_out, lsems, 1),
    ]
    begin_all(conv)
    for work in small:
        begin_all(work)
    tok = row_copies("tokens", tok_ref, tok_out, rsems, 2)
    begin_all(tok)
    end_all(conv)
    conv = Gather.of(conv_cut, lambda z: conv_out.at[z], zsems)
    conv.start()
    first = ffn_ref.shape[1]
    ffn = row_copies("weights", ffn_ref, ffn_out.at[pl.ds(0, first)], rsems, 3)
    begin_all(ffn)
    down = row_copies("weights", down_ref, ffn_out.at[pl.ds(first, down_ref.shape[1])], rsems, 4)
    begin_all(down)
    for work in small + [tok]:
        end_all(work)
    conv.relay()
    end_all(ffn)
    end_all(down)
    conv.finish()


def second_kernel(sides, attn_ref, ffn_ref, down_ref, attn_out, ffn_out, asems, rsems):
    greet_box(1)
    begin, end = attention_spread(attn_ref, attn_out, asems)
    start_sides(sides)
    begin()
    first = ffn_ref.shape[1]
    ffn = row_copies("weights", ffn_ref, ffn_out.at[pl.ds(0, first)], rsems, 0)
    begin_all(ffn)
    down = row_copies("weights", down_ref, ffn_out.at[pl.ds(first, down_ref.shape[1])], rsems, 1)
    begin_all(down)
    end()
    end_all(ffn)
    end_all(down)
    finish_sides(sides)


def start_exchange(cid, conv, tok, ffn, down, gain, tap, length, rows, cols):
    outs = (
        shape((cols, conv.shape[1], D), bf16), shape((tok.shape[0], tok.shape[1] // rows, D), f32),
        shape((ffn.shape[1] + down.shape[1], D), bf16), shape((8, D), f32), shape((cols,) + tap.shape, f32),
        shape((2,) + length.shape, length.dtype),
    )
    return call(
        start_kernel, "start", cid, outs, (ANY,) * 6, (ANY,) * 7,
        [pltpu.VMEM((conv.shape[1], D), bf16), DMA((2, 5, 4)), DMA((2, 2, 4)), DMA((2, 5))],
        (conv, tok, ffn, down, gain, tap, length),
    )


def second_exchange(cid, attn, ffn, down, sides):
    return call(
        second_kernel, "second", cid,
        (shape((attn.shape[2], D), bf16), shape((ffn.shape[1] + down.shape[1], D), bf16)), (ANY,) * 2, (ANY,) * 3,
        [DMA((2, 8)), DMA((2, 2, 4))], (attn, ffn, down), sides=sides,
    )


def plane_peer(j):
    pm, hm = place(j // 2)
    d, r = lax.axis_index("dp"), lax.axis_index("rows")
    row = hm * 2 + lax.rem(lax.rem(r, 2) + j % 2, 2)
    return pm, row, {"dp": d - lax.rem(d, 2) + pm, "rows": row}


class Plane:
    def __init__(self, src, dst, lo, w, sems):
        rows = lax.axis_size("rows")
        d, r = lax.axis_index("dp"), lax.axis_index("rows")
        pair = lax.rem(d, 2)
        n, width = src.shape[0], dst.shape[2]
        other = {"dp": d + 1 - 2 * pair}
        self.steps, self.gets = [], []
        for i, (g, at, here, n) in enumerate(segments(lo, src.shape[0], w)):

            def block(p, row, g=g, at=at, n=n):
                return dst.at[g, pl.ds(pl.multiple_of((p * rows + row) * w + at, 16), n)]

            def piece(row, here=here, n=n):
                return band(src.at[pl.ds(here, n)], row, width)

            sem = sems.at[i]
            local = pltpu.make_async_copy(piece(r), block(pair, r), sem.at[0, 0])
            sends = [local]
            turns = [(local, True, remote(block(pair, r), block(pair, r), sem.at[2, 0], sem.at[3, 0], other))]
            self.gets.append(
                remote(block(1 - pair, r), block(1 - pair, r), sem.at[2, 0], sem.at[3, 0], other)
            )
            for k in range(1, rows):
                to, come = lax.rem(r + k, rows), lax.rem(r + rows - k, rows)
                send = remote(piece(to), block(pair, r), sem.at[0, k], sem.at[1, k], {"rows": to})
                get = remote(piece(to), block(pair, come), sem.at[0, k], sem.at[1, k], {"rows": to})
                on = remote(block(pair, come), block(pair, come), sem.at[2, k], sem.at[3, k], other)
                sends.append(send)
                turns.append((get, False, on))
                self.gets.append(
                    remote(block(1 - pair, come), block(1 - pair, come), sem.at[2, k], sem.at[3, k], other)
                )
            self.steps.append((sends, turns))

    def start(self):
        for sends, _ in self.steps:
            for copy in sends:
                copy.start()

    def turn(self):
        for _, turns in self.steps:
            for get, local, on in turns:
                if local:
                    get.wait()
                else:
                    get.wait_recv()
                on.start()

    def finish(self):
        for copy in self.gets:
            copy.wait_recv()
        for sends, turns in self.steps:
            for copy in sends[1:]:
                copy.wait_send()
            for _, _, on in turns:
                on.wait_send()


def conv_finish_kernel(sh, wide, chan, los, chunks, per_col, sides, *refs):
    core, refs = refs[:9], refs[9:]
    gains_ref, heads_ref, ffn_ref, attn_ref = refs[:4]
    arrays, refs = refs[4 : 4 + len(los)], refs[4 + len(los) :]
    o2_ref, o1_ref, oc_ref, os_ref, taps_ref, ot_ref, mid_ref, oa_ref = refs[:8]
    grad_s, gain_s, taps_s, dw_s = refs[8:12]
    conv_scratch, refs = refs[12:31], refs[31:]
    pack, small, srecv, ssum, precv, psems, rsems, ssems, asems, msems = refs[:10]
    scratch = refs[10:]
    rows, cols = lax.axis_size("rows"), lax.axis_size("cols")
    d, c = lax.axis_index("dp"), lax.axis_index("cols")
    pair = lax.rem(d, 2)
    me = pair * rows + lax.axis_index("rows")
    work = [(ffn_ref.at[:, pl.ds(*chunks[0])], o1_ref, chunks[0][0], wide), (pack, oc_ref, 0, chan)]
    work += [(ffn_ref.at[:, pl.ds(lo, n)], o1_ref, lo, wide) for lo, n in chunks[1:]]
    sums = []
    for i, (src, _, _, _) in enumerate(work):
        own = scratch[5 * i : 5 * i + 5]
        sums.append(Reduce.of(src, own[0], own[1:]))
    heads = AttentionReturn(attn_ref, mid_ref, asems, per_col)

    class Ahead(Side):
        phase = 0

        def start(self):
            heads.start()
            sums[0].start()

        def relay(self):
            sums[0].relay()

        def finish(self):
            pass

    def hook():
        count = dw_s.shape[0] // (cols * chan)
        for g in range(count):
            for z in range(cols):
                pack[z, g * chan : (g + 1) * chan] = dw_s[(g * cols + z) * chan : (g * cols + z + 1) * chan]
        for one in sums[1:]:
            one.start_far()
        for one in sums[1:]:
            one.start_near()

    conv_backward_kernel(sh, hook, [Ahead()], *core, grad_s, gain_s, taps_s, dw_s, *conv_scratch)
    planes = [Plane(a, o2_ref, lo, wide, psems.at[i]) for i, (a, lo) in enumerate(zip(arrays, los))]
    count = len(planes)
    for plane in planes:
        plane.start()
    for one in sums[1:]:
        one.relay()
    small[0:1] = gain_s[...]
    small[1:4] = gains_ref[...]
    small[4:5] = heads_ref[...]
    small[5:8] = jnp.zeros((3, D), f32)
    small[5:8, : taps_s.shape[1]] = taps_s[...]
    line = line_copies("cols", small, srecv, ssems, 0)
    begin_all(line)
    tok = row_copies("back", grad_s, ot_ref, rsems, 0)
    begin_all(tok)
    sums[0].finish()
    last = [Plane(sums[0].out, o1_ref, chunks[0][0], wide, psems.at[count])]
    last[0].start()
    for plane in planes:
        plane.turn()
    heads.finish()
    holds = per_col * c // rows == pair
    share_copy = remote(mid_ref, oa_ref, msems.at[0], msems.at[1], {"dp": d + 1 - 2 * pair})
    keep_copy = pltpu.make_async_copy(mid_ref, oa_ref, msems.at[2])

    @pl.when(holds)
    def _():
        share_copy.start()
        keep_copy.start()

    for i in range(1, len(work)):
        sums[i].finish()
        last[-1].turn()
        last.append(Plane(sums[i].out, work[i][1], work[i][2], work[i][3], psems.at[count + i]))
        last[-1].start()
    end_all(line)
    ssum[...] = jnp.sum(srecv[...], axis=0)
    precv[me] = ssum[...]
    for j in range(1, 8):
        to = plane_peer(j)[2]
        remote(ssum, precv.at[me], ssems.at[2, 0, j], ssems.at[3, 0, j], to).start()
    last[-1].turn()
    for j in range(1, 8):
        pm, row, to = plane_peer(j)
        copy = remote(ssum, precv.at[pm * rows + row], ssems.at[2, 0, j], ssems.at[3, 0, j], to)
        copy.wait_recv()
        copy.wait_send()
    os_ref[...] = jnp.sum(precv[...], axis=0)
    taps_ref[...] = precv[:, :, : taps_s.shape[1]]
    end_all(tok)
    for plane in planes + last:
        plane.finish()

    @pl.when(holds)
    def _():
        share_copy.wait_send()
        keep_copy.wait()

    @pl.when(jnp.logical_not(holds))
    def _():
        share_copy.wait_recv()


def conv_finish(cid, core, gains, heads, ffn, attn, arrays, los, chunks, wide, chan, per_col):
    seqs, sh, _ = core[1].shape
    w = core[3]
    cols, rows = lax.axis_size("cols"), lax.axis_size("rows")
    feat = D // rows
    full = (2, seqs, 2, 2 * sh)
    ch = cols * chan
    nc = w.shape[1]
    quarter = (per_col, cols, attn.shape[0], feat)
    outs = (
        shape((3, 8 * wide, feat), bf16), shape((3, 8 * wide, feat), bf16), shape((nc // chan, 8 * chan, feat), bf16),
        shape((8, D), f32), shape((8, 8, ch), f32), shape((seqs, sh * rows, feat), f32),
        shape(quarter, bf16), shape(quarter, bf16),
    )
    scratch = [
        pltpu.VMEM((seqs, sh, D), f32), pltpu.VMEM((1, D), f32), pltpu.VMEM((CONV, ch), f32),
        pltpu.VMEM((4 * ch, D), bf16),
        pltpu.VMEM((4 * ch, D), bf16), DMA((4 * cols,)),
        pltpu.VMEM(full + (3 * ch,), f32), pltpu.VMEM((2 * seqs, 4 * sh + 8, ch), f32),
        pltpu.VMEM((2 * seqs, 8, ch), f32),
        pltpu.VMEM(full + (D,), bf16), pltpu.VMEM(full + (D,), bf16),
        pltpu.VMEM((2 * seqs, 4 * sh + 8, ch), f32), pltpu.VMEM(full + (ch,), f32),
        pltpu.VMEM(full + (3 * ch,), bf16), pltpu.VMEM(full + (ch,), bf16), pltpu.VMEM((2, 2, seqs, 16, D), bf16),
    ] + scatter_scratch(seqs, sh) + [DMA((12, 4)), DMA((2, 16)), DMA((4,))]
    scratch += [
        pltpu.VMEM((cols, nc, D), bf16), pltpu.VMEM((8, D), f32), pltpu.VMEM((cols, 8, D), f32),
        pltpu.VMEM((8, D), f32), pltpu.VMEM((8, 8, D), f32),
        DMA((len(arrays) + len(chunks) + 1, 4, 4, 4)), DMA((2, 1, 4)), DMA((4, 1, 8)), DMA((4, 8)), DMA((3,)),
    ]
    for n in [chunks[0][1], nc] + [n for _, n in chunks[1:]]:
        scratch += [pltpu.VMEM((n, D), bf16)] + Reduce.buffers(n)
    return call(
        functools.partial(conv_finish_kernel, sh, wide, chan, los, chunks, per_col), "conv_finish", cid, outs,
        (ANY, ANY, ANY, VMEM, VMEM, ANY, ANY, ANY),
        (VMEM, VMEM, VMEM, ANY, VMEM) + (ANY,) * 4 + (VMEM, VMEM) + (ANY,) * (2 + len(arrays)), scratch,
        tuple(core) + (gains, heads, ffn, attn) + tuple(arrays),
    )


def turn_kernel(x1_ref, x2_ref, xc_ref, xa_ref, *refs):
    outs, (x1, x2, xc, xa), bufs, sem = refs[:9], refs[9:13], refs[13:22], refs[22]
    loads = save_all(sem, (xc_ref, xc), (xa_ref, xa), (x1_ref, x1), (x2_ref, x2))
    loads[0].wait()
    for g in range(3):
        bufs[4][g] = xc[g].astype(f32).T
    bufs[5][...] = xc[3].astype(f32)
    loads[1].wait()
    q, k = 2 * HD, HD
    for h in range(2):
        bufs[6][:, h * q : (h + 1) * q] = xa[h, :q].astype(f32).T
        bufs[8][h * q : (h + 1) * q] = xa[h, q + 2 * k :].astype(f32)
        at = slice(q + h * k, q + (h + 1) * k)
        both = jnp.concatenate([xa[0, at], xa[1, at]], axis=0)
        bufs[7][:, h, :] = both.astype(f32).T
    stores = save_all(sem, *zip(bufs[4:], outs[4:]), first=4)
    for n, (load, x) in enumerate(((loads[2], x1), (loads[3], x2))):
        load.wait()
        a, b = bufs[2 * n], bufs[2 * n + 1]
        for lo in range(0, x.shape[1], 128):
            at = slice(lo, lo + 128)
            for g in range(2):
                a[:, g, at] = x[g, at].astype(f32).T
            b[at] = x[2, at].astype(f32)
        stores += save_all(sem, (a, outs[2 * n]), (b, outs[2 * n + 1]), first=9 + 2 * n)
    for copy in stores:
        copy.wait()


def turn(x1, x2, xc, xa):
    _, n, feat = x1.shape
    m = xc.shape[1]
    out = (shape((feat, 2, n), f32), shape((n, feat), f32)) * 2 + (
        shape((3, feat, m), f32), shape((m, feat), f32),
        shape((feat, 4 * HD), f32), shape((feat, 2, 2 * HD), f32), shape((4 * HD, feat), f32),
    )
    args = (x1, x2, xc, xa)
    return pl.pallas_call(
        turn_kernel, name="turn", out_shape=out, in_specs=[ANY] * 4, out_specs=(ANY,) * 9,
        scratch_shapes=[pltpu.VMEM(x.shape, bf16) for x in args] + [pltpu.VMEM(x.shape, f32) for x in out] + [DMA((13,))],
        compiler_params=pltpu.CompilerParams(vmem_limit_bytes=LIMIT << 20),
    )(*args)


def per_device(
    hidden_in, lengths, conv_norm, conv_in, conv_kernel, conv_out, conv_ffn_norm, conv_ffn_in,
    conv_ffn_out, attn_norm, attn_q, attn_kv, q_gain, k_gain, attn_out, attn_ffn_norm,
    attn_ffn_in, attn_ffn_out, grad_out,
):
    rows, cols, dps = lax.axis_size("rows"), lax.axis_size("cols"), lax.axis_size("dp")
    tp = 2 * rows
    r, c, d = lax.axis_index("rows"), lax.axis_index("cols"), lax.axis_index("dp")
    pair = lax.rem(d, 2)
    me = pair * rows + r
    slots, seqs, feat = hidden_in.shape
    sh = slots // rows

    def halves(x, axis):
        return lax.dynamic_slice_in_dim(x, pair * rows, rows, axis)

    def cut_in(w):
        parts, width = w.shape[1], w.shape[2] // tp
        x = w.astype(bf16).transpose(1, 2, 0).reshape(parts, tp, width, feat)
        return halves(x, 1).transpose(1, 0, 2, 3).reshape(rows, parts * width, feat)

    def cut_out(w):
        return halves(w.astype(bf16).reshape(tp, -1, feat), 0)

    def cut(w_in, w_out):
        return jnp.concatenate([cut_in(w_in), cut_out(w_out)], axis=1)

    wide = conv_ffn_in.shape[2] // tp
    chan = conv_in.shape[2] // tp
    channels = cols * chan
    slot_ids = c * slots + jnp.arange(slots, dtype=jnp.int32)
    keep = (slot_ids[None, :] < lengths[:, None]).astype(f32)[:, :, None]
    gains_own = jnp.stack([conv_norm, conv_ffn_norm, attn_norm, attn_ffn_norm])
    conv_all, begin, ffn1_cut, gains, taps, lens = start_exchange(
        1, cut(conv_in, conv_out), hidden_in.transpose(1, 0, 2) * keep, cut_in(conv_ffn_in), cut_out(conv_ffn_out),
        jnp.pad(gains_own, ((0, 4), (0, 0))), jnp.pad(conv_kernel, ((0, 8 - CONV), (0, 0))),
        jnp.pad(lengths[None], ((0, 7), (0, 128 - seqs))), rows, cols,
    )
    gains = gains[:4, None]
    kern = lax.dynamic_slice_in_dim(taps[:, :CONV], me * chan, chan, 2)
    kern = kern.transpose(1, 0, 2).reshape(CONV, channels)
    length = lax.dynamic_slice_in_dim(lens[:, 0, :seqs].reshape(2 * seqs), c, 1)

    per_col = tp // cols
    q_w = attn_q.shape[1] // per_col
    kv_w = attn_kv.shape[2] // per_col
    parts = jnp.concatenate(
        [
            attn_q.astype(bf16).T.reshape(per_col, q_w, feat),
            attn_kv[:, 0].astype(bf16).T.reshape(per_col, kv_w, feat),
            attn_kv[:, 1].astype(bf16).T.reshape(per_col, kv_w, feat),
            attn_out.astype(bf16).reshape(per_col, q_w, feat),
        ],
        axis=1,
    )
    w_ffn1 = lax.all_gather(ffn1_cut, "cols", axis=0)

    def after(x, y):
        return lax.optimization_barrier((x, y))[0]

    after_conv, n_conv, mixed, product, gate_edge = conv_forward(3, begin, gains[0], conv_all, kern)
    attn_cut, ffn2_cut = second_exchange(
        2, after(parts, after_conv).reshape(per_col, cols, -1, feat), cut_in(after(attn_ffn_in, after_conv)),
        cut_out(after(attn_ffn_out, after_conv)), ()
    )
    f2_rows = SECOND_ROWS
    f2_at = [sum(f2_rows[:i]) for i in range(4)]
    after_ffn, n_1, gu_1, w_1, attn_all, f2_a = ffn_forward(
        4, after_conv, gains[1], (w_ffn1,), wide,
        [Gather(attn_cut, 0, attn_cut.shape[0]), Gather(ffn2_cut, f2_at[0], f2_rows[0])],
    )
    attn_all = attn_all.reshape(-1, D)
    frequency = jnp.power(rope_base, -(jnp.arange(HD // 2, dtype=f32) * 2.0) / HD)
    angles = slot_ids.astype(f32)[:, None] * frequency[None, :]
    cos, sin = jnp.cos(angles), jnp.sin(angles)
    tables = (
        jnp.concatenate([cos] * 4, axis=1).reshape(2, 2 * sh, 2 * HD),
        jnp.concatenate([-sin, sin] * 2, axis=1).reshape(2, 2 * sh, 2 * HD),
        jnp.tile(q_gain, 2)[None],
        jnp.tile(k_gain, 2)[None],
    )
    after_attn, n_attn, raw, seq, attended, grad_final, f2_b, f2_c, f2_d = attention_forward(
        5, after_ffn, gains[2], attn_all, tables, length,
        [
            Rows("tokens", grad_out.transpose(1, 0, 2) * keep, 1),
            Gather(ffn2_cut, f2_at[1], f2_rows[1], 0), Gather(ffn2_cut, f2_at[2], f2_rows[2], 1),
            Gather(ffn2_cut, f2_at[3], f2_rows[3], 2),
        ],
    )
    final, grad_attn_res, gain_p3, dw_2 = ffn_both(
        6, after_attn, gains[3], grad_final, (f2_a, f2_b, f2_c, f2_d), wide, ffn2_cut
    )

    def over_pairs(x):
        return x if dps == 2 else lax.psum(x * jnp.asarray(0.5, x.dtype), "dp")

    def native(x):
        return x[:-1].transpose(2, 0, 1).astype(f32), x[-1].astype(f32)

    b2_rows, b1_rows = SECOND_BACK, FIRST_BACK
    b2_at = [sum(b2_rows[:i]) for i in range(4)]
    grad_after_ffn, gain_p2, head_parts, grad_attn, final_here, r2_a, r2_b, r2_c = attention_backward(
        8, grad_attn_res, after_ffn, gains[2], attn_all, tables, length, n_attn, raw, seq, attended,
        [Rows("back", final, 1), Reduce(dw_2, 0, b2_rows[0], 0),
         Reduce(dw_2, b2_at[1], b2_rows[1], 1), Reduce(dw_2, b2_at[2], b2_rows[2], 2)],
    )
    grad_attn = grad_attn.reshape(cols, -1, D)
    grad_after_conv, gain_p1, dw_1, r_attn, r2_d = ffn_backward(
        9, grad_after_ffn, after_conv, gains[1], w_1, n_1, gu_1, wide, cols,
        [Reduce(grad_attn, 0, grad_attn.shape[1]), Reduce(dw_2, b2_at[3], b2_rows[3])],
    )
    output = (final_here * keep).transpose(1, 0, 2)
    zero = jnp.zeros((), jnp.int32)
    heads = jnp.concatenate([head_parts[:1, :HD] + head_parts[:1, HD:], head_parts[1:, :HD]], axis=1)
    got2, got1, got0, sums, taps_all, grad_here, _, got_a = conv_finish(
        10, (grad_after_conv, begin, gains[0], conv_all, kern, n_conv, mixed, product, gate_edge),
        jnp.concatenate([gain_p1, gain_p2, gain_p3]), jnp.pad(heads, ((0, 0), (0, D - 2 * HD))), dw_1, r_attn,
        (r2_a, r2_b, r2_c, r2_d), b2_at, [(sum(b1_rows[:i]), n) for i, n in enumerate(b1_rows)], wide, chan, per_col,
    )
    got2, got1, got0, got_a, sums, taps_all = (over_pairs(x) for x in (got2, got1, got0, got_a, sums, taps_all))
    assert per_col == 2 and q_w == 2 * HD and kv_w == HD
    got_a = got_a.reshape(per_col, -1, feat)
    g_attn_ffn_in, g_attn_ffn_out, g_conv_ffn_in, g_conv_ffn_out, g_conv_in, g_conv_out, g_q, g_kv, g_aout = turn(
        got2, got1, got0, got_a
    )
    g_conv_in = g_conv_in.transpose(1, 0, 2)
    grad_in = (grad_here * keep).transpose(1, 0, 2)
    g_gain = lax.dynamic_slice(sums, (zero, r * feat), (4, feat))
    g_kern = lax.dynamic_slice(taps_all, (zero, jnp.int32(5), c * chan), (tp, CONV, chan))
    g_kern = g_kern.transpose(1, 0, 2).reshape(conv_kernel.shape)
    return (
        output, grad_in, g_gain[0], g_conv_in, g_kern, g_conv_out, g_gain[1],
        g_conv_ffn_in, g_conv_ffn_out, g_gain[2], g_q, g_kv, sums[4, :HD], sums[4, HD : 2 * HD], g_aout,
        g_gain[3], g_attn_ffn_in, g_attn_ffn_out,
    )


def solution(mesh):
    tokens, vec, mat = P("cols", "dp", "rows"), P("rows"), P("rows", "cols")
    mat3, out, taps = P("rows", None, "cols"), P("cols", "rows"), P(None, "cols")
    weights = (vec, mat3, taps, out, vec, mat3, out, vec, mat, mat3, P(), P(), out, vec, mat3, out)
    return jax.shard_map(
        per_device,
        mesh=mesh,
        in_specs=(tokens, P("dp")) + weights + (tokens,),
        out_specs=(tokens, tokens) + weights,
        check_vma=False,
    )
```
